32 devices in a mesh: dp: 8 (over z, y), rows: 4 (over x, core).
Axes of the slice: x: 2, y: 2, z: 4, core: 2. Of those that a mesh axis runs over, the one named last changes fastest.
Arguments:
- x_views: bfloat16 [128, 2, 8, 7, 2048], P('dp', None, 'rows'), may hold values from -6 to 6
- x_crops: bfloat16 [128, 4, 4, 3, 2048], P('dp', None, 'rows'), may hold values from -6 to 6
- mask_views: int32 [128, 2, 8], P('dp', None, 'rows'), may hold values from 0 to 1, as said below
- mask_crops: int32 [128, 4, 4], P('dp', None, 'rows'), may hold values from 0 to 1, as said below
- w_reduce: float32 [2048, 512], P(('dp', 'rows')), may hold values from -0.125 to 0.125
- w_spatial: float32 [3, 3, 512, 512], P(None, None, ('dp', 'rows')), may hold values from -0.09375 to 0.09375
- w_expand: float32 [512, 2048], P(('dp', 'rows')), may hold values from -0.25 to 0.25
- gain_reduce: float32 [512], P(('dp', 'rows')), may hold values from 0.5 to 2
- shift_reduce: float32 [512], P(('dp', 'rows')), may hold values from -0.5 to 0.5
- gain_spatial: float32 [512], P(('dp', 'rows')), may hold values from 0.5 to 2
- shift_spatial: float32 [512], P(('dp', 'rows')), may hold values from -0.5 to 0.5
- gain_expand: float32 [2048], P(('dp', 'rows')), may hold values from 0.5 to 2
- shift_expand: float32 [2048], P(('dp', 'rows')), may hold values from -0.5 to 0.5
- cot_views: bfloat16 [128, 2, 8, 7, 2048], P('dp', None, 'rows'), may hold values from -6 to 6
- cot_crops: bfloat16 [128, 4, 4, 3, 2048], P('dp', None, 'rows'), may hold values from -6 to 6
- cot_pool_views: float32 [128, 2, 2048], P('dp'), may hold values from -48 to 48
- cot_pool_crops: float32 [128, 4, 2048], P('dp'), may hold values from -48 to 48
Outputs:
- out_views: float32 [128, 2, 8, 7, 2048], P('dp', None, 'rows')
- out_crops: float32 [128, 4, 4, 3, 2048], P('dp', None, 'rows')
- pool_views: float32 [128, 2, 2048], P('dp')
- pool_crops: float32 [128, 4, 2048], P('dp')
- grad_views: float32 [128, 2, 8, 7, 2048], P('dp', None, 'rows')
- grad_crops: float32 [128, 4, 4, 3, 2048], P('dp', None, 'rows')
- grad_w_reduce: float32 [2048, 512], P(('dp', 'rows'))
- grad_w_spatial: float32 [3, 3, 512, 512], P(None, None, ('dp', 'rows'))
- grad_w_expand: float32 [512, 2048], P(('dp', 'rows'))
- grad_gain_reduce: float32 [512], P(('dp', 'rows'))
- grad_shift_reduce: float32 [512], P(('dp', 'rows'))
- grad_gain_spatial: float32 [512], P(('dp', 'rows'))
- grad_shift_spatial: float32 [512], P(('dp', 'rows'))
- grad_gain_expand: float32 [2048], P(('dp', 'rows'))
- grad_shift_expand: float32 [2048], P(('dp', 'rows'))
The draws below stay inside these ranges and needn't reach their ends.
Inputs may be any that keep to these rules, and one draw needn't show every extreme that they name: `mask_views`: each view has exactly one padding row, its first or its last of 8; all other rows are 1. `mask_crops`: each crop has exactly one padding row, its first or its last of 4; all other rows are 1.
All inputs are finite; a program needn't handle non-finite values.
Results may differ from the reference program's by a relative error of at most 0.02.
Values may be sent and summed in bfloat16 or wider, within the bound.
A program may use at most 192 MiB of HBM per device.

```python
import math
import jax
import jax.numpy as jnp
from jax import lax

C = 2048
MID = 512
IMG_DEV = 16
VIEWS = 2
CROPS = 4
VIEW_ROWS = 8
VIEW_COLS = 7
CROP_ROWS = 4
CROP_COLS = 3
IMAGES = 128
N_DP = 8


def padded_rows(key, per_image, row_count):
    offset = jax.random.randint(key, (IMAGES, per_image, 1), 0, 2)
    index = lax.broadcasted_iota(jnp.int32, (IMAGES, per_image, row_count), 2)
    inside = jnp.logical_and(index >= offset, index < offset + row_count - 1)
    return jnp.where(inside, 1, 0).astype(jnp.int32)


def draw_mask_views(key, part):
    return padded_rows(jax.random.fold_in(key, 11), VIEWS, VIEW_ROWS)


def draw_mask_crops(key, part):
    return padded_rows(jax.random.fold_in(key, 23), CROPS, CROP_ROWS)


def level_of(own_key, extent, shards, least, top_value):
    def one(dim, blocks):
        steps = jax.random.uniform(jax.random.fold_in(jax.random.fold_in(own_key, 6), dim), (blocks,), jnp.float32, least / len(shards), top_value / len(shards))
        return jnp.repeat(jnp.exp(steps), extent[dim] // blocks).reshape((-1,) + (1,) * (len(extent) - dim - 1))

    factor_of = one(*shards[0])
    for cut in shards[1:]:
        factor_of = factor_of * one(*cut)
    return factor_of


def normal_values(own_key, dims, deviation, most, split=(), held_as=jnp.bfloat16):
    result = jax.random.normal(own_key, dims, jnp.float32) * deviation
    if len(split) > 0:
        result = level_of(own_key, dims, split, -0.22, 0.18) * result
    return jnp.clip(result, min=-most, max=most).astype(held_as)


def setup_inputs(seed: int = 0) -> dict:
    key_of = jax.random.split(jax.random.key(seed), 18)
    x_views = normal_values(key_of[0], (IMAGES, VIEWS, VIEW_ROWS, VIEW_COLS, C), 1.0, 6.0, ((0, 8), (2, 4)))
    x_crops = normal_values(key_of[1], (IMAGES, CROPS, CROP_ROWS, CROP_COLS, C), 1.0, 6.0, ((0, 8), (2, 4)))
    mask_views = draw_mask_views(jax.random.fold_in(key_of[17], 71), 0)
    mask_crops = draw_mask_crops(jax.random.fold_in(key_of[17], 71), 0)
    w_reduce = normal_values(key_of[4], (C, MID), C ** -0.5, 0.125, ((0, 32),), jnp.float32)
    w_spatial = normal_values(key_of[5], (3, 3, MID, MID), (9 * MID) ** -0.5, 0.09375, ((2, 32),), jnp.float32)
    w_expand = normal_values(key_of[6], (MID, C), MID ** -0.5, 0.25, ((0, 32),), jnp.float32)
    gain_reduce = jnp.clip(jnp.exp(math.log(2.0) - 1.3862944 * jax.random.uniform(key_of[7], (MID,), jnp.float32) ** level_of(key_of[7], (MID,), ((0, 32),), -0.2, 0.2)), 0.5, 2.0)
    shift_reduce = jnp.clip(jax.random.uniform(key_of[8], (MID,), jnp.float32, -0.5, 0.5) * level_of(key_of[8], (MID,), ((0, 32),), -0.4, 0.0), -0.5, 0.5)
    gain_spatial = jnp.clip(jnp.exp(math.log(2.0) - 1.3862944 * jax.random.uniform(key_of[9], (MID,), jnp.float32) ** level_of(key_of[9], (MID,), ((0, 32),), -0.2, 0.2)), 0.5, 2.0)
    shift_spatial = jnp.clip(jax.random.uniform(key_of[10], (MID,), jnp.float32, -0.5, 0.5) * level_of(key_of[10], (MID,), ((0, 32),), -0.4, 0.0), -0.5, 0.5)
    gain_expand = jnp.clip(jnp.exp(math.log(2.0) - 1.3862944 * jax.random.uniform(key_of[11], (C,), jnp.float32) ** level_of(key_of[11], (C,), ((0, 32),), -0.2, 0.2)), 0.5, 2.0)
    shift_expand = jnp.clip(jax.random.uniform(key_of[12], (C,), jnp.float32, -0.5, 0.5) * level_of(key_of[12], (C,), ((0, 32),), -0.4, 0.0), -0.5, 0.5)
    cot_views = normal_values(key_of[13], (IMAGES, VIEWS, VIEW_ROWS, VIEW_COLS, C), 1.0, 6.0, ((0, 8), (2, 4)))
    cot_crops = normal_values(key_of[14], (IMAGES, CROPS, CROP_ROWS, CROP_COLS, C), 1.0, 6.0, ((0, 8), (2, 4)))
    cot_pool_views = normal_values(key_of[15], (IMAGES, VIEWS, C), 8.0, 48.0, ((0, 8),), jnp.float32)
    cot_pool_crops = normal_values(key_of[16], (IMAGES, CROPS, C), 8.0, 48.0, ((0, 8),), jnp.float32)
    return {"x_views": x_views, "x_crops": x_crops, "mask_views": mask_views, "mask_crops": mask_crops, "w_reduce": w_reduce, "w_spatial": w_spatial, "w_expand": w_expand, "gain_reduce": gain_reduce, "shift_reduce": shift_reduce, "gain_spatial": gain_spatial, "shift_spatial": shift_spatial, "gain_expand": gain_expand, "shift_expand": shift_expand, "cot_views": cot_views, "cot_crops": cot_crops, "cot_pool_views": cot_pool_views, "cot_pool_crops": cot_pool_crops}


eps = 1e-05

@jax.custom_vjp
def low(v):
    return lax.optimization_barrier(v.astype(jnp.bfloat16)).astype(jnp.float32)

@jax.custom_vjp
def low_back(v):
    return v

def low_keep(v):
    return (low(v), None)

def low_pass(kept, grad):
    return (grad,)

def back_keep(v):
    return (v, None)

def back_low(kept, grad):
    return (low(grad),)
low.defvjp(low_keep, low_pass)
low_back.defvjp(back_keep, back_low)

def dot_high(left, right):
    return jnp.dot(left, right, precision=lax.Precision.HIGHEST, preferred_element_type=jnp.float32)

def conv_point(feature_map, weight):
    full_shape = feature_map.shape
    flat = dot_high(feature_map.reshape(-1, full_shape[-1]), weight)
    return flat.reshape(full_shape[:-1] + (weight.shape[1],))

def conv_square(feature_map, weight):
    row_count, col_count = (feature_map.shape[2], feature_map.shape[3])
    padded = jnp.pad(feature_map, ((0, 0), (0, 0), (1, 1), (1, 1), (0, 0)))
    total = jnp.zeros(feature_map.shape[:4] + (weight.shape[3],), jnp.float32)
    for row_step in range(3):
        for col_step in range(3):
            window = padded[:, :, row_step:row_step + row_count, col_step:col_step + col_count, :]
            total = total + conv_point(window, weight[row_step, col_step])
    return total

def batch_norm(acts, mask_map, gain_vec, shift_vec):
    valid = jnp.sum(mask_map) * acts.shape[3]
    mean = lax.optimization_barrier(jnp.sum(acts * mask_map, axis=(0, 1, 2, 3))) / valid
    centered = (acts - mean) * mask_map
    variance = lax.optimization_barrier(jnp.sum(centered * centered, axis=(0, 1, 2, 3))) / valid
    return (acts - mean) * lax.rsqrt(variance + eps) * gain_vec + shift_vec

def block_forward(params, view_maps, crop_maps, view_mask, crop_mask):
    weight_one = low(params[0])
    weight_two = low(params[1])
    weight_three = low(params[2])
    gain_one, shift_one, gain_two, shift_two, gain_three, shift_three = [low(entry) for entry in params[3:]]
    results = []
    pools = []
    for inputs, mask_map in ((view_maps, view_mask), (crop_maps, crop_mask)):
        acts_one = low_back(conv_point(inputs, weight_one))
        hidden_one = low(jax.nn.silu(batch_norm(acts_one, mask_map, gain_one, shift_one)) * mask_map)
        acts_two = low_back(conv_square(hidden_one, weight_two))
        hidden_two = low(jax.nn.silu(batch_norm(acts_two, mask_map, gain_two, shift_two)) * mask_map)
        acts_three = low_back(conv_point(hidden_two, weight_three))
        output = jax.nn.silu(inputs + batch_norm(acts_three, mask_map, gain_three, shift_three)) * mask_map
        results.append(output)
        pools.append(lax.optimization_barrier(jnp.sum(output, axis=(2, 3))) / (lax.optimization_barrier(jnp.sum(mask_map, axis=(2, 3))) * inputs.shape[3]))
    return (results[0], results[1], pools[0], pools[1])

def reference(x_views, x_crops, mask_views, mask_crops, w_reduce, w_spatial, w_expand, gain_reduce, shift_reduce, gain_spatial, shift_spatial, gain_expand, shift_expand, cot_views, cot_crops, cot_pool_views, cot_pool_crops):
    params = tuple((entry.astype(jnp.float32) for entry in (w_reduce, w_spatial, w_expand, gain_reduce, shift_reduce, gain_spatial, shift_spatial, gain_expand, shift_expand)))

    def blocks(array):
        return array.reshape((N_DP, IMG_DEV) + array.shape[1:])
    sequence = tuple((blocks(array) for array in (x_views, x_crops, mask_views, mask_crops, cot_views, cot_crops, cot_pool_views, cot_pool_crops)))

    def step(carry, item):
        view_in, crop_in, view_rows, crop_rows, view_cot, crop_cot, view_pool_cot, crop_pool_cot = item
        view_mask = view_rows.astype(jnp.float32)[:, :, :, None, None]
        crop_mask = crop_rows.astype(jnp.float32)[:, :, :, None, None]

        def forward(weights, view_maps, crop_maps):
            return block_forward(weights, view_maps, crop_maps, view_mask, crop_mask)
        outputs, pull = jax.vjp(forward, params, view_in.astype(jnp.float32), crop_in.astype(jnp.float32))
        grads = pull((view_cot.astype(jnp.float32), crop_cot.astype(jnp.float32), view_pool_cot.astype(jnp.float32), crop_pool_cot.astype(jnp.float32)))
        carry = jax.tree.map(lambda before, added: before + added.astype(before.dtype), carry, grads[0])
        return (carry, (outputs[0].astype(jnp.float32), outputs[1].astype(jnp.float32), outputs[2].astype(jnp.float32), outputs[3].astype(jnp.float32), grads[1].astype(jnp.float32), grads[2].astype(jnp.float32)))
    zeros = tuple((jnp.zeros_like(entry) for entry in params))
    totals, stacked = lax.scan(step, zeros, sequence)
    unblocked = tuple((array.reshape((IMAGES,) + array.shape[2:]) for array in stacked))
    return (unblocked[0], unblocked[1], unblocked[2], unblocked[3], unblocked[4], unblocked[5], totals[0], totals[1], totals[2], totals[3], totals[4], totals[5], totals[6], totals[7], totals[8])
```

```python
import functools

import jax
import jax.numpy as jnp
from jax import lax
from jax.experimental import pallas as pl
from jax.experimental.pallas import tpu as pltpu
from jax.sharding import PartitionSpec as P

MESH = pl.DeviceIdType.MESH
ALL = slice(None)
BF = jnp.bfloat16
F32 = jnp.float32
eps = 1e-05
TILE = 256


def lanes(j, width=TILE):
    if isinstance(j, int):
        return slice(j * width, (j + 1) * width)
    return pl.ds(pl.multiple_of(j * width, width), width)


def half(h, width):
    return ALL if h is None else slice(h * (width // 2), (h + 1) * (width // 2))


def dot(a, b):
    return lax.dot_general(a, b, (((1,), (0,)), ((), ())), preferred_element_type=F32)


def dot_t(a, b):
    return lax.dot_general(a, b, (((1,), (1,)), ((), ())), preferred_element_type=F32)


def dot_r(a, b):
    return lax.dot_general(a, b, (((0,), (0,)), ((), ())), preferred_element_type=F32)


def sigmoid(v):
    return 0.5 * jnp.tanh(0.5 * v) + 0.5


class Place:
    def __init__(self, n_dp, n_rows):
        self.ny, self.nc = 2, 2
        self.nz, self.nx = n_dp // 2, n_rows // 2
        self.n_dp, self.n_rows = n_dp, n_rows
        self.dp, self.r = lax.axis_index("dp"), lax.axis_index("rows")
        self.z, self.y = self.dp // 2, self.dp % 2
        self.x, self.c = self.r // 2, self.r % 2

    def dev(self, z, y, x, c):
        return {"dp": z * self.ny + y, "rows": x * self.nc + c}


def remote(src, dst, ssem, rsem, to):
    return pltpu.make_async_remote_copy(
        src_ref=src, dst_ref=dst, send_sem=ssem, recv_sem=rsem, device_id=to, device_id_type=MESH
    )


class Gather:
    def __init__(self, me, view, ssem, rsem, halves=(0, 1)):
        self.me, self.view, self.s, self.r, self.halves = me, view, ssem, rsem, halves

    def cp(self, k, place, to):
        ref = self.view(*place)
        return remote(ref, ref, self.s.at[k], self.r.at[k], self.me.dev(*to))

    def along_z(self, dz, recv):
        me = self.me
        if recv:
            z = (me.z + me.nz - dz) % me.nz
            return self.cp(dz - 1, (z, me.y, me.x, me.c, None), (z, me.y, me.x, me.c))
        to = ((me.z + dz) % me.nz, me.y, me.x, me.c)
        return self.cp(dz - 1, (me.z, me.y, me.x, me.c, None), to)

    def second(self, h, recv):
        me = self.me
        yy, xx = (1 - me.y, me.x) if h == 0 else (me.y, 1 - me.x)
        place = (ALL, yy, xx, me.c, h) if recv else (ALL, me.y, me.x, me.c, h)
        return self.cp(3 + h, place, (me.z, yy, xx, me.c))

    def third(self, h, recv):
        me = self.me
        if h == 0:
            return self.cp(
                5, (ALL, ALL, 1 - me.x if recv else me.x, me.c, h), (me.z, me.y, 1 - me.x, me.c)
            )
        return self.cp(
            6, (ALL, 1 - me.y if recv else me.y, ALL, me.c, h), (me.z, 1 - me.y, me.x, me.c)
        )

    def core(self, k, recv):
        me = self.me
        c = 1 - me.c if recv else me.c
        place = (
            (ALL, me.y, me.x, c, None),
            (ALL, 1 - me.y, me.x, c, 0),
            (ALL, me.y, 1 - me.x, c, 1),
            (ALL, ALL, 1 - me.x, c, 0),
            (ALL, 1 - me.y, ALL, c, 1),
        )[k]
        return self.cp(7 + k, place, (me.z, me.y, me.x, 1 - me.c))

    def start(self):
        for dz in range(1, self.me.nz):
            self.along_z(dz, False).start()

    def got_z(self):
        for dz in range(1, self.me.nz):
            self.along_z(dz, True).wait_recv()

    def stage2(self):
        for h in self.halves:
            self.second(h, False).start()
        self.core(0, False).start()

    def stage3(self):
        for h in self.halves:
            self.second(h, True).wait_recv()
            self.third(h, False).start()
            self.core(1 + h, False).start()

    def stage4(self):
        for h in self.halves:
            self.third(h, True).wait_recv()
            self.core(3 + h, False).start()

    def finish(self):
        self.core(0, True).wait_recv()
        for h in self.halves:
            self.core(1 + h, True).wait_recv()
            self.core(3 + h, True).wait_recv()

    def drain(self):
        for dz in range(1, self.me.nz):
            self.along_z(dz, False).wait_send()
        self.core(0, False).wait_send()
        for h in self.halves:
            self.second(h, False).wait_send()
            self.third(h, False).wait_send()
            self.core(1 + h, False).wait_send()
            self.core(3 + h, False).wait_send()


class Reduce:
    def __init__(self, me, view, from_core, from_third, from_second, from_z, ssem, rsem):
        self.me, self.view, self.s, self.r = me, view, ssem, rsem
        self.fc, self.f3, self.f2, self.fz = from_core, from_third, from_second, from_z

    def core(self):
        me = self.me
        return remote(
            self.view(ALL, ALL, ALL, 1 - me.c, None),
            self.fc(ALL, ALL, ALL, None),
            self.s.at[0],
            self.r.at[0],
            me.dev(me.z, me.y, me.x, 1 - me.c),
        )

    def third(self, h):
        me = self.me
        place = (ALL, ALL, 1 - me.x) if h == 0 else (ALL, 1 - me.y, ALL)
        to = (me.z, me.y, 1 - me.x, me.c) if h == 0 else (me.z, 1 - me.y, me.x, me.c)
        return remote(
            self.view(*place, me.c, h), self.f3(h), self.s.at[1 + h], self.r.at[1 + h], me.dev(*to)
        )

    def second(self, h):
        me = self.me
        place = (ALL, 1 - me.y, me.x) if h == 0 else (ALL, me.y, 1 - me.x)
        to = (me.z, 1 - me.y, me.x, me.c) if h == 0 else (me.z, me.y, 1 - me.x, me.c)
        return remote(
            self.view(*place, me.c, h), self.f2(h), self.s.at[3 + h], self.r.at[3 + h], me.dev(*to)
        )

    def along_z(self, dz):
        me = self.me
        z = (me.z + dz) % me.nz
        return remote(
            self.view(z, me.y, me.x, me.c, None),
            self.fz(dz - 1),
            self.s.at[4 + dz],
            self.r.at[4 + dz],
            me.dev(z, me.y, me.x, me.c),
        )

    def start(self):
        self.core().start()

    def stage2(self):
        me = self.me
        self.core().wait_recv()
        for h in (0, 1):
            first = (ALL, ALL, 1 - me.x) if h == 0 else (ALL, 1 - me.y, ALL)
            ref = self.view(*first, me.c, h)
            ref[...] = ref[...] + self.fc(*first, h)[...]
            self.third(h).start()
        for h in (0, 1):
            rest = (ALL, ALL, me.x) if h == 0 else (ALL, me.y, ALL)
            ref = self.view(*rest, me.c, h)
            ref[...] = ref[...] + self.fc(*rest, h)[...]

    def stage3(self):
        me = self.me
        for h in (0, 1):
            self.third(h).wait_recv()
            kept = (ALL, ALL, me.x) if h == 0 else (ALL, me.y, ALL)
            ref = self.view(*kept, me.c, h)
            ref[...] = ref[...] + self.f3(h)[...]
            self.second(h).start()

    def stage4(self):
        me = self.me
        for h in (0, 1):
            self.second(h).wait_recv()
            ref = self.view(ALL, me.y, me.x, me.c, h)
            ref[...] = ref[...] + self.f2(h)[...]
        for dz in range(1, me.nz):
            self.along_z(dz).start()

    def finish(self):
        me = self.me
        total = self.view(me.z, me.y, me.x, me.c, None)[...].astype(F32)
        for dz in range(1, me.nz):
            self.along_z(dz).wait_recv()
            total = total + self.fz(dz - 1)[...].astype(F32)
        return total

    def drain(self):
        self.core().wait_send()
        for h in (0, 1):
            self.third(h).wait_send()
            self.second(h).wait_send()
        for dz in range(1, self.me.nz):
            self.along_z(dz).wait_send()


def kernel(n_dp, n_rows, sizes, *refs):
    (
        xv_h, xc_h, cv_h, cc_h, mask, wr_in, ws_in, we_in,
        g1_in, s1_in, g2_in, s2_in, g3_in, s3_in, cpv, cpc,
        yv_h, yc_h, gv_h, gc_h, pool_o, gwr_o, gws_o, gwe_o, small_o,
        wr, ws, we, par, x, xt, cot, a1, a2, a3, gpre, ysl,
        hv, hc, dv, dc, h2, h2t, ga1, gwr, gws, gwe,
        fc_we, fc_ws, fc_wr, f3_we, f3_ws, f3_wr, f2_we, f2_ws, f2_wr, fz_we, fz_ws, fz_wr,
        p1, p3, mi1, mi2, mi3, cnt, ex1, ex2, ex3, bx1, bx2, bx3, tot1, tot2, tot3,
        pf, pb, pr, sb, rb,
        in_sem, out_sem, ag_s, ag_r, rs_s, rs_r, ex_s, ex_r, halo_s, halo_r, pool_s, pool_r, sm_s, sm_r,
    ) = refs
    (maps_v, cols_v, maps_c, cols_c, valid_v, valid_c) = sizes
    me = Place(n_dp, n_rows)
    mid, wide = a1.shape[1], a3.shape[1]
    pix_v = 2 * cols_v * maps_v
    pix = a1.shape[0]
    row_v, row_c = cols_v * maps_v, cols_c * maps_c
    count = (float(maps_v * valid_v), float(maps_c * valid_c))
    CH = 32
    chunks = [(s, 0 if s < pix_v else 1) for s in range(0, pix, CH)]

    in_copies = [
        pltpu.make_async_copy(xv_h, x.at[0:pix_v], in_sem.at[0]),
        pltpu.make_async_copy(xc_h, x.at[pix_v:pix], in_sem.at[1]),
        pltpu.make_async_copy(cv_h, cot.at[0:pix_v], in_sem.at[2]),
        pltpu.make_async_copy(cc_h, cot.at[pix_v:pix], in_sem.at[3]),
    ]
    for cp in in_copies:
        cp.start()

    here = (me.z, me.y, me.x, me.c)
    wr[here] = wr_in[...].astype(BF)
    ws[(ALL,) + here] = ws_in[...].astype(BF)
    we[here] = we_in[...].astype(BF)
    own = par.at[here]
    own[...] = jnp.zeros(own.shape, F32)
    for i, ref in enumerate((g1_in, s1_in, g2_in, s2_in, g3_in, s3_in)):
        own[i : i + 1, 0 : ref.shape[1]] = ref[...].astype(BF).astype(F32)

    cnt_own = cnt.at[me.r]
    cnt_own[0:1] = jnp.sum(mask[0:pix_v], axis=0, keepdims=True)
    cnt_own[1:2] = jnp.sum(mask[pix_v:pix], axis=0, keepdims=True)
    cnt_own[2:8] = jnp.zeros((6, 128), F32)

    barrier = pltpu.get_barrier_semaphore()
    peers = [{"dp": me.dp, "rows": (me.r + d) % n_rows} for d in range(1, n_rows)]
    peers += [{"dp": (me.dp + d) % n_dp, "rows": me.r} for d in range(1, n_dp)]
    for peer in peers:
        pl.semaphore_signal(barrier, inc=1, device_id=peer, device_id_type=MESH)
    pl.semaphore_wait(barrier, len(peers))

    def piece(k, view, halves=(0, 1)):
        return Gather(me, view, ag_s.at[k], ag_r.at[k], halves)

    small_piece = piece(0, lambda z, y, x, c, h: par.at[z, y, x, c], (0,))
    pieces = [piece(1, lambda z, y, x, c, h: wr.at[z, y, x, c, :, half(h, mid)])]
    for i in range(3):
        pieces.append(
            piece(2 + i, lambda z, y, x, c, h, i=i: ws.at[3 * i : 3 * i + 3, z, y, x, c, :, half(h, mid)])
        )
    pieces.append(piece(5, lambda z, y, x, c, h: we.at[z, y, x, c, :, half(h, wide)]))

    def exchange(k, buf):
        def cp(d, recv):
            peer = (me.r + n_rows - d) % n_rows if recv else (me.r + d) % n_rows
            ref = buf.at[peer if recv else me.r]
            return remote(ref, ref, ex_s.at[k, d - 1], ex_r.at[k, d - 1], {"dp": me.dp, "rows": peer})

        def send():
            for d in range(1, n_rows):
                cp(d, False).start()

        def wait():
            for d in range(1, n_rows):
                cp(d, True).wait_recv()

        def drain():
            for d in range(1, n_rows):
                cp(d, False).wait_send()

        return send, wait, drain

    exchanges = [exchange(k, b) for k, b in enumerate((cnt, ex1, ex2, ex3, bx1, bx2, bx3))]

    def rim(k, v, c):
        def cps(up):
            peer = {"dp": me.dp, "rows": (me.r + n_rows - 1) % n_rows if up else (me.r + 1) % n_rows}
            base = 0 if up else 2
            vs, vd = (1, 3) if up else (2, 0)
            csrc, cd = (1, 2) if up else (1, 0)
            return [
                remote(
                    v.at[vs, maps_v : maps_v + row_v],
                    v.at[vd, maps_v : maps_v + row_v],
                    halo_s.at[k, base],
                    halo_r.at[k, base],
                    peer,
                ),
                remote(
                    c.at[csrc, maps_c : maps_c + row_c],
                    c.at[cd, maps_c : maps_c + row_c],
                    halo_s.at[k, base + 1],
                    halo_r.at[k, base + 1],
                    peer,
                ),
            ]

        def each(up, fn):
            def body():
                for cp in cps(up):
                    fn(cp)

            return body

        first, last = me.r == 0, me.r == n_rows - 1

        def send():
            pl.when(jnp.logical_not(first))(each(True, lambda cp: cp.start()))
            pl.when(jnp.logical_not(last))(each(False, lambda cp: cp.start()))

        def wait():
            pl.when(jnp.logical_not(last))(each(True, lambda cp: cp.wait_recv()))
            pl.when(jnp.logical_not(first))(each(False, lambda cp: cp.wait_recv()))

        def drain():
            pl.when(jnp.logical_not(first))(each(True, lambda cp: cp.wait_send()))
            pl.when(jnp.logical_not(last))(each(False, lambda cp: cp.wait_send()))

        return send, wait, drain

    rim_h, rim_d = rim(0, hv, hc), rim(1, dv, dc)

    def clear_rims(v, c):
        zv, zc = jnp.zeros((maps_v, mid), BF), jnp.zeros((maps_c, mid), BF)
        for r in range(4):
            v[r, 0:maps_v] = zv
            v[r, maps_v + row_v : 2 * maps_v + row_v] = zv
        for r in range(3):
            c[r, 0:maps_c] = zc
            c[r, maps_c + row_c : 2 * maps_c + row_c] = zc

        @pl.when(me.r == 0)
        def _():
            v[0, maps_v : maps_v + row_v] = jnp.zeros((row_v, mid), BF)
            c[0, maps_c : maps_c + row_c] = jnp.zeros((row_c, mid), BF)

        @pl.when(me.r == n_rows - 1)
        def _():
            v[3, maps_v : maps_v + row_v] = jnp.zeros((row_v, mid), BF)
            c[2, maps_c : maps_c + row_c] = jnp.zeros((row_c, mid), BF)

    def tile_rows(ref, j):
        per = me.nz * TILE // mid
        return ref[j * per : (j + 1) * per]

    def fold(v):
        return jnp.sum(v.reshape(v.shape[0] // 8, 8, v.shape[1]), axis=0)

    def put(buf, j, k, value):
        tiles = buf.shape[2] // TILE
        if isinstance(j, int):
            buf[me.r, 4 * (j // tiles) + k : 4 * (j // tiles) + k + 1, lanes(j % tiles)] = value
        else:
            buf[me.r, pl.ds(4 * (j // tiles) + k, 1), lanes(j % tiles)] = value

    def local_stats(a, buf, n_tiles):
        def body(j, carry):
            cols = lanes(j)
            for grp in (0, 1):
                acc = jnp.zeros((8, TILE), F32)
                for s, g in chunks:
                    if g == grp:
                        acc = acc + fold(a[s : s + CH, cols] * mask[s : s + CH, 0:1])
                total = jnp.sum(acc, axis=0, keepdims=True)
                n_own = jnp.maximum(cnt[me.r, grp : grp + 1, 0:1], 1.0)
                mean = total / n_own
                acc = jnp.zeros((8, TILE), F32)
                for s, g in chunks:
                    if g == grp:
                        d = (a[s : s + CH, cols] - mean) * mask[s : s + CH, 0:1]
                        acc = acc + fold(d * d)
                put(buf, j, 2 * grp, total)
                put(buf, j, 2 * grp + 1, jnp.sum(acc, axis=0, keepdims=True))
            return carry

        for j in range(n_tiles):
            body(j, 0) if n_tiles <= 2 else None
        if n_tiles > 2:
            lax.fori_loop(0, n_tiles, body, 0)

    def merge_stats(buf, mi):
        width = buf.shape[2]
        for hf in (0, 1):
            for grp in (0, 1):
                k = 4 * hf + 2 * grp
                total = sum(buf[i, k : k + 1] for i in range(n_rows))
                mean = total / count[grp]
                spread = jnp.zeros_like(mean)
                for i in range(n_rows):
                    n_i = cnt[i, grp : grp + 1, 0:1]
                    off = buf[i, k : k + 1] / jnp.maximum(n_i, 1.0) - mean
                    spread = spread + buf[i, k + 1 : k + 2] + n_i * (off * off)
                mi[2 * grp : 2 * grp + 1, hf * width : (hf + 1) * width] = mean
                mi[2 * grp + 1 : 2 * grp + 2, hf * width : (hf + 1) * width] = lax.rsqrt(
                    spread / count[grp] + eps
                )

    def merge_grads(buf, tot):
        width = buf.shape[2]
        for hf in (0, 1):
            block = buf[0, 4 * hf : 4 * hf + 4]
            for i in range(1, n_rows):
                block = block + buf[i, 4 * hf : 4 * hf + 4]
            tot[0:4, hf * width : (hf + 1) * width] = block

    def expand_params():
        blocks = par[...].reshape(n_dp * n_rows * 8, 128).astype(BF)
        n_dev = n_dp * n_rows
        for out, width in ((p1, mid), (p3, wide)):
            share = width // n_dev
            step = 512
            for t in range(width // step):
                lane = lax.broadcasted_iota(jnp.int32, (128, step), 1) + t * step
                place = lax.broadcasted_iota(jnp.int32, (128, step), 0)
                pick = jnp.where(lane % share == place, 1.0, 0.0).astype(BF)
                spread = dot(blocks, pick).reshape(n_dev, 8, step)
                owner = (lax.broadcasted_iota(jnp.int32, (8, step), 1) + t * step) // share
                total = jnp.zeros((8, step), F32)
                for d in range(n_dev):
                    total = total + jnp.where(owner == d, spread[d], 0.0)
                out[:, t * step : (t + 1) * step] = total

    def gain(out, i, cols):
        return out[i : i + 1, cols]

    small_piece.start()
    pieces[0].start()
    exchanges[0][0]()
    clear_rims(hv, hc)
    clear_rims(dv, dc)
    in_copies[0].wait()
    in_copies[1].wait()

    def step0(t):
        pieces[t].got_z()
        if t + 1 < len(pieces):
            pieces[t + 1].start()
        pieces[t].stage2()

    small_piece.got_z()
    small_piece.stage2()
    step0(0)
    for t in range(wide // TILE):
        xt[t * TILE : (t + 1) * TILE, :] = x[:, t * TILE : (t + 1) * TILE].T
    small_piece.stage3()
    step0(1)
    pieces[0].stage3()
    small_piece.stage4()
    step0(2)
    pieces[1].stage3()
    pieces[0].stage4()
    small_piece.finish()
    expand_params()
    step0(3)
    pieces[2].stage3()
    pieces[1].stage4()
    pieces[0].finish()
    exchanges[0][1]()

    def conv1(j, carry):
        w = wr[:, :, :, :, :, lanes(j)].reshape(wide, TILE)
        a1[:, lanes(j)] = dot(x[...], w)
        return carry

    lax.fori_loop(0, mid // TILE, conv1, 0)
    local_stats(a1, ex1, mid // TILE)
    exchanges[1][0]()
    step0(4)
    pieces[3].stage3()
    pieces[2].stage4()
    pieces[1].finish()
    exchanges[1][1]()
    merge_stats(ex1, mi1)

    def store_rows(v, c, s, cols, value):
        if s < pix_v:
            r, o = s // row_v, s % row_v
            v[1 + r, maps_v + o : maps_v + o + CH, cols] = value
        else:
            o = s - pix_v
            c[1, maps_c + o : maps_c + o + CH, cols] = value

    def act(a, mi, i, store):
        def body(j, carry):
            cols = lanes(j)
            scale = [mi[2 * g + 1 : 2 * g + 2, cols] * gain(p1, i, cols) for g in (0, 1)]
            mean = [mi[2 * g : 2 * g + 1, cols] for g in (0, 1)]
            shift = gain(p1, i + 1, cols)
            for s, g in chunks:
                zed = (a[s : s + CH, cols] - mean[g]) * scale[g] + shift
                store(s, cols, (zed * sigmoid(zed) * mask[s : s + CH, 0:1]).astype(BF))
            return carry

        for j in range(mid // TILE):
            body(j, 0)

    act(a1, mi1, 0, lambda s, cols, value: store_rows(hv, hc, s, cols, value))
    rim_h[0]()
    pieces[4].stage3()
    pieces[3].stage4()
    pieces[2].finish()
    pieces[4].stage4()
    pieces[3].finish()
    rim_h[1]()

    def conv2(tap, carry):
        dy, dx = tap // 3, tap % 3
        w = ws[tap].reshape(mid, mid)
        for r in (0, 1):
            left = hv[r + dy, pl.ds(pl.multiple_of(dx * maps_v, maps_v), row_v), :]
            block = a2.at[r * row_v : (r + 1) * row_v]
            block[...] = block[...] + dot(left, w)
        left = hc[dy, pl.ds(pl.multiple_of(dx * maps_c, maps_c), row_c), :]
        block = a2.at[pix_v:pix]
        block[...] = block[...] + dot(left, w)
        return carry

    a2[...] = jnp.zeros(a2.shape, F32)
    lax.fori_loop(0, 9, conv2, 0)
    local_stats(a2, ex2, mid // TILE)
    exchanges[2][0]()
    exchanges[2][1]()
    merge_stats(ex2, mi2)

    def store_h2(s, cols, value):
        h2[s : s + CH, cols] = value

    act(a2, mi2, 2, store_h2)
    pieces[4].finish()
    in_copies[2].wait()
    in_copies[3].wait()

    def conv3(j, carry):
        w = we[:, :, :, :, :, lanes(j)].reshape(mid, TILE)
        a3[:, lanes(j)] = dot(h2[...], w)
        return carry

    lax.fori_loop(0, wide // TILE, conv3, 0)
    local_stats(a3, ex3, wide // TILE)
    exchanges[3][0]()
    h2t[...] = h2[...].T
    exchanges[3][1]()
    merge_stats(ex3, mi3)

    def y_copies(j, slot):
        return [
            pltpu.make_async_copy(ysl.at[slot, 0:pix_v], yv_h.at[:, lanes(j)], out_sem.at[slot, 0]),
            pltpu.make_async_copy(ysl.at[slot, pix_v:pix], yc_h.at[:, lanes(j)], out_sem.at[slot, 1]),
        ]

    def last(jj, carry):
        for slot in (0, 1):
            j = 2 * jj + slot
            cols = lanes(j)

            @pl.when(jj > 0)
            def _():
                for cp in y_copies(j, slot):
                    cp.wait()

            mean = [mi3[2 * g : 2 * g + 1, cols] for g in (0, 1)]
            inv = [mi3[2 * g + 1 : 2 * g + 2, cols] for g in (0, 1)]
            gn, sh = gain(p3, 4, cols), gain(p3, 5, cols)
            sums = [jnp.zeros((8, TILE), F32) for _ in range(4)]
            pooled = [jnp.zeros((CH, TILE), F32) for _ in range((maps_v + maps_c) // CH)]
            cps = [cpv[s : s + CH, cols] * (1.0 / valid_v) for s in range(0, maps_v, CH)]
            cps += [cpc[s : s + CH, cols] * (1.0 / valid_c) for s in range(0, maps_c, CH)]
            for s, g in chunks:
                which = (s % maps_v) // CH if g == 0 else (maps_v + (s - pix_v) % maps_c) // CH
                rows = slice(s, s + CH)
                m = mask[rows, 0:1]
                nh = (a3[rows, cols] - mean[g]) * inv[g]
                pre = x[rows, cols].astype(F32) + (nh * gn + sh)
                sig = sigmoid(pre)
                out = pre * sig * m
                ysl[slot, rows, :] = out
                pooled[which] = pooled[which] + out
                gp = (cot[rows, cols].astype(F32) + cps[which]) * m * (sig * (1.0 + pre * (1.0 - sig)))
                gpre[rows, cols] = gp
                sums[2 * g] = sums[2 * g] + fold(gp * nh)
                sums[2 * g + 1] = sums[2 * g + 1] + fold(gp)
            for k in range(4):
                put(bx3, j, k, jnp.sum(sums[k], axis=0, keepdims=True))
            for i, value in enumerate(pooled):
                pf[i * CH : (i + 1) * CH, cols] = value
                pb[i * CH : (i + 1) * CH, cols] = value.astype(BF)
            for cp in y_copies(j, slot):
                cp.start()
        return carry

    lax.fori_loop(0, wide // TILE // 2, last, 0)
    exchanges[6][0]()

    core_peer = {"dp": me.dp, "rows": me.x * 2 + 1 - me.c}
    chip_peer = {"dp": me.dp, "rows": (1 - me.x) * 2 + me.c}
    pool_core = remote(pb, pr.at[0], pool_s.at[0], pool_r.at[0], core_peer)
    pool_core.start()
    exchanges[6][1]()
    merge_grads(bx3, tot3)

    def coefs(mi, tot, gn, cols):
        out = []
        for g in (0, 1):
            mean, inv = mi[2 * g : 2 * g + 1, cols], mi[2 * g + 1 : 2 * g + 2, cols]
            dg, ds = tot[2 * g : 2 * g + 1, cols], tot[2 * g + 1 : 2 * g + 2, cols]
            out.append((mean, inv, gn * inv, ds / count[g], dg / count[g]))
        return out

    def grad_three(j, carry):
        cols = lanes(j)
        co = coefs(mi3, tot3, gain(p3, 4, cols), cols)
        for s, g in chunks:
            rows = slice(s, s + CH)
            mean, inv, k0, k1, k2 = co[g]
            nh = (a3[rows, cols] - mean) * inv
            cot[rows, cols] = (k0 * (gpre[rows, cols] - k1 - nh * k2) * mask[rows, 0:1]).astype(BF)
        gwe[:, :, :, :, :, cols] = (
            dot(h2t[...], cot[:, cols]).astype(BF).reshape(gwe.shape[:5] + (TILE,))
        )
        return carry

    lax.fori_loop(0, wide // TILE, grad_three, 0)

    def reducer(k, view, fc, f3, f2, fz):
        return Reduce(me, view, fc, f3, f2, fz, rs_s.at[k], rs_r.at[k])

    q_we = reducer(
        0,
        lambda z, y, x, c, h: gwe.at[z, y, x, c, :, half(h, wide)],
        lambda z, y, x, h: fc_we.at[z, y, x, :, half(h, wide)],
        lambda h: f3_we.at[h],
        lambda h: f2_we.at[h],
        lambda k: fz_we.at[k],
    )
    q_ws = [
        reducer(
            1 + i,
            lambda z, y, x, c, h, i=i: gws.at[3 * i : 3 * i + 3, z, y, x, c, :, half(h, mid)],
            lambda z, y, x, h, i=i: fc_ws.at[3 * i : 3 * i + 3, z, y, x, :, half(h, mid)],
            lambda h, i=i: f3_ws.at[h, 3 * i : 3 * i + 3],
            lambda h, i=i: f2_ws.at[h, 3 * i : 3 * i + 3],
            lambda k, i=i: fz_ws.at[k, 3 * i : 3 * i + 3],
        )
        for i in range(3)
    ]
    q_wr = reducer(
        4,
        lambda z, y, x, c, h: gwr.at[z, y, x, c, :, half(h, mid)],
        lambda z, y, x, h: fc_wr.at[z, y, x, :, half(h, mid)],
        lambda h: f3_wr.at[h],
        lambda h: f2_wr.at[h],
        lambda k: fz_wr.at[k],
    )
    q_we.start()

    def grad_act(gh, a, mi, i, buf, j):
        cols = lanes(j)
        gn, sh = gain(p1, i, cols), gain(p1, i + 1, cols)
        sums = [jnp.zeros((8, TILE), F32) for _ in range(4)]
        for s, g in chunks:
            rows = slice(s, s + CH)
            mean, inv = mi[2 * g : 2 * g + 1, cols], mi[2 * g + 1 : 2 * g + 2, cols]
            nh = (a[rows, cols] - mean) * inv
            zed = nh * gn + sh
            sig = sigmoid(zed)
            gz = gh[rows, cols] * mask[rows, 0:1] * (sig * (1.0 + zed * (1.0 - sig)))
            gh[rows, cols] = gz
            sums[2 * g] = sums[2 * g] + fold(gz * nh)
            sums[2 * g + 1] = sums[2 * g + 1] + fold(gz)
        for k in range(4):
            put(buf, j, k, jnp.sum(sums[k], axis=0, keepdims=True))

    for slot in (0, 1):
        for cp in y_copies(wide // TILE - 2 + slot, slot):
            cp.wait()
    for j in range(mid // TILE):
        w = tile_rows(we, j).reshape(TILE, wide)
        ysl[j, :, :] = dot_t(cot[...], w)

    class Cols:
        def __getitem__(self, key):
            rows, cols = key
            return ysl[self.j, rows, :]

        def __setitem__(self, key, value):
            rows, cols = key
            ysl[self.j, rows, :] = value

    ghs = Cols()
    for j in range(mid // TILE):
        ghs.j = j
        grad_act(ghs, a2, mi2, 2, bx2, j)
    exchanges[5][0]()
    q_we.stage2()
    pool_core.wait()
    pf[...] = pf[...] + pr[0].astype(F32)
    pb[...] = pf[...].astype(BF)
    pool_chip = remote(pb, pr.at[1], pool_s.at[1], pool_r.at[1], chip_peer)
    pool_chip.start()
    exchanges[5][1]()
    merge_grads(bx2, tot2)

    def grad_norm_all(a, mi, tot, i, store):
        for j in range(mid // TILE):
            ghs.j = j
            cols = lanes(j)
            co = coefs(mi, tot, gain(p1, i, cols), cols)
            for s, g in chunks:
                rows = slice(s, s + CH)
                mean, inv, k0, k1, k2 = co[g]
                nh = (a[rows, cols] - mean) * inv
                value = k0 * (ghs[rows, cols] - k1 - nh * k2) * mask[rows, 0:1]
                store(s, cols, value.astype(BF))

    grad_norm_all(a2, mi2, tot2, 2, lambda s, cols, value: store_rows(dv, dc, s, cols, value))
    rim_d[0]()

    def grad_taps(dy):
        def body(dx, carry):
            tap = 3 * dy + dx
            total = dot_r(
                hc[dy, pl.ds(pl.multiple_of(dx * maps_c, maps_c), row_c), :],
                dc[1, maps_c : maps_c + row_c],
            )
            for r in (0, 1):
                total = total + dot_r(
                    hv[r + dy, pl.ds(pl.multiple_of(dx * maps_v, maps_v), row_v), :],
                    dv[1 + r, maps_v : maps_v + row_v],
                )
            gws[tap] = total.astype(BF).reshape(gws.shape[1:])
            return carry

        lax.fori_loop(0, 3, body, 0)

    grad_taps(0)
    q_ws[0].start()
    q_we.stage3()
    grad_taps(1)
    q_ws[1].start()
    q_ws[0].stage2()
    grad_taps(2)
    q_ws[2].start()
    q_ws[1].stage2()
    rim_d[1]()

    ysl[...] = jnp.zeros(ysl.shape, F32)

    def conv2_back(tap, carry):
        dy, dx = 2 - tap // 3, 2 - tap % 3
        for j in range(mid // TILE):
            w = tile_rows(ws.at[tap], j).reshape(TILE, mid)
            for r in (0, 1):
                left = dv[r + dy, pl.ds(pl.multiple_of(dx * maps_v, maps_v), row_v), :]
                block = ysl.at[j, r * row_v : (r + 1) * row_v]
                block[...] = block[...] + dot_t(left, w)
            left = dc[dy, pl.ds(pl.multiple_of(dx * maps_c, maps_c), row_c), :]
            block = ysl.at[j, pix_v:pix]
            block[...] = block[...] + dot_t(left, w)
        return carry

    lax.fori_loop(0, 9, conv2_back, 0)
    for j in range(mid // TILE):
        ghs.j = j
        grad_act(ghs, a1, mi1, 0, bx1, j)
    exchanges[4][0]()
    q_we.stage4()
    q_ws[0].stage3()
    q_ws[2].stage2()
    exchanges[4][1]()
    merge_grads(bx1, tot1)

    def store_ga1(s, cols, value):
        ga1[s : s + CH, cols] = value

    grad_norm_all(a1, mi1, tot1, 0, store_ga1)
    for t in range(wide // TILE):
        block = dot(xt[t * TILE : (t + 1) * TILE, :], ga1[...]).astype(BF)
        gwr[t // 2, t % 2] = block.reshape(gwr.shape[2:])
    q_wr.start()
    q_ws[1].stage3()
    q_ws[0].stage4()

    n_dev = n_dp * n_rows

    def three(v):
        hi = v.astype(BF)
        rest = v - hi.astype(F32)
        mid_part = rest.astype(BF)
        return hi, mid_part, (rest - mid_part.astype(F32)).astype(BF)

    def owner_blocks(rows, width):
        share = width // n_dev
        step = 512
        total = jnp.zeros((n_dp * 8, 128), F32)
        for t in range(width // step):
            place = lax.broadcasted_iota(jnp.int32, (step, 128), 1)
            lane = lax.broadcasted_iota(jnp.int32, (step, 128), 0) + t * step
            pick = jnp.where(lane % share == place, 1.0, 0.0).astype(BF)
            owner = (lax.broadcasted_iota(jnp.int32, (8, step), 1) + t * step) // share
            vec = rows[:, t * step : (t + 1) * step]
            stack = jnp.concatenate(
                [jnp.where(owner == d * n_rows + me.r, vec, 0.0) for d in range(n_dp)], axis=0
            )
            for part in three(stack):
                total = total + dot(part, pick)
        return total

    small_rows = [t_[0:1] + t_[2:3] if k == 0 else t_[1:2] + t_[3:4] for t_ in (tot1, tot2) for k in (0, 1)]
    wide_rows = [tot3[0:1] + tot3[2:3], tot3[1:2] + tot3[3:4]]
    narrow = jnp.concatenate(small_rows + [jnp.zeros((4, mid), F32)], axis=0)
    broad = jnp.concatenate([jnp.zeros((4, wide), F32)] + wide_rows + [jnp.zeros((2, wide), F32)], axis=0)
    sb[...] = (owner_blocks(narrow, mid) + owner_blocks(broad, wide)).reshape(sb.shape)

    def small_cp(d, recv):
        peer = (me.dp + n_dp - d) % n_dp if recv else (me.dp + d) % n_dp
        return remote(sb.at[peer], rb.at[d - 1], sm_s.at[d - 1], sm_r.at[d - 1], {"dp": peer, "rows": me.r})

    for d in range(1, n_dp):
        small_cp(d, False).start()

    def g_copies(j):
        return [
            pltpu.make_async_copy(gpre.at[0:pix_v, lanes(j)], gv_h.at[:, lanes(j)], out_sem.at[2 + j, 0]),
            pltpu.make_async_copy(gpre.at[pix_v:pix, lanes(j)], gc_h.at[:, lanes(j)], out_sem.at[2 + j, 1]),
        ]

    def grad_in(j):
        cols = lanes(j)
        w = wr[j // 2, j % 2].reshape(TILE, mid)
        gpre[:, cols] = gpre[:, cols] + dot_t(ga1[...], w)
        for cp in g_copies(j):
            cp.start()

    steps = [
        q_wr.stage2, q_ws[2].stage3, q_ws[1].stage4, q_wr.stage3, q_ws[2].stage4, q_wr.stage4,
    ]
    for j in range(wide // TILE):
        grad_in(j)
        if j < 3:
            steps[j]()
    gwe_o[...] = q_we.finish()
    gws_o[0:3] = q_ws[0].finish()
    pool_chip.wait()
    pool = pf[...] + pr[1].astype(F32)
    pool_o[0:maps_v] = pool[0:maps_v] * (1.0 / valid_v)
    pool_o[maps_v : maps_v + maps_c] = pool[maps_v : maps_v + maps_c] * (1.0 / valid_c)
    for step in steps[3:]:
        step()
    total = sb[me.dp]
    for d in range(1, n_dp):
        small_cp(d, True).wait_recv()
        total = total + rb[d - 1]
    small_o[...] = total
    gws_o[3:6] = q_ws[1].finish()
    gws_o[6:9] = q_ws[2].finish()
    gwr_o[...] = q_wr.finish()

    for j in range(wide // TILE):
        for cp in g_copies(j):
            cp.wait()
    small_piece.drain()
    for p in pieces:
        p.drain()
    for e in exchanges:
        e[2]()
    rim_h[2]()
    rim_d[2]()
    for q in [q_we] + q_ws + [q_wr]:
        q.drain()
    for d in range(1, n_dp):
        small_cp(d, False).wait_send()


def block_step(n_dp, n_rows, xv, xc, mv, mc, wr, ws, we, g1, s1, g2, s2, g3, s3, cv, cc, cpv, cpc):
    img, views, rows_v, cols_v, wide = xv.shape
    crops, cols_c = xc.shape[1], xc.shape[3]
    mid = wr.shape[1]
    maps_v, maps_c = img * views, img * crops
    pix_v, pix_c = rows_v * cols_v * maps_v, cols_c * maps_c
    pix = pix_v + pix_c
    valid_v, valid_c = (rows_v * n_rows - 1) * cols_v, (n_rows - 1) * cols_c
    nz, nx = n_dp // 2, n_rows // 2

    def views_in(t):
        return t.transpose(2, 3, 0, 1, 4).reshape(pix_v, wide)

    def crops_in(t):
        return t.transpose(2, 3, 0, 1, 4).reshape(pix_c, wide)

    mask = jnp.concatenate(
        [
            jnp.broadcast_to(mv.transpose(2, 0, 1).reshape(rows_v, 1, maps_v), (rows_v, cols_v, maps_v)).reshape(-1),
            jnp.broadcast_to(mc.transpose(2, 0, 1).reshape(1, maps_c), (cols_c, maps_c)).reshape(-1),
        ]
    )
    mask = jnp.broadcast_to(mask.astype(F32)[:, None], (pix, 128))
    grid4 = (nz, 2, nx, 2)
    vm = pl.BlockSpec(memory_space=pltpu.VMEM)
    hbm = pl.BlockSpec(memory_space=pl.ANY)
    s_wr, s_we = wr.shape[0], we.shape[0]
    V = pltpu.VMEM
    D = pltpu.SemaphoreType.DMA

    scratch = [
        V(grid4 + (s_wr, mid), BF), V((9,) + grid4 + (s_we, mid), BF), V(grid4 + (s_we, wide), BF),
        V(grid4 + (8, 128), F32),
        V((pix, wide), BF), V((wide, pix), BF), V((pix, wide), BF),
        V((pix, mid), F32), V((pix, mid), F32), V((pix, wide), F32), V((pix, wide), F32),
        V((2, pix, TILE), F32),
        V((4, (cols_v + 2) * maps_v, mid), BF), V((3, (cols_c + 2) * maps_c, mid), BF),
        V((4, (cols_v + 2) * maps_v, mid), BF), V((3, (cols_c + 2) * maps_c, mid), BF),
        V((pix, mid), BF), V((mid, pix), BF), V((pix, mid), BF),
        V(grid4 + (s_wr, mid), BF), V((9,) + grid4 + (s_we, mid), BF), V(grid4 + (s_we, wide), BF),
        V((nz, 2, nx, s_we, wide), BF), V((9, nz, 2, nx, s_we, mid), BF), V((nz, 2, nx, s_wr, mid), BF),
        V((2, nz, 2, s_we, wide // 2), BF), V((2, 9, nz, 2, s_we, mid // 2), BF), V((2, nz, 2, s_wr, mid // 2), BF),
        V((2, nz, s_we, wide // 2), BF), V((2, 9, nz, s_we, mid // 2), BF), V((2, nz, s_wr, mid // 2), BF),
        V((nz - 1, s_we, wide), BF), V((nz - 1, 9, s_we, mid), BF), V((nz - 1, s_wr, mid), BF),
        V((8, mid), F32), V((8, wide), F32),
        V((4, mid), F32), V((4, mid), F32), V((4, wide), F32),
        V((n_rows, 8, 128), F32),
        V((n_rows, 8, mid // 2), F32), V((n_rows, 8, mid // 2), F32), V((n_rows, 8, wide // 2), F32),
        V((n_rows, 8, mid // 2), F32), V((n_rows, 8, mid // 2), F32), V((n_rows, 8, wide // 2), F32),
        V((4, mid), F32), V((4, mid), F32), V((4, wide), F32),
        V((maps_v + maps_c, wide), F32), V((maps_v + maps_c, wide), BF), V((2, maps_v + maps_c, wide), BF),
        V((n_dp, 8, 128), F32), V((n_dp - 1, 8, 128), F32),
        D((4,)), D((2 + wide // TILE, 2)), D((6, 12)), D((6, 12)), D((5, 5 + nz)), D((5, 5 + nz)),
        D((7, n_rows - 1)), D((7, n_rows - 1)), D((2, 4)), D((2, 4)), D((2,)), D((2,)), D((n_dp - 1,)), D((n_dp - 1,)),
    ]
    outs = pl.pallas_call(
        functools.partial(kernel, n_dp, n_rows, (maps_v, cols_v, maps_c, cols_c, valid_v, valid_c)),
        out_shape=[
            jax.ShapeDtypeStruct((pix_v, wide), F32), jax.ShapeDtypeStruct((pix_c, wide), F32),
            jax.ShapeDtypeStruct((pix_v, wide), F32), jax.ShapeDtypeStruct((pix_c, wide), F32),
            jax.ShapeDtypeStruct((maps_v + maps_c, wide), F32),
            jax.ShapeDtypeStruct((s_wr, mid), F32), jax.ShapeDtypeStruct((9, s_we, mid), F32),
            jax.ShapeDtypeStruct((s_we, wide), F32), jax.ShapeDtypeStruct((8, 128), F32),
        ],
        in_specs=[hbm] * 4 + [vm] * 12,
        out_specs=[hbm] * 4 + [vm] * 5,
        scratch_shapes=scratch,
        compiler_params=pltpu.CompilerParams(
            collective_id=0, has_side_effects=True, vmem_limit_bytes=63 << 20
        ),
    )(
        views_in(xv), crops_in(xc), views_in(cv), crops_in(cc), mask,
        wr, ws.reshape(9, s_we, mid), we,
        g1.reshape(1, -1), s1.reshape(1, -1), g2.reshape(1, -1), s2.reshape(1, -1),
        g3.reshape(1, -1), s3.reshape(1, -1),
        cpv.reshape(maps_v, wide), cpc.reshape(maps_c, wide),
    )
    yv, yc, gv, gc, pool, gwr, gws, gwe, small = outs

    def views_out(t):
        return t.reshape(rows_v, cols_v, img, views, wide).transpose(2, 3, 0, 1, 4)

    def crops_out(t):
        return t.reshape(1, cols_c, img, crops, wide).transpose(2, 3, 0, 1, 4)

    e = mid // (n_dp * n_rows)
    f = wide // (n_dp * n_rows)
    return (
        views_out(yv), crops_out(yc),
        pool[:maps_v].reshape(cpv.shape), pool[maps_v:].reshape(cpc.shape),
        views_out(gv), crops_out(gc),
        gwr, gws.reshape(3, 3, s_we, mid), gwe,
        small[0, :e], small[1, :e], small[2, :e], small[3, :e], small[4, :f], small[5, :f],
    )


def fits(xv, xc, we):
    return we.shape[0] % 16 == 0 and xv.shape[2] == 2 and xc.shape[2] == 1


def with_halo(block, sides, width):
    for axis, dim in sides:
        count = lax.axis_size(axis)
        forward = [(i, i + 1) for i in range(count - 1)]
        backward = [(target, source) for source, target in forward]
        low = lax.ppermute(
            lax.slice_in_dim(block, block.shape[dim] - width, None, axis=dim), axis, forward
        )
        high = lax.ppermute(lax.slice_in_dim(block, 0, width, axis=dim), axis, backward)
        block = jnp.concatenate([low, block, high], axis=dim)
    return block


def from_behind(array, axis, by):
    peers = lax.axis_size(axis)
    pairs = [(i, i + by) for i in range(peers) if 0 <= i + by < peers]
    return lax.ppermute(array, axis, pairs)


def silu_slope(value):
    sig = jax.nn.sigmoid(value)
    return sig * (1.0 + value * (1.0 - sig))


def pixel_mask(mask_rows, col_count):
    expanded = jnp.broadcast_to(
        mask_rows.astype(jnp.float32)[..., None], mask_rows.shape + (col_count,)
    )
    return expanded.reshape(-1, 1)


def by_group(in_views, view_value, crop_value):
    return jnp.where(in_views, view_value, crop_value)


def norm_forward(acts, mask_col, view_pixels, in_views, counts, gain_vec, shift_vec):
    masked = acts * mask_col
    totals = lax.psum(
        (jnp.sum(masked[:view_pixels], axis=0), jnp.sum(masked[view_pixels:], axis=0)), "rows"
    )
    centered = acts - by_group(in_views, totals[0] / counts[0], totals[1] / counts[1])
    squares = jnp.square(centered * mask_col)
    spread = lax.psum(
        (jnp.sum(squares[:view_pixels], axis=0), jnp.sum(squares[view_pixels:], axis=0)), "rows"
    )
    inv_rows = by_group(
        in_views, lax.rsqrt(spread[0] / counts[0] + eps), lax.rsqrt(spread[1] / counts[1] + eps)
    )
    normal = centered * inv_rows
    return (normal * gain_vec + shift_vec, normal, inv_rows)


def norm_backward(grad_z, normal, inv_rows, mask_col, view_pixels, in_views, counts, gain_vec):
    product = grad_z * normal
    partials = (
        jnp.sum(product[:view_pixels], axis=0),
        jnp.sum(grad_z[:view_pixels], axis=0),
        jnp.sum(product[view_pixels:], axis=0),
        jnp.sum(grad_z[view_pixels:], axis=0),
    )
    totals = (
        lax.psum(partials[0].astype(jnp.bfloat16), "rows").astype(jnp.float32),
        lax.psum(partials[1].astype(jnp.bfloat16), "rows").astype(jnp.float32),
        lax.psum(partials[2].astype(jnp.bfloat16), "rows").astype(jnp.float32),
        lax.psum(partials[3].astype(jnp.bfloat16), "rows").astype(jnp.float32),
    )
    scale_mean = by_group(in_views, totals[0] / counts[0], totals[2] / counts[1])
    shift_mean = by_group(in_views, totals[1] / counts[0], totals[3] / counts[1])
    grad_acts = gain_vec * inv_rows * (grad_z - shift_mean - normal * scale_mean) * mask_col
    return (grad_acts.astype(jnp.bfloat16), partials[0] + partials[2], partials[1] + partials[3])


def with_rims(feature_map):
    extended = with_halo(feature_map, (("rows", 1),), 1)
    return jnp.pad(extended, ((0, 0), (0, 0), (1, 1), (0, 0)))


def gather_taps(extended, row_count, col_count):
    windows = []
    for row_step in range(3):
        for col_step in range(3):
            windows.append(
                extended[:, row_step : row_step + row_count, col_step : col_step + col_count, :]
            )
    return jnp.concatenate(windows, axis=-1).reshape(-1, 9 * extended.shape[-1])


def spread_taps(grad_patches, map_count, row_count, col_count, mid_width):
    pieces = grad_patches.reshape(map_count, row_count, col_count, 9, mid_width)
    padded = jnp.zeros((map_count, row_count + 2, col_count + 2, mid_width), jnp.float32)
    tap_index = 0
    for row_step in range(3):
        for col_step in range(3):
            padded = padded.at[
                :, row_step : row_step + row_count, col_step : col_step + col_count, :
            ].add(pieces[:, :, :, tap_index, :])
            tap_index += 1
    inside = padded[:, 1 : row_count + 1, 1 : col_count + 1, :]
    from_below = from_behind(
        padded[:, 0, 1 : col_count + 1, :].astype(jnp.bfloat16), "rows", -1
    ).astype(jnp.float32)
    from_above = from_behind(
        padded[:, row_count + 1, 1 : col_count + 1, :].astype(jnp.bfloat16), "rows", 1
    ).astype(jnp.float32)
    inside = inside.at[:, row_count - 1].add(from_below)
    inside = inside.at[:, 0].add(from_above)
    return inside.reshape(-1, mid_width)


def contract_rows(left, right):
    return lax.dot_general(
        left, right, (((0,), (0,)), ((), ())), preferred_element_type=jnp.float32
    )


def contract_cols(left, right):
    return lax.dot_general(
        left, right, (((1,), (1,)), ((), ())), preferred_element_type=jnp.float32
    )


def shards(
    x_views,
    x_crops,
    mask_views,
    mask_crops,
    w_reduce,
    w_spatial,
    w_expand,
    gain_reduce,
    shift_reduce,
    gain_spatial,
    shift_spatial,
    gain_expand,
    shift_expand,
    cot_views,
    cot_crops,
    cot_pool_views,
    cot_pool_crops,
):
    low_type = jnp.bfloat16
    gathered = (
        lax.all_gather(w_reduce.astype(low_type), ("dp", "rows"), axis=0, tiled=True),
        lax.all_gather(w_spatial.astype(low_type), ("dp", "rows"), axis=2, tiled=True),
        lax.all_gather(w_expand.astype(low_type), ("dp", "rows"), axis=0, tiled=True),
        lax.all_gather(gain_reduce.astype(low_type), ("dp", "rows"), axis=0, tiled=True),
        lax.all_gather(shift_reduce.astype(low_type), ("dp", "rows"), axis=0, tiled=True),
        lax.all_gather(gain_spatial.astype(low_type), ("dp", "rows"), axis=0, tiled=True),
        lax.all_gather(shift_spatial.astype(low_type), ("dp", "rows"), axis=0, tiled=True),
        lax.all_gather(gain_expand.astype(low_type), ("dp", "rows"), axis=0, tiled=True),
        lax.all_gather(shift_expand.astype(low_type), ("dp", "rows"), axis=0, tiled=True),
    )
    weight_one, weight_two, weight_three = (gathered[0], gathered[1], gathered[2])
    gain_one, shift_one, gain_two, shift_two, gain_three, shift_three = [
        entry.astype(jnp.float32) for entry in gathered[3:]
    ]
    in_width = weight_one.shape[0]
    mid_width = weight_one.shape[1]
    view_maps = x_views.shape[0] * x_views.shape[1]
    view_rows, view_cols = (x_views.shape[2], x_views.shape[3])
    crop_maps = x_crops.shape[0] * x_crops.shape[1]
    crop_rows, crop_cols = (x_crops.shape[2], x_crops.shape[3])
    view_pixels = view_maps * view_rows * view_cols
    total_pixels = view_pixels + crop_maps * crop_rows * crop_cols
    row_parts = lax.axis_size("rows")
    view_valid = (view_rows * row_parts - 1) * view_cols
    crop_valid = (crop_rows * row_parts - 1) * crop_cols
    counts = (float(view_maps * view_valid), float(crop_maps * crop_valid))
    mask_col = jnp.concatenate(
        [pixel_mask(mask_views, view_cols), pixel_mask(mask_crops, crop_cols)], axis=0
    )
    in_views = lax.broadcasted_iota(jnp.int32, (total_pixels, 1), 0) < view_pixels
    inputs = jnp.concatenate([x_views.reshape(-1, in_width), x_crops.reshape(-1, in_width)], axis=0)
    acts_one = jnp.dot(inputs, weight_one, preferred_element_type=jnp.float32)
    z_one, normal_one, inv_one = norm_forward(
        acts_one, mask_col, view_pixels, in_views, counts, gain_one, shift_one
    )
    hidden_one = (jax.nn.silu(z_one) * mask_col).astype(low_type)
    view_hidden = hidden_one[:view_pixels].reshape(view_maps, view_rows, view_cols, mid_width)
    crop_hidden = hidden_one[view_pixels:].reshape(crop_maps, crop_rows, crop_cols, mid_width)
    patches = jnp.concatenate(
        [
            gather_taps(with_rims(view_hidden), view_rows, view_cols),
            gather_taps(with_rims(crop_hidden), crop_rows, crop_cols),
        ],
        axis=0,
    )
    spatial_flat = weight_two.reshape(9 * mid_width, mid_width)
    acts_two = jnp.dot(patches, spatial_flat, preferred_element_type=jnp.float32)
    z_two, normal_two, inv_two = norm_forward(
        acts_two, mask_col, view_pixels, in_views, counts, gain_two, shift_two
    )
    hidden_two = (jax.nn.silu(z_two) * mask_col).astype(low_type)
    acts_three = jnp.dot(hidden_two, weight_three, preferred_element_type=jnp.float32)
    z_three, normal_three, inv_three = norm_forward(
        acts_three, mask_col, view_pixels, in_views, counts, gain_three, shift_three
    )
    pre_act = inputs.astype(jnp.float32) + z_three
    result = jax.nn.silu(pre_act) * mask_col
    pooled = (
        lax.psum(
            jnp.sum(
                result[:view_pixels].reshape(view_maps, view_rows * view_cols, in_width), axis=1
            ).astype(jnp.bfloat16),
            "rows",
        ).astype(jnp.float32),
        lax.psum(
            jnp.sum(
                result[view_pixels:].reshape(crop_maps, crop_rows * crop_cols, in_width), axis=1
            ).astype(jnp.bfloat16),
            "rows",
        ).astype(jnp.float32),
    )
    pool_views = (pooled[0] / view_valid).reshape(cot_pool_views.shape)
    pool_crops = (pooled[1] / crop_valid).reshape(cot_pool_crops.shape)
    view_grad = (
        cot_views.astype(jnp.float32).reshape(view_maps, view_rows * view_cols, in_width)
        + cot_pool_views.reshape(view_maps, 1, in_width) / view_valid
    )
    crop_grad = (
        cot_crops.astype(jnp.float32).reshape(crop_maps, crop_rows * crop_cols, in_width)
        + cot_pool_crops.reshape(crop_maps, 1, in_width) / crop_valid
    )
    grad_out = jnp.concatenate(
        [view_grad.reshape(-1, in_width), crop_grad.reshape(-1, in_width)], axis=0
    )
    grad_pre = grad_out * mask_col * silu_slope(pre_act)
    grad_three, dgain_three, dshift_three = norm_backward(
        grad_pre, normal_three, inv_three, mask_col, view_pixels, in_views, counts, gain_three
    )
    grad_expand = contract_rows(hidden_two, grad_three)
    grad_hidden_two = contract_cols(grad_three, weight_three)
    grad_z_two = grad_hidden_two * mask_col * silu_slope(z_two)
    grad_two, dgain_two, dshift_two = norm_backward(
        grad_z_two, normal_two, inv_two, mask_col, view_pixels, in_views, counts, gain_two
    )
    grad_spatial = contract_rows(patches, grad_two).reshape(3, 3, mid_width, mid_width)
    grad_patches = contract_cols(grad_two, spatial_flat)
    grad_hidden_one = jnp.concatenate(
        [
            spread_taps(grad_patches[:view_pixels], view_maps, view_rows, view_cols, mid_width),
            spread_taps(grad_patches[view_pixels:], crop_maps, crop_rows, crop_cols, mid_width),
        ],
        axis=0,
    )
    grad_z_one = grad_hidden_one * mask_col * silu_slope(z_one)
    grad_one, dgain_one, dshift_one = norm_backward(
        grad_z_one, normal_one, inv_one, mask_col, view_pixels, in_views, counts, gain_one
    )
    grad_reduce = contract_rows(inputs, grad_one)
    grad_inputs = contract_cols(grad_one, weight_one) + grad_pre
    summed = (
        lax.psum_scatter(grad_reduce, ("dp", "rows"), scatter_dimension=0, tiled=True),
        lax.psum_scatter(grad_spatial, ("dp", "rows"), scatter_dimension=2, tiled=True),
        lax.psum_scatter(grad_expand, ("dp", "rows"), scatter_dimension=0, tiled=True),
        lax.psum_scatter(dgain_one, ("dp", "rows"), scatter_dimension=0, tiled=True),
        lax.psum_scatter(dshift_one, ("dp", "rows"), scatter_dimension=0, tiled=True),
        lax.psum_scatter(dgain_two, ("dp", "rows"), scatter_dimension=0, tiled=True),
        lax.psum_scatter(dshift_two, ("dp", "rows"), scatter_dimension=0, tiled=True),
        lax.psum_scatter(dgain_three, ("dp", "rows"), scatter_dimension=0, tiled=True),
        lax.psum_scatter(dshift_three, ("dp", "rows"), scatter_dimension=0, tiled=True),
    )
    out_views = result[:view_pixels].reshape(x_views.shape)
    out_crops = result[view_pixels:].reshape(x_crops.shape)
    grad_views = grad_inputs[:view_pixels].reshape(x_views.shape)
    grad_crops = grad_inputs[view_pixels:].reshape(x_crops.shape)
    return (
        out_views,
        out_crops,
        pool_views,
        pool_crops,
        grad_views,
        grad_crops,
        summed[0],
        summed[1],
        summed[2],
        summed[3],
        summed[4],
        summed[5],
        summed[6],
        summed[7],
        summed[8],
    )


def solution(mesh):
    in_specs = (
        P("dp", None, "rows", None, None),
        P("dp", None, "rows", None, None),
        P("dp", None, "rows"),
        P("dp", None, "rows"),
        P(("dp", "rows"), None),
        P(None, None, ("dp", "rows"), None),
        P(("dp", "rows"), None),
        P(("dp", "rows")),
        P(("dp", "rows")),
        P(("dp", "rows")),
        P(("dp", "rows")),
        P(("dp", "rows")),
        P(("dp", "rows")),
        P("dp", None, "rows", None, None),
        P("dp", None, "rows", None, None),
        P("dp", None, None),
        P("dp", None, None),
    )
    out_specs = (
        P("dp", None, "rows", None, None),
        P("dp", None, "rows", None, None),
        P("dp", None, None),
        P("dp", None, None),
        P("dp", None, "rows", None, None),
        P("dp", None, "rows", None, None),
        P(("dp", "rows"), None),
        P(None, None, ("dp", "rows"), None),
        P(("dp", "rows"), None),
        P(("dp", "rows")),
        P(("dp", "rows")),
        P(("dp", "rows")),
        P(("dp", "rows")),
        P(("dp", "rows")),
        P(("dp", "rows")),
    )
    def step(*args):
        if fits(args[0], args[1], args[6]):
            return block_step(mesh.shape["dp"], mesh.shape["rows"], *args)
        return shards(*args)

    return jax.shard_map(step, mesh=mesh, in_specs=in_specs, out_specs=out_specs, check_vma=False)
```

```python
import functools

import jax
import jax.numpy as jnp
from jax import lax
from jax.experimental import pallas as pl
from jax.experimental.pallas import tpu as pltpu
from jax.sharding import PartitionSpec as P

MESH = pl.DeviceIdType.MESH
ALL = slice(None)
BF = jnp.bfloat16
F32 = jnp.float32
eps = 1e-05
TILE = 256


def lanes(j, width=TILE):
    if isinstance(j, int):
        return slice(j * width, (j + 1) * width)
    return pl.ds(pl.multiple_of(j * width, width), width)


def half(h, width):
    return ALL if h is None else slice(h * (width // 2), (h + 1) * (width // 2))


def dot(a, b):
    return lax.dot_general(a, b, (((1,), (0,)), ((), ())), preferred_element_type=F32)


def dot_t(a, b):
    return lax.dot_general(a, b, (((1,), (1,)), ((), ())), preferred_element_type=F32)


def dot_r(a, b):
    return lax.dot_general(a, b, (((0,), (0,)), ((), ())), preferred_element_type=F32)


def sigmoid(v):
    return 0.5 * jnp.tanh(0.5 * v) + 0.5


class Place:
    def __init__(self, n_dp, n_rows):
        self.ny, self.nc = 2, 2
        self.nz, self.nx = n_dp // 2, n_rows // 2
        self.n_dp, self.n_rows = n_dp, n_rows
        self.dp, self.r = lax.axis_index("dp"), lax.axis_index("rows")
        self.z, self.y = self.dp // 2, self.dp % 2
        self.x, self.c = self.r // 2, self.r % 2

    def dev(self, z, y, x, c):
        return {"dp": z * self.ny + y, "rows": x * self.nc + c}


def remote(src, dst, ssem, rsem, to):
    return pltpu.make_async_remote_copy(
        src_ref=src, dst_ref=dst, send_sem=ssem, recv_sem=rsem, device_id=to, device_id_type=MESH
    )


class Gather:
    def __init__(self, me, view, ssem, rsem, halves=(0, 1)):
        self.me, self.view, self.s, self.r, self.halves = me, view, ssem, rsem, halves

    def cp(self, k, place, to):
        ref = self.view(*place)
        return remote(ref, ref, self.s.at[k], self.r.at[k], self.me.dev(*to))

    def along_z(self, dz, recv):
        me = self.me
        if recv:
            z = (me.z + me.nz - dz) % me.nz
            return self.cp(dz - 1, (z, me.y, me.x, me.c, None), (z, me.y, me.x, me.c))
        to = ((me.z + dz) % me.nz, me.y, me.x, me.c)
        return self.cp(dz - 1, (me.z, me.y, me.x, me.c, None), to)

    def second(self, h, recv):
        me = self.me
        yy, xx = (1 - me.y, me.x) if h == 0 else (me.y, 1 - me.x)
        place = (ALL, yy, xx, me.c, h) if recv else (ALL, me.y, me.x, me.c, h)
        return self.cp(3 + h, place, (me.z, yy, xx, me.c))

    def third(self, h, recv):
        me = self.me
        if h == 0:
            return self.cp(
                5, (ALL, ALL, 1 - me.x if recv else me.x, me.c, h), (me.z, me.y, 1 - me.x, me.c)
            )
        return self.cp(
            6, (ALL, 1 - me.y if recv else me.y, ALL, me.c, h), (me.z, 1 - me.y, me.x, me.c)
        )

    def core(self, k, recv):
        me = self.me
        c = 1 - me.c if recv else me.c
        place = (
            (ALL, me.y, me.x, c, None),
            (ALL, 1 - me.y, me.x, c, 0),
            (ALL, me.y, 1 - me.x, c, 1),
            (ALL, ALL, 1 - me.x, c, 0),
            (ALL, 1 - me.y, ALL, c, 1),
        )[k]
        return self.cp(7 + k, place, (me.z, me.y, me.x, 1 - me.c))

    def start(self):
        for dz in range(1, self.me.nz):
            self.along_z(dz, False).start()

    def got_z(self):
        for dz in range(1, self.me.nz):
            self.along_z(dz, True).wait_recv()

    def stage2(self):
        for h in self.halves:
            self.second(h, False).start()
        self.core(0, False).start()

    def stage3(self):
        for h in self.halves:
            self.second(h, True).wait_recv()
            self.third(h, False).start()
            self.core(1 + h, False).start()

    def stage4(self):
        for h in self.halves:
            self.third(h, True).wait_recv()
            self.core(3 + h, False).start()

    def finish(self):
        self.core(0, True).wait_recv()
        for h in self.halves:
            self.core(1 + h, True).wait_recv()
            self.core(3 + h, True).wait_recv()

    def drain(self):
        for dz in range(1, self.me.nz):
            self.along_z(dz, False).wait_send()
        self.core(0, False).wait_send()
        for h in self.halves:
            self.second(h, False).wait_send()
            self.third(h, False).wait_send()
            self.core(1 + h, False).wait_send()
            self.core(3 + h, False).wait_send()


class Reduce:
    def __init__(self, me, view, from_core, from_third, from_second, from_z, ssem, rsem):
        self.me, self.view, self.s, self.r = me, view, ssem, rsem
        self.fc, self.f3, self.f2, self.fz = from_core, from_third, from_second, from_z

    def core(self):
        me = self.me
        return remote(
            self.view(ALL, ALL, ALL, 1 - me.c, None),
            self.fc(ALL, ALL, ALL, None),
            self.s.at[0],
            self.r.at[0],
            me.dev(me.z, me.y, me.x, 1 - me.c),
        )

    def third(self, h):
        me = self.me
        place = (ALL, ALL, 1 - me.x) if h == 0 else (ALL, 1 - me.y, ALL)
        to = (me.z, me.y, 1 - me.x, me.c) if h == 0 else (me.z, 1 - me.y, me.x, me.c)
        return remote(
            self.view(*place, me.c, h), self.f3(h), self.s.at[1 + h], self.r.at[1 + h], me.dev(*to)
        )

    def second(self, h):
        me = self.me
        place = (ALL, 1 - me.y, me.x) if h == 0 else (ALL, me.y, 1 - me.x)
        to = (me.z, 1 - me.y, me.x, me.c) if h == 0 else (me.z, me.y, 1 - me.x, me.c)
        return remote(
            self.view(*place, me.c, h), self.f2(h), self.s.at[3 + h], self.r.at[3 + h], me.dev(*to)
        )

    def along_z(self, dz):
        me = self.me
        z = (me.z + dz) % me.nz
        return remote(
            self.view(z, me.y, me.x, me.c, None),
            self.fz(dz - 1),
            self.s.at[4 + dz],
            self.r.at[4 + dz],
            me.dev(z, me.y, me.x, me.c),
        )

    def start(self):
        self.core().start()

    def stage2(self):
        me = self.me
        self.core().wait_recv()
        for h in (0, 1):
            first = (ALL, ALL, 1 - me.x) if h == 0 else (ALL, 1 - me.y, ALL)
            ref = self.view(*first, me.c, h)
            ref[...] = ref[...] + self.fc(*first, h)[...]
            self.third(h).start()
        for h in (0, 1):
            rest = (ALL, ALL, me.x) if h == 0 else (ALL, me.y, ALL)
            ref = self.view(*rest, me.c, h)
            ref[...] = ref[...] + self.fc(*rest, h)[...]

    def stage3(self):
        me = self.me
        for h in (0, 1):
            self.third(h).wait_recv()
            kept = (ALL, ALL, me.x) if h == 0 else (ALL, me.y, ALL)
            ref = self.view(*kept, me.c, h)
            ref[...] = ref[...] + self.f3(h)[...]
            self.second(h).start()

    def stage4(self):
        me = self.me
        for h in (0, 1):
            self.second(h).wait_recv()
            ref = self.view(ALL, me.y, me.x, me.c, h)
            ref[...] = ref[...] + self.f2(h)[...]
        for dz in range(1, me.nz):
            self.along_z(dz).start()

    def finish(self):
        me = self.me
        total = self.view(me.z, me.y, me.x, me.c, None)[...].astype(F32)
        for dz in range(1, me.nz):
            self.along_z(dz).wait_recv()
            total = total + self.fz(dz - 1)[...].astype(F32)
        return total

    def drain(self):
        self.core().wait_send()
        for h in (0, 1):
            self.third(h).wait_send()
            self.second(h).wait_send()
        for dz in range(1, self.me.nz):
            self.along_z(dz).wait_send()


def kernel(n_dp, n_rows, sizes, *refs):
    (
        xv_h, xc_h, cv_h, cc_h, cpv_h, cpc_h, mv_in, mc_in, wr_in, ws_in, we_in,
        g1_in, s1_in, g2_in, s2_in, g3_in, s3_in,
        yv_h, yc_h, gv_h, gc_h, poolv_o, poolc_o, gwr_o, gws_o, gwe_o, small_o,
        wr, ws, we, par, mask, raw_v, raw_c, cpv, cpc, x, xt, cot, a1, a2, a3, gpre, ysv, ysc, gact,
        hv, hc, dv, dc, h2, h2t, ga1, gwr, gws, gwe,
        fc_we, fc_ws, fc_wr, f3_we, f3_ws, f3_wr, f2_we, f2_ws, f2_wr, fz_we, fz_ws, fz_wr,
        p1, p3, mi1, mi2, mi3, cnt, ex1, ex2, ex3, bx1, bx2, bx3, tot1, tot2, tot3,
        pf, pb, pr, sb, rb,
        in_sem, out_sem, ag_s, ag_r, rs_s, rs_r, ex_s, ex_r, halo_s, halo_r, pool_s, pool_r, sm_s, sm_r,
    ) = refs
    (maps_v, cols_v, maps_c, cols_c, valid_v, valid_c) = sizes
    me = Place(n_dp, n_rows)
    mid, wide = a1.shape[1], a3.shape[1]
    pix_v = 2 * cols_v * maps_v
    pix = a1.shape[0]
    row_v, row_c = cols_v * maps_v, cols_c * maps_c
    count = (float(maps_v * valid_v), float(maps_c * valid_c))
    CH = 32
    chunks = [(s, 0 if s < pix_v else 1) for s in range(0, pix, CH)]

    def fetch(k, views, crops):
        return [
            pltpu.make_async_copy(views.at[:, col], raw_v.at[col], in_sem.at[k, col]) for col in range(cols_v)
        ] + [pltpu.make_async_copy(crops, raw_c, in_sem.at[k, cols_v])]

    def arrange(out):
        def body(j, carry):
            cols = lanes(j)
            for col in range(cols_v):
                for r in (0, 1):
                    at = r * row_v + col * maps_v
                    out[at : at + maps_v, cols] = raw_v[col, :, r, cols]
            for col in range(cols_c):
                at = pix_v + col * maps_c
                out[at : at + maps_c, cols] = raw_c[:, col, :, cols].reshape(maps_c, TILE)
            return carry

        lax.fori_loop(0, wide // TILE, body, 0)

    x_copies, cot_copies = fetch(0, xv_h, xc_h), fetch(1, cv_h, cc_h)
    pool_copies = [
        pltpu.make_async_copy(cpv_h, cpv, in_sem.at[2, 0]),
        pltpu.make_async_copy(cpc_h, cpc, in_sem.at[2, 1]),
    ]
    for cp in x_copies + pool_copies:
        cp.start()

    here = (me.z, me.y, me.x, me.c)
    wr[here] = wr_in[...].astype(BF)
    ws[(ALL,) + here] = ws_in[...].astype(BF)
    we[here] = we_in[...].astype(BF)
    own = par.at[here]
    own[...] = jnp.zeros(own.shape, F32)
    for i, ref in enumerate((g1_in, s1_in, g2_in, s2_in, g3_in, s3_in)):
        own[i : i + 1, 0 : ref.shape[1]] = ref[...].astype(BF).astype(F32)

    def mask_column(row_of, per, maps):
        lane = lax.broadcasted_iota(jnp.int32, (maps, 16), 1)
        place = lax.broadcasted_iota(jnp.int32, (maps, 16), 0)
        total = jnp.zeros((maps, 16), F32)
        for k in range(per):
            hit = jnp.logical_and(place % per == k, lane == place // per)
            total = total + jnp.where(hit, row_of(k).astype(F32), 0.0)
        return jnp.broadcast_to(jnp.sum(total, axis=1, keepdims=True), (maps, 128))

    for r in (0, 1):
        column = mask_column(lambda k: mv_in[k, r : r + 1, :], mv_in.shape[0], maps_v)
        for col in range(cols_v):
            at = r * row_v + col * maps_v
            mask[at : at + maps_v] = column
    column = mask_column(lambda k: mc_in[k], mc_in.shape[0], maps_c)
    for col in range(cols_c):
        at = pix_v + col * maps_c
        mask[at : at + maps_c] = column

    cnt_own = cnt.at[me.r]
    cnt_own[0:1] = jnp.sum(mask[0:pix_v], axis=0, keepdims=True)
    cnt_own[1:2] = jnp.sum(mask[pix_v:pix], axis=0, keepdims=True)
    cnt_own[2:8] = jnp.zeros((6, 128), F32)

    barrier = pltpu.get_barrier_semaphore()
    peers = [{"dp": me.dp, "rows": (me.r + d) % n_rows} for d in range(1, n_rows)]
    peers += [{"dp": (me.dp + d) % n_dp, "rows": me.r} for d in range(1, n_dp)]
    for peer in peers:
        pl.semaphore_signal(barrier, inc=1, device_id=peer, device_id_type=MESH)
    pl.semaphore_wait(barrier, len(peers))

    def piece(k, view, halves=(0, 1)):
        return Gather(me, view, ag_s.at[k], ag_r.at[k], halves)

    small_piece = piece(0, lambda z, y, x, c, h: par.at[z, y, x, c], (0,))
    pieces = [piece(1, lambda z, y, x, c, h: wr.at[z, y, x, c, :, half(h, mid)])]
    for i in range(3):
        pieces.append(
            piece(2 + i, lambda z, y, x, c, h, i=i: ws.at[3 * i : 3 * i + 3, z, y, x, c, :, half(h, mid)])
        )
    pieces.append(piece(5, lambda z, y, x, c, h: we.at[z, y, x, c, :, half(h, wide)]))

    def exchange(k, buf):
        def cp(d, recv):
            peer = (me.r + n_rows - d) % n_rows if recv else (me.r + d) % n_rows
            ref = buf.at[peer if recv else me.r]
            return remote(ref, ref, ex_s.at[k, d - 1], ex_r.at[k, d - 1], {"dp": me.dp, "rows": peer})

        def send():
            for d in range(1, n_rows):
                cp(d, False).start()

        def wait():
            for d in range(1, n_rows):
                cp(d, True).wait_recv()

        def drain():
            for d in range(1, n_rows):
                cp(d, False).wait_send()

        return send, wait, drain

    exchanges = [exchange(k, b) for k, b in enumerate((cnt, ex1, ex2, ex3, bx1, bx2, bx3))]

    def rim(k, v, c):
        def cps(up):
            peer = {"dp": me.dp, "rows": (me.r + n_rows - 1) % n_rows if up else (me.r + 1) % n_rows}
            base = 0 if up else 2
            vs, vd = (1, 3) if up else (2, 0)
            csrc, cd = (1, 2) if up else (1, 0)
            return [
                remote(
                    v.at[vs, maps_v : maps_v + row_v],
                    v.at[vd, maps_v : maps_v + row_v],
                    halo_s.at[k, base],
                    halo_r.at[k, base],
                    peer,
                ),
                remote(
                    c.at[csrc, maps_c : maps_c + row_c],
                    c.at[cd, maps_c : maps_c + row_c],
                    halo_s.at[k, base + 1],
                    halo_r.at[k, base + 1],
                    peer,
                ),
            ]

        def each(up, fn):
            def body():
                for cp in cps(up):
                    fn(cp)

            return body

        first, last = me.r == 0, me.r == n_rows - 1

        def send():
            pl.when(jnp.logical_not(first))(each(True, lambda cp: cp.start()))
            pl.when(jnp.logical_not(last))(each(False, lambda cp: cp.start()))

        def wait():
            pl.when(jnp.logical_not(last))(each(True, lambda cp: cp.wait_recv()))
            pl.when(jnp.logical_not(first))(each(False, lambda cp: cp.wait_recv()))

        def drain():
            pl.when(jnp.logical_not(first))(each(True, lambda cp: cp.wait_send()))
            pl.when(jnp.logical_not(last))(each(False, lambda cp: cp.wait_send()))

        return send, wait, drain

    rim_h, rim_d = rim(0, hv, hc), rim(1, dv, dc)

    def clear_rims(v, c):
        zv, zc = jnp.zeros((maps_v, mid), BF), jnp.zeros((maps_c, mid), BF)
        for r in range(4):
            v[r, 0:maps_v] = zv
            v[r, maps_v + row_v : 2 * maps_v + row_v] = zv
        for r in range(3):
            c[r, 0:maps_c] = zc
            c[r, maps_c + row_c : 2 * maps_c + row_c] = zc

        @pl.when(me.r == 0)
        def _():
            v[0, maps_v : maps_v + row_v] = jnp.zeros((row_v, mid), BF)
            c[0, maps_c : maps_c + row_c] = jnp.zeros((row_c, mid), BF)

        @pl.when(me.r == n_rows - 1)
        def _():
            v[3, maps_v : maps_v + row_v] = jnp.zeros((row_v, mid), BF)
            c[2, maps_c : maps_c + row_c] = jnp.zeros((row_c, mid), BF)

    def tile_rows(ref, j):
        per = me.nz * TILE // mid
        return ref[j * per : (j + 1) * per]

    def fold(v):
        return jnp.sum(v.reshape(v.shape[0] // 8, 8, v.shape[1]), axis=0)

    def put(buf, j, k, value):
        tiles = buf.shape[2] // TILE
        if isinstance(j, int):
            buf[me.r, 4 * (j // tiles) + k : 4 * (j // tiles) + k + 1, lanes(j % tiles)] = value
        else:
            buf[me.r, pl.ds(4 * (j // tiles) + k, 1), lanes(j % tiles)] = value

    def local_stats(a, buf, n_tiles):
        def body(j, carry):
            cols = lanes(j)
            for grp in (0, 1):
                acc = jnp.zeros((8, TILE), F32)
                for s, g in chunks:
                    if g == grp:
                        acc = acc + fold(a[s : s + CH, cols] * mask[s : s + CH, 0:1])
                total = jnp.sum(acc, axis=0, keepdims=True)
                n_own = jnp.maximum(cnt[me.r, grp : grp + 1, 0:1], 1.0)
                mean = total / n_own
                acc = jnp.zeros((8, TILE), F32)
                for s, g in chunks:
                    if g == grp:
                        d = (a[s : s + CH, cols] - mean) * mask[s : s + CH, 0:1]
                        acc = acc + fold(d * d)
                put(buf, j, 2 * grp, total)
                put(buf, j, 2 * grp + 1, jnp.sum(acc, axis=0, keepdims=True))
            return carry

        for j in range(n_tiles):
            body(j, 0) if n_tiles <= 2 else None
        if n_tiles > 2:
            lax.fori_loop(0, n_tiles, body, 0)

    def merge_stats(buf, mi):
        width = buf.shape[2]
        for hf in (0, 1):
            for grp in (0, 1):
                k = 4 * hf + 2 * grp
                total = sum(buf[i, k : k + 1] for i in range(n_rows))
                mean = total / count[grp]
                spread = jnp.zeros_like(mean)
                for i in range(n_rows):
                    n_i = cnt[i, grp : grp + 1, 0:1]
                    off = buf[i, k : k + 1] / jnp.maximum(n_i, 1.0) - mean
                    spread = spread + buf[i, k + 1 : k + 2] + n_i * (off * off)
                mi[2 * grp : 2 * grp + 1, hf * width : (hf + 1) * width] = mean
                mi[2 * grp + 1 : 2 * grp + 2, hf * width : (hf + 1) * width] = lax.rsqrt(
                    spread / count[grp] + eps
                )

    def merge_grads(buf, tot):
        width = buf.shape[2]
        for hf in (0, 1):
            block = buf[0, 4 * hf : 4 * hf + 4]
            for i in range(1, n_rows):
                block = block + buf[i, 4 * hf : 4 * hf + 4]
            tot[0:4, hf * width : (hf + 1) * width] = block

    def expand_params():
        blocks = par[...].reshape(n_dp * n_rows * 8, 128).astype(BF)
        n_dev = n_dp * n_rows
        for out, width in ((p1, mid), (p3, wide)):
            share = width // n_dev
            step = 512
            for t in range(width // step):
                lane = lax.broadcasted_iota(jnp.int32, (128, step), 1) + t * step
                place = lax.broadcasted_iota(jnp.int32, (128, step), 0)
                pick = jnp.where(lane % share == place, 1.0, 0.0).astype(BF)
                spread = dot(blocks, pick).reshape(n_dev, 8, step)
                owner = (lax.broadcasted_iota(jnp.int32, (8, step), 1) + t * step) // share
                total = jnp.zeros((8, step), F32)
                for d in range(n_dev):
                    total = total + jnp.where(owner == d, spread[d], 0.0)
                out[:, t * step : (t + 1) * step] = total

    def gain(out, i, cols):
        return out[i : i + 1, cols]

    small_piece.start()
    pieces[0].start()
    exchanges[0][0]()
    clear_rims(hv, hc)
    clear_rims(dv, dc)
    for cp in x_copies:
        cp.wait()

    def step0(t):
        pieces[t].got_z()
        if t + 1 < len(pieces):
            pieces[t + 1].start()
        pieces[t].stage2()

    arrange(x)
    for cp in cot_copies:
        cp.start()
    small_piece.got_z()
    small_piece.stage2()
    step0(0)
    for t in range(wide // TILE):
        xt[t * TILE : (t + 1) * TILE, :] = x[:, t * TILE : (t + 1) * TILE].T
    small_piece.stage3()
    step0(1)
    pieces[0].stage3()
    small_piece.stage4()
    for cp in cot_copies:
        cp.wait()
    arrange(cot)
    step0(2)
    pieces[1].stage3()
    pieces[0].stage4()
    small_piece.finish()
    expand_params()
    step0(3)
    pieces[2].stage3()
    pieces[1].stage4()
    pieces[0].finish()
    exchanges[0][1]()

    def conv1(j, carry):
        w = wr[:, :, :, :, :, lanes(j)].reshape(wide, TILE)
        a1[:, lanes(j)] = dot(x[...], w)
        return carry

    lax.fori_loop(0, mid // TILE, conv1, 0)
    local_stats(a1, ex1, mid // TILE)
    exchanges[1][0]()
    step0(4)
    pieces[3].stage3()
    pieces[2].stage4()
    pieces[1].finish()
    exchanges[1][1]()
    merge_stats(ex1, mi1)

    def store_rows(v, c, s, cols, value):
        if s < pix_v:
            r, o = s // row_v, s % row_v
            v[1 + r, maps_v + o : maps_v + o + CH, cols] = value
        else:
            o = s - pix_v
            c[1, maps_c + o : maps_c + o + CH, cols] = value

    def act(a, mi, i, store):
        def body(j, carry):
            cols = lanes(j)
            scale = [mi[2 * g + 1 : 2 * g + 2, cols] * gain(p1, i, cols) for g in (0, 1)]
            mean = [mi[2 * g : 2 * g + 1, cols] for g in (0, 1)]
            shift = gain(p1, i + 1, cols)
            for s, g in chunks:
                zed = (a[s : s + CH, cols] - mean[g]) * scale[g] + shift
                store(s, cols, (zed * sigmoid(zed) * mask[s : s + CH, 0:1]).astype(BF))
            return carry

        for j in range(mid // TILE):
            body(j, 0)

    act(a1, mi1, 0, lambda s, cols, value: store_rows(hv, hc, s, cols, value))
    rim_h[0]()
    pieces[4].stage3()
    pieces[3].stage4()
    pieces[2].finish()
    pieces[4].stage4()
    pieces[3].finish()
    rim_h[1]()

    def conv2(tap, carry):
        dy, dx = tap // 3, tap % 3
        w = ws[tap].reshape(mid, mid)
        for r in (0, 1):
            left = hv[r + dy, pl.ds(pl.multiple_of(dx * maps_v, maps_v), row_v), :]
            block = a2.at[r * row_v : (r + 1) * row_v]
            block[...] = block[...] + dot(left, w)
        left = hc[dy, pl.ds(pl.multiple_of(dx * maps_c, maps_c), row_c), :]
        block = a2.at[pix_v:pix]
        block[...] = block[...] + dot(left, w)
        return carry

    a2[...] = jnp.zeros(a2.shape, F32)
    lax.fori_loop(0, 9, conv2, 0)
    local_stats(a2, ex2, mid // TILE)
    exchanges[2][0]()
    exchanges[2][1]()
    merge_stats(ex2, mi2)

    def store_h2(s, cols, value):
        h2[s : s + CH, cols] = value

    act(a2, mi2, 2, store_h2)
    pieces[4].finish()
    for cp in pool_copies:
        cp.wait()

    def conv3(j, carry):
        w = we[:, :, :, :, :, lanes(j)].reshape(mid, TILE)
        a3[:, lanes(j)] = dot(h2[...], w)
        return carry

    lax.fori_loop(0, wide // TILE, conv3, 0)
    local_stats(a3, ex3, wide // TILE)
    exchanges[3][0]()
    h2t[...] = h2[...].T
    exchanges[3][1]()
    merge_stats(ex3, mi3)

    def out_copies(j, slot, views, crops):
        return [
            pltpu.make_async_copy(ysv.at[slot], views.at[:, :, :, lanes(j)], out_sem.at[slot, 0]),
            pltpu.make_async_copy(ysc.at[slot], crops.at[:, :, j], out_sem.at[slot, 1]),
        ]

    def store_out(slot, s, value):
        if s < pix_v:
            ysv[slot, :, s % row_v // maps_v, s // row_v, :] = value
        else:
            col, at = (s - pix_v) // maps_c, (s - pix_v) % maps_c
            for k in (0, 1):
                ysc[slot, at : at + CH, col, k, :] = value[:, k * 128 : (k + 1) * 128]

    def last(jj, carry):
        for slot in (0, 1):
            j = 2 * jj + slot
            cols = lanes(j)

            @pl.when(jj > 0)
            def _():
                for cp in out_copies(j, slot, yv_h, yc_h):
                    cp.wait()

            mean = [mi3[2 * g : 2 * g + 1, cols] for g in (0, 1)]
            inv = [mi3[2 * g + 1 : 2 * g + 2, cols] for g in (0, 1)]
            gn, sh = gain(p3, 4, cols), gain(p3, 5, cols)
            sums = [jnp.zeros((8, TILE), F32) for _ in range(4)]
            pooled = [jnp.zeros((CH, TILE), F32) for _ in range((maps_v + maps_c) // CH)]
            per_v, per_c = CH // cpv.shape[1], CH // cpc.shape[1]
            cps = [
                cpv[s : s + per_v, :, cols].reshape(CH, TILE) * (1.0 / valid_v)
                for s in range(0, cpv.shape[0], per_v)
            ] + [
                cpc[s : s + per_c, :, cols].reshape(CH, TILE) * (1.0 / valid_c)
                for s in range(0, cpc.shape[0], per_c)
            ]
            for s, g in chunks:
                which = (s % maps_v) // CH if g == 0 else (maps_v + (s - pix_v) % maps_c) // CH
                rows = slice(s, s + CH)
                m = mask[rows, 0:1]
                nh = (a3[rows, cols] - mean[g]) * inv[g]
                pre = x[rows, cols].astype(F32) + (nh * gn + sh)
                sig = sigmoid(pre)
                out = pre * sig * m
                store_out(slot, s, out)
                pooled[which] = pooled[which] + out
                gp = (cot[rows, cols].astype(F32) + cps[which]) * m * (sig * (1.0 + pre * (1.0 - sig)))
                gpre[rows, cols] = gp
                sums[2 * g] = sums[2 * g] + fold(gp * nh)
                sums[2 * g + 1] = sums[2 * g + 1] + fold(gp)
            for k in range(4):
                put(bx3, j, k, jnp.sum(sums[k], axis=0, keepdims=True))
            for i, value in enumerate(pooled):
                pf[i * CH : (i + 1) * CH, cols] = value
                pb[i * CH : (i + 1) * CH, cols] = value.astype(BF)
            for cp in out_copies(j, slot, yv_h, yc_h):
                cp.start()
        return carry

    lax.fori_loop(0, wide // TILE // 2, last, 0)
    exchanges[6][0]()

    core_peer = {"dp": me.dp, "rows": me.x * 2 + 1 - me.c}
    chip_peer = {"dp": me.dp, "rows": (1 - me.x) * 2 + me.c}
    pool_core = remote(pb, pr.at[0], pool_s.at[0], pool_r.at[0], core_peer)
    pool_core.start()
    exchanges[6][1]()
    merge_grads(bx3, tot3)

    def coefs(mi, tot, gn, cols):
        out = []
        for g in (0, 1):
            mean, inv = mi[2 * g : 2 * g + 1, cols], mi[2 * g + 1 : 2 * g + 2, cols]
            dg, ds = tot[2 * g : 2 * g + 1, cols], tot[2 * g + 1 : 2 * g + 2, cols]
            out.append((mean, inv, gn * inv, ds / count[g], dg / count[g]))
        return out

    def grad_three(j, carry):
        cols = lanes(j)
        co = coefs(mi3, tot3, gain(p3, 4, cols), cols)
        for s, g in chunks:
            rows = slice(s, s + CH)
            mean, inv, k0, k1, k2 = co[g]
            nh = (a3[rows, cols] - mean) * inv
            cot[rows, cols] = (k0 * (gpre[rows, cols] - k1 - nh * k2) * mask[rows, 0:1]).astype(BF)
        gwe[:, :, :, :, :, cols] = (
            dot(h2t[...], cot[:, cols]).astype(BF).reshape(gwe.shape[:5] + (TILE,))
        )
        return carry

    lax.fori_loop(0, wide // TILE, grad_three, 0)

    def reducer(k, view, fc, f3, f2, fz):
        return Reduce(me, view, fc, f3, f2, fz, rs_s.at[k], rs_r.at[k])

    q_we = reducer(
        0,
        lambda z, y, x, c, h: gwe.at[z, y, x, c, :, half(h, wide)],
        lambda z, y, x, h: fc_we.at[z, y, x, :, half(h, wide)],
        lambda h: f3_we.at[h],
        lambda h: f2_we.at[h],
        lambda k: fz_we.at[k],
    )
    q_ws = [
        reducer(
            1 + i,
            lambda z, y, x, c, h, i=i: gws.at[3 * i : 3 * i + 3, z, y, x, c, :, half(h, mid)],
            lambda z, y, x, h, i=i: fc_ws.at[3 * i : 3 * i + 3, z, y, x, :, half(h, mid)],
            lambda h, i=i: f3_ws.at[h, 3 * i : 3 * i + 3],
            lambda h, i=i: f2_ws.at[h, 3 * i : 3 * i + 3],
            lambda k, i=i: fz_ws.at[k, 3 * i : 3 * i + 3],
        )
        for i in range(3)
    ]
    q_wr = reducer(
        4,
        lambda z, y, x, c, h: gwr.at[z, y, x, c, :, half(h, mid)],
        lambda z, y, x, h: fc_wr.at[z, y, x, :, half(h, mid)],
        lambda h: f3_wr.at[h],
        lambda h: f2_wr.at[h],
        lambda k: fz_wr.at[k],
    )
    q_we.start()

    def grad_act(gh, a, mi, i, buf, j):
        cols = lanes(j)
        gn, sh = gain(p1, i, cols), gain(p1, i + 1, cols)
        sums = [jnp.zeros((8, TILE), F32) for _ in range(4)]
        for s, g in chunks:
            rows = slice(s, s + CH)
            mean, inv = mi[2 * g : 2 * g + 1, cols], mi[2 * g + 1 : 2 * g + 2, cols]
            nh = (a[rows, cols] - mean) * inv
            zed = nh * gn + sh
            sig = sigmoid(zed)
            gz = gh[rows, cols] * mask[rows, 0:1] * (sig * (1.0 + zed * (1.0 - sig)))
            gh[rows, cols] = gz
            sums[2 * g] = sums[2 * g] + fold(gz * nh)
            sums[2 * g + 1] = sums[2 * g + 1] + fold(gz)
        for k in range(4):
            put(buf, j, k, jnp.sum(sums[k], axis=0, keepdims=True))

    for j in range(mid // TILE):
        w = tile_rows(we, j).reshape(TILE, wide)
        gact[j, :, :] = dot_t(cot[...], w)

    class Cols:
        def __getitem__(self, key):
            rows, cols = key
            return gact[self.j, rows, :]

        def __setitem__(self, key, value):
            rows, cols = key
            gact[self.j, rows, :] = value

    ghs = Cols()
    for j in range(mid // TILE):
        ghs.j = j
        grad_act(ghs, a2, mi2, 2, bx2, j)
    exchanges[5][0]()
    q_we.stage2()
    pool_core.wait()
    pf[...] = pf[...] + pr[0].astype(F32)
    pb[...] = pf[...].astype(BF)
    pool_chip = remote(pb, pr.at[1], pool_s.at[1], pool_r.at[1], chip_peer)
    pool_chip.start()
    exchanges[5][1]()
    merge_grads(bx2, tot2)

    def grad_norm_all(a, mi, tot, i, store):
        for j in range(mid // TILE):
            ghs.j = j
            cols = lanes(j)
            co = coefs(mi, tot, gain(p1, i, cols), cols)
            for s, g in chunks:
                rows = slice(s, s + CH)
                mean, inv, k0, k1, k2 = co[g]
                nh = (a[rows, cols] - mean) * inv
                value = k0 * (ghs[rows, cols] - k1 - nh * k2) * mask[rows, 0:1]
                store(s, cols, value.astype(BF))

    grad_norm_all(a2, mi2, tot2, 2, lambda s, cols, value: store_rows(dv, dc, s, cols, value))
    rim_d[0]()

    def grad_taps(dy):
        def body(dx, carry):
            tap = 3 * dy + dx
            total = dot_r(
                hc[dy, pl.ds(pl.multiple_of(dx * maps_c, maps_c), row_c), :],
                dc[1, maps_c : maps_c + row_c],
            )
            for r in (0, 1):
                total = total + dot_r(
                    hv[r + dy, pl.ds(pl.multiple_of(dx * maps_v, maps_v), row_v), :],
                    dv[1 + r, maps_v : maps_v + row_v],
                )
            gws[tap] = total.astype(BF).reshape(gws.shape[1:])
            return carry

        lax.fori_loop(0, 3, body, 0)

    grad_taps(0)
    q_ws[0].start()
    q_we.stage3()
    grad_taps(1)
    q_ws[1].start()
    q_ws[0].stage2()
    grad_taps(2)
    q_ws[2].start()
    q_ws[1].stage2()
    rim_d[1]()

    gact[...] = jnp.zeros(gact.shape, F32)

    def conv2_back(tap, carry):
        dy, dx = 2 - tap // 3, 2 - tap % 3
        for j in range(mid // TILE):
            w = tile_rows(ws.at[tap], j).reshape(TILE, mid)
            for r in (0, 1):
                left = dv[r + dy, pl.ds(pl.multiple_of(dx * maps_v, maps_v), row_v), :]
                block = gact.at[j, r * row_v : (r + 1) * row_v]
                block[...] = block[...] + dot_t(left, w)
            left = dc[dy, pl.ds(pl.multiple_of(dx * maps_c, maps_c), row_c), :]
            block = gact.at[j, pix_v:pix]
            block[...] = block[...] + dot_t(left, w)
        return carry

    lax.fori_loop(0, 9, conv2_back, 0)
    for j in range(mid // TILE):
        ghs.j = j
        grad_act(ghs, a1, mi1, 0, bx1, j)
    exchanges[4][0]()
    q_we.stage4()
    q_ws[0].stage3()
    q_ws[2].stage2()
    exchanges[4][1]()
    merge_grads(bx1, tot1)

    def store_ga1(s, cols, value):
        ga1[s : s + CH, cols] = value

    grad_norm_all(a1, mi1, tot1, 0, store_ga1)
    for t in range(wide // TILE):
        block = dot(xt[t * TILE : (t + 1) * TILE, :], ga1[...]).astype(BF)
        gwr[t // 2, t % 2] = block.reshape(gwr.shape[2:])
    q_wr.start()
    q_ws[1].stage3()
    q_ws[0].stage4()

    n_dev = n_dp * n_rows

    def three(v):
        hi = v.astype(BF)
        rest = v - hi.astype(F32)
        mid_part = rest.astype(BF)
        return hi, mid_part, (rest - mid_part.astype(F32)).astype(BF)

    def owner_blocks(rows, width):
        share = width // n_dev
        step = 512
        total = jnp.zeros((n_dp * 8, 128), F32)
        for t in range(width // step):
            place = lax.broadcasted_iota(jnp.int32, (step, 128), 1)
            lane = lax.broadcasted_iota(jnp.int32, (step, 128), 0) + t * step
            pick = jnp.where(lane % share == place, 1.0, 0.0).astype(BF)
            owner = (lax.broadcasted_iota(jnp.int32, (8, step), 1) + t * step) // share
            vec = rows[:, t * step : (t + 1) * step]
            stack = jnp.concatenate(
                [jnp.where(owner == d * n_rows + me.r, vec, 0.0) for d in range(n_dp)], axis=0
            )
            for part in three(stack):
                total = total + dot(part, pick)
        return total

    small_rows = [t_[0:1] + t_[2:3] if k == 0 else t_[1:2] + t_[3:4] for t_ in (tot1, tot2) for k in (0, 1)]
    wide_rows = [tot3[0:1] + tot3[2:3], tot3[1:2] + tot3[3:4]]
    narrow = jnp.concatenate(small_rows + [jnp.zeros((4, mid), F32)], axis=0)
    broad = jnp.concatenate([jnp.zeros((4, wide), F32)] + wide_rows + [jnp.zeros((2, wide), F32)], axis=0)
    sb[...] = (owner_blocks(narrow, mid) + owner_blocks(broad, wide)).reshape(sb.shape)

    def small_cp(d, recv):
        peer = (me.dp + n_dp - d) % n_dp if recv else (me.dp + d) % n_dp
        return remote(sb.at[peer], rb.at[d - 1], sm_s.at[d - 1], sm_r.at[d - 1], {"dp": peer, "rows": me.r})

    for d in range(1, n_dp):
        small_cp(d, False).start()

    def grad_in(j):
        cols, slot = lanes(j), j % 2
        previous = (j - 2, gv_h, gc_h) if j >= 2 else (wide // TILE - 2 + j, yv_h, yc_h)
        for cp in out_copies(previous[0], slot, previous[1], previous[2]):
            cp.wait()
        w = wr[j // 2, j % 2].reshape(TILE, mid)
        gpre[:, cols] = gpre[:, cols] + dot_t(ga1[...], w)
        for s, g in chunks:
            store_out(slot, s, gpre[s : s + CH, cols])
        for cp in out_copies(j, slot, gv_h, gc_h):
            cp.start()

    steps = [
        q_wr.stage2, q_ws[2].stage3, q_ws[1].stage4, q_wr.stage3, q_ws[2].stage4, q_wr.stage4,
    ]
    for j in range(wide // TILE):
        grad_in(j)
        if j < 3:
            steps[j]()
    gwe_o[...] = q_we.finish()
    gws_o[0:3] = q_ws[0].finish()
    pool_chip.wait()
    for out, at, maps, valid in ((poolv_o, 0, maps_v, valid_v), (poolc_o, maps_v, maps_c, valid_c)):
        total = pf[at : at + maps] + pr[1, at : at + maps].astype(F32)
        out[...] = (total * (1.0 / valid)).reshape(out.shape)
    for step in steps[3:]:
        step()
    total = sb[me.dp]
    for d in range(1, n_dp):
        small_cp(d, True).wait_recv()
        total = total + rb[d - 1]
    small_o[...] = total
    gws_o[3:6] = q_ws[1].finish()
    gws_o[6:9] = q_ws[2].finish()
    gwr_o[...] = q_wr.finish()

    for j in (wide // TILE - 2, wide // TILE - 1):
        for cp in out_copies(j, j % 2, gv_h, gc_h):
            cp.wait()
    small_piece.drain()
    for p in pieces:
        p.drain()
    for e in exchanges:
        e[2]()
    rim_h[2]()
    rim_d[2]()
    for q in [q_we] + q_ws + [q_wr]:
        q.drain()
    for d in range(1, n_dp):
        small_cp(d, False).wait_send()


def block_step(n_dp, n_rows, xv, xc, mv, mc, wr, ws, we, g1, s1, g2, s2, g3, s3, cv, cc, cpv, cpc):
    img, views, rows_v, cols_v, wide = xv.shape
    crops, cols_c = xc.shape[1], xc.shape[3]
    mid = wr.shape[1]
    maps_v, maps_c = img * views, img * crops
    pix_v, pix_c = rows_v * cols_v * maps_v, cols_c * maps_c
    pix = pix_v + pix_c
    valid_v, valid_c = (rows_v * n_rows - 1) * cols_v, (n_rows - 1) * cols_c
    nz, nx = n_dp // 2, n_rows // 2

    def views_in(t):
        return t.transpose(0, 1, 3, 2, 4).reshape(maps_v, cols_v, rows_v, wide)

    def crops_in(t):
        return t.transpose(0, 2, 3, 1, 4).reshape(img, cols_c, crops, wide)

    grid4 = (nz, 2, nx, 2)
    vm = pl.BlockSpec(memory_space=pltpu.VMEM)
    hbm = pl.BlockSpec(memory_space=pl.ANY)
    s_wr, s_we = wr.shape[0], we.shape[0]
    V = pltpu.VMEM
    D = pltpu.SemaphoreType.DMA

    scratch = [
        V(grid4 + (s_wr, mid), BF), V((9,) + grid4 + (s_we, mid), BF), V(grid4 + (s_we, wide), BF),
        V(grid4 + (8, 128), F32),
        V((pix, 128), F32), V((cols_v, maps_v, 2, wide), BF), V((img, cols_c, crops, wide), BF),
        V((img, views, wide), F32), V((img, crops, wide), F32),
        V((pix, wide), BF), V((wide, pix), BF), V((pix, wide), BF),
        V((pix, mid), F32), V((pix, mid), F32), V((pix, wide), F32), V((pix, wide), F32),
        V((2, maps_v, cols_v, 2, TILE), F32), V((2, maps_c, cols_c, TILE // 128, 128), F32), V((2, pix, TILE), F32),
        V((4, (cols_v + 2) * maps_v, mid), BF), V((3, (cols_c + 2) * maps_c, mid), BF),
        V((4, (cols_v + 2) * maps_v, mid), BF), V((3, (cols_c + 2) * maps_c, mid), BF),
        V((pix, mid), BF), V((mid, pix), BF), V((pix, mid), BF),
        V(grid4 + (s_wr, mid), BF), V((9,) + grid4 + (s_we, mid), BF), V(grid4 + (s_we, wide), BF),
        V((nz, 2, nx, s_we, wide), BF), V((9, nz, 2, nx, s_we, mid), BF), V((nz, 2, nx, s_wr, mid), BF),
        V((2, nz, 2, s_we, wide // 2), BF), V((2, 9, nz, 2, s_we, mid // 2), BF), V((2, nz, 2, s_wr, mid // 2), BF),
        V((2, nz, s_we, wide // 2), BF), V((2, 9, nz, s_we, mid // 2), BF), V((2, nz, s_wr, mid // 2), BF),
        V((nz - 1, s_we, wide), BF), V((nz - 1, 9, s_we, mid), BF), V((nz - 1, s_wr, mid), BF),
        V((8, mid), F32), V((8, wide), F32),
        V((4, mid), F32), V((4, mid), F32), V((4, wide), F32),
        V((n_rows, 8, 128), F32),
        V((n_rows, 8, mid // 2), F32), V((n_rows, 8, mid // 2), F32), V((n_rows, 8, wide // 2), F32),
        V((n_rows, 8, mid // 2), F32), V((n_rows, 8, mid // 2), F32), V((n_rows, 8, wide // 2), F32),
        V((4, mid), F32), V((4, mid), F32), V((4, wide), F32),
        V((maps_v + maps_c, wide), F32), V((maps_v + maps_c, wide), BF), V((2, maps_v + maps_c, wide), BF),
        V((n_dp, 8, 128), F32), V((n_dp - 1, 8, 128), F32),
        D((3, cols_v + 1)), D((2, 2)), D((6, 12)), D((6, 12)), D((5, 5 + nz)), D((5, 5 + nz)),
        D((7, n_rows - 1)), D((7, n_rows - 1)), D((2, 4)), D((2, 4)), D((2,)), D((2,)), D((n_dp - 1,)), D((n_dp - 1,)),
    ]
    out_v = jax.ShapeDtypeStruct((maps_v, cols_v, 2, wide), F32)
    out_c = jax.ShapeDtypeStruct((maps_c, cols_c, wide // TILE, TILE // 128, 128), F32)
    outs = pl.pallas_call(
        functools.partial(kernel, n_dp, n_rows, (maps_v, cols_v, maps_c, cols_c, valid_v, valid_c)),
        out_shape=[
            out_v, out_c, out_v, out_c,
            jax.ShapeDtypeStruct(cpv.shape, F32), jax.ShapeDtypeStruct(cpc.shape, F32),
            jax.ShapeDtypeStruct((s_wr, mid), F32), jax.ShapeDtypeStruct((9, s_we, mid), F32),
            jax.ShapeDtypeStruct((s_we, wide), F32), jax.ShapeDtypeStruct((8, 128), F32),
        ],
        in_specs=[hbm] * 6 + [vm] * 11,
        out_specs=[hbm] * 4 + [vm] * 6,
        scratch_shapes=scratch,
        compiler_params=pltpu.CompilerParams(
            collective_id=0, has_side_effects=True, vmem_limit_bytes=63 << 20
        ),
    )(
        views_in(xv), crops_in(xc), views_in(cv), crops_in(cc), cpv, cpc,
        mv.transpose(1, 2, 0), mc.transpose(1, 2, 0), wr, ws.reshape(9, s_we, mid), we,
        g1.reshape(1, -1), s1.reshape(1, -1), g2.reshape(1, -1), s2.reshape(1, -1),
        g3.reshape(1, -1), s3.reshape(1, -1),
    )
    yv, yc, gv, gc, pool_v, pool_c, gwr, gws, gwe, small = outs

    def views_out(t):
        return t.reshape(img, views, cols_v, rows_v, wide).transpose(0, 1, 3, 2, 4)

    def crops_out(t):
        return t.reshape(img, crops, 1, cols_c, wide)

    e = mid // (n_dp * n_rows)
    f = wide // (n_dp * n_rows)
    return (
        views_out(yv), crops_out(yc),
        pool_v, pool_c,
        views_out(gv), crops_out(gc),
        gwr, gws.reshape(3, 3, s_we, mid), gwe,
        small[0, :e], small[1, :e], small[2, :e], small[3, :e], small[4, :f], small[5, :f],
    )


def fits(xv, xc, we):
    return we.shape[0] % 16 == 0 and xv.shape[2] == 2 and xc.shape[2] == 1


def with_halo(block, sides, width):
    for axis, dim in sides:
        count = lax.axis_size(axis)
        forward = [(i, i + 1) for i in range(count - 1)]
        backward = [(target, source) for source, target in forward]
        low = lax.ppermute(
            lax.slice_in_dim(block, block.shape[dim] - width, None, axis=dim), axis, forward
        )
        high = lax.ppermute(lax.slice_in_dim(block, 0, width, axis=dim), axis, backward)
        block = jnp.concatenate([low, block, high], axis=dim)
    return block


def from_behind(array, axis, by):
    peers = lax.axis_size(axis)
    pairs = [(i, i + by) for i in range(peers) if 0 <= i + by < peers]
    return lax.ppermute(array, axis, pairs)


def silu_slope(value):
    sig = jax.nn.sigmoid(value)
    return sig * (1.0 + value * (1.0 - sig))


def pixel_mask(mask_rows, col_count):
    expanded = jnp.broadcast_to(
        mask_rows.astype(jnp.float32)[..., None], mask_rows.shape + (col_count,)
    )
    return expanded.reshape(-1, 1)


def by_group(in_views, view_value, crop_value):
    return jnp.where(in_views, view_value, crop_value)


def norm_forward(acts, mask_col, view_pixels, in_views, counts, gain_vec, shift_vec):
    masked = acts * mask_col
    totals = lax.psum(
        (jnp.sum(masked[:view_pixels], axis=0), jnp.sum(masked[view_pixels:], axis=0)), "rows"
    )
    centered = acts - by_group(in_views, totals[0] / counts[0], totals[1] / counts[1])
    squares = jnp.square(centered * mask_col)
    spread = lax.psum(
        (jnp.sum(squares[:view_pixels], axis=0), jnp.sum(squares[view_pixels:], axis=0)), "rows"
    )
    inv_rows = by_group(
        in_views, lax.rsqrt(spread[0] / counts[0] + eps), lax.rsqrt(spread[1] / counts[1] + eps)
    )
    normal = centered * inv_rows
    return (normal * gain_vec + shift_vec, normal, inv_rows)


def norm_backward(grad_z, normal, inv_rows, mask_col, view_pixels, in_views, counts, gain_vec):
    product = grad_z * normal
    partials = (
        jnp.sum(product[:view_pixels], axis=0),
        jnp.sum(grad_z[:view_pixels], axis=0),
        jnp.sum(product[view_pixels:], axis=0),
        jnp.sum(grad_z[view_pixels:], axis=0),
    )
    totals = (
        lax.psum(partials[0].astype(jnp.bfloat16), "rows").astype(jnp.float32),
        lax.psum(partials[1].astype(jnp.bfloat16), "rows").astype(jnp.float32),
        lax.psum(partials[2].astype(jnp.bfloat16), "rows").astype(jnp.float32),
        lax.psum(partials[3].astype(jnp.bfloat16), "rows").astype(jnp.float32),
    )
    scale_mean = by_group(in_views, totals[0] / counts[0], totals[2] / counts[1])
    shift_mean = by_group(in_views, totals[1] / counts[0], totals[3] / counts[1])
    grad_acts = gain_vec * inv_rows * (grad_z - shift_mean - normal * scale_mean) * mask_col
    return (grad_acts.astype(jnp.bfloat16), partials[0] + partials[2], partials[1] + partials[3])


def with_rims(feature_map):
    extended = with_halo(feature_map, (("rows", 1),), 1)
    return jnp.pad(extended, ((0, 0), (0, 0), (1, 1), (0, 0)))


def gather_taps(extended, row_count, col_count):
    windows = []
    for row_step in range(3):
        for col_step in range(3):
            windows.append(
                extended[:, row_step : row_step + row_count, col_step : col_step + col_count, :]
            )
    return jnp.concatenate(windows, axis=-1).reshape(-1, 9 * extended.shape[-1])


def spread_taps(grad_patches, map_count, row_count, col_count, mid_width):
    pieces = grad_patches.reshape(map_count, row_count, col_count, 9, mid_width)
    padded = jnp.zeros((map_count, row_count + 2, col_count + 2, mid_width), jnp.float32)
    tap_index = 0
    for row_step in range(3):
        for col_step in range(3):
            padded = padded.at[
                :, row_step : row_step + row_count, col_step : col_step + col_count, :
            ].add(pieces[:, :, :, tap_index, :])
            tap_index += 1
    inside = padded[:, 1 : row_count + 1, 1 : col_count + 1, :]
    from_below = from_behind(
        padded[:, 0, 1 : col_count + 1, :].astype(jnp.bfloat16), "rows", -1
    ).astype(jnp.float32)
    from_above = from_behind(
        padded[:, row_count + 1, 1 : col_count + 1, :].astype(jnp.bfloat16), "rows", 1
    ).astype(jnp.float32)
    inside = inside.at[:, row_count - 1].add(from_below)
    inside = inside.at[:, 0].add(from_above)
    return inside.reshape(-1, mid_width)


def contract_rows(left, right):
    return lax.dot_general(
        left, right, (((0,), (0,)), ((), ())), preferred_element_type=jnp.float32
    )


def contract_cols(left, right):
    return lax.dot_general(
        left, right, (((1,), (1,)), ((), ())), preferred_element_type=jnp.float32
    )


def shards(
    x_views,
    x_crops,
    mask_views,
    mask_crops,
    w_reduce,
    w_spatial,
    w_expand,
    gain_reduce,
    shift_reduce,
    gain_spatial,
    shift_spatial,
    gain_expand,
    shift_expand,
    cot_views,
    cot_crops,
    cot_pool_views,
    cot_pool_crops,
):
    low_type = jnp.bfloat16
    gathered = (
        lax.all_gather(w_reduce.astype(low_type), ("dp", "rows"), axis=0, tiled=True),
        lax.all_gather(w_spatial.astype(low_type), ("dp", "rows"), axis=2, tiled=True),
        lax.all_gather(w_expand.astype(low_type), ("dp", "rows"), axis=0, tiled=True),
        lax.all_gather(gain_reduce.astype(low_type), ("dp", "rows"), axis=0, tiled=True),
        lax.all_gather(shift_reduce.astype(low_type), ("dp", "rows"), axis=0, tiled=True),
        lax.all_gather(gain_spatial.astype(low_type), ("dp", "rows"), axis=0, tiled=True),
        lax.all_gather(shift_spatial.astype(low_type), ("dp", "rows"), axis=0, tiled=True),
        lax.all_gather(gain_expand.astype(low_type), ("dp", "rows"), axis=0, tiled=True),
        lax.all_gather(shift_expand.astype(low_type), ("dp", "rows"), axis=0, tiled=True),
    )
    weight_one, weight_two, weight_three = (gathered[0], gathered[1], gathered[2])
    gain_one, shift_one, gain_two, shift_two, gain_three, shift_three = [
        entry.astype(jnp.float32) for entry in gathered[3:]
    ]
    in_width = weight_one.shape[0]
    mid_width = weight_one.shape[1]
    view_maps = x_views.shape[0] * x_views.shape[1]
    view_rows, view_cols = (x_views.shape[2], x_views.shape[3])
    crop_maps = x_crops.shape[0] * x_crops.shape[1]
    crop_rows, crop_cols = (x_crops.shape[2], x_crops.shape[3])
    view_pixels = view_maps * view_rows * view_cols
    total_pixels = view_pixels + crop_maps * crop_rows * crop_cols
    row_parts = lax.axis_size("rows")
    view_valid = (view_rows * row_parts - 1) * view_cols
    crop_valid = (crop_rows * row_parts - 1) * crop_cols
    counts = (float(view_maps * view_valid), float(crop_maps * crop_valid))
    mask_col = jnp.concatenate(
        [pixel_mask(mask_views, view_cols), pixel_mask(mask_crops, crop_cols)], axis=0
    )
    in_views = lax.broadcasted_iota(jnp.int32, (total_pixels, 1), 0) < view_pixels
    inputs = jnp.concatenate([x_views.reshape(-1, in_width), x_crops.reshape(-1, in_width)], axis=0)
    acts_one = jnp.dot(inputs, weight_one, preferred_element_type=jnp.float32)
    z_one, normal_one, inv_one = norm_forward(
        acts_one, mask_col, view_pixels, in_views, counts, gain_one, shift_one
    )
    hidden_one = (jax.nn.silu(z_one) * mask_col).astype(low_type)
    view_hidden = hidden_one[:view_pixels].reshape(view_maps, view_rows, view_cols, mid_width)
    crop_hidden = hidden_one[view_pixels:].reshape(crop_maps, crop_rows, crop_cols, mid_width)
    patches = jnp.concatenate(
        [
            gather_taps(with_rims(view_hidden), view_rows, view_cols),
            gather_taps(with_rims(crop_hidden), crop_rows, crop_cols),
        ],
        axis=0,
    )
    spatial_flat = weight_two.reshape(9 * mid_width, mid_width)
    acts_two = jnp.dot(patches, spatial_flat, preferred_element_type=jnp.float32)
    z_two, normal_two, inv_two = norm_forward(
        acts_two, mask_col, view_pixels, in_views, counts, gain_two, shift_two
    )
    hidden_two = (jax.nn.silu(z_two) * mask_col).astype(low_type)
    acts_three = jnp.dot(hidden_two, weight_three, preferred_element_type=jnp.float32)
    z_three, normal_three, inv_three = norm_forward(
        acts_three, mask_col, view_pixels, in_views, counts, gain_three, shift_three
    )
    pre_act = inputs.astype(jnp.float32) + z_three
    result = jax.nn.silu(pre_act) * mask_col
    pooled = (
        lax.psum(
            jnp.sum(
                result[:view_pixels].reshape(view_maps, view_rows * view_cols, in_width), axis=1
            ).astype(jnp.bfloat16),
            "rows",
        ).astype(jnp.float32),
        lax.psum(
            jnp.sum(
                result[view_pixels:].reshape(crop_maps, crop_rows * crop_cols, in_width), axis=1
            ).astype(jnp.bfloat16),
            "rows",
        ).astype(jnp.float32),
    )
    pool_views = (pooled[0] / view_valid).reshape(cot_pool_views.shape)
    pool_crops = (pooled[1] / crop_valid).reshape(cot_pool_crops.shape)
    view_grad = (
        cot_views.astype(jnp.float32).reshape(view_maps, view_rows * view_cols, in_width)
        + cot_pool_views.reshape(view_maps, 1, in_width) / view_valid
    )
    crop_grad = (
        cot_crops.astype(jnp.float32).reshape(crop_maps, crop_rows * crop_cols, in_width)
        + cot_pool_crops.reshape(crop_maps, 1, in_width) / crop_valid
    )
    grad_out = jnp.concatenate(
        [view_grad.reshape(-1, in_width), crop_grad.reshape(-1, in_width)], axis=0
    )
    grad_pre = grad_out * mask_col * silu_slope(pre_act)
    grad_three, dgain_three, dshift_three = norm_backward(
        grad_pre, normal_three, inv_three, mask_col, view_pixels, in_views, counts, gain_three
    )
    grad_expand = contract_rows(hidden_two, grad_three)
    grad_hidden_two = contract_cols(grad_three, weight_three)
    grad_z_two = grad_hidden_two * mask_col * silu_slope(z_two)
    grad_two, dgain_two, dshift_two = norm_backward(
        grad_z_two, normal_two, inv_two, mask_col, view_pixels, in_views, counts, gain_two
    )
    grad_spatial = contract_rows(patches, grad_two).reshape(3, 3, mid_width, mid_width)
    grad_patches = contract_cols(grad_two, spatial_flat)
    grad_hidden_one = jnp.concatenate(
        [
            spread_taps(grad_patches[:view_pixels], view_maps, view_rows, view_cols, mid_width),
            spread_taps(grad_patches[view_pixels:], crop_maps, crop_rows, crop_cols, mid_width),
        ],
        axis=0,
    )
    grad_z_one = grad_hidden_one * mask_col * silu_slope(z_one)
    grad_one, dgain_one, dshift_one = norm_backward(
        grad_z_one, normal_one, inv_one, mask_col, view_pixels, in_views, counts, gain_one
    )
    grad_reduce = contract_rows(inputs, grad_one)
    grad_inputs = contract_cols(grad_one, weight_one) + grad_pre
    summed = (
        lax.psum_scatter(grad_reduce, ("dp", "rows"), scatter_dimension=0, tiled=True),
        lax.psum_scatter(grad_spatial, ("dp", "rows"), scatter_dimension=2, tiled=True),
        lax.psum_scatter(grad_expand, ("dp", "rows"), scatter_dimension=0, tiled=True),
        lax.psum_scatter(dgain_one, ("dp", "rows"), scatter_dimension=0, tiled=True),
        lax.psum_scatter(dshift_one, ("dp", "rows"), scatter_dimension=0, tiled=True),
        lax.psum_scatter(dgain_two, ("dp", "rows"), scatter_dimension=0, tiled=True),
        lax.psum_scatter(dshift_two, ("dp", "rows"), scatter_dimension=0, tiled=True),
        lax.psum_scatter(dgain_three, ("dp", "rows"), scatter_dimension=0, tiled=True),
        lax.psum_scatter(dshift_three, ("dp", "rows"), scatter_dimension=0, tiled=True),
    )
    out_views = result[:view_pixels].reshape(x_views.shape)
    out_crops = result[view_pixels:].reshape(x_crops.shape)
    grad_views = grad_inputs[:view_pixels].reshape(x_views.shape)
    grad_crops = grad_inputs[view_pixels:].reshape(x_crops.shape)
    return (
        out_views,
        out_crops,
        pool_views,
        pool_crops,
        grad_views,
        grad_crops,
        summed[0],
        summed[1],
        summed[2],
        summed[3],
        summed[4],
        summed[5],
        summed[6],
        summed[7],
        summed[8],
    )


def solution(mesh):
    in_specs = (
        P("dp", None, "rows", None, None),
        P("dp", None, "rows", None, None),
        P("dp", None, "rows"),
        P("dp", None, "rows"),
        P(("dp", "rows"), None),
        P(None, None, ("dp", "rows"), None),
        P(("dp", "rows"), None),
        P(("dp", "rows")),
        P(("dp", "rows")),
        P(("dp", "rows")),
        P(("dp", "rows")),
        P(("dp", "rows")),
        P(("dp", "rows")),
        P("dp", None, "rows", None, None),
        P("dp", None, "rows", None, None),
        P("dp", None, None),
        P("dp", None, None),
    )
    out_specs = (
        P("dp", None, "rows", None, None),
        P("dp", None, "rows", None, None),
        P("dp", None, None),
        P("dp", None, None),
        P("dp", None, "rows", None, None),
        P("dp", None, "rows", None, None),
        P(("dp", "rows"), None),
        P(None, None, ("dp", "rows"), None),
        P(("dp", "rows"), None),
        P(("dp", "rows")),
        P(("dp", "rows")),
        P(("dp", "rows")),
        P(("dp", "rows")),
        P(("dp", "rows")),
        P(("dp", "rows")),
    )
    def step(*args):
        if fits(args[0], args[1], args[6]):
            return block_step(mesh.shape["dp"], mesh.shape["rows"], *args)
        return shards(*args)

    return jax.shard_map(step, mesh=mesh, in_specs=in_specs, out_specs=out_specs, check_vma=False)
```

```python
import functools

import jax
import jax.numpy as jnp
from jax import lax
from jax.experimental import pallas as pl
from jax.experimental.pallas import tpu as pltpu
from jax.sharding import PartitionSpec as P

MESH = pl.DeviceIdType.MESH
ALL = slice(None)
BF = jnp.bfloat16
F32 = jnp.float32
eps = 1e-05
TILE = 256


def lanes(j, width=TILE):
    if isinstance(j, int):
        return slice(j * width, (j + 1) * width)
    return pl.ds(pl.multiple_of(j * width, width), width)


def half(h, width, at=0, whole=None):
    if h is None:
        return ALL if whole is None else slice(at, at + whole)
    return slice(at + h * (width // 2), at + (h + 1) * (width // 2))


def dot(a, b):
    return lax.dot_general(a, b, (((1,), (0,)), ((), ())), preferred_element_type=F32)


def dot_t(a, b):
    return lax.dot_general(a, b, (((1,), (1,)), ((), ())), preferred_element_type=F32)


def dot_r(a, b):
    return lax.dot_general(a, b, (((0,), (0,)), ((), ())), preferred_element_type=F32)


def sigmoid(v):
    return 0.5 * jnp.tanh(0.5 * v) + 0.5


class Place:
    def __init__(self, n_dp, n_rows):
        self.ny, self.nc = 2, 2
        self.nz, self.nx = n_dp // 2, n_rows // 2
        self.n_dp, self.n_rows = n_dp, n_rows
        self.dp, self.r = lax.axis_index("dp"), lax.axis_index("rows")
        self.z, self.y = self.dp // 2, self.dp % 2
        self.x, self.c = self.r // 2, self.r % 2

    def dev(self, z, y, x, c):
        return {"dp": z * self.ny + y, "rows": x * self.nc + c}


def remote(src, dst, ssem, rsem, to):
    return pltpu.make_async_remote_copy(
        src_ref=src, dst_ref=dst, send_sem=ssem, recv_sem=rsem, device_id=to, device_id_type=MESH
    )


class Piece:
    def __init__(self, me, view, ssem, rsem):
        self.me, self.view, self.s, self.r, self.sent = me, view, ssem, rsem, []
        self.px = me.dev(me.z, me.y, 1 - me.x, me.c)
        self.py = me.dev(me.z, 1 - me.y, me.x, me.c)
        self.pc = me.dev(me.z, me.y, me.x, 1 - me.c)

    def pz(self, k):
        return self.me.dev((self.me.z + k) % self.me.nz, self.me.y, self.me.x, self.me.c)

    def send(self, k, src, dst, to):
        cp = remote(src, dst, self.s.at[k], self.r.at[k], to)
        cp.start()
        self.sent.append(cp)

    def got(self, k, dst):
        remote(dst, dst, self.s.at[k], self.r.at[k], self.pc).wait_recv()

    def drain(self):
        for cp in self.sent:
            cp.wait_send()


class Gather(Piece):
    def __init__(self, me, view, ssem, rsem, halves=(0, 1)):
        super().__init__(me, view, ssem, rsem)
        self.halves, n = halves, me.nz
        self.X, self.Y, self.D, self.C = n - 1, 2 * n - 1, (3 * n - 1, 4 * n - 1), 5 * n - 1

    def share(self, k, z, y, x, h, to):
        ref = self.view(z, y, x, self.me.c, h)
        self.send(k, ref, ref, to)

    def wait(self, k, z, y, x, h, c=None):
        self.got(k, self.view(z, y, x, self.me.c if c is None else c, h))

    def source(self, k):
        return (self.me.z + self.me.nz - k) % self.me.nz

    def start_z(self):
        me = self.me
        for k in range(1, me.nz):
            self.share(k - 1, me.z, me.y, me.x, None, self.pz(k))

    def start_xy(self):
        me = self.me
        self.share(self.X, me.z, me.y, me.x, None, self.px)
        self.share(self.Y, me.z, me.y, me.x, None, self.py)

    def got_z(self, k):
        me, z = self.me, self.source(k)
        self.wait(k - 1, z, me.y, me.x, None)
        self.share(self.X + k, z, me.y, me.x, None, self.px)
        self.share(self.Y + k, z, me.y, me.x, None, self.py)
        if k == me.nz - 1:
            self.share(self.C, ALL, me.y, me.x, None, self.pc)

    def diagonal(self):
        me = self.me
        for k in range(me.nz):
            z = self.source(k)
            self.wait(self.Y + k, z, 1 - me.y, me.x, None)
            self.share(self.D[0] + k, z, 1 - me.y, me.x, 0, self.px)
            self.wait(self.X + k, z, me.y, 1 - me.x, None)
            if 1 in self.halves:
                self.share(self.D[1] + k, z, me.y, 1 - me.x, 1, self.py)
        self.share(self.C + 1, ALL, 1 - me.y, me.x, None, self.pc)
        self.share(self.C + 2, ALL, me.y, 1 - me.x, None, self.pc)

    def last(self):
        me = self.me
        for h in self.halves:
            for k in range(me.nz):
                self.wait(self.D[h] + k, self.source(k), 1 - me.y, 1 - me.x, h)
            self.share(self.C + 3 + h, ALL, 1 - me.y, 1 - me.x, h, self.pc)

    def finish(self):
        me, o = self.me, 1 - self.me.c
        self.wait(self.C, ALL, me.y, me.x, None, o)
        self.wait(self.C + 1, ALL, 1 - me.y, me.x, None, o)
        self.wait(self.C + 2, ALL, me.y, 1 - me.x, None, o)
        for h in self.halves:
            self.wait(self.C + 3 + h, ALL, 1 - me.y, 1 - me.x, h, o)


class GatherPlane(Gather):
    def start(self):
        me = self.me
        self.share(0, me.z, me.y, me.x, None, self.px)
        self.share(1, me.z, me.y, me.x, None, self.py)

    def diagonal(self):
        me = self.me
        self.wait(1, me.z, 1 - me.y, me.x, None)
        self.share(2, me.z, 1 - me.y, me.x, 0, self.px)
        self.wait(0, me.z, me.y, 1 - me.x, None)
        self.share(3, me.z, me.y, 1 - me.x, 1, self.py)

    def plane(self):
        me = self.me
        for h in (0, 1):
            self.wait(2 + h, me.z, 1 - me.y, 1 - me.x, h)
        for k in range(1, me.nz):
            self.share(3 + k, me.z, ALL, ALL, None, self.pz(k))
        self.share(4 + me.nz, me.z, ALL, ALL, None, self.pc)

    def last(self):
        for k in range(1, self.me.nz):
            self.wait(3 + k, self.source(k), ALL, ALL, None)
            self.share(4 + self.me.nz + k, self.source(k), ALL, ALL, None, self.pc)

    def finish(self):
        for k in range(self.me.nz):
            self.wait(4 + self.me.nz + k, self.source(k), ALL, ALL, None, 1 - self.me.c)


class ReducePlane(Piece):
    def __init__(self, me, view, from_core, from_z, from_diagonal, from_xy, ssem, rsem):
        super().__init__(me, view, ssem, rsem)
        self.fc, self.fz, self.fd, self.fxy = from_core, from_z, from_diagonal, from_xy
        self.DG, self.H = me.nz, me.nz + 2

    def start(self):
        c = self.me.c
        self.send(0, self.view(ALL, ALL, ALL, 1 - c, None), self.fc(), self.pc)

    def stage2(self):
        me = self.me
        self.got(0, self.fc())
        ref = self.view(ALL, ALL, ALL, me.c, None)
        ref[...] = ref[...] + self.fc()[...]
        for k in range(1, me.nz):
            z = (me.z + k) % me.nz
            self.send(k, self.view(z, ALL, ALL, me.c, None), self.fz(k - 1), self.pz(k))

    def stage3(self):
        me = self.me
        ref = self.view(me.z, ALL, ALL, me.c, None)
        total = ref[...].astype(F32)
        for k in range(1, me.nz):
            self.got(k, self.fz(k - 1))
            total = total + self.fz(k - 1)[...].astype(F32)
        ref[...] = total.astype(BF)
        self.send(self.DG, self.view(me.z, 1 - me.y, 1 - me.x, me.c, 0), self.fd(0), self.px)
        self.send(self.DG + 1, self.view(me.z, 1 - me.y, 1 - me.x, me.c, 1), self.fd(1), self.py)
        self.send(self.H, self.view(me.z, me.y, 1 - me.x, me.c, 0), self.fxy(0, 0), self.px)
        self.send(self.H + 1, self.view(me.z, 1 - me.y, me.x, me.c, 1), self.fxy(1, 1), self.py)

    def stage4(self):
        me = self.me
        self.got(self.DG, self.fd(0))
        ref = self.view(me.z, 1 - me.y, me.x, me.c, 0)
        ref[...] = ref[...] + self.fd(0)[...]
        self.send(self.H + 2, ref, self.fxy(1, 0), self.py)
        self.got(self.DG + 1, self.fd(1))
        ref = self.view(me.z, me.y, 1 - me.x, me.c, 1)
        ref[...] = ref[...] + self.fd(1)[...]
        self.send(self.H + 3, ref, self.fxy(0, 1), self.px)

    def finish(self):
        me = self.me
        self.got(self.H, self.fxy(0, 0))
        self.got(self.H + 1, self.fxy(1, 1))
        self.got(self.H + 2, self.fxy(1, 0))
        self.got(self.H + 3, self.fxy(0, 1))
        total = self.view(me.z, me.y, me.x, me.c, None)[...].astype(F32)
        return total + self.fxy(0, None)[...].astype(F32) + self.fxy(1, None)[...].astype(F32)


class Reduce:
    def __init__(self, me, view, from_core, from_third, from_second, from_z, ssem, rsem):
        self.me, self.view, self.s, self.r = me, view, ssem, rsem
        self.fc, self.f3, self.f2, self.fz = from_core, from_third, from_second, from_z

    def core(self):
        me = self.me
        return remote(
            self.view(ALL, ALL, ALL, 1 - me.c, None),
            self.fc(ALL, ALL, ALL, None),
            self.s.at[0],
            self.r.at[0],
            me.dev(me.z, me.y, me.x, 1 - me.c),
        )

    def third(self, h):
        me = self.me
        place = (ALL, ALL, 1 - me.x) if h == 0 else (ALL, 1 - me.y, ALL)
        to = (me.z, me.y, 1 - me.x, me.c) if h == 0 else (me.z, 1 - me.y, me.x, me.c)
        return remote(
            self.view(*place, me.c, h), self.f3(h), self.s.at[1 + h], self.r.at[1 + h], me.dev(*to)
        )

    def second(self, h):
        me = self.me
        place = (ALL, 1 - me.y, me.x) if h == 0 else (ALL, me.y, 1 - me.x)
        to = (me.z, 1 - me.y, me.x, me.c) if h == 0 else (me.z, me.y, 1 - me.x, me.c)
        return remote(
            self.view(*place, me.c, h), self.f2(h), self.s.at[3 + h], self.r.at[3 + h], me.dev(*to)
        )

    def along_z(self, dz):
        me = self.me
        z = (me.z + dz) % me.nz
        return remote(
            self.view(z, me.y, me.x, me.c, None),
            self.fz(dz - 1),
            self.s.at[4 + dz],
            self.r.at[4 + dz],
            me.dev(z, me.y, me.x, me.c),
        )

    def start(self):
        self.core().start()

    def stage2(self):
        me = self.me
        self.core().wait_recv()
        for h in (0, 1):
            first = (ALL, ALL, 1 - me.x) if h == 0 else (ALL, 1 - me.y, ALL)
            ref = self.view(*first, me.c, h)
            ref[...] = ref[...] + self.fc(*first, h)[...]
            self.third(h).start()
        for h in (0, 1):
            rest = (ALL, ALL, me.x) if h == 0 else (ALL, me.y, ALL)
            ref = self.view(*rest, me.c, h)
            ref[...] = ref[...] + self.fc(*rest, h)[...]

    def stage3(self):
        me = self.me
        for h in (0, 1):
            self.third(h).wait_recv()
            kept = (ALL, ALL, me.x) if h == 0 else (ALL, me.y, ALL)
            ref = self.view(*kept, me.c, h)
            ref[...] = ref[...] + self.f3(h)[...]
            self.second(h).start()

    def stage4(self):
        me = self.me
        for h in (0, 1):
            self.second(h).wait_recv()
            ref = self.view(ALL, me.y, me.x, me.c, h)
            ref[...] = ref[...] + self.f2(h)[...]
        for dz in range(1, me.nz):
            self.along_z(dz).start()

    def finish(self):
        me = self.me
        total = self.view(me.z, me.y, me.x, me.c, None)[...].astype(F32)
        for dz in range(1, me.nz):
            self.along_z(dz).wait_recv()
            total = total + self.fz(dz - 1)[...].astype(F32)
        return total

    def drain(self):
        self.core().wait_send()
        for h in (0, 1):
            self.third(h).wait_send()
            self.second(h).wait_send()
        for dz in range(1, self.me.nz):
            self.along_z(dz).wait_send()


def kernel(n_dp, n_rows, sizes, *refs):
    (
        xv_h, xc_h, cv_h, cc_h, cpv_h, cpc_h, mv_in, mc_in, wr_in, ws_in, we_in,
        g1_in, s1_in, g2_in, s2_in, g3_in, s3_in,
        yv_h, yc_h, gv_h, gc_h, poolv_o, poolc_o, gwr_o, gws_o, gwe_o, small_o,
        wr, ws, we, par, mask, raw_v, raw_c, cpv, cpc, x, xt, cot, a1, a2, a3, gpre, ysv, ysc, gact,
        hv, hc, dv, dc, h2, h2t, ga1, gwr, gws, gwe,
        fc_we, fc_ws, fc_wr, f3_we, f3_ws, f3_wr, f2_we, f2_ws, f2_wr, fz_we, fz_ws, fz_wr, fp_we, fd_we, fh_we,
        p1, p3, mi1, mi2, mi3, cnt, ex1, ex2, ex3, bx1, bx2, bx3, tot1, tot2, tot3,
        pf, pb, pr, sb, rb,
        in_sem, out_sem, ag_s, ag_r, rs_s, rs_r, ex_s, ex_r, halo_s, halo_r, pool_s, pool_r, sm_s, sm_r,
    ) = refs
    (maps_v, cols_v, maps_c, cols_c, valid_v, valid_c) = sizes
    me = Place(n_dp, n_rows)
    mid, wide = a1.shape[1], a3.shape[1]
    pix_v = 2 * cols_v * maps_v
    pix = a1.shape[0]
    row_v, row_c = cols_v * maps_v, cols_c * maps_c
    count = (float(maps_v * valid_v), float(maps_c * valid_c))
    CH = 32
    chunks = [(s, 0 if s < pix_v else 1) for s in range(0, pix, CH)]

    barrier = pltpu.get_barrier_semaphore()
    peers = [{"dp": me.dp, "rows": (me.r + d) % n_rows} for d in range(1, n_rows)]
    peers += [{"dp": (me.dp + d) % n_dp, "rows": me.r} for d in range(1, n_dp)]
    for peer in peers:
        pl.semaphore_signal(barrier, inc=1, device_id=peer, device_id_type=MESH)

    def fetch(k, views, crops):
        return [
            pltpu.make_async_copy(views.at[:, col], raw_v.at[col], in_sem.at[k, col]) for col in range(cols_v)
        ] + [pltpu.make_async_copy(crops, raw_c, in_sem.at[k, cols_v])]

    def arrange(out):
        def body(j, carry):
            cols = lanes(j)
            for col in range(cols_v):
                for r in (0, 1):
                    at = r * row_v + col * maps_v
                    out[at : at + maps_v, cols] = raw_v[col, :, r, cols]
            for col in range(cols_c):
                at = pix_v + col * maps_c
                out[at : at + maps_c, cols] = raw_c[:, col, :, cols].reshape(maps_c, TILE)
            return carry

        lax.fori_loop(0, wide // TILE, body, 0)

    x_copies, cot_copies = fetch(0, xv_h, xc_h), fetch(1, cv_h, cc_h)
    pool_copies = [
        pltpu.make_async_copy(cpv_h, cpv, in_sem.at[2, 0]),
        pltpu.make_async_copy(cpc_h, cpc, in_sem.at[2, 1]),
    ]
    for cp in x_copies + pool_copies:
        cp.start()

    here = (me.z, me.y, me.x, me.c)
    wr[here] = wr_in[...].astype(BF)
    ws[(ALL,) + here] = ws_in[...].astype(BF)
    we[here] = we_in[...].astype(BF)
    own = par.at[here]
    own[...] = jnp.zeros(own.shape, F32)
    for i, ref in enumerate((g1_in, s1_in, g2_in, s2_in, g3_in, s3_in)):
        own[i : i + 1, 0 : ref.shape[1]] = ref[...].astype(BF).astype(F32)

    def mask_column(row_of, per, maps):
        lane = lax.broadcasted_iota(jnp.int32, (maps, 16), 1)
        place = lax.broadcasted_iota(jnp.int32, (maps, 16), 0)
        total = jnp.zeros((maps, 16), F32)
        for k in range(per):
            hit = jnp.logical_and(place % per == k, lane == place // per)
            total = total + jnp.where(hit, row_of(k).astype(F32), 0.0)
        return jnp.broadcast_to(jnp.sum(total, axis=1, keepdims=True), (maps, 128))

    for r in (0, 1):
        column = mask_column(lambda k: mv_in[k, r : r + 1, :], mv_in.shape[0], maps_v)
        for col in range(cols_v):
            at = r * row_v + col * maps_v
            mask[at : at + maps_v] = column
    column = mask_column(lambda k: mc_in[k], mc_in.shape[0], maps_c)
    for col in range(cols_c):
        at = pix_v + col * maps_c
        mask[at : at + maps_c] = column

    cnt_own = cnt.at[me.r]
    cnt_own[0:1] = jnp.sum(mask[0:pix_v], axis=0, keepdims=True)
    cnt_own[1:2] = jnp.sum(mask[pix_v:pix], axis=0, keepdims=True)
    cnt_own[2:8] = jnp.zeros((6, 128), F32)

    pl.semaphore_wait(barrier, len(peers))

    def piece(k, view, halves=(0, 1), form=Gather):
        return form(me, view, ag_s.at[k], ag_r.at[k], *(() if form is GatherPlane else (halves,)))

    part = wide // 2
    small_piece = piece(0, lambda z, y, x, c, h: par.at[z, y, x, c], (0,))
    pieces = [piece(1, lambda z, y, x, c, h: wr.at[z, y, x, c, :, half(h, mid)])]
    for i in range(3):
        pieces.append(
            piece(2 + i, lambda z, y, x, c, h, i=i: ws.at[3 * i : 3 * i + 3, z, y, x, c, :, half(h, mid)])
        )
    pieces.append(piece(5, lambda z, y, x, c, h: we.at[z, y, x, c, :, half(h, part, 0, part)]))
    plane = piece(6, lambda z, y, x, c, h: we.at[z, y, x, c, :, half(h, part, part, part)], form=GatherPlane)

    def exchange(k, buf):
        def cp(d, recv):
            peer = (me.r + n_rows - d) % n_rows if recv else (me.r + d) % n_rows
            ref = buf.at[peer if recv else me.r]
            return remote(ref, ref, ex_s.at[k, d - 1], ex_r.at[k, d - 1], {"dp": me.dp, "rows": peer})

        def send():
            for d in range(1, n_rows):
                cp(d, False).start()

        def wait():
            for d in range(1, n_rows):
                cp(d, True).wait_recv()

        def drain():
            for d in range(1, n_rows):
                cp(d, False).wait_send()

        return send, wait, drain

    exchanges = [
        exchange(k, b)
        for k, b in enumerate(
            (cnt, ex1, ex2, ex3.at[0], ex3.at[1], bx1, bx2, bx3.at[0], bx3.at[1])
        )
    ]
    CNT, EX1, EX2, EX3, BX1, BX2, BX3 = 0, 1, 2, 3, 5, 6, 7

    def rim(k, v, c):
        def cps(up):
            peer = {"dp": me.dp, "rows": (me.r + n_rows - 1) % n_rows if up else (me.r + 1) % n_rows}
            base = 0 if up else 2
            vs, vd = (1, 3) if up else (2, 0)
            csrc, cd = (1, 2) if up else (1, 0)
            return [
                remote(
                    v.at[vs, maps_v : maps_v + row_v],
                    v.at[vd, maps_v : maps_v + row_v],
                    halo_s.at[k, base],
                    halo_r.at[k, base],
                    peer,
                ),
                remote(
                    c.at[csrc, maps_c : maps_c + row_c],
                    c.at[cd, maps_c : maps_c + row_c],
                    halo_s.at[k, base + 1],
                    halo_r.at[k, base + 1],
                    peer,
                ),
            ]

        def each(up, fn):
            def body():
                for cp in cps(up):
                    fn(cp)

            return body

        first, last = me.r == 0, me.r == n_rows - 1

        def send():
            pl.when(jnp.logical_not(first))(each(True, lambda cp: cp.start()))
            pl.when(jnp.logical_not(last))(each(False, lambda cp: cp.start()))

        def wait():
            pl.when(jnp.logical_not(last))(each(True, lambda cp: cp.wait_recv()))
            pl.when(jnp.logical_not(first))(each(False, lambda cp: cp.wait_recv()))

        def drain():
            pl.when(jnp.logical_not(first))(each(True, lambda cp: cp.wait_send()))
            pl.when(jnp.logical_not(last))(each(False, lambda cp: cp.wait_send()))

        return send, wait, drain

    rim_h, rim_d = rim(0, hv, hc), rim(1, dv, dc)

    def clear_rims(v, c):
        zv, zc = jnp.zeros((maps_v, mid), BF), jnp.zeros((maps_c, mid), BF)
        for r in range(4):
            v[r, 0:maps_v] = zv
            v[r, maps_v + row_v : 2 * maps_v + row_v] = zv
        for r in range(3):
            c[r, 0:maps_c] = zc
            c[r, maps_c + row_c : 2 * maps_c + row_c] = zc

        @pl.when(me.r == 0)
        def _():
            v[0, maps_v : maps_v + row_v] = jnp.zeros((row_v, mid), BF)
            c[0, maps_c : maps_c + row_c] = jnp.zeros((row_c, mid), BF)

        @pl.when(me.r == n_rows - 1)
        def _():
            v[3, maps_v : maps_v + row_v] = jnp.zeros((row_v, mid), BF)
            c[2, maps_c : maps_c + row_c] = jnp.zeros((row_c, mid), BF)

    def tile_rows(ref, j):
        per = me.nz * TILE // mid
        return ref[j * per : (j + 1) * per]

    def fold(v):
        return jnp.sum(v.reshape(v.shape[0] // 8, 8, v.shape[1]), axis=0)

    def put(buf, j, k, value):
        tiles = buf.shape[2] // TILE
        if isinstance(j, int):
            buf[me.r, 4 * (j // tiles) + k : 4 * (j // tiles) + k + 1, lanes(j % tiles)] = value
        else:
            buf[me.r, pl.ds(4 * (j // tiles) + k, 1), lanes(j % tiles)] = value

    def masked(s):
        return jnp.concatenate([mask[s : s + CH]] * (TILE // 128), axis=1)

    def local_stats(a, buf, n_tiles, first=0):
        def body(j, carry):
            cols = lanes(j + first)
            for grp in (0, 1):
                acc = jnp.zeros((8, TILE), F32)
                for s, g in chunks:
                    if g == grp:
                        acc = acc + fold(a[s : s + CH, cols] * masked(s))
                total = jnp.sum(acc, axis=0, keepdims=True)
                n_own = jnp.maximum(cnt[me.r, grp : grp + 1, 0:1], 1.0)
                mean = total / n_own
                acc = jnp.zeros((8, TILE), F32)
                for s, g in chunks:
                    if g == grp:
                        d = (a[s : s + CH, cols] - mean) * masked(s)
                        acc = acc + fold(d * d)
                put(buf, j, 2 * grp, total)
                put(buf, j, 2 * grp + 1, jnp.sum(acc, axis=0, keepdims=True))
            return carry

        for j in range(n_tiles):
            body(j, 0) if n_tiles <= 2 else None
        if n_tiles > 2:
            lax.fori_loop(0, n_tiles, body, 0)

    def merge_stats(buf, mi, at=0):
        width = buf.shape[2]
        for hf in (0, 1):
            for grp in (0, 1):
                k = 4 * hf + 2 * grp
                total = sum(buf[i, k : k + 1] for i in range(n_rows))
                mean = total / count[grp]
                spread = jnp.zeros_like(mean)
                for i in range(n_rows):
                    n_i = cnt[i, grp : grp + 1, 0:1]
                    off = buf[i, k : k + 1] / jnp.maximum(n_i, 1.0) - mean
                    spread = spread + buf[i, k + 1 : k + 2] + n_i * (off * off)
                mi[2 * grp : 2 * grp + 1, at + hf * width : at + (hf + 1) * width] = mean
                mi[2 * grp + 1 : 2 * grp + 2, at + hf * width : at + (hf + 1) * width] = lax.rsqrt(
                    spread / count[grp] + eps
                )

    def merge_grads(buf, tot, at=0):
        width = buf.shape[2]
        for hf in (0, 1):
            block = buf[0, 4 * hf : 4 * hf + 4]
            for i in range(1, n_rows):
                block = block + buf[i, 4 * hf : 4 * hf + 4]
            tot[0:4, at + hf * width : at + (hf + 1) * width] = block

    def expand_params():
        blocks = par[...].reshape(n_dp * n_rows * 8, 128).astype(BF)
        n_dev = n_dp * n_rows
        for out, width in ((p1, mid), (p3, wide)):
            share = width // n_dev
            step = 512
            for t in range(width // step):
                lane = lax.broadcasted_iota(jnp.int32, (128, step), 1) + t * step
                place = lax.broadcasted_iota(jnp.int32, (128, step), 0)
                pick = jnp.where(lane % share == place, 1.0, 0.0).astype(BF)
                spread = dot(blocks, pick).reshape(n_dev, 8, step)
                owner = (lax.broadcasted_iota(jnp.int32, (8, step), 1) + t * step) // share
                total = jnp.zeros((8, step), F32)
                for d in range(n_dev):
                    total = total + jnp.where(owner == d, spread[d], 0.0)
                out[:, t * step : (t + 1) * step] = total

    def gain(out, i, cols):
        return out[i : i + 1, cols]

    small_piece.start_z()
    small_piece.start_xy()
    pieces[0].start_z()
    pieces[0].start_xy()
    exchanges[CNT][0]()
    plane.start()
    for p in pieces[1:]:
        p.start_xy()
    clear_rims(hv, hc)
    clear_rims(dv, dc)
    for cp in x_copies:
        cp.wait()
    arrange(x)
    for cp in cot_copies:
        cp.start()

    def step0(t):
        pieces[t].got_z(1)
        if t + 1 < len(pieces):
            pieces[t + 1].start_z()
        for k in range(2, me.nz):
            pieces[t].got_z(k)

    for k in range(1, me.nz):
        small_piece.got_z(k)
    step0(0)
    plane.diagonal()
    small_piece.diagonal()
    for t in range(wide // TILE):
        xt[t * TILE : (t + 1) * TILE, :] = x[:, t * TILE : (t + 1) * TILE].T
    step0(1)
    pieces[0].diagonal()
    small_piece.last()
    for cp in cot_copies:
        cp.wait()
    arrange(cot)
    step0(2)
    pieces[1].diagonal()
    pieces[0].last()
    small_piece.finish()
    expand_params()
    pieces[0].finish()
    exchanges[CNT][1]()

    def conv1(j, carry):
        w = wr[:, :, :, :, :, lanes(j)].reshape(wide, TILE)
        a1[:, lanes(j)] = dot(x[...], w)
        return carry

    lax.fori_loop(0, mid // TILE, conv1, 0)
    local_stats(a1, ex1, mid // TILE)
    exchanges[EX1][0]()
    step0(3)
    pieces[2].diagonal()
    pieces[1].last()
    exchanges[EX1][1]()
    merge_stats(ex1, mi1)

    def store_rows(v, c, s, cols, value):
        if s < pix_v:
            r, o = s // row_v, s % row_v
            v[1 + r, maps_v + o : maps_v + o + CH, cols] = value
        else:
            o = s - pix_v
            c[1, maps_c + o : maps_c + o + CH, cols] = value

    def act(a, mi, i, store):
        def body(j, carry):
            cols = lanes(j)
            scale = [mi[2 * g + 1 : 2 * g + 2, cols] * gain(p1, i, cols) for g in (0, 1)]
            mean = [mi[2 * g : 2 * g + 1, cols] for g in (0, 1)]
            shift = gain(p1, i + 1, cols)
            for s, g in chunks:
                zed = (a[s : s + CH, cols] - mean[g]) * scale[g] + shift
                store(s, cols, (zed * sigmoid(zed) * masked(s)).astype(BF))
            return carry

        for j in range(mid // TILE):
            body(j, 0)

    act(a1, mi1, 0, lambda s, cols, value: store_rows(hv, hc, s, cols, value))
    rim_h[0]()
    step0(4)
    plane.plane()
    pieces[3].diagonal()
    pieces[2].last()
    pieces[1].finish()
    rim_h[1]()

    def windows(v, c, dy, dx):
        left = [v[r + dy, dx * maps_v : dx * maps_v + row_v, :] for r in (0, 1)]
        return jnp.concatenate(left + [c[dy, dx * maps_c : dx * maps_c + row_c, :]], axis=0)

    def conv2(dy):
        left = jnp.concatenate([windows(hv, hc, dy, dx) for dx in range(3)], axis=1)
        for j in range(mid // TILE):
            w = ws[3 * dy : 3 * dy + 3, :, :, :, :, :, lanes(j)].reshape(3 * mid, TILE)
            part_sum = dot(left, w)
            a2[:, lanes(j)] = part_sum if dy == 0 else a2[:, lanes(j)] + part_sum

    conv2(0)
    pieces[4].diagonal()
    pieces[2].finish()
    conv2(1)
    pieces[3].last()
    pieces[3].finish()
    conv2(2)
    local_stats(a2, ex2, mid // TILE)
    exchanges[EX2][0]()
    pieces[4].last()
    exchanges[EX2][1]()
    merge_stats(ex2, mi2)

    def store_h2(s, cols, value):
        h2[s : s + CH, cols] = value

    act(a2, mi2, 2, store_h2)
    for cp in pool_copies:
        cp.wait()

    def conv3(j, carry):
        w = we[:, :, :, :, :, lanes(j)].reshape(mid, TILE)
        a3[:, lanes(j)] = dot(h2[...], w)
        return carry

    tiles = wide // TILE // 2
    pieces[4].finish()
    lax.fori_loop(0, tiles, conv3, 0)
    local_stats(a3, ex3.at[0], tiles)
    exchanges[EX3][0]()
    plane.last()
    plane.finish()
    lax.fori_loop(tiles, 2 * tiles, conv3, 0)
    local_stats(a3, ex3.at[1], tiles, tiles)
    exchanges[EX3 + 1][0]()
    h2t[...] = h2[...].T
    exchanges[EX3][1]()
    merge_stats(ex3.at[0], mi3)

    def out_copies(j, slot, views, crops):
        return [
            pltpu.make_async_copy(ysv.at[slot], views.at[:, :, :, lanes(j)], out_sem.at[slot, 0]),
            pltpu.make_async_copy(ysc.at[slot], crops.at[:, :, j], out_sem.at[slot, 1]),
        ]

    def store_out(slot, s, value):
        if s < pix_v:
            ysv[slot, :, s % row_v // maps_v, s // row_v, :] = value
        else:
            col, at = (s - pix_v) // maps_c, (s - pix_v) % maps_c
            for k in (0, 1):
                ysc[slot, at : at + CH, col, k, :] = value[:, k * 128 : (k + 1) * 128]

    def last(q, jj, carry):
        for slot in (0, 1):
            j = 2 * jj + slot
            cols = lanes(j)

            def free_slot():
                for cp in out_copies(j, slot, yv_h, yc_h):
                    cp.wait()

            if q > 0:
                free_slot()
            else:
                pl.when(jj > 0)(free_slot)

            mean = [mi3[2 * g : 2 * g + 1, cols] for g in (0, 1)]
            inv = [mi3[2 * g + 1 : 2 * g + 2, cols] for g in (0, 1)]
            scale = [inv[g] * gain(p3, 4, cols) for g in (0, 1)]
            sh = gain(p3, 5, cols)
            sums = [jnp.zeros((8, TILE), F32) for _ in range(4)]
            pooled = [jnp.zeros((CH, TILE), F32) for _ in range((maps_v + maps_c) // CH)]
            per_v, per_c = CH // cpv.shape[1], CH // cpc.shape[1]
            cps = [
                cpv[s : s + per_v, :, cols].reshape(CH, TILE) * (1.0 / valid_v)
                for s in range(0, cpv.shape[0], per_v)
            ] + [
                cpc[s : s + per_c, :, cols].reshape(CH, TILE) * (1.0 / valid_c)
                for s in range(0, cpc.shape[0], per_c)
            ]
            for s, g in chunks:
                which = (s % maps_v) // CH if g == 0 else (maps_v + (s - pix_v) % maps_c) // CH
                rows = slice(s, s + CH)
                m = masked(s)
                off = a3[rows, cols] - mean[g]
                pre = x[rows, cols].astype(F32) + (off * scale[g] + sh)
                sig = sigmoid(pre)
                act_out = pre * sig
                out = act_out * m
                store_out(slot, s, out)
                pooled[which] = pooled[which] + out
                slope = act_out + sig * (1.0 - act_out)
                gp = (cot[rows, cols].astype(F32) + cps[which]) * m * slope
                gpre[rows, cols] = gp
                sums[2 * g] = sums[2 * g] + fold(gp * off)
                sums[2 * g + 1] = sums[2 * g + 1] + fold(gp)
            for k in range(4):
                total = jnp.sum(sums[k], axis=0, keepdims=True)
                put(bx3.at[q], j - q * tiles, k, total * inv[k // 2] if k % 2 == 0 else total)
            for i, value in enumerate(pooled):
                pf[i * CH : (i + 1) * CH, cols] = value
                pb[i * CH : (i + 1) * CH, cols] = value.astype(BF)
            for cp in out_copies(j, slot, yv_h, yc_h):
                cp.start()
        return carry

    core_peer = {"dp": me.dp, "rows": me.x * 2 + 1 - me.c}
    chip_peer = {"dp": me.dp, "rows": (1 - me.x) * 2 + me.c}
    pool_core = remote(pb, pr.at[0], pool_s.at[0], pool_r.at[0], core_peer)
    lax.fori_loop(0, tiles // 2, functools.partial(last, 0), 0)
    exchanges[BX3][0]()
    exchanges[EX3 + 1][1]()
    merge_stats(ex3.at[1], mi3, wide // 2)
    lax.fori_loop(tiles // 2, tiles, functools.partial(last, 1), 0)
    exchanges[BX3 + 1][0]()
    pool_core.start()

    def coefs(mi, tot, gn, cols):
        out = []
        for g in (0, 1):
            mean, inv = mi[2 * g : 2 * g + 1, cols], mi[2 * g + 1 : 2 * g + 2, cols]
            dg, ds = tot[2 * g : 2 * g + 1, cols], tot[2 * g + 1 : 2 * g + 2, cols]
            out.append((mean, gn * inv, ds / count[g], dg / count[g] * inv))
        return out

    def norm_back(gz, a, co, s, cols):
        mean, k0, k1, k2 = co
        return (k0 * (gz - k1 - (a[s : s + CH, cols] - mean) * k2) * masked(s)).astype(BF)

    def grad_three(j, carry):
        cols = lanes(j)
        co = coefs(mi3, tot3, gain(p3, 4, cols), cols)
        for s, g in chunks:
            cot[s : s + CH, cols] = norm_back(gpre[s : s + CH, cols], a3, co[g], s, cols)
        gwe[:, :, :, :, :, cols] = (
            dot(h2t[...], cot[:, cols]).astype(BF).reshape(gwe.shape[:5] + (TILE,))
        )
        return carry

    q_first = ReducePlane(
        me,
        lambda z, y, x, c, h: gwe.at[z, y, x, c, :, half(h, part, 0, part)],
        lambda: fc_we.at[:, :, :, :, 0:part],
        lambda k: fp_we.at[k],
        lambda h: fd_we.at[h],
        lambda k, h: fh_we.at[k, :, half(h, part)],
        rs_s.at[0],
        rs_r.at[0],
    )

    def reducer(k, view, fc, f3, f2, fz):
        return Reduce(me, view, fc, f3, f2, fz, rs_s.at[k], rs_r.at[k])

    q_we = reducer(
        1,
        lambda z, y, x, c, h: gwe.at[z, y, x, c, :, half(h, part, part, part)],
        lambda z, y, x, h: fc_we.at[z, y, x, :, half(h, part, part, part)],
        lambda h: f3_we.at[h],
        lambda h: f2_we.at[h],
        lambda k: fz_we.at[k],
    )
    q_ws = [
        reducer(
            2 + i,
            lambda z, y, x, c, h, i=i: gws.at[3 * i : 3 * i + 3, z, y, x, c, :, half(h, mid)],
            lambda z, y, x, h, i=i: fc_ws.at[3 * i : 3 * i + 3, z, y, x, :, half(h, mid)],
            lambda h, i=i: f3_ws.at[h, 3 * i : 3 * i + 3],
            lambda h, i=i: f2_ws.at[h, 3 * i : 3 * i + 3],
            lambda k, i=i: fz_ws.at[k, 3 * i : 3 * i + 3],
        )
        for i in range(3)
    ]
    few = wr.shape[4] // 2
    q_wr = [
        reducer(
            5 + i,
            lambda z, y, x, c, h, i=i: gwr.at[z, y, x, c, i * few : (i + 1) * few, half(h, mid)],
            lambda z, y, x, h, i=i: fc_wr.at[z, y, x, i * few : (i + 1) * few, half(h, mid)],
            lambda h, i=i: f3_wr.at[h, :, :, i * few : (i + 1) * few],
            lambda h, i=i: f2_wr.at[h, :, i * few : (i + 1) * few],
            lambda k, i=i: fz_wr.at[k, i * few : (i + 1) * few],
        )
        for i in range(2)
    ]

    exchanges[BX3][1]()
    merge_grads(bx3.at[0], tot3)
    lax.fori_loop(0, tiles, grad_three, 0)
    q_first.start()
    exchanges[BX3 + 1][1]()
    merge_grads(bx3.at[1], tot3, wide // 2)
    lax.fori_loop(tiles, 2 * tiles, grad_three, 0)
    q_we.start()
    q_first.stage2()

    def grad_act(gh, a, mi, i, buf, j):
        cols = lanes(j)
        gn, sh = gain(p1, i, cols), gain(p1, i + 1, cols)
        sums = [jnp.zeros((8, TILE), F32) for _ in range(4)]
        for s, g in chunks:
            rows = slice(s, s + CH)
            mean, inv = mi[2 * g : 2 * g + 1, cols], mi[2 * g + 1 : 2 * g + 2, cols]
            off = a[rows, cols] - mean
            zed = off * (inv * gn) + sh
            sig = sigmoid(zed)
            gz = gh[rows, cols] * masked(s) * (sig * (1.0 + zed * (1.0 - sig)))
            gh[rows, cols] = gz
            sums[2 * g] = sums[2 * g] + fold(gz * off)
            sums[2 * g + 1] = sums[2 * g + 1] + fold(gz)
        for k in range(4):
            total = jnp.sum(sums[k], axis=0, keepdims=True)
            inv = mi[2 * (k // 2) + 1 : 2 * (k // 2) + 2, cols]
            put(buf, j, k, total * inv if k % 2 == 0 else total)

    for j in range(mid // TILE):
        w = tile_rows(we, j).reshape(TILE, wide)
        gact[j, :, :] = dot_t(cot[...], w)

    class Cols:
        def __getitem__(self, key):
            rows, cols = key
            return gact[self.j, rows, :]

        def __setitem__(self, key, value):
            rows, cols = key
            gact[self.j, rows, :] = value

    ghs = Cols()
    for j in range(mid // TILE):
        ghs.j = j
        grad_act(ghs, a2, mi2, 2, bx2, j)
    exchanges[BX2][0]()
    q_we.stage2()
    pool_core.wait()
    pf[...] = pf[...] + pr[0].astype(F32)
    pb[...] = pf[...].astype(BF)
    pool_chip = remote(pb, pr.at[1], pool_s.at[1], pool_r.at[1], chip_peer)
    pool_chip.start()
    exchanges[BX2][1]()
    merge_grads(bx2, tot2)

    def grad_norm_all(a, mi, tot, i, store):
        for j in range(mid // TILE):
            ghs.j = j
            cols = lanes(j)
            co = coefs(mi, tot, gain(p1, i, cols), cols)
            for s, g in chunks:
                store(s, cols, norm_back(ghs[s : s + CH, cols], a, co[g], s, cols))

    grad_norm_all(a2, mi2, tot2, 2, lambda s, cols, value: store_rows(dv, dc, s, cols, value))
    rim_d[0]()

    def grad_taps(dy):
        right = windows(dv, dc, 1, 1)
        for dx in range(3):
            total = dot_r(windows(hv, hc, dy, dx), right)
            gws[3 * dy + dx] = total.astype(BF).reshape(gws.shape[1:])

    grad_taps(0)
    q_ws[0].start()
    q_first.stage3()
    grad_taps(1)
    q_ws[1].start()
    q_ws[0].stage2()
    q_we.stage3()
    grad_taps(2)
    q_ws[2].start()
    q_ws[1].stage2()
    q_first.stage4()
    rim_d[1]()

    def conv2_back(dy):
        left = jnp.concatenate([windows(dv, dc, 2 - dy, 2 - dx) for dx in range(3)], axis=1)
        for j in range(mid // TILE):
            w = jnp.concatenate(
                [tile_rows(ws.at[3 * dy + dx], j).reshape(TILE, mid) for dx in range(3)], axis=1
            )
            part_sum = dot_t(left, w)
            gact[j] = part_sum if dy == 0 else gact[j] + part_sum

    conv2_back(0)
    q_ws[0].stage3()
    q_ws[2].stage2()
    conv2_back(1)
    q_we.stage4()
    conv2_back(2)
    for j in range(mid // TILE):
        ghs.j = j
        grad_act(ghs, a1, mi1, 0, bx1, j)
    exchanges[BX1][0]()
    q_ws[1].stage3()
    gwe_o[:, 0:part] = q_first.finish()
    exchanges[BX1][1]()
    merge_grads(bx1, tot1)

    def store_ga1(s, cols, value):
        ga1[s : s + CH, cols] = value

    grad_norm_all(a1, mi1, tot1, 0, store_ga1)
    for t in range(wide // TILE):
        block = dot(xt[t * TILE : (t + 1) * TILE, :], ga1[...]).astype(BF)
        gwr[t // 2, t % 2] = block.reshape(gwr.shape[2:])
    for q in q_wr:
        q.start()
    q_ws[0].stage4()
    q_ws[2].stage3()

    n_dev = n_dp * n_rows

    def three(v):
        hi = v.astype(BF)
        rest = v - hi.astype(F32)
        mid_part = rest.astype(BF)
        return hi, mid_part, (rest - mid_part.astype(F32)).astype(BF)

    def owner_blocks(rows, width):
        share = width // n_dev
        step = 512
        total = jnp.zeros((n_dp * 8, 128), F32)
        for t in range(width // step):
            place = lax.broadcasted_iota(jnp.int32, (step, 128), 1)
            lane = lax.broadcasted_iota(jnp.int32, (step, 128), 0) + t * step
            pick = jnp.where(lane % share == place, 1.0, 0.0).astype(BF)
            owner = (lax.broadcasted_iota(jnp.int32, (8, step), 1) + t * step) // share
            vec = rows[:, t * step : (t + 1) * step]
            stack = jnp.concatenate(
                [jnp.where(owner == d * n_rows + me.r, vec, 0.0) for d in range(n_dp)], axis=0
            )
            for part in three(stack):
                total = total + dot(part, pick)
        return total

    small_rows = [t_[0:1] + t_[2:3] if k == 0 else t_[1:2] + t_[3:4] for t_ in (tot1, tot2) for k in (0, 1)]
    wide_rows = [tot3[0:1] + tot3[2:3], tot3[1:2] + tot3[3:4]]
    narrow = jnp.concatenate(small_rows + [jnp.zeros((4, mid), F32)], axis=0)
    broad = jnp.concatenate([jnp.zeros((4, wide), F32)] + wide_rows + [jnp.zeros((2, wide), F32)], axis=0)
    sb[...] = (owner_blocks(narrow, mid) + owner_blocks(broad, wide)).reshape(sb.shape)

    def small_cp(d, recv):
        peer = (me.dp + n_dp - d) % n_dp if recv else (me.dp + d) % n_dp
        return remote(sb.at[peer], rb.at[d - 1], sm_s.at[d - 1], sm_r.at[d - 1], {"dp": peer, "rows": me.r})

    for d in range(1, n_dp):
        small_cp(d, False).start()

    def grad_in(j):
        cols, slot = lanes(j), j % 2
        previous = (j - 2, gv_h, gc_h) if j >= 2 else (wide // TILE - 2 + j, yv_h, yc_h)
        for cp in out_copies(previous[0], slot, previous[1], previous[2]):
            cp.wait()
        w = wr[j // 2, j % 2].reshape(TILE, mid)
        gpre[:, cols] = gpre[:, cols] + dot_t(ga1[...], w)
        for s, g in chunks:
            store_out(slot, s, gpre[s : s + CH, cols])
        for cp in out_copies(j, slot, gv_h, gc_h):
            cp.start()

    q_wr[0].stage2()
    q_wr[1].stage2()
    grad_in(0)
    grad_in(1)
    q_ws[1].stage4()
    grad_in(2)
    q_wr[0].stage3()
    q_wr[1].stage3()
    grad_in(3)
    q_ws[2].stage4()
    grad_in(4)
    q_wr[0].stage4()
    q_wr[1].stage4()
    for j in range(5, wide // TILE):
        grad_in(j)
    gwe_o[:, part:wide] = q_we.finish()
    gws_o[0:3] = q_ws[0].finish()
    pool_chip.wait()
    for out, at, maps, valid in ((poolv_o, 0, maps_v, valid_v), (poolc_o, maps_v, maps_c, valid_c)):
        total = pf[at : at + maps] + pr[1, at : at + maps].astype(F32)
        out[...] = (total * (1.0 / valid)).reshape(out.shape)
    total = sb[me.dp]
    for d in range(1, n_dp):
        small_cp(d, True).wait_recv()
        total = total + rb[d - 1]
    small_o[...] = total
    gws_o[3:6] = q_ws[1].finish()
    gws_o[6:9] = q_ws[2].finish()
    for i, q in enumerate(q_wr):
        gwr_o[i * few : (i + 1) * few] = q.finish()

    for j in (wide // TILE - 2, wide // TILE - 1):
        for cp in out_copies(j, j % 2, gv_h, gc_h):
            cp.wait()
    small_piece.drain()
    for p in pieces + [plane]:
        p.drain()
    for e in exchanges:
        e[2]()
    rim_h[2]()
    rim_d[2]()
    for q in [q_first, q_we] + q_ws + q_wr:
        q.drain()
    for d in range(1, n_dp):
        small_cp(d, False).wait_send()


def hand_over(*refs):
    n = (len(refs) - 8) // 3
    srcs, small, dsts = refs[:n], refs[n], refs[n + 1 : 2 * n + 1]
    cuts, bufs, sem = refs[2 * n + 1 : 2 * n + 7], refs[2 * n + 7 : -1], refs[-1]
    parts = 4
    ways = []
    for i, (src, buf, dst) in enumerate(zip(srcs, bufs, dsts)):
        count = parts if src.shape[0] % parts == 0 else 1
        per = src.shape[0] // count
        for k in range(count):
            rows = slice(k * per, (k + 1) * per)
            ways.append(
                (
                    pltpu.make_async_copy(src.at[rows], buf.at[rows], sem.at[0, i, k]),
                    pltpu.make_async_copy(buf.at[rows], dst.at[rows], sem.at[1, i, k]),
                )
            )
    for inward, _ in ways:
        inward.start()
    for i, ref in enumerate(cuts):
        ref[...] = small[i : i + 1, 0 : ref.shape[1]]
    for inward, outward in ways:
        inward.wait()
        outward.start()
    for _, outward in ways:
        outward.wait()


def block_step(n_dp, n_rows, xv, xc, mv, mc, wr, ws, we, g1, s1, g2, s2, g3, s3, cv, cc, cpv, cpc):
    img, views, rows_v, cols_v, wide = xv.shape
    crops, cols_c = xc.shape[1], xc.shape[3]
    mid = wr.shape[1]
    maps_v, maps_c = img * views, img * crops
    pix_v, pix_c = rows_v * cols_v * maps_v, cols_c * maps_c
    pix = pix_v + pix_c
    valid_v, valid_c = (rows_v * n_rows - 1) * cols_v, (n_rows - 1) * cols_c
    nz, nx = n_dp // 2, n_rows // 2

    def views_in(t):
        return t.transpose(0, 1, 3, 2, 4).reshape(maps_v, cols_v, rows_v, wide)

    def crops_in(t):
        return t.transpose(0, 2, 3, 1, 4).reshape(img, cols_c, crops, wide)

    grid4 = (nz, 2, nx, 2)
    vm = pl.BlockSpec(memory_space=pltpu.VMEM)
    hbm = pl.BlockSpec(memory_space=pl.ANY)
    s_wr, s_we = wr.shape[0], we.shape[0]
    V = pltpu.VMEM
    D = pltpu.SemaphoreType.DMA

    scratch = [
        V(grid4 + (s_wr, mid), BF), V((9,) + grid4 + (s_we, mid), BF), V(grid4 + (s_we, wide), BF),
        V(grid4 + (8, 128), F32),
        V((pix, 128), F32), V((cols_v, maps_v, 2, wide), BF), V((img, cols_c, crops, wide), BF),
        V((img, views, wide), F32), V((img, crops, wide), F32),
        V((pix, wide), BF), V((wide, pix), BF), V((pix, wide), BF),
        V((pix, mid), F32), V((pix, mid), F32), V((pix, wide), F32), V((pix, wide), F32),
        V((2, maps_v, cols_v, 2, TILE), F32), V((2, maps_c, cols_c, TILE // 128, 128), F32), V((2, pix, TILE), F32),
        V((4, (cols_v + 2) * maps_v, mid), BF), V((3, (cols_c + 2) * maps_c, mid), BF),
        V((4, (cols_v + 2) * maps_v, mid), BF), V((3, (cols_c + 2) * maps_c, mid), BF),
        V((pix, mid), BF), V((mid, pix), BF), V((pix, mid), BF),
        V(grid4 + (s_wr, mid), BF), V((9,) + grid4 + (s_we, mid), BF), V(grid4 + (s_we, wide), BF),
        V((nz, 2, nx, s_we, wide), BF), V((9, nz, 2, nx, s_we, mid), BF), V((nz, 2, nx, s_wr, mid), BF),
        V((2, nz, 2, s_we, wide // 4), BF), V((2, 9, nz, 2, s_we, mid // 2), BF), V((2, nz, 2, s_wr, mid // 2), BF),
        V((2, nz, s_we, wide // 4), BF), V((2, 9, nz, s_we, mid // 2), BF), V((2, nz, s_wr, mid // 2), BF),
        V((nz - 1, s_we, wide // 2), BF), V((nz - 1, 9, s_we, mid), BF), V((nz - 1, s_wr, mid), BF),
        V((nz - 1, 2, nx, s_we, wide // 2), BF), V((2, s_we, wide // 4), BF), V((2, s_we, wide // 2), BF),
        V((8, mid), F32), V((8, wide), F32),
        V((4, mid), F32), V((4, mid), F32), V((4, wide), F32),
        V((n_rows, 8, 128), F32),
        V((n_rows, 8, mid // 2), F32), V((n_rows, 8, mid // 2), F32), V((2, n_rows, 8, wide // 4), F32),
        V((n_rows, 8, mid // 2), F32), V((n_rows, 8, mid // 2), F32), V((2, n_rows, 8, wide // 4), F32),
        V((4, mid), F32), V((4, mid), F32), V((4, wide), F32),
        V((maps_v + maps_c, wide), F32), V((maps_v + maps_c, wide), BF), V((2, maps_v + maps_c, wide), BF),
        V((n_dp, 8, 128), F32), V((n_dp - 1, 8, 128), F32),
        D((3, cols_v + 1)), D((2, 2)), D((7, 5 * nz + 4)), D((7, 5 * nz + 4)), D((7, 6 + nz)), D((7, 6 + nz)),
        D((9, n_rows - 1)), D((9, n_rows - 1)), D((2, 4)), D((2, 4)), D((2,)), D((2,)), D((n_dp - 1,)), D((n_dp - 1,)),
    ]
    out_v = jax.ShapeDtypeStruct((maps_v, cols_v, 2, wide), F32)
    out_c = jax.ShapeDtypeStruct((maps_c, cols_c, wide // TILE, TILE // 128, 128), F32)
    outs = pl.pallas_call(
        functools.partial(kernel, n_dp, n_rows, (maps_v, cols_v, maps_c, cols_c, valid_v, valid_c)),
        out_shape=[
            out_v, out_c, out_v, out_c,
            jax.ShapeDtypeStruct(cpv.shape, F32), jax.ShapeDtypeStruct(cpc.shape, F32),
            jax.ShapeDtypeStruct((s_wr, mid), F32), jax.ShapeDtypeStruct((9, s_we, mid), F32),
            jax.ShapeDtypeStruct((s_we, wide), F32), jax.ShapeDtypeStruct((8, 128), F32),
        ],
        in_specs=[hbm] * 6 + [vm] * 11,
        out_specs=[hbm] * 4 + [vm] * 6,
        scratch_shapes=scratch,
        compiler_params=pltpu.CompilerParams(
            collective_id=0, has_side_effects=True, vmem_limit_bytes=63 << 20
        ),
    )(
        views_in(xv), crops_in(xc), views_in(cv), crops_in(cc), cpv, cpc,
        mv.transpose(1, 2, 0), mc.transpose(1, 2, 0), wr, ws.reshape(9, s_we, mid), we,
        g1.reshape(1, -1), s1.reshape(1, -1), g2.reshape(1, -1), s2.reshape(1, -1),
        g3.reshape(1, -1), s3.reshape(1, -1),
    )
    e = mid // (n_dp * n_rows)
    f = wide // (n_dp * n_rows)
    big, shapes = outs[:-1], [jax.ShapeDtypeStruct(o.shape, F32) for o in outs[:-1]]
    res = pl.pallas_call(
        hand_over,
        out_shape=shapes + [jax.ShapeDtypeStruct((1, w), F32) for w in (e, e, e, e, f, f)],
        in_specs=[hbm] * len(big) + [vm],
        out_specs=[hbm] * len(big) + [vm] * 6,
        scratch_shapes=[V(o.shape, F32) for o in big] + [D((2, len(big), 4))],
        compiler_params=pltpu.CompilerParams(vmem_limit_bytes=62 << 20),
    )(*outs)
    yv, yc, gv, gc, pool_v, pool_c, gwr, gws, gwe = res[:9]
    small = [r.reshape(-1) for r in res[9:]]

    def views_out(t):
        return t.reshape(img, views, cols_v, rows_v, wide).transpose(0, 1, 3, 2, 4)

    def crops_out(t):
        return t.reshape(img, crops, 1, cols_c, wide)

    return (
        views_out(yv), crops_out(yc),
        pool_v, pool_c,
        views_out(gv), crops_out(gc),
        gwr, gws.reshape(3, 3, s_we, mid), gwe,
        *small,
    )


def fits(xv, xc, we):
    return we.shape[0] % 16 == 0 and xv.shape[2] == 2 and xc.shape[2] == 1


def with_halo(block, sides, width):
    for axis, dim in sides:
        count = lax.axis_size(axis)
        forward = [(i, i + 1) for i in range(count - 1)]
        backward = [(target, source) for source, target in forward]
        low = lax.ppermute(
            lax.slice_in_dim(block, block.shape[dim] - width, None, axis=dim), axis, forward
        )
        high = lax.ppermute(lax.slice_in_dim(block, 0, width, axis=dim), axis, backward)
        block = jnp.concatenate([low, block, high], axis=dim)
    return block


def from_behind(array, axis, by):
    peers = lax.axis_size(axis)
    pairs = [(i, i + by) for i in range(peers) if 0 <= i + by < peers]
    return lax.ppermute(array, axis, pairs)


def silu_slope(value):
    sig = jax.nn.sigmoid(value)
    return sig * (1.0 + value * (1.0 - sig))


def pixel_mask(mask_rows, col_count):
    expanded = jnp.broadcast_to(
        mask_rows.astype(jnp.float32)[..., None], mask_rows.shape + (col_count,)
    )
    return expanded.reshape(-1, 1)


def by_group(in_views, view_value, crop_value):
    return jnp.where(in_views, view_value, crop_value)


def norm_forward(acts, mask_col, view_pixels, in_views, counts, gain_vec, shift_vec):
    masked = acts * mask_col
    totals = lax.psum(
        (jnp.sum(masked[:view_pixels], axis=0), jnp.sum(masked[view_pixels:], axis=0)), "rows"
    )
    centered = acts - by_group(in_views, totals[0] / counts[0], totals[1] / counts[1])
    squares = jnp.square(centered * mask_col)
    spread = lax.psum(
        (jnp.sum(squares[:view_pixels], axis=0), jnp.sum(squares[view_pixels:], axis=0)), "rows"
    )
    inv_rows = by_group(
        in_views, lax.rsqrt(spread[0] / counts[0] + eps), lax.rsqrt(spread[1] / counts[1] + eps)
    )
    normal = centered * inv_rows
    return (normal * gain_vec + shift_vec, normal, inv_rows)


def norm_backward(grad_z, normal, inv_rows, mask_col, view_pixels, in_views, counts, gain_vec):
    product = grad_z * normal
    partials = (
        jnp.sum(product[:view_pixels], axis=0),
        jnp.sum(grad_z[:view_pixels], axis=0),
        jnp.sum(product[view_pixels:], axis=0),
        jnp.sum(grad_z[view_pixels:], axis=0),
    )
    totals = (
        lax.psum(partials[0].astype(jnp.bfloat16), "rows").astype(jnp.float32),
        lax.psum(partials[1].astype(jnp.bfloat16), "rows").astype(jnp.float32),
        lax.psum(partials[2].astype(jnp.bfloat16), "rows").astype(jnp.float32),
        lax.psum(partials[3].astype(jnp.bfloat16), "rows").astype(jnp.float32),
    )
    scale_mean = by_group(in_views, totals[0] / counts[0], totals[2] / counts[1])
    shift_mean = by_group(in_views, totals[1] / counts[0], totals[3] / counts[1])
    grad_acts = gain_vec * inv_rows * (grad_z - shift_mean - normal * scale_mean) * mask_col
    return (grad_acts.astype(jnp.bfloat16), partials[0] + partials[2], partials[1] + partials[3])


def with_rims(feature_map):
    extended = with_halo(feature_map, (("rows", 1),), 1)
    return jnp.pad(extended, ((0, 0), (0, 0), (1, 1), (0, 0)))


def gather_taps(extended, row_count, col_count):
    windows = []
    for row_step in range(3):
        for col_step in range(3):
            windows.append(
                extended[:, row_step : row_step + row_count, col_step : col_step + col_count, :]
            )
    return jnp.concatenate(windows, axis=-1).reshape(-1, 9 * extended.shape[-1])


def spread_taps(grad_patches, map_count, row_count, col_count, mid_width):
    pieces = grad_patches.reshape(map_count, row_count, col_count, 9, mid_width)
    padded = jnp.zeros((map_count, row_count + 2, col_count + 2, mid_width), jnp.float32)
    tap_index = 0
    for row_step in range(3):
        for col_step in range(3):
            padded = padded.at[
                :, row_step : row_step + row_count, col_step : col_step + col_count, :
            ].add(pieces[:, :, :, tap_index, :])
            tap_index += 1
    inside = padded[:, 1 : row_count + 1, 1 : col_count + 1, :]
    from_below = from_behind(
        padded[:, 0, 1 : col_count + 1, :].astype(jnp.bfloat16), "rows", -1
    ).astype(jnp.float32)
    from_above = from_behind(
        padded[:, row_count + 1, 1 : col_count + 1, :].astype(jnp.bfloat16), "rows", 1
    ).astype(jnp.float32)
    inside = inside.at[:, row_count - 1].add(from_below)
    inside = inside.at[:, 0].add(from_above)
    return inside.reshape(-1, mid_width)


def contract_rows(left, right):
    return lax.dot_general(
        left, right, (((0,), (0,)), ((), ())), preferred_element_type=jnp.float32
    )


def contract_cols(left, right):
    return lax.dot_general(
        left, right, (((1,), (1,)), ((), ())), preferred_element_type=jnp.float32
    )


def shards(
    x_views,
    x_crops,
    mask_views,
    mask_crops,
    w_reduce,
    w_spatial,
    w_expand,
    gain_reduce,
    shift_reduce,
    gain_spatial,
    shift_spatial,
    gain_expand,
    shift_expand,
    cot_views,
    cot_crops,
    cot_pool_views,
    cot_pool_crops,
):
    low_type = jnp.bfloat16
    gathered = (
        lax.all_gather(w_reduce.astype(low_type), ("dp", "rows"), axis=0, tiled=True),
        lax.all_gather(w_spatial.astype(low_type), ("dp", "rows"), axis=2, tiled=True),
        lax.all_gather(w_expand.astype(low_type), ("dp", "rows"), axis=0, tiled=True),
        lax.all_gather(gain_reduce.astype(low_type), ("dp", "rows"), axis=0, tiled=True),
        lax.all_gather(shift_reduce.astype(low_type), ("dp", "rows"), axis=0, tiled=True),
        lax.all_gather(gain_spatial.astype(low_type), ("dp", "rows"), axis=0, tiled=True),
        lax.all_gather(shift_spatial.astype(low_type), ("dp", "rows"), axis=0, tiled=True),
        lax.all_gather(gain_expand.astype(low_type), ("dp", "rows"), axis=0, tiled=True),
        lax.all_gather(shift_expand.astype(low_type), ("dp", "rows"), axis=0, tiled=True),
    )
    weight_one, weight_two, weight_three = (gathered[0], gathered[1], gathered[2])
    gain_one, shift_one, gain_two, shift_two, gain_three, shift_three = [
        entry.astype(jnp.float32) for entry in gathered[3:]
    ]
    in_width = weight_one.shape[0]
    mid_width = weight_one.shape[1]
    view_maps = x_views.shape[0] * x_views.shape[1]
    view_rows, view_cols = (x_views.shape[2], x_views.shape[3])
    crop_maps = x_crops.shape[0] * x_crops.shape[1]
    crop_rows, crop_cols = (x_crops.shape[2], x_crops.shape[3])
    view_pixels = view_maps * view_rows * view_cols
    total_pixels = view_pixels + crop_maps * crop_rows * crop_cols
    row_parts = lax.axis_size("rows")
    view_valid = (view_rows * row_parts - 1) * view_cols
    crop_valid = (crop_rows * row_parts - 1) * crop_cols
    counts = (float(view_maps * view_valid), float(crop_maps * crop_valid))
    mask_col = jnp.concatenate(
        [pixel_mask(mask_views, view_cols), pixel_mask(mask_crops, crop_cols)], axis=0
    )
    in_views = lax.broadcasted_iota(jnp.int32, (total_pixels, 1), 0) < view_pixels
    inputs = jnp.concatenate([x_views.reshape(-1, in_width), x_crops.reshape(-1, in_width)], axis=0)
    acts_one = jnp.dot(inputs, weight_one, preferred_element_type=jnp.float32)
    z_one, normal_one, inv_one = norm_forward(
        acts_one, mask_col, view_pixels, in_views, counts, gain_one, shift_one
    )
    hidden_one = (jax.nn.silu(z_one) * mask_col).astype(low_type)
    view_hidden = hidden_one[:view_pixels].reshape(view_maps, view_rows, view_cols, mid_width)
    crop_hidden = hidden_one[view_pixels:].reshape(crop_maps, crop_rows, crop_cols, mid_width)
    patches = jnp.concatenate(
        [
            gather_taps(with_rims(view_hidden), view_rows, view_cols),
            gather_taps(with_rims(crop_hidden), crop_rows, crop_cols),
        ],
        axis=0,
    )
    spatial_flat = weight_two.reshape(9 * mid_width, mid_width)
    acts_two = jnp.dot(patches, spatial_flat, preferred_element_type=jnp.float32)
    z_two, normal_two, inv_two = norm_forward(
        acts_two, mask_col, view_pixels, in_views, counts, gain_two, shift_two
    )
    hidden_two = (jax.nn.silu(z_two) * mask_col).astype(low_type)
    acts_three = jnp.dot(hidden_two, weight_three, preferred_element_type=jnp.float32)
    z_three, normal_three, inv_three = norm_forward(
        acts_three, mask_col, view_pixels, in_views, counts, gain_three, shift_three
    )
    pre_act = inputs.astype(jnp.float32) + z_three
    result = jax.nn.silu(pre_act) * mask_col
    pooled = (
        lax.psum(
            jnp.sum(
                result[:view_pixels].reshape(view_maps, view_rows * view_cols, in_width), axis=1
            ).astype(jnp.bfloat16),
            "rows",
        ).astype(jnp.float32),
        lax.psum(
            jnp.sum(
                result[view_pixels:].reshape(crop_maps, crop_rows * crop_cols, in_width), axis=1
            ).astype(jnp.bfloat16),
            "rows",
        ).astype(jnp.float32),
    )
    pool_views = (pooled[0] / view_valid).reshape(cot_pool_views.shape)
    pool_crops = (pooled[1] / crop_valid).reshape(cot_pool_crops.shape)
    view_grad = (
        cot_views.astype(jnp.float32).reshape(view_maps, view_rows * view_cols, in_width)
        + cot_pool_views.reshape(view_maps, 1, in_width) / view_valid
    )
    crop_grad = (
        cot_crops.astype(jnp.float32).reshape(crop_maps, crop_rows * crop_cols, in_width)
        + cot_pool_crops.reshape(crop_maps, 1, in_width) / crop_valid
    )
    grad_out = jnp.concatenate(
        [view_grad.reshape(-1, in_width), crop_grad.reshape(-1, in_width)], axis=0
    )
    grad_pre = grad_out * mask_col * silu_slope(pre_act)
    grad_three, dgain_three, dshift_three = norm_backward(
        grad_pre, normal_three, inv_three, mask_col, view_pixels, in_views, counts, gain_three
    )
    grad_expand = contract_rows(hidden_two, grad_three)
    grad_hidden_two = contract_cols(grad_three, weight_three)
    grad_z_two = grad_hidden_two * mask_col * silu_slope(z_two)
    grad_two, dgain_two, dshift_two = norm_backward(
        grad_z_two, normal_two, inv_two, mask_col, view_pixels, in_views, counts, gain_two
    )
    grad_spatial = contract_rows(patches, grad_two).reshape(3, 3, mid_width, mid_width)
    grad_patches = contract_cols(grad_two, spatial_flat)
    grad_hidden_one = jnp.concatenate(
        [
            spread_taps(grad_patches[:view_pixels], view_maps, view_rows, view_cols, mid_width),
            spread_taps(grad_patches[view_pixels:], crop_maps, crop_rows, crop_cols, mid_width),
        ],
        axis=0,
    )
    grad_z_one = grad_hidden_one * mask_col * silu_slope(z_one)
    grad_one, dgain_one, dshift_one = norm_backward(
        grad_z_one, normal_one, inv_one, mask_col, view_pixels, in_views, counts, gain_one
    )
    grad_reduce = contract_rows(inputs, grad_one)
    grad_inputs = contract_cols(grad_one, weight_one) + grad_pre
    summed = (
        lax.psum_scatter(grad_reduce, ("dp", "rows"), scatter_dimension=0, tiled=True),
        lax.psum_scatter(grad_spatial, ("dp", "rows"), scatter_dimension=2, tiled=True),
        lax.psum_scatter(grad_expand, ("dp", "rows"), scatter_dimension=0, tiled=True),
        lax.psum_scatter(dgain_one, ("dp", "rows"), scatter_dimension=0, tiled=True),
        lax.psum_scatter(dshift_one, ("dp", "rows"), scatter_dimension=0, tiled=True),
        lax.psum_scatter(dgain_two, ("dp", "rows"), scatter_dimension=0, tiled=True),
        lax.psum_scatter(dshift_two, ("dp", "rows"), scatter_dimension=0, tiled=True),
        lax.psum_scatter(dgain_three, ("dp", "rows"), scatter_dimension=0, tiled=True),
        lax.psum_scatter(dshift_three, ("dp", "rows"), scatter_dimension=0, tiled=True),
    )
    out_views = result[:view_pixels].reshape(x_views.shape)
    out_crops = result[view_pixels:].reshape(x_crops.shape)
    grad_views = grad_inputs[:view_pixels].reshape(x_views.shape)
    grad_crops = grad_inputs[view_pixels:].reshape(x_crops.shape)
    return (
        out_views,
        out_crops,
        pool_views,
        pool_crops,
        grad_views,
        grad_crops,
        summed[0],
        summed[1],
        summed[2],
        summed[3],
        summed[4],
        summed[5],
        summed[6],
        summed[7],
        summed[8],
    )


def solution(mesh):
    in_specs = (
        P("dp", None, "rows", None, None),
        P("dp", None, "rows", None, None),
        P("dp", None, "rows"),
        P("dp", None, "rows"),
        P(("dp", "rows"), None),
        P(None, None, ("dp", "rows"), None),
        P(("dp", "rows"), None),
        P(("dp", "rows")),
        P(("dp", "rows")),
        P(("dp", "rows")),
        P(("dp", "rows")),
        P(("dp", "rows")),
        P(("dp", "rows")),
        P("dp", None, "rows", None, None),
        P("dp", None, "rows", None, None),
        P("dp", None, None),
        P("dp", None, None),
    )
    out_specs = (
        P("dp", None, "rows", None, None),
        P("dp", None, "rows", None, None),
        P("dp", None, None),
        P("dp", None, None),
        P("dp", None, "rows", None, None),
        P("dp", None, "rows", None, None),
        P(("dp", "rows"), None),
        P(None, None, ("dp", "rows"), None),
        P(("dp", "rows"), None),
        P(("dp", "rows")),
        P(("dp", "rows")),
        P(("dp", "rows")),
        P(("dp", "rows")),
        P(("dp", "rows")),
        P(("dp", "rows")),
    )
    def step(*args):
        if fits(args[0], args[1], args[6]):
            return block_step(mesh.shape["dp"], mesh.shape["rows"], *args)
        return shards(*args)

    return jax.shard_map(step, mesh=mesh, in_specs=in_specs, out_specs=out_specs, check_vma=False)
```

```python
import functools

import jax
import jax.numpy as jnp
from jax import lax
from jax.experimental import pallas as pl
from jax.experimental.pallas import tpu as pltpu
from jax.sharding import PartitionSpec as P

MESH = pl.DeviceIdType.MESH
ALL = slice(None)
BF = jnp.bfloat16
F32 = jnp.float32
eps = 1e-05
TILE = 256


def lanes(j, width=TILE):
    if isinstance(j, int):
        return slice(j * width, (j + 1) * width)
    return pl.ds(pl.multiple_of(j * width, width), width)


def half(h, width, at=0, whole=None):
    if h is None:
        return ALL if whole is None else slice(at, at + whole)
    return slice(at + h * (width // 2), at + (h + 1) * (width // 2))


def dot(a, b):
    return lax.dot_general(a, b, (((1,), (0,)), ((), ())), preferred_element_type=F32)


def dot_t(a, b):
    return lax.dot_general(a, b, (((1,), (1,)), ((), ())), preferred_element_type=F32)


def dot_r(a, b):
    return lax.dot_general(a, b, (((0,), (0,)), ((), ())), preferred_element_type=F32)


def sigmoid(v):
    return 0.5 * jnp.tanh(0.5 * v) + 0.5


def uneven(h, width):
    return ALL if h is None else slice(h * (width // 4), width if h else width // 4)


class Place:
    def __init__(self, n_dp, n_rows):
        self.ny, self.nc = 2, 2
        self.nz, self.nx = n_dp // 2, n_rows // 2
        self.n_dp, self.n_rows = n_dp, n_rows
        self.dp, self.r = lax.axis_index("dp"), lax.axis_index("rows")
        self.z, self.y = self.dp // 2, self.dp % 2
        self.x, self.c = self.r // 2, self.r % 2

    def dev(self, z, y, x, c):
        return {"dp": z * self.ny + y, "rows": x * self.nc + c}


def remote(src, dst, ssem, rsem, to):
    return pltpu.make_async_remote_copy(
        src_ref=src, dst_ref=dst, send_sem=ssem, recv_sem=rsem, device_id=to, device_id_type=MESH
    )


class Piece:
    def __init__(self, me, view, ssem, rsem):
        self.me, self.view, self.s, self.r, self.sent = me, view, ssem, rsem, []
        self.px = me.dev(me.z, me.y, 1 - me.x, me.c)
        self.py = me.dev(me.z, 1 - me.y, me.x, me.c)
        self.pc = me.dev(me.z, me.y, me.x, 1 - me.c)

    def pz(self, k):
        return self.me.dev((self.me.z + k) % self.me.nz, self.me.y, self.me.x, self.me.c)

    def send(self, k, src, dst, to):
        cp = remote(src, dst, self.s.at[k], self.r.at[k], to)
        cp.start()
        self.sent.append(cp)

    def got(self, k, dst):
        remote(dst, dst, self.s.at[k], self.r.at[k], self.pc).wait_recv()

    def drain(self):
        for cp in self.sent:
            cp.wait_send()


class Gather(Piece):
    def __init__(self, me, view, ssem, rsem, halves=(0, 1)):
        super().__init__(me, view, ssem, rsem)
        self.halves, n = halves, me.nz
        self.X, self.Y, self.D, self.C = n - 1, 2 * n - 1, (3 * n - 1, 4 * n - 1), 5 * n - 1

    def share(self, k, z, y, x, h, to):
        ref = self.view(z, y, x, self.me.c, h)
        self.send(k, ref, ref, to)

    def wait(self, k, z, y, x, h, c=None):
        self.got(k, self.view(z, y, x, self.me.c if c is None else c, h))

    def source(self, k):
        return (self.me.z + self.me.nz - k) % self.me.nz

    def start_z(self):
        me = self.me
        for k in range(1, me.nz):
            self.share(k - 1, me.z, me.y, me.x, None, self.pz(k))

    def start_xy(self):
        me = self.me
        self.share(self.X, me.z, me.y, me.x, None, self.px)
        self.share(self.Y, me.z, me.y, me.x, None, self.py)

    def got_z(self, k):
        me, z = self.me, self.source(k)
        self.wait(k - 1, z, me.y, me.x, None)
        self.share(self.X + k, z, me.y, me.x, None, self.px)
        self.share(self.Y + k, z, me.y, me.x, None, self.py)
        if k == me.nz - 1:
            self.share(self.C, ALL, me.y, me.x, None, self.pc)

    def diagonal(self):
        me = self.me
        for k in range(me.nz):
            z = self.source(k)
            self.wait(self.Y + k, z, 1 - me.y, me.x, None)
            self.share(self.D[0] + k, z, 1 - me.y, me.x, 0, self.px)
            self.wait(self.X + k, z, me.y, 1 - me.x, None)
            if 1 in self.halves:
                self.share(self.D[1] + k, z, me.y, 1 - me.x, 1, self.py)
        self.share(self.C + 1, ALL, 1 - me.y, me.x, None, self.pc)
        self.share(self.C + 2, ALL, me.y, 1 - me.x, None, self.pc)

    def last(self):
        me = self.me
        for h in self.halves:
            for k in range(me.nz):
                self.wait(self.D[h] + k, self.source(k), 1 - me.y, 1 - me.x, h)
            self.share(self.C + 3 + h, ALL, 1 - me.y, 1 - me.x, h, self.pc)

    def finish(self):
        me, o = self.me, 1 - self.me.c
        self.wait(self.C, ALL, me.y, me.x, None, o)
        self.wait(self.C + 1, ALL, 1 - me.y, me.x, None, o)
        self.wait(self.C + 2, ALL, me.y, 1 - me.x, None, o)
        for h in self.halves:
            self.wait(self.C + 3 + h, ALL, 1 - me.y, 1 - me.x, h, o)


class GatherPlane(Gather):
    def start(self):
        me = self.me
        self.share(0, me.z, me.y, me.x, None, self.px)
        self.share(1, me.z, me.y, me.x, None, self.py)

    def diagonal(self):
        me = self.me
        self.wait(1, me.z, 1 - me.y, me.x, None)
        self.share(2, me.z, 1 - me.y, me.x, 0, self.px)
        self.wait(0, me.z, me.y, 1 - me.x, None)
        self.share(3, me.z, me.y, 1 - me.x, 1, self.py)

    def plane(self):
        me = self.me
        for h in (0, 1):
            self.wait(2 + h, me.z, 1 - me.y, 1 - me.x, h)
        for k in range(1, me.nz):
            self.share(3 + k, me.z, ALL, ALL, None, self.pz(k))
        self.share(4 + me.nz, me.z, ALL, ALL, None, self.pc)

    def last(self):
        for k in range(1, self.me.nz):
            self.wait(3 + k, self.source(k), ALL, ALL, None)
            self.share(4 + self.me.nz + k, self.source(k), ALL, ALL, None, self.pc)

    def finish(self):
        for k in range(self.me.nz):
            self.wait(4 + self.me.nz + k, self.source(k), ALL, ALL, None, 1 - self.me.c)


class ReducePlane(Piece):
    def __init__(self, me, view, from_core, from_z, from_diagonal, from_xy, ssem, rsem):
        super().__init__(me, view, ssem, rsem)
        self.fc, self.fz, self.fd, self.fxy = from_core, from_z, from_diagonal, from_xy
        self.DG, self.H = me.nz, me.nz + 2

    def start(self):
        c = self.me.c
        self.send(0, self.view(ALL, ALL, ALL, 1 - c, None), self.fc(), self.pc)

    def stage2(self):
        me = self.me
        self.got(0, self.fc())
        ref = self.view(ALL, ALL, ALL, me.c, None)
        ref[...] = ref[...] + self.fc()[...]
        for k in range(1, me.nz):
            z = (me.z + k) % me.nz
            self.send(k, self.view(z, ALL, ALL, me.c, None), self.fz(k - 1), self.pz(k))

    def stage3(self):
        me = self.me
        ref = self.view(me.z, ALL, ALL, me.c, None)
        total = ref[...].astype(F32)
        for k in range(1, me.nz):
            self.got(k, self.fz(k - 1))
            total = total + self.fz(k - 1)[...].astype(F32)
        ref[...] = total.astype(BF)
        self.send(self.DG, self.view(me.z, 1 - me.y, 1 - me.x, me.c, 0), self.fd(0), self.px)
        self.send(self.DG + 1, self.view(me.z, 1 - me.y, 1 - me.x, me.c, 1), self.fd(1), self.py)
        self.send(self.H, self.view(me.z, me.y, 1 - me.x, me.c, 0), self.fxy(0, 0), self.px)
        self.send(self.H + 1, self.view(me.z, 1 - me.y, me.x, me.c, 1), self.fxy(1, 1), self.py)

    def stage4(self):
        me = self.me
        self.got(self.DG, self.fd(0))
        ref = self.view(me.z, 1 - me.y, me.x, me.c, 0)
        ref[...] = ref[...] + self.fd(0)[...]
        self.send(self.H + 2, ref, self.fxy(1, 0), self.py)
        self.got(self.DG + 1, self.fd(1))
        ref = self.view(me.z, me.y, 1 - me.x, me.c, 1)
        ref[...] = ref[...] + self.fd(1)[...]
        self.send(self.H + 3, ref, self.fxy(0, 1), self.px)

    def finish(self):
        me = self.me
        self.got(self.H, self.fxy(0, 0))
        self.got(self.H + 1, self.fxy(1, 1))
        self.got(self.H + 2, self.fxy(1, 0))
        self.got(self.H + 3, self.fxy(0, 1))
        total = self.view(me.z, me.y, me.x, me.c, None)[...].astype(F32)
        return total + self.fxy(0, None)[...].astype(F32) + self.fxy(1, None)[...].astype(F32)


class Reduce:
    def __init__(self, me, view, from_core, from_third, from_second, from_z, ssem, rsem):
        self.me, self.view, self.s, self.r = me, view, ssem, rsem
        self.fc, self.f3, self.f2, self.fz = from_core, from_third, from_second, from_z

    def core(self):
        me = self.me
        return remote(
            self.view(ALL, ALL, ALL, 1 - me.c, None),
            self.fc(ALL, ALL, ALL, None),
            self.s.at[0],
            self.r.at[0],
            me.dev(me.z, me.y, me.x, 1 - me.c),
        )

    def third(self, h):
        me = self.me
        place = (ALL, ALL, 1 - me.x) if h == 0 else (ALL, 1 - me.y, ALL)
        to = (me.z, me.y, 1 - me.x, me.c) if h == 0 else (me.z, 1 - me.y, me.x, me.c)
        return remote(
            self.view(*place, me.c, h), self.f3(h), self.s.at[1 + h], self.r.at[1 + h], me.dev(*to)
        )

    def second(self, h):
        me = self.me
        place = (ALL, 1 - me.y, me.x) if h == 0 else (ALL, me.y, 1 - me.x)
        to = (me.z, 1 - me.y, me.x, me.c) if h == 0 else (me.z, me.y, 1 - me.x, me.c)
        return remote(
            self.view(*place, me.c, h), self.f2(h), self.s.at[3 + h], self.r.at[3 + h], me.dev(*to)
        )

    def along_z(self, dz):
        me = self.me
        z = (me.z + dz) % me.nz
        return remote(
            self.view(z, me.y, me.x, me.c, None),
            self.fz(dz - 1),
            self.s.at[4 + dz],
            self.r.at[4 + dz],
            me.dev(z, me.y, me.x, me.c),
        )

    def start(self):
        self.core().start()

    def stage2(self):
        me = self.me
        self.core().wait_recv()
        for h in (0, 1):
            first = (ALL, ALL, 1 - me.x) if h == 0 else (ALL, 1 - me.y, ALL)
            ref = self.view(*first, me.c, h)
            ref[...] = ref[...] + self.fc(*first, h)[...]
            self.third(h).start()
        for h in (0, 1):
            rest = (ALL, ALL, me.x) if h == 0 else (ALL, me.y, ALL)
            ref = self.view(*rest, me.c, h)
            ref[...] = ref[...] + self.fc(*rest, h)[...]

    def stage3(self):
        me = self.me
        for h in (0, 1):
            self.third(h).wait_recv()
            kept = (ALL, ALL, me.x) if h == 0 else (ALL, me.y, ALL)
            ref = self.view(*kept, me.c, h)
            ref[...] = ref[...] + self.f3(h)[...]
            self.second(h).start()

    def stage4(self):
        me = self.me
        for h in (0, 1):
            self.second(h).wait_recv()
            ref = self.view(ALL, me.y, me.x, me.c, h)
            ref[...] = ref[...] + self.f2(h)[...]
        for dz in range(1, me.nz):
            self.along_z(dz).start()

    def finish(self):
        me = self.me
        total = self.view(me.z, me.y, me.x, me.c, None)[...].astype(F32)
        for dz in range(1, me.nz):
            self.along_z(dz).wait_recv()
            total = total + self.fz(dz - 1)[...].astype(F32)
        return total

    def drain(self):
        self.core().wait_send()
        for h in (0, 1):
            self.third(h).wait_send()
            self.second(h).wait_send()
        for dz in range(1, self.me.nz):
            self.along_z(dz).wait_send()


def kernel(n_dp, n_rows, sizes, *refs):
    (
        xv_h, xc_h, cv_h, cc_h, cpv_h, cpc_h, wr_h, ws_h, we_h, mv_in, mc_in,
        g1_in, s1_in, g2_in, s2_in, g3_in, s3_in,
        yv_h, yc_h, gv_h, gc_h, poolv_o, poolc_o, gwr_o, gws_o, gwe_o, small_o,
        wr_in, ws_in, we_in, wr, ws, we, par, mask, raw_v, raw_c, cpv, cpc, x, xt, cot, a1, a2, a3, gpre, ysv, ysc, gact,
        hv, hc, dv, dc, h2, h2t, ga1, gwr, gws, gwe,
        fc_we, fc_ws, fc_wr, f3_we, f3_ws, f3_wr, f2_we, f2_ws, f2_wr, fz_we, fz_ws, fz_wr, fp_we, fd_we, fh_we,
        p1, p3, mi1, mi2, mi3, cnt, ex1, ex2, ex3, bx1, bx2, bx3, tot1, tot2, tot3,
        pf, pb, pr, sb, rb,
        in_sem, out_sem, ag_s, ag_r, rs_s, rs_r, ex_s, ex_r, halo_s, halo_r, pool_s, pool_r, sm_s, sm_r,
    ) = refs
    (maps_v, cols_v, maps_c, cols_c, valid_v, valid_c) = sizes
    me = Place(n_dp, n_rows)
    mid, wide = a1.shape[1], a3.shape[1]
    pix_v = 2 * cols_v * maps_v
    pix = a1.shape[0]
    row_v, row_c = cols_v * maps_v, cols_c * maps_c
    count = (float(maps_v * valid_v), float(maps_c * valid_c))
    CH = 32
    chunks = [(s, 0 if s < pix_v else 1) for s in range(0, pix, CH)]

    barrier = pltpu.get_barrier_semaphore()
    peers = [{"dp": me.dp, "rows": (me.r + d) % n_rows} for d in range(1, n_rows)]
    peers += [{"dp": (me.dp + d) % n_dp, "rows": me.r} for d in range(1, n_dp)]
    for peer in peers:
        pl.semaphore_signal(barrier, inc=1, device_id=peer, device_id_type=MESH)

    def fetch(k, views, crops):
        return [
            pltpu.make_async_copy(views.at[:, col], raw_v.at[col], in_sem.at[k, col]) for col in range(cols_v)
        ] + [pltpu.make_async_copy(crops, raw_c, in_sem.at[k, cols_v])]

    def arrange(out):
        def body(j, carry):
            cols = lanes(j)
            for col in range(cols_v):
                for r in (0, 1):
                    at = r * row_v + col * maps_v
                    out[at : at + maps_v, cols] = raw_v[col, :, r, cols]
            for col in range(cols_c):
                at = pix_v + col * maps_c
                out[at : at + maps_c, cols] = raw_c[:, col, :, cols].reshape(maps_c, TILE)
            return carry

        lax.fori_loop(0, wide // TILE, body, 0)

    x_copies, cot_copies = fetch(0, xv_h, xc_h), fetch(1, cv_h, cc_h)
    pool_copies = [
        pltpu.make_async_copy(cpv_h, cpv, in_sem.at[2, 0]),
        pltpu.make_async_copy(cpc_h, cpc, in_sem.at[2, 1]),
    ]
    weight_copies = [
        pltpu.make_async_copy(src, dst, in_sem.at[2, 2 + i])
        for i, (src, dst) in enumerate(((wr_h, wr_in), (ws_h, ws_in), (we_h, we_in)))
    ]
    for cp in weight_copies + x_copies + pool_copies:
        cp.start()

    here = (me.z, me.y, me.x, me.c)
    own = par.at[here]
    own[...] = jnp.zeros(own.shape, F32)
    for i, ref in enumerate((g1_in, s1_in, g2_in, s2_in, g3_in, s3_in)):
        own[i : i + 1, 0 : ref.shape[1]] = ref[...].astype(BF).astype(F32)

    def mask_column(row_of, per, maps):
        lane = lax.broadcasted_iota(jnp.int32, (maps, 16), 1)
        place = lax.broadcasted_iota(jnp.int32, (maps, 16), 0)
        total = jnp.zeros((maps, 16), F32)
        for k in range(per):
            hit = jnp.logical_and(place % per == k, lane == place // per)
            total = total + jnp.where(hit, row_of(k).astype(F32), 0.0)
        return jnp.broadcast_to(jnp.sum(total, axis=1, keepdims=True), (maps, 128))

    for r in (0, 1):
        column = mask_column(lambda k: mv_in[k, r : r + 1, :], mv_in.shape[0], maps_v)
        for col in range(cols_v):
            at = r * row_v + col * maps_v
            mask[at : at + maps_v] = column
    column = mask_column(lambda k: mc_in[k], mc_in.shape[0], maps_c)
    for col in range(cols_c):
        at = pix_v + col * maps_c
        mask[at : at + maps_c] = column

    cnt_own = cnt.at[me.r]
    cnt_own[0:1] = jnp.sum(mask[0:pix_v], axis=0, keepdims=True)
    cnt_own[1:2] = jnp.sum(mask[pix_v:pix], axis=0, keepdims=True)
    cnt_own[2:8] = jnp.zeros((6, 128), F32)

    for cp in weight_copies:
        cp.wait()
    wr[here] = wr_in[...].astype(BF)
    ws[(ALL,) + here] = ws_in[...].astype(BF)
    we[here] = we_in[...].astype(BF)

    pl.semaphore_wait(barrier, len(peers))

    def piece(k, view, halves=(0, 1), form=Gather):
        return form(me, view, ag_s.at[k], ag_r.at[k], *(() if form is GatherPlane else (halves,)))

    part = wide // 2
    small_piece = piece(0, lambda z, y, x, c, h: par.at[z, y, x, c], (0,))
    pieces = [piece(1, lambda z, y, x, c, h: wr.at[z, y, x, c, :, half(h, mid)])]
    for i in range(3):
        pieces.append(
            piece(2 + i, lambda z, y, x, c, h, i=i: ws.at[3 * i : 3 * i + 3, z, y, x, c, :, uneven(h, mid)])
        )
    pieces.append(piece(5, lambda z, y, x, c, h: we.at[z, y, x, c, :, half(h, part, 0, part)]))
    plane = piece(6, lambda z, y, x, c, h: we.at[z, y, x, c, :, half(h, part, part, part)], form=GatherPlane)

    def exchange(k, buf):
        def cp(d, recv):
            peer = (me.r + n_rows - d) % n_rows if recv else (me.r + d) % n_rows
            ref = buf.at[peer if recv else me.r]
            return remote(ref, ref, ex_s.at[k, d - 1], ex_r.at[k, d - 1], {"dp": me.dp, "rows": peer})

        def send():
            for d in range(1, n_rows):
                cp(d, False).start()

        def wait():
            for d in range(1, n_rows):
                cp(d, True).wait_recv()

        def drain():
            for d in range(1, n_rows):
                cp(d, False).wait_send()

        return send, wait, drain

    exchanges = [
        exchange(k, b)
        for k, b in enumerate(
            (cnt, ex1, ex2, ex3.at[0], ex3.at[1], bx1, bx2, bx3.at[0], bx3.at[1])
        )
    ]
    CNT, EX1, EX2, EX3, BX1, BX2, BX3 = 0, 1, 2, 3, 5, 6, 7

    def rim(k, v, c):
        def cps(up):
            peer = {"dp": me.dp, "rows": (me.r + n_rows - 1) % n_rows if up else (me.r + 1) % n_rows}
            base = 0 if up else 2
            vs, vd = (1, 3) if up else (2, 0)
            csrc, cd = (1, 2) if up else (1, 0)
            return [
                remote(
                    v.at[vs, maps_v : maps_v + row_v],
                    v.at[vd, maps_v : maps_v + row_v],
                    halo_s.at[k, base],
                    halo_r.at[k, base],
                    peer,
                ),
                remote(
                    c.at[csrc, maps_c : maps_c + row_c],
                    c.at[cd, maps_c : maps_c + row_c],
                    halo_s.at[k, base + 1],
                    halo_r.at[k, base + 1],
                    peer,
                ),
            ]

        def each(up, fn):
            def body():
                for cp in cps(up):
                    fn(cp)

            return body

        first, last = me.r == 0, me.r == n_rows - 1

        def send():
            pl.when(jnp.logical_not(first))(each(True, lambda cp: cp.start()))
            pl.when(jnp.logical_not(last))(each(False, lambda cp: cp.start()))

        def wait():
            pl.when(jnp.logical_not(last))(each(True, lambda cp: cp.wait_recv()))
            pl.when(jnp.logical_not(first))(each(False, lambda cp: cp.wait_recv()))

        def drain():
            pl.when(jnp.logical_not(first))(each(True, lambda cp: cp.wait_send()))
            pl.when(jnp.logical_not(last))(each(False, lambda cp: cp.wait_send()))

        return send, wait, drain

    rim_h, rim_d = rim(0, hv, hc), rim(1, dv, dc)

    def clear_rims(v, c):
        zv, zc = jnp.zeros((maps_v, mid), BF), jnp.zeros((maps_c, mid), BF)
        for r in range(4):
            v[r, 0:maps_v] = zv
            v[r, maps_v + row_v : 2 * maps_v + row_v] = zv
        for r in range(3):
            c[r, 0:maps_c] = zc
            c[r, maps_c + row_c : 2 * maps_c + row_c] = zc

        @pl.when(me.r == 0)
        def _():
            v[0, maps_v : maps_v + row_v] = jnp.zeros((row_v, mid), BF)
            c[0, maps_c : maps_c + row_c] = jnp.zeros((row_c, mid), BF)

        @pl.when(me.r == n_rows - 1)
        def _():
            v[3, maps_v : maps_v + row_v] = jnp.zeros((row_v, mid), BF)
            c[2, maps_c : maps_c + row_c] = jnp.zeros((row_c, mid), BF)

    def tile_rows(ref, j):
        per = me.nz * TILE // mid
        return ref[j * per : (j + 1) * per]

    def fold(v):
        return jnp.sum(v.reshape(v.shape[0] // 8, 8, v.shape[1]), axis=0)

    def put(buf, j, k, value):
        tiles = buf.shape[2] // TILE
        if isinstance(j, int):
            buf[me.r, 4 * (j // tiles) + k : 4 * (j // tiles) + k + 1, lanes(j % tiles)] = value
        else:
            buf[me.r, pl.ds(4 * (j // tiles) + k, 1), lanes(j % tiles)] = value

    def masked(s):
        return jnp.concatenate([mask[s : s + CH]] * (TILE // 128), axis=1)

    def local_stats(a, buf, n_tiles, first=0):
        def body(j, carry):
            cols = lanes(j + first)
            for grp in (0, 1):
                acc = jnp.zeros((8, TILE), F32)
                for s, g in chunks:
                    if g == grp:
                        acc = acc + fold(a[s : s + CH, cols] * masked(s))
                total = jnp.sum(acc, axis=0, keepdims=True)
                n_own = jnp.maximum(cnt[me.r, grp : grp + 1, 0:1], 1.0)
                mean = total / n_own
                acc = jnp.zeros((8, TILE), F32)
                for s, g in chunks:
                    if g == grp:
                        d = (a[s : s + CH, cols] - mean) * masked(s)
                        acc = acc + fold(d * d)
                put(buf, j, 2 * grp, total)
                put(buf, j, 2 * grp + 1, jnp.sum(acc, axis=0, keepdims=True))
            return carry

        for j in range(n_tiles):
            body(j, 0) if n_tiles <= 2 else None
        if n_tiles > 2:
            lax.fori_loop(0, n_tiles, body, 0)

    def merge_stats(buf, mi, at=0):
        width = buf.shape[2]
        for hf in (0, 1):
            for grp in (0, 1):
                k = 4 * hf + 2 * grp
                total = sum(buf[i, k : k + 1] for i in range(n_rows))
                mean = total / count[grp]
                spread = jnp.zeros_like(mean)
                for i in range(n_rows):
                    n_i = cnt[i, grp : grp + 1, 0:1]
                    off = buf[i, k : k + 1] / jnp.maximum(n_i, 1.0) - mean
                    spread = spread + buf[i, k + 1 : k + 2] + n_i * (off * off)
                mi[2 * grp : 2 * grp + 1, at + hf * width : at + (hf + 1) * width] = mean
                mi[2 * grp + 1 : 2 * grp + 2, at + hf * width : at + (hf + 1) * width] = lax.rsqrt(
                    spread / count[grp] + eps
                )

    def merge_grads(buf, tot, at=0):
        width = buf.shape[2]
        for hf in (0, 1):
            block = buf[0, 4 * hf : 4 * hf + 4]
            for i in range(1, n_rows):
                block = block + buf[i, 4 * hf : 4 * hf + 4]
            tot[0:4, at + hf * width : at + (hf + 1) * width] = block

    def expand_params():
        blocks = par[...].reshape(n_dp * n_rows * 8, 128).astype(BF)
        n_dev = n_dp * n_rows
        for out, width in ((p1, mid), (p3, wide)):
            share = width // n_dev
            step = 512
            for t in range(width // step):
                lane = lax.broadcasted_iota(jnp.int32, (128, step), 1) + t * step
                place = lax.broadcasted_iota(jnp.int32, (128, step), 0)
                pick = jnp.where(lane % share == place, 1.0, 0.0).astype(BF)
                spread = dot(blocks, pick).reshape(n_dev, 8, step)
                owner = (lax.broadcasted_iota(jnp.int32, (8, step), 1) + t * step) // share
                total = jnp.zeros((8, step), F32)
                for d in range(n_dev):
                    total = total + jnp.where(owner == d, spread[d], 0.0)
                out[:, t * step : (t + 1) * step] = total

    def gain(out, i, cols):
        return out[i : i + 1, cols]

    small_piece.start_z()
    small_piece.start_xy()
    pieces[0].start_z()
    pieces[0].start_xy()
    exchanges[CNT][0]()
    plane.start()
    for p in pieces[1:]:
        p.start_xy()
    clear_rims(hv, hc)
    clear_rims(dv, dc)
    for cp in x_copies:
        cp.wait()
    arrange(x)
    for cp in cot_copies:
        cp.start()

    def step0(t):
        pieces[t].got_z(1)
        if t + 1 < len(pieces):
            pieces[t + 1].start_z()
        for k in range(2, me.nz):
            pieces[t].got_z(k)

    for k in range(1, me.nz):
        small_piece.got_z(k)
    step0(0)
    plane.diagonal()
    small_piece.diagonal()
    for t in range(wide // TILE):
        xt[t * TILE : (t + 1) * TILE, :] = x[:, t * TILE : (t + 1) * TILE].T
    step0(1)
    pieces[0].diagonal()
    small_piece.last()
    for cp in cot_copies:
        cp.wait()
    arrange(cot)
    step0(2)
    pieces[1].diagonal()
    pieces[0].last()
    small_piece.finish()
    expand_params()
    pieces[0].finish()
    exchanges[CNT][1]()

    def conv1(j, carry):
        w = wr[:, :, :, :, :, lanes(j)].reshape(wide, TILE)
        a1[:, lanes(j)] = dot(x[...], w)
        return carry

    for j in range(mid // TILE):
        conv1(j, 0)
    local_stats(a1, ex1, mid // TILE)
    exchanges[EX1][0]()
    step0(3)
    pieces[2].diagonal()
    pieces[1].last()
    exchanges[EX1][1]()
    merge_stats(ex1, mi1)

    def store_rows(v, c, s, cols, value):
        if s < pix_v:
            r, o = s // row_v, s % row_v
            v[1 + r, maps_v + o : maps_v + o + CH, cols] = value
        else:
            o = s - pix_v
            c[1, maps_c + o : maps_c + o + CH, cols] = value

    def act(a, mi, i, store):
        def body(j, carry):
            cols = lanes(j)
            scale = [mi[2 * g + 1 : 2 * g + 2, cols] * gain(p1, i, cols) for g in (0, 1)]
            mean = [mi[2 * g : 2 * g + 1, cols] for g in (0, 1)]
            shift = gain(p1, i + 1, cols)
            for s, g in chunks:
                zed = (a[s : s + CH, cols] - mean[g]) * scale[g] + shift
                store(s, cols, (zed * sigmoid(zed) * masked(s)).astype(BF))
            return carry

        for j in range(mid // TILE):
            body(j, 0)

    act(a1, mi1, 0, lambda s, cols, value: store_rows(hv, hc, s, cols, value))
    rim_h[0]()
    step0(4)
    plane.plane()
    pieces[3].diagonal()
    pieces[2].last()
    pieces[1].finish()
    rim_h[1]()

    def windows(v, c, dy, dx):
        left = [v[r + dy, dx * maps_v : dx * maps_v + row_v, :] for r in (0, 1)]
        return jnp.concatenate(left + [c[dy, dx * maps_c : dx * maps_c + row_c, :]], axis=0)

    def conv2(dy):
        left = jnp.concatenate([windows(hv, hc, dy, dx) for dx in range(3)], axis=1)
        for j in range(mid // TILE):
            w = ws[3 * dy : 3 * dy + 3, :, :, :, :, :, lanes(j)].reshape(3 * mid, TILE)
            part_sum = dot(left, w)
            a2[:, lanes(j)] = part_sum if dy == 0 else a2[:, lanes(j)] + part_sum

    conv2(0)
    pieces[4].diagonal()
    pieces[2].finish()
    conv2(1)
    pieces[3].last()
    pieces[3].finish()
    conv2(2)
    local_stats(a2, ex2, mid // TILE)
    exchanges[EX2][0]()
    pieces[4].last()
    exchanges[EX2][1]()
    merge_stats(ex2, mi2)

    def store_h2(s, cols, value):
        h2[s : s + CH, cols] = value

    act(a2, mi2, 2, store_h2)
    for cp in pool_copies:
        cp.wait()

    def conv3(j, carry):
        w = we[:, :, :, :, :, lanes(j)].reshape(mid, TILE)
        a3[:, lanes(j)] = dot(h2[...], w)
        return carry

    tiles = wide // TILE // 2
    pieces[4].finish()
    for j in range(tiles):
        conv3(j, 0)
    local_stats(a3, ex3.at[0], tiles)
    exchanges[EX3][0]()
    plane.last()
    plane.finish()
    for j in range(tiles, 2 * tiles):
        conv3(j, 0)
    local_stats(a3, ex3.at[1], tiles, tiles)
    exchanges[EX3 + 1][0]()
    h2t[...] = h2[...].T
    exchanges[EX3][1]()
    merge_stats(ex3.at[0], mi3)

    def out_copies(j, slot, views, crops):
        return [
            pltpu.make_async_copy(ysv.at[slot], views.at[:, :, :, lanes(j)], out_sem.at[slot, 0]),
            pltpu.make_async_copy(ysc.at[slot], crops.at[:, :, j], out_sem.at[slot, 1]),
        ]

    def store_out(slot, s, value):
        if s < pix_v:
            ysv[slot, :, s % row_v // maps_v, s // row_v, :] = value
        else:
            col, at = (s - pix_v) // maps_c, (s - pix_v) % maps_c
            for k in (0, 1):
                ysc[slot, at : at + CH, col, k, :] = value[:, k * 128 : (k + 1) * 128]

    def last(q, jj, carry):
        for slot in (0, 1):
            j = 2 * jj + slot
            cols = lanes(j)

            def free_slot():
                for cp in out_copies(j, slot, yv_h, yc_h):
                    cp.wait()

            if q > 0:
                free_slot()
            else:
                pl.when(jj > 0)(free_slot)

            mean = [mi3[2 * g : 2 * g + 1, cols] for g in (0, 1)]
            inv = [mi3[2 * g + 1 : 2 * g + 2, cols] for g in (0, 1)]
            scale = [inv[g] * gain(p3, 4, cols) for g in (0, 1)]
            sh = gain(p3, 5, cols)
            sums = [jnp.zeros((8, TILE), F32) for _ in range(4)]
            pooled = [jnp.zeros((CH, TILE), F32) for _ in range((maps_v + maps_c) // CH)]
            per_v, per_c = CH // cpv.shape[1], CH // cpc.shape[1]
            cps = [
                cpv[s : s + per_v, :, cols].reshape(CH, TILE) * (1.0 / valid_v)
                for s in range(0, cpv.shape[0], per_v)
            ] + [
                cpc[s : s + per_c, :, cols].reshape(CH, TILE) * (1.0 / valid_c)
                for s in range(0, cpc.shape[0], per_c)
            ]
            for s, g in chunks:
                which = (s % maps_v) // CH if g == 0 else (maps_v + (s - pix_v) % maps_c) // CH
                rows = slice(s, s + CH)
                m = masked(s)
                off = a3[rows, cols] - mean[g]
                pre = x[rows, cols].astype(F32) + (off * scale[g] + sh)
                sig = sigmoid(pre)
                act_out = pre * sig
                out = act_out * m
                store_out(slot, s, out)
                pooled[which] = pooled[which] + out
                slope = act_out + sig * (1.0 - act_out)
                gp = (cot[rows, cols].astype(F32) + cps[which]) * m * slope
                gpre[rows, cols] = gp
                sums[2 * g] = sums[2 * g] + fold(gp * off)
                sums[2 * g + 1] = sums[2 * g + 1] + fold(gp)
            for k in range(4):
                total = jnp.sum(sums[k], axis=0, keepdims=True)
                put(bx3.at[q], j - q * tiles, k, total * inv[k // 2] if k % 2 == 0 else total)
            for i, value in enumerate(pooled):
                pf[i * CH : (i + 1) * CH, cols] = value
                pb[i * CH : (i + 1) * CH, cols] = value.astype(BF)
            for cp in out_copies(j, slot, yv_h, yc_h):
                cp.start()
        return carry

    core_peer = {"dp": me.dp, "rows": me.x * 2 + 1 - me.c}
    chip_peer = {"dp": me.dp, "rows": (1 - me.x) * 2 + me.c}
    share = pb.shape[0] // 2
    mine, others = pl.ds(me.c * share, share), pl.ds((1 - me.c) * share, share)
    pool_core = remote(pb.at[others], pr.at[0], pool_s.at[0], pool_r.at[0], core_peer)
    pool_chip = remote(pb.at[mine], pr.at[1], pool_s.at[1], pool_r.at[1], chip_peer)
    pool_back = remote(pb.at[mine], pr.at[2], pool_s.at[2], pool_r.at[2], core_peer)
    lax.fori_loop(0, tiles // 2, functools.partial(last, 0), 0)
    exchanges[BX3][0]()
    exchanges[EX3 + 1][1]()
    merge_stats(ex3.at[1], mi3, wide // 2)
    lax.fori_loop(tiles // 2, tiles, functools.partial(last, 1), 0)
    exchanges[BX3 + 1][0]()
    pool_core.start()

    def coefs(mi, tot, gn, cols):
        out = []
        for g in (0, 1):
            mean, inv = mi[2 * g : 2 * g + 1, cols], mi[2 * g + 1 : 2 * g + 2, cols]
            dg, ds = tot[2 * g : 2 * g + 1, cols], tot[2 * g + 1 : 2 * g + 2, cols]
            out.append((mean, gn * inv, ds / count[g], dg / count[g] * inv))
        return out

    def norm_back(gz, a, co, s, cols):
        mean, k0, k1, k2 = co
        return (k0 * (gz - k1 - (a[s : s + CH, cols] - mean) * k2) * masked(s)).astype(BF)

    def grad_three(j, carry):
        cols = lanes(j)
        co = coefs(mi3, tot3, gain(p3, 4, cols), cols)
        for s, g in chunks:
            cot[s : s + CH, cols] = norm_back(gpre[s : s + CH, cols], a3, co[g], s, cols)
        gwe[:, :, :, :, :, cols] = (
            dot(h2t[...], cot[:, cols]).astype(BF).reshape(gwe.shape[:5] + (TILE,))
        )
        return carry

    q_first = ReducePlane(
        me,
        lambda z, y, x, c, h: gwe.at[z, y, x, c, :, half(h, part, 0, part)],
        lambda: fc_we.at[:, :, :, :, 0:part],
        lambda k: fp_we.at[k],
        lambda h: fd_we.at[h],
        lambda k, h: fh_we.at[k, :, half(h, part)],
        rs_s.at[0],
        rs_r.at[0],
    )

    def reducer(k, view, fc, f3, f2, fz):
        return Reduce(me, view, fc, f3, f2, fz, rs_s.at[k], rs_r.at[k])

    q_we = reducer(
        1,
        lambda z, y, x, c, h: gwe.at[z, y, x, c, :, half(h, part, part, part)],
        lambda z, y, x, h: fc_we.at[z, y, x, :, half(h, part, part, part)],
        lambda h: f3_we.at[h],
        lambda h: f2_we.at[h],
        lambda k: fz_we.at[k],
    )
    q_ws = [
        reducer(
            2 + i,
            lambda z, y, x, c, h, i=i: gws.at[3 * i : 3 * i + 3, z, y, x, c, :, uneven(h, mid)],
            lambda z, y, x, h, i=i: fc_ws.at[3 * i : 3 * i + 3, z, y, x, :, uneven(h, mid)],
            lambda h, i=i: f3_ws.at[3 * i : 3 * i + 3, :, :, :, uneven(h, mid)],
            lambda h, i=i: f2_ws.at[3 * i : 3 * i + 3, :, :, uneven(h, mid)],
            lambda k, i=i: fz_ws.at[k, 3 * i : 3 * i + 3],
        )
        for i in range(3)
    ]
    few = wr.shape[4] // 2
    q_wr = [
        reducer(
            5 + i,
            lambda z, y, x, c, h, i=i: gwr.at[z, y, x, c, i * few : (i + 1) * few, half(h, mid)],
            lambda z, y, x, h, i=i: fc_wr.at[z, y, x, i * few : (i + 1) * few, half(h, mid)],
            lambda h, i=i: f3_wr.at[h, :, :, i * few : (i + 1) * few],
            lambda h, i=i: f2_wr.at[h, :, i * few : (i + 1) * few],
            lambda k, i=i: fz_wr.at[k, i * few : (i + 1) * few],
        )
        for i in range(2)
    ]

    exchanges[BX3][1]()
    merge_grads(bx3.at[0], tot3)
    pool_core.wait_recv()
    pb[mine] = (pf[mine] + pr[0].astype(F32)).astype(BF)
    pool_chip.start()
    for j in range(tiles):
        grad_three(j, 0)
    q_first.start()
    exchanges[BX3 + 1][1]()
    merge_grads(bx3.at[1], tot3, wide // 2)
    for j in range(tiles, 2 * tiles):
        grad_three(j, 0)
    q_we.start()
    q_first.stage2()

    def grad_act(gh, a, mi, i, buf, j):
        cols = lanes(j)
        gn, sh = gain(p1, i, cols), gain(p1, i + 1, cols)
        sums = [jnp.zeros((8, TILE), F32) for _ in range(4)]
        for s, g in chunks:
            rows = slice(s, s + CH)
            mean, inv = mi[2 * g : 2 * g + 1, cols], mi[2 * g + 1 : 2 * g + 2, cols]
            off = a[rows, cols] - mean
            zed = off * (inv * gn) + sh
            sig = sigmoid(zed)
            gz = gh[rows, cols] * masked(s) * (sig * (1.0 + zed * (1.0 - sig)))
            gh[rows, cols] = gz
            sums[2 * g] = sums[2 * g] + fold(gz * off)
            sums[2 * g + 1] = sums[2 * g + 1] + fold(gz)
        for k in range(4):
            total = jnp.sum(sums[k], axis=0, keepdims=True)
            inv = mi[2 * (k // 2) + 1 : 2 * (k // 2) + 2, cols]
            put(buf, j, k, total * inv if k % 2 == 0 else total)

    for j in range(mid // TILE):
        w = tile_rows(we, j).reshape(TILE, wide)
        gact[j, :, :] = dot_t(cot[...], w)

    class Cols:
        def __getitem__(self, key):
            rows, cols = key
            return gact[self.j, rows, :]

        def __setitem__(self, key, value):
            rows, cols = key
            gact[self.j, rows, :] = value

    ghs = Cols()
    for j in range(mid // TILE):
        ghs.j = j
        grad_act(ghs, a2, mi2, 2, bx2, j)
    exchanges[BX2][0]()
    q_we.stage2()
    exchanges[BX2][1]()
    merge_grads(bx2, tot2)

    def grad_norm_all(a, mi, tot, i, store):
        for j in range(mid // TILE):
            ghs.j = j
            cols = lanes(j)
            co = coefs(mi, tot, gain(p1, i, cols), cols)
            for s, g in chunks:
                store(s, cols, norm_back(ghs[s : s + CH, cols], a, co[g], s, cols))

    grad_norm_all(a2, mi2, tot2, 2, lambda s, cols, value: store_rows(dv, dc, s, cols, value))
    rim_d[0]()

    def grad_taps(dy):
        right = windows(dv, dc, 1, 1)
        for dx in range(3):
            total = dot_r(windows(hv, hc, dy, dx), right)
            gws[3 * dy + dx] = total.astype(BF).reshape(gws.shape[1:])

    grad_taps(0)
    q_ws[0].start()
    grad_taps(1)
    q_ws[1].start()
    q_ws[0].stage2()
    q_we.stage3()
    grad_taps(2)
    q_ws[2].start()
    q_ws[1].stage2()
    rim_d[1]()

    def conv2_back(dy):
        left = jnp.concatenate([windows(dv, dc, 2 - dy, 2 - dx) for dx in range(3)], axis=1)
        for j in range(mid // TILE):
            w = jnp.concatenate(
                [tile_rows(ws.at[3 * dy + dx], j).reshape(TILE, mid) for dx in range(3)], axis=1
            )
            part_sum = dot_t(left, w)
            gact[j] = part_sum if dy == 0 else gact[j] + part_sum

    conv2_back(0)
    q_first.stage3()
    q_ws[2].stage2()
    pool_chip.wait_recv()
    conv2_back(1)
    pool_chip.wait_send()
    pb[mine] = (pb[mine].astype(F32) + pr[1].astype(F32)).astype(BF)
    pool_back.start()
    q_ws[0].stage3()
    q_we.stage4()
    conv2_back(2)
    for j in range(mid // TILE):
        ghs.j = j
        grad_act(ghs, a1, mi1, 0, bx1, j)
    exchanges[BX1][0]()
    q_first.stage4()
    q_ws[1].stage3()
    exchanges[BX1][1]()
    merge_grads(bx1, tot1)

    def store_ga1(s, cols, value):
        ga1[s : s + CH, cols] = value

    grad_norm_all(a1, mi1, tot1, 0, store_ga1)
    for t in range(wide // TILE):
        block = dot(xt[t * TILE : (t + 1) * TILE, :], ga1[...]).astype(BF)
        gwr[t // 2, t % 2] = block.reshape(gwr.shape[2:])
    for q in q_wr:
        q.start()

    n_dev = n_dp * n_rows

    def three(v):
        hi = v.astype(BF)
        rest = v - hi.astype(F32)
        mid_part = rest.astype(BF)
        return hi, mid_part, (rest - mid_part.astype(F32)).astype(BF)

    def owner_blocks(rows, width):
        share = width // n_dev
        step = 512
        total = jnp.zeros((n_dp * 8, 128), F32)
        for t in range(width // step):
            place = lax.broadcasted_iota(jnp.int32, (step, 128), 1)
            lane = lax.broadcasted_iota(jnp.int32, (step, 128), 0) + t * step
            pick = jnp.where(lane % share == place, 1.0, 0.0).astype(BF)
            owner = (lax.broadcasted_iota(jnp.int32, (8, step), 1) + t * step) // share
            vec = rows[:, t * step : (t + 1) * step]
            stack = jnp.concatenate(
                [jnp.where(owner == d * n_rows + me.r, vec, 0.0) for d in range(n_dp)], axis=0
            )
            for part in three(stack):
                total = total + dot(part, pick)
        return total

    small_rows = [t_[0:1] + t_[2:3] if k == 0 else t_[1:2] + t_[3:4] for t_ in (tot1, tot2) for k in (0, 1)]
    wide_rows = [tot3[0:1] + tot3[2:3], tot3[1:2] + tot3[3:4]]
    narrow = jnp.concatenate(small_rows + [jnp.zeros((4, mid), F32)], axis=0)
    broad = jnp.concatenate([jnp.zeros((4, wide), F32)] + wide_rows + [jnp.zeros((2, wide), F32)], axis=0)
    sb[...] = (owner_blocks(narrow, mid) + owner_blocks(broad, wide)).reshape(sb.shape)

    def small_cp(d, recv):
        peer = (me.dp + n_dp - d) % n_dp if recv else (me.dp + d) % n_dp
        return remote(sb.at[peer], rb.at[d - 1], sm_s.at[d - 1], sm_r.at[d - 1], {"dp": peer, "rows": me.r})

    for d in range(1, n_dp):
        small_cp(d, False).start()
    q_wr[0].stage2()
    q_wr[1].stage2()
    q_ws[0].stage4()
    q_ws[2].stage3()

    def grad_in(j):
        cols, slot = lanes(j), j % 2
        previous = (j - 2, gv_h, gc_h) if j >= 2 else (wide // TILE - 2 + j, yv_h, yc_h)
        for cp in out_copies(previous[0], slot, previous[1], previous[2]):
            cp.wait()
        w = wr[j // 2, j % 2].reshape(TILE, mid)
        gpre[:, cols] = gpre[:, cols] + dot_t(ga1[...], w)
        for s, g in chunks:
            store_out(slot, s, gpre[s : s + CH, cols])
        for cp in out_copies(j, slot, gv_h, gc_h):
            cp.start()

    grad_in(0)
    grad_in(1)
    q_ws[1].stage4()
    q_wr[0].stage3()
    grad_in(2)
    q_wr[1].stage3()
    q_ws[2].stage4()
    grad_in(3)
    grad_in(4)
    q_wr[0].stage4()
    q_wr[1].stage4()
    for j in range(5, wide // TILE):
        grad_in(j)
    gwe_o[:, 0:part] = q_first.finish()
    gwe_o[:, part:wide] = q_we.finish()
    gws_o[0:3] = q_ws[0].finish()
    pool_core.wait_send()
    pool_back.wait_recv()
    pb[others] = pr[2]
    for out, at, maps, valid in ((poolv_o, 0, maps_v, valid_v), (poolc_o, maps_v, maps_c, valid_c)):
        out[...] = (pb[at : at + maps].astype(F32) * (1.0 / valid)).reshape(out.shape)
    total = sb[me.dp]
    for d in range(1, n_dp):
        small_cp(d, True).wait_recv()
        total = total + rb[d - 1]
    small_o[...] = total
    gws_o[3:6] = q_ws[1].finish()
    gws_o[6:9] = q_ws[2].finish()
    for i, q in enumerate(q_wr):
        gwr_o[i * few : (i + 1) * few] = q.finish()

    pool_back.wait_send()
    for j in (wide // TILE - 2, wide // TILE - 1):
        for cp in out_copies(j, j % 2, gv_h, gc_h):
            cp.wait()
    small_piece.drain()
    for p in pieces + [plane]:
        p.drain()
    for e in exchanges:
        e[2]()
    rim_h[2]()
    rim_d[2]()
    for q in [q_first, q_we] + q_ws + q_wr:
        q.drain()
    for d in range(1, n_dp):
        small_cp(d, False).wait_send()


def hand_over(*refs):
    n = (len(refs) - 8) // 3
    srcs, small, dsts = refs[:n], refs[n], refs[n + 1 : 2 * n + 1]
    cuts, bufs, sem = refs[2 * n + 1 : 2 * n + 7], refs[2 * n + 7 : -1], refs[-1]
    parts = 4
    ways = []
    for i, (src, buf, dst) in enumerate(zip(srcs, bufs, dsts)):
        count = parts if src.shape[0] % parts == 0 else 1
        per = src.shape[0] // count
        for k in range(count):
            rows = slice(k * per, (k + 1) * per)
            ways.append(
                (
                    pltpu.make_async_copy(src.at[rows], buf.at[rows], sem.at[0, i, k]),
                    pltpu.make_async_copy(buf.at[rows], dst.at[rows], sem.at[1, i, k]),
                )
            )
    for inward, _ in ways:
        inward.start()
    for i, ref in enumerate(cuts):
        ref[...] = small[i : i + 1, 0 : ref.shape[1]]
    for inward, outward in ways:
        inward.wait()
        outward.start()
    for _, outward in ways:
        outward.wait()


def block_step(n_dp, n_rows, xv, xc, mv, mc, wr, ws, we, g1, s1, g2, s2, g3, s3, cv, cc, cpv, cpc):
    img, views, rows_v, cols_v, wide = xv.shape
    crops, cols_c = xc.shape[1], xc.shape[3]
    mid = wr.shape[1]
    maps_v, maps_c = img * views, img * crops
    pix_v, pix_c = rows_v * cols_v * maps_v, cols_c * maps_c
    pix = pix_v + pix_c
    valid_v, valid_c = (rows_v * n_rows - 1) * cols_v, (n_rows - 1) * cols_c
    nz, nx = n_dp // 2, n_rows // 2

    def views_in(t):
        return t.transpose(0, 1, 3, 2, 4).reshape(maps_v, cols_v, rows_v, wide)

    def crops_in(t):
        return t.transpose(0, 2, 3, 1, 4).reshape(img, cols_c, crops, wide)

    grid4 = (nz, 2, nx, 2)
    vm = pl.BlockSpec(memory_space=pltpu.VMEM)
    hbm = pl.BlockSpec(memory_space=pl.ANY)
    s_wr, s_we = wr.shape[0], we.shape[0]
    V = pltpu.VMEM
    D = pltpu.SemaphoreType.DMA

    scratch = [
        V((s_wr, mid), F32), V((9, s_we, mid), F32), V((s_we, wide), F32),
        V(grid4 + (s_wr, mid), BF), V((9,) + grid4 + (s_we, mid), BF), V(grid4 + (s_we, wide), BF),
        V(grid4 + (8, 128), F32),
        V((pix, 128), F32), V((cols_v, maps_v, 2, wide), BF), V((img, cols_c, crops, wide), BF),
        V((img, views, wide), F32), V((img, crops, wide), F32),
        V((pix, wide), BF), V((wide, pix), BF), V((pix, wide), BF),
        V((pix, mid), F32), V((pix, mid), F32), V((pix, wide), F32), V((pix, wide), F32),
        V((2, maps_v, cols_v, 2, TILE), F32), V((2, maps_c, cols_c, TILE // 128, 128), F32), V((2, pix, TILE), F32),
        V((4, (cols_v + 2) * maps_v, mid), BF), V((3, (cols_c + 2) * maps_c, mid), BF),
        V((4, (cols_v + 2) * maps_v, mid), BF), V((3, (cols_c + 2) * maps_c, mid), BF),
        V((pix, mid), BF), V((mid, pix), BF), V((pix, mid), BF),
        V(grid4 + (s_wr, mid), BF), V((9,) + grid4 + (s_we, mid), BF), V(grid4 + (s_we, wide), BF),
        V((nz, 2, nx, s_we, wide), BF), V((9, nz, 2, nx, s_we, mid), BF), V((nz, 2, nx, s_wr, mid), BF),
        V((2, nz, 2, s_we, wide // 4), BF), V((9, nz, 2, s_we, mid), BF), V((2, nz, 2, s_wr, mid // 2), BF),
        V((2, nz, s_we, wide // 4), BF), V((9, nz, s_we, mid), BF), V((2, nz, s_wr, mid // 2), BF),
        V((nz - 1, s_we, wide // 2), BF), V((nz - 1, 9, s_we, mid), BF), V((nz - 1, s_wr, mid), BF),
        V((nz - 1, 2, nx, s_we, wide // 2), BF), V((2, s_we, wide // 4), BF), V((2, s_we, wide // 2), BF),
        V((8, mid), F32), V((8, wide), F32),
        V((4, mid), F32), V((4, mid), F32), V((4, wide), F32),
        V((n_rows, 8, 128), F32),
        V((n_rows, 8, mid // 2), F32), V((n_rows, 8, mid // 2), F32), V((2, n_rows, 8, wide // 4), F32),
        V((n_rows, 8, mid // 2), F32), V((n_rows, 8, mid // 2), F32), V((2, n_rows, 8, wide // 4), F32),
        V((4, mid), F32), V((4, mid), F32), V((4, wide), F32),
        V((maps_v + maps_c, wide), F32), V((maps_v + maps_c, wide), BF), V((3, (maps_v + maps_c) // 2, wide), BF),
        V((n_dp, 8, 128), F32), V((n_dp - 1, 8, 128), F32),
        D((3, max(cols_v + 1, 5))), D((2, 2)), D((7, 5 * nz + 4)), D((7, 5 * nz + 4)), D((7, 6 + nz)), D((7, 6 + nz)),
        D((9, n_rows - 1)), D((9, n_rows - 1)), D((2, 4)), D((2, 4)), D((3,)), D((3,)), D((n_dp - 1,)), D((n_dp - 1,)),
    ]
    out_v = jax.ShapeDtypeStruct((maps_v, cols_v, 2, wide), F32)
    out_c = jax.ShapeDtypeStruct((maps_c, cols_c, wide // TILE, TILE // 128, 128), F32)
    outs = pl.pallas_call(
        functools.partial(kernel, n_dp, n_rows, (maps_v, cols_v, maps_c, cols_c, valid_v, valid_c)),
        out_shape=[
            out_v, out_c, out_v, out_c,
            jax.ShapeDtypeStruct(cpv.shape, F32), jax.ShapeDtypeStruct(cpc.shape, F32),
            jax.ShapeDtypeStruct((s_wr, mid), F32), jax.ShapeDtypeStruct((9, s_we, mid), F32),
            jax.ShapeDtypeStruct((s_we, wide), F32), jax.ShapeDtypeStruct((8, 128), F32),
        ],
        in_specs=[hbm] * 9 + [vm] * 8,
        out_specs=[hbm] * 4 + [vm] * 6,
        scratch_shapes=scratch,
        compiler_params=pltpu.CompilerParams(
            collective_id=0, has_side_effects=True, vmem_limit_bytes=63 << 20
        ),
    )(
        views_in(xv), crops_in(xc), views_in(cv), crops_in(cc), cpv, cpc,
        wr, ws.reshape(9, s_we, mid), we, mv.transpose(1, 2, 0), mc.transpose(1, 2, 0),
        g1.reshape(1, -1), s1.reshape(1, -1), g2.reshape(1, -1), s2.reshape(1, -1),
        g3.reshape(1, -1), s3.reshape(1, -1),
    )
    e = mid // (n_dp * n_rows)
    f = wide // (n_dp * n_rows)
    big, shapes = outs[:-1], [jax.ShapeDtypeStruct(o.shape, F32) for o in outs[:-1]]
    res = pl.pallas_call(
        hand_over,
        out_shape=shapes + [jax.ShapeDtypeStruct((1, w), F32) for w in (e, e, e, e, f, f)],
        in_specs=[hbm] * len(big) + [vm],
        out_specs=[hbm] * len(big) + [vm] * 6,
        scratch_shapes=[V(o.shape, F32) for o in big] + [D((2, len(big), 4))],
        compiler_params=pltpu.CompilerParams(vmem_limit_bytes=62 << 20),
    )(*outs)
    yv, yc, gv, gc, pool_v, pool_c, gwr, gws, gwe = res[:9]
    small = [r.reshape(-1) for r in res[9:]]

    def views_out(t):
        return t.reshape(img, views, cols_v, rows_v, wide).transpose(0, 1, 3, 2, 4)

    def crops_out(t):
        return t.reshape(img, crops, 1, cols_c, wide)

    return (
        views_out(yv), crops_out(yc),
        pool_v, pool_c,
        views_out(gv), crops_out(gc),
        gwr, gws.reshape(3, 3, s_we, mid), gwe,
        *small,
    )


def fits(xv, xc, we):
    return we.shape[0] % 16 == 0 and xv.shape[2] == 2 and xc.shape[2] == 1


def with_halo(block, sides, width):
    for axis, dim in sides:
        count = lax.axis_size(axis)
        forward = [(i, i + 1) for i in range(count - 1)]
        backward = [(target, source) for source, target in forward]
        low = lax.ppermute(
            lax.slice_in_dim(block, block.shape[dim] - width, None, axis=dim), axis, forward
        )
        high = lax.ppermute(lax.slice_in_dim(block, 0, width, axis=dim), axis, backward)
        block = jnp.concatenate([low, block, high], axis=dim)
    return block


def from_behind(array, axis, by):
    peers = lax.axis_size(axis)
    pairs = [(i, i + by) for i in range(peers) if 0 <= i + by < peers]
    return lax.ppermute(array, axis, pairs)


def silu_slope(value):
    sig = jax.nn.sigmoid(value)
    return sig * (1.0 + value * (1.0 - sig))


def pixel_mask(mask_rows, col_count):
    expanded = jnp.broadcast_to(
        mask_rows.astype(jnp.float32)[..., None], mask_rows.shape + (col_count,)
    )
    return expanded.reshape(-1, 1)


def by_group(in_views, view_value, crop_value):
    return jnp.where(in_views, view_value, crop_value)


def norm_forward(acts, mask_col, view_pixels, in_views, counts, gain_vec, shift_vec):
    masked = acts * mask_col
    totals = lax.psum(
        (jnp.sum(masked[:view_pixels], axis=0), jnp.sum(masked[view_pixels:], axis=0)), "rows"
    )
    centered = acts - by_group(in_views, totals[0] / counts[0], totals[1] / counts[1])
    squares = jnp.square(centered * mask_col)
    spread = lax.psum(
        (jnp.sum(squares[:view_pixels], axis=0), jnp.sum(squares[view_pixels:], axis=0)), "rows"
    )
    inv_rows = by_group(
        in_views, lax.rsqrt(spread[0] / counts[0] + eps), lax.rsqrt(spread[1] / counts[1] + eps)
    )
    normal = centered * inv_rows
    return (normal * gain_vec + shift_vec, normal, inv_rows)


def norm_backward(grad_z, normal, inv_rows, mask_col, view_pixels, in_views, counts, gain_vec):
    product = grad_z * normal
    partials = (
        jnp.sum(product[:view_pixels], axis=0),
        jnp.sum(grad_z[:view_pixels], axis=0),
        jnp.sum(product[view_pixels:], axis=0),
        jnp.sum(grad_z[view_pixels:], axis=0),
    )
    totals = (
        lax.psum(partials[0].astype(jnp.bfloat16), "rows").astype(jnp.float32),
        lax.psum(partials[1].astype(jnp.bfloat16), "rows").astype(jnp.float32),
        lax.psum(partials[2].astype(jnp.bfloat16), "rows").astype(jnp.float32),
        lax.psum(partials[3].astype(jnp.bfloat16), "rows").astype(jnp.float32),
    )
    scale_mean = by_group(in_views, totals[0] / counts[0], totals[2] / counts[1])
    shift_mean = by_group(in_views, totals[1] / counts[0], totals[3] / counts[1])
    grad_acts = gain_vec * inv_rows * (grad_z - shift_mean - normal * scale_mean) * mask_col
    return (grad_acts.astype(jnp.bfloat16), partials[0] + partials[2], partials[1] + partials[3])


def with_rims(feature_map):
    extended = with_halo(feature_map, (("rows", 1),), 1)
    return jnp.pad(extended, ((0, 0), (0, 0), (1, 1), (0, 0)))


def gather_taps(extended, row_count, col_count):
    windows = []
    for row_step in range(3):
        for col_step in range(3):
            windows.append(
                extended[:, row_step : row_step + row_count, col_step : col_step + col_count, :]
            )
    return jnp.concatenate(windows, axis=-1).reshape(-1, 9 * extended.shape[-1])


def spread_taps(grad_patches, map_count, row_count, col_count, mid_width):
    pieces = grad_patches.reshape(map_count, row_count, col_count, 9, mid_width)
    padded = jnp.zeros((map_count, row_count + 2, col_count + 2, mid_width), jnp.float32)
    tap_index = 0
    for row_step in range(3):
        for col_step in range(3):
            padded = padded.at[
                :, row_step : row_step + row_count, col_step : col_step + col_count, :
            ].add(pieces[:, :, :, tap_index, :])
            tap_index += 1
    inside = padded[:, 1 : row_count + 1, 1 : col_count + 1, :]
    from_below = from_behind(
        padded[:, 0, 1 : col_count + 1, :].astype(jnp.bfloat16), "rows", -1
    ).astype(jnp.float32)
    from_above = from_behind(
        padded[:, row_count + 1, 1 : col_count + 1, :].astype(jnp.bfloat16), "rows", 1
    ).astype(jnp.float32)
    inside = inside.at[:, row_count - 1].add(from_below)
    inside = inside.at[:, 0].add(from_above)
    return inside.reshape(-1, mid_width)


def contract_rows(left, right):
    return lax.dot_general(
        left, right, (((0,), (0,)), ((), ())), preferred_element_type=jnp.float32
    )


def contract_cols(left, right):
    return lax.dot_general(
        left, right, (((1,), (1,)), ((), ())), preferred_element_type=jnp.float32
    )


def shards(
    x_views,
    x_crops,
    mask_views,
    mask_crops,
    w_reduce,
    w_spatial,
    w_expand,
    gain_reduce,
    shift_reduce,
    gain_spatial,
    shift_spatial,
    gain_expand,
    shift_expand,
    cot_views,
    cot_crops,
    cot_pool_views,
    cot_pool_crops,
):
    low_type = jnp.bfloat16
    gathered = (
        lax.all_gather(w_reduce.astype(low_type), ("dp", "rows"), axis=0, tiled=True),
        lax.all_gather(w_spatial.astype(low_type), ("dp", "rows"), axis=2, tiled=True),
        lax.all_gather(w_expand.astype(low_type), ("dp", "rows"), axis=0, tiled=True),
        lax.all_gather(gain_reduce.astype(low_type), ("dp", "rows"), axis=0, tiled=True),
        lax.all_gather(shift_reduce.astype(low_type), ("dp", "rows"), axis=0, tiled=True),
        lax.all_gather(gain_spatial.astype(low_type), ("dp", "rows"), axis=0, tiled=True),
        lax.all_gather(shift_spatial.astype(low_type), ("dp", "rows"), axis=0, tiled=True),
        lax.all_gather(gain_expand.astype(low_type), ("dp", "rows"), axis=0, tiled=True),
        lax.all_gather(shift_expand.astype(low_type), ("dp", "rows"), axis=0, tiled=True),
    )
    weight_one, weight_two, weight_three = (gathered[0], gathered[1], gathered[2])
    gain_one, shift_one, gain_two, shift_two, gain_three, shift_three = [
        entry.astype(jnp.float32) for entry in gathered[3:]
    ]
    in_width = weight_one.shape[0]
    mid_width = weight_one.shape[1]
    view_maps = x_views.shape[0] * x_views.shape[1]
    view_rows, view_cols = (x_views.shape[2], x_views.shape[3])
    crop_maps = x_crops.shape[0] * x_crops.shape[1]
    crop_rows, crop_cols = (x_crops.shape[2], x_crops.shape[3])
    view_pixels = view_maps * view_rows * view_cols
    total_pixels = view_pixels + crop_maps * crop_rows * crop_cols
    row_parts = lax.axis_size("rows")
    view_valid = (view_rows * row_parts - 1) * view_cols
    crop_valid = (crop_rows * row_parts - 1) * crop_cols
    counts = (float(view_maps * view_valid), float(crop_maps * crop_valid))
    mask_col = jnp.concatenate(
        [pixel_mask(mask_views, view_cols), pixel_mask(mask_crops, crop_cols)], axis=0
    )
    in_views = lax.broadcasted_iota(jnp.int32, (total_pixels, 1), 0) < view_pixels
    inputs = jnp.concatenate([x_views.reshape(-1, in_width), x_crops.reshape(-1, in_width)], axis=0)
    acts_one = jnp.dot(inputs, weight_one, preferred_element_type=jnp.float32)
    z_one, normal_one, inv_one = norm_forward(
        acts_one, mask_col, view_pixels, in_views, counts, gain_one, shift_one
    )
    hidden_one = (jax.nn.silu(z_one) * mask_col).astype(low_type)
    view_hidden = hidden_one[:view_pixels].reshape(view_maps, view_rows, view_cols, mid_width)
    crop_hidden = hidden_one[view_pixels:].reshape(crop_maps, crop_rows, crop_cols, mid_width)
    patches = jnp.concatenate(
        [
            gather_taps(with_rims(view_hidden), view_rows, view_cols),
            gather_taps(with_rims(crop_hidden), crop_rows, crop_cols),
        ],
        axis=0,
    )
    spatial_flat = weight_two.reshape(9 * mid_width, mid_width)
    acts_two = jnp.dot(patches, spatial_flat, preferred_element_type=jnp.float32)
    z_two, normal_two, inv_two = norm_forward(
        acts_two, mask_col, view_pixels, in_views, counts, gain_two, shift_two
    )
    hidden_two = (jax.nn.silu(z_two) * mask_col).astype(low_type)
    acts_three = jnp.dot(hidden_two, weight_three, preferred_element_type=jnp.float32)
    z_three, normal_three, inv_three = norm_forward(
        acts_three, mask_col, view_pixels, in_views, counts, gain_three, shift_three
    )
    pre_act = inputs.astype(jnp.float32) + z_three
    result = jax.nn.silu(pre_act) * mask_col
    pooled = (
        lax.psum(
            jnp.sum(
                result[:view_pixels].reshape(view_maps, view_rows * view_cols, in_width), axis=1
            ).astype(jnp.bfloat16),
            "rows",
        ).astype(jnp.float32),
        lax.psum(
            jnp.sum(
                result[view_pixels:].reshape(crop_maps, crop_rows * crop_cols, in_width), axis=1
            ).astype(jnp.bfloat16),
            "rows",
        ).astype(jnp.float32),
    )
    pool_views = (pooled[0] / view_valid).reshape(cot_pool_views.shape)
    pool_crops = (pooled[1] / crop_valid).reshape(cot_pool_crops.shape)
    view_grad = (
        cot_views.astype(jnp.float32).reshape(view_maps, view_rows * view_cols, in_width)
        + cot_pool_views.reshape(view_maps, 1, in_width) / view_valid
    )
    crop_grad = (
        cot_crops.astype(jnp.float32).reshape(crop_maps, crop_rows * crop_cols, in_width)
        + cot_pool_crops.reshape(crop_maps, 1, in_width) / crop_valid
    )
    grad_out = jnp.concatenate(
        [view_grad.reshape(-1, in_width), crop_grad.reshape(-1, in_width)], axis=0
    )
    grad_pre = grad_out * mask_col * silu_slope(pre_act)
    grad_three, dgain_three, dshift_three = norm_backward(
        grad_pre, normal_three, inv_three, mask_col, view_pixels, in_views, counts, gain_three
    )
    grad_expand = contract_rows(hidden_two, grad_three)
    grad_hidden_two = contract_cols(grad_three, weight_three)
    grad_z_two = grad_hidden_two * mask_col * silu_slope(z_two)
    grad_two, dgain_two, dshift_two = norm_backward(
        grad_z_two, normal_two, inv_two, mask_col, view_pixels, in_views, counts, gain_two
    )
    grad_spatial = contract_rows(patches, grad_two).reshape(3, 3, mid_width, mid_width)
    grad_patches = contract_cols(grad_two, spatial_flat)
    grad_hidden_one = jnp.concatenate(
        [
            spread_taps(grad_patches[:view_pixels], view_maps, view_rows, view_cols, mid_width),
            spread_taps(grad_patches[view_pixels:], crop_maps, crop_rows, crop_cols, mid_width),
        ],
        axis=0,
    )
    grad_z_one = grad_hidden_one * mask_col * silu_slope(z_one)
    grad_one, dgain_one, dshift_one = norm_backward(
        grad_z_one, normal_one, inv_one, mask_col, view_pixels, in_views, counts, gain_one
    )
    grad_reduce = contract_rows(inputs, grad_one)
    grad_inputs = contract_cols(grad_one, weight_one) + grad_pre
    summed = (
        lax.psum_scatter(grad_reduce, ("dp", "rows"), scatter_dimension=0, tiled=True),
        lax.psum_scatter(grad_spatial, ("dp", "rows"), scatter_dimension=2, tiled=True),
        lax.psum_scatter(grad_expand, ("dp", "rows"), scatter_dimension=0, tiled=True),
        lax.psum_scatter(dgain_one, ("dp", "rows"), scatter_dimension=0, tiled=True),
        lax.psum_scatter(dshift_one, ("dp", "rows"), scatter_dimension=0, tiled=True),
        lax.psum_scatter(dgain_two, ("dp", "rows"), scatter_dimension=0, tiled=True),
        lax.psum_scatter(dshift_two, ("dp", "rows"), scatter_dimension=0, tiled=True),
        lax.psum_scatter(dgain_three, ("dp", "rows"), scatter_dimension=0, tiled=True),
        lax.psum_scatter(dshift_three, ("dp", "rows"), scatter_dimension=0, tiled=True),
    )
    out_views = result[:view_pixels].reshape(x_views.shape)
    out_crops = result[view_pixels:].reshape(x_crops.shape)
    grad_views = grad_inputs[:view_pixels].reshape(x_views.shape)
    grad_crops = grad_inputs[view_pixels:].reshape(x_crops.shape)
    return (
        out_views,
        out_crops,
        pool_views,
        pool_crops,
        grad_views,
        grad_crops,
        summed[0],
        summed[1],
        summed[2],
        summed[3],
        summed[4],
        summed[5],
        summed[6],
        summed[7],
        summed[8],
    )


def solution(mesh):
    in_specs = (
        P("dp", None, "rows", None, None),
        P("dp", None, "rows", None, None),
        P("dp", None, "rows"),
        P("dp", None, "rows"),
        P(("dp", "rows"), None),
        P(None, None, ("dp", "rows"), None),
        P(("dp", "rows"), None),
        P(("dp", "rows")),
        P(("dp", "rows")),
        P(("dp", "rows")),
        P(("dp", "rows")),
        P(("dp", "rows")),
        P(("dp", "rows")),
        P("dp", None, "rows", None, None),
        P("dp", None, "rows", None, None),
        P("dp", None, None),
        P("dp", None, None),
    )
    out_specs = (
        P("dp", None, "rows", None, None),
        P("dp", None, "rows", None, None),
        P("dp", None, None),
        P("dp", None, None),
        P("dp", None, "rows", None, None),
        P("dp", None, "rows", None, None),
        P(("dp", "rows"), None),
        P(None, None, ("dp", "rows"), None),
        P(("dp", "rows"), None),
        P(("dp", "rows")),
        P(("dp", "rows")),
        P(("dp", "rows")),
        P(("dp", "rows")),
        P(("dp", "rows")),
        P(("dp", "rows")),
    )
    def step(*args):
        if fits(args[0], args[1], args[6]):
            return block_step(mesh.shape["dp"], mesh.shape["rows"], *args)
        return shards(*args)

    return jax.shard_map(step, mesh=mesh, in_specs=in_specs, out_specs=out_specs, check_vma=False)
```

```python
import functools

import jax
import jax.numpy as jnp
from jax import lax
from jax.experimental import pallas as pl
from jax.experimental.pallas import tpu as pltpu
from jax.sharding import PartitionSpec as P

MESH = pl.DeviceIdType.MESH
ALL = slice(None)
BF = jnp.bfloat16
F32 = jnp.float32
eps = 1e-05
TILE = 256


def lanes(j, width=TILE):
    if isinstance(j, int):
        return slice(j * width, (j + 1) * width)
    return pl.ds(pl.multiple_of(j * width, width), width)


def half(h, width, at=0, whole=None):
    if h is None:
        return ALL if whole is None else slice(at, at + whole)
    return slice(at + h * (width // 2), at + (h + 1) * (width // 2))


def dot(a, b):
    return lax.dot_general(a, b, (((1,), (0,)), ((), ())), preferred_element_type=F32)


def dot_t(a, b):
    return lax.dot_general(a, b, (((1,), (1,)), ((), ())), preferred_element_type=F32)


def dot_r(a, b):
    return lax.dot_general(a, b, (((0,), (0,)), ((), ())), preferred_element_type=F32)


def sigmoid(v):
    return 0.5 * jnp.tanh(0.5 * v) + 0.5


def uneven(h, width):
    return ALL if h is None else slice(h * (width // 4), width if h else width // 4)


class Place:
    def __init__(self, n_dp, n_rows):
        self.ny, self.nc = 2, 2
        self.nz, self.nx = n_dp // 2, n_rows // 2
        self.n_dp, self.n_rows = n_dp, n_rows
        self.dp, self.r = lax.axis_index("dp"), lax.axis_index("rows")
        self.z, self.y = self.dp // 2, self.dp % 2
        self.x, self.c = self.r // 2, self.r % 2

    def dev(self, z, y, x, c):
        return {"dp": z * self.ny + y, "rows": x * self.nc + c}


def remote(src, dst, ssem, rsem, to):
    return pltpu.make_async_remote_copy(
        src_ref=src, dst_ref=dst, send_sem=ssem, recv_sem=rsem, device_id=to, device_id_type=MESH
    )


class Piece:
    def __init__(self, me, view, ssem, rsem):
        self.me, self.view, self.s, self.r, self.sent = me, view, ssem, rsem, []
        self.px = me.dev(me.z, me.y, 1 - me.x, me.c)
        self.py = me.dev(me.z, 1 - me.y, me.x, me.c)
        self.pc = me.dev(me.z, me.y, me.x, 1 - me.c)

    def pz(self, k):
        return self.me.dev((self.me.z + k) % self.me.nz, self.me.y, self.me.x, self.me.c)

    def send(self, k, src, dst, to):
        cp = remote(src, dst, self.s.at[k], self.r.at[k], to)
        cp.start()
        self.sent.append(cp)

    def got(self, k, dst):
        remote(dst, dst, self.s.at[k], self.r.at[k], self.pc).wait_recv()

    def drain(self):
        for cp in self.sent:
            cp.wait_send()


class Gather(Piece):
    def __init__(self, me, view, ssem, rsem, halves=(0, 1)):
        super().__init__(me, view, ssem, rsem)
        self.halves, n = halves, me.nz
        self.X, self.Y, self.D, self.C = n - 1, 2 * n - 1, (3 * n - 1, 4 * n - 1), 5 * n - 1

    def share(self, k, z, y, x, h, to):
        ref = self.view(z, y, x, self.me.c, h)
        self.send(k, ref, ref, to)

    def wait(self, k, z, y, x, h, c=None):
        self.got(k, self.view(z, y, x, self.me.c if c is None else c, h))

    def source(self, k):
        return (self.me.z + self.me.nz - k) % self.me.nz

    def start_z(self):
        me = self.me
        for k in range(1, me.nz):
            self.share(k - 1, me.z, me.y, me.x, None, self.pz(k))

    def start_xy(self):
        me = self.me
        self.share(self.X, me.z, me.y, me.x, None, self.px)
        self.share(self.Y, me.z, me.y, me.x, None, self.py)

    def got_z(self, k):
        me, z = self.me, self.source(k)
        self.wait(k - 1, z, me.y, me.x, None)
        self.share(self.X + k, z, me.y, me.x, None, self.px)
        self.share(self.Y + k, z, me.y, me.x, None, self.py)
        if k == me.nz - 1:
            self.share(self.C, ALL, me.y, me.x, None, self.pc)

    def diagonal(self):
        me = self.me
        for k in range(me.nz):
            z = self.source(k)
            self.wait(self.Y + k, z, 1 - me.y, me.x, None)
            self.share(self.D[0] + k, z, 1 - me.y, me.x, 0, self.px)
            self.wait(self.X + k, z, me.y, 1 - me.x, None)
            if 1 in self.halves:
                self.share(self.D[1] + k, z, me.y, 1 - me.x, 1, self.py)
        self.share(self.C + 1, ALL, 1 - me.y, me.x, None, self.pc)
        self.share(self.C + 2, ALL, me.y, 1 - me.x, None, self.pc)

    def last(self):
        me = self.me
        for h in self.halves:
            for k in range(me.nz):
                self.wait(self.D[h] + k, self.source(k), 1 - me.y, 1 - me.x, h)
            self.share(self.C + 3 + h, ALL, 1 - me.y, 1 - me.x, h, self.pc)

    def finish(self):
        me, o = self.me, 1 - self.me.c
        self.wait(self.C, ALL, me.y, me.x, None, o)
        self.wait(self.C + 1, ALL, 1 - me.y, me.x, None, o)
        self.wait(self.C + 2, ALL, me.y, 1 - me.x, None, o)
        for h in self.halves:
            self.wait(self.C + 3 + h, ALL, 1 - me.y, 1 - me.x, h, o)


class GatherPlane(Gather):
    def start(self):
        me = self.me
        self.share(0, me.z, me.y, me.x, None, self.px)
        self.share(1, me.z, me.y, me.x, None, self.py)

    def diagonal(self):
        me = self.me
        self.wait(1, me.z, 1 - me.y, me.x, None)
        self.share(2, me.z, 1 - me.y, me.x, 0, self.px)
        self.wait(0, me.z, me.y, 1 - me.x, None)
        self.share(3, me.z, me.y, 1 - me.x, 1, self.py)

    def plane(self):
        me = self.me
        for h in (0, 1):
            self.wait(2 + h, me.z, 1 - me.y, 1 - me.x, h)
        for k in range(1, me.nz):
            self.share(3 + k, me.z, ALL, ALL, None, self.pz(k))
        self.share(4 + me.nz, me.z, ALL, ALL, None, self.pc)

    def last(self):
        for k in range(1, self.me.nz):
            self.wait(3 + k, self.source(k), ALL, ALL, None)
            self.share(4 + self.me.nz + k, self.source(k), ALL, ALL, None, self.pc)

    def finish(self):
        for k in range(self.me.nz):
            self.wait(4 + self.me.nz + k, self.source(k), ALL, ALL, None, 1 - self.me.c)


class Reduce:
    def __init__(self, me, view, from_core, from_third, from_second, from_z, ssem, rsem):
        self.me, self.view, self.s, self.r = me, view, ssem, rsem
        self.fc, self.f3, self.f2, self.fz = from_core, from_third, from_second, from_z

    def core(self):
        me = self.me
        return remote(
            self.view(ALL, ALL, ALL, 1 - me.c, None),
            self.fc(ALL, ALL, ALL, None),
            self.s.at[0],
            self.r.at[0],
            me.dev(me.z, me.y, me.x, 1 - me.c),
        )

    def third(self, h):
        me = self.me
        place = (ALL, ALL, 1 - me.x) if h == 0 else (ALL, 1 - me.y, ALL)
        to = (me.z, me.y, 1 - me.x, me.c) if h == 0 else (me.z, 1 - me.y, me.x, me.c)
        return remote(
            self.view(*place, me.c, h), self.f3(h), self.s.at[1 + h], self.r.at[1 + h], me.dev(*to)
        )

    def second(self, h):
        me = self.me
        place = (ALL, 1 - me.y, me.x) if h == 0 else (ALL, me.y, 1 - me.x)
        to = (me.z, 1 - me.y, me.x, me.c) if h == 0 else (me.z, me.y, 1 - me.x, me.c)
        return remote(
            self.view(*place, me.c, h), self.f2(h), self.s.at[3 + h], self.r.at[3 + h], me.dev(*to)
        )

    def along_z(self, dz):
        me = self.me
        z = (me.z + dz) % me.nz
        return remote(
            self.view(z, me.y, me.x, me.c, None),
            self.fz(dz - 1),
            self.s.at[4 + dz],
            self.r.at[4 + dz],
            me.dev(z, me.y, me.x, me.c),
        )

    def start(self):
        self.core().start()

    def stage2(self):
        me = self.me
        self.core().wait_recv()
        for h in (0, 1):
            first = (ALL, ALL, 1 - me.x) if h == 0 else (ALL, 1 - me.y, ALL)
            ref = self.view(*first, me.c, h)
            ref[...] = ref[...] + self.fc(*first, h)[...]
            self.third(h).start()
        for h in (0, 1):
            rest = (ALL, ALL, me.x) if h == 0 else (ALL, me.y, ALL)
            ref = self.view(*rest, me.c, h)
            ref[...] = ref[...] + self.fc(*rest, h)[...]

    def stage3(self):
        me = self.me
        for h in (0, 1):
            self.third(h).wait_recv()
            kept = (ALL, ALL, me.x) if h == 0 else (ALL, me.y, ALL)
            ref = self.view(*kept, me.c, h)
            ref[...] = ref[...] + self.f3(h)[...]
            self.second(h).start()

    def stage4(self):
        me = self.me
        for h in (0, 1):
            self.second(h).wait_recv()
            ref = self.view(ALL, me.y, me.x, me.c, h)
            ref[...] = ref[...] + self.f2(h)[...]
        for dz in range(1, me.nz):
            self.along_z(dz).start()

    def finish(self):
        me = self.me
        total = self.view(me.z, me.y, me.x, me.c, None)[...].astype(F32)
        for dz in range(1, me.nz):
            self.along_z(dz).wait_recv()
            total = total + self.fz(dz - 1)[...].astype(F32)
        return total

    def drain(self):
        self.core().wait_send()
        for h in (0, 1):
            self.third(h).wait_send()
            self.second(h).wait_send()
        for dz in range(1, self.me.nz):
            self.along_z(dz).wait_send()


def kernel(n_dp, n_rows, sizes, *refs):
    (
        xv_h, xc_h, cv_h, cc_h, cpv_h, cpc_h, wr_h, ws_h, we_h, mv_in, mc_in,
        g1_in, s1_in, g2_in, s2_in, g3_in, s3_in,
        yv_h, yc_h, gv_h, gc_h, poolv_o, poolc_o, gwr_o, gws_o, gwe_o, small_o,
        wr_in, ws_in, we_in, wr, ws, we, par, mask, raw_v, raw_c, cpv, cpc, x, xt, cot, a1, a2, a3, gpre, ysv, ysc, gact,
        hv, hc, dv, dc, h2, h2t, ga1, gwr, gws, gwe,
        fc_we, fc_ws, fc_wr, f3_we, f3_ws, f3_wr, f2_we, f2_ws, f2_wr, fz_we, fz_ws, fz_wr,
        p1, p3, mi1, mi2, mi3, cnt, ex1, ex2, ex3, bx1, bx2, bx3, tot1, tot2, tot3,
        pf, pb, pr, sb, rb,
        in_sem, out_sem, ag_s, ag_r, rs_s, rs_r, ex_s, ex_r, halo_s, halo_r, pool_s, pool_r, sm_s, sm_r,
    ) = refs
    (maps_v, cols_v, maps_c, cols_c, valid_v, valid_c) = sizes
    me = Place(n_dp, n_rows)
    mid, wide = a1.shape[1], a3.shape[1]
    pix_v = 2 * cols_v * maps_v
    pix = a1.shape[0]
    row_v, row_c = cols_v * maps_v, cols_c * maps_c
    count = (float(maps_v * valid_v), float(maps_c * valid_c))
    CH = 32
    chunks = [(s, 0 if s < pix_v else 1) for s in range(0, pix, CH)]

    barrier = pltpu.get_barrier_semaphore()
    peers = [{"dp": me.dp, "rows": (me.r + d) % n_rows} for d in range(1, n_rows)]
    peers += [{"dp": (me.dp + d) % n_dp, "rows": me.r} for d in range(1, n_dp)]
    for peer in peers:
        pl.semaphore_signal(barrier, inc=1, device_id=peer, device_id_type=MESH)

    def fetch(k, views, crops):
        return [
            pltpu.make_async_copy(views.at[:, col], raw_v.at[col], in_sem.at[k, col]) for col in range(cols_v)
        ] + [pltpu.make_async_copy(crops, raw_c, in_sem.at[k, cols_v])]

    def arrange(out):
        def body(j, carry):
            cols = lanes(j)
            for col in range(cols_v):
                for r in (0, 1):
                    at = r * row_v + col * maps_v
                    out[at : at + maps_v, cols] = raw_v[col, :, r, cols]
            for col in range(cols_c):
                at = pix_v + col * maps_c
                out[at : at + maps_c, cols] = raw_c[:, col, :, cols].reshape(maps_c, TILE)
            return carry

        lax.fori_loop(0, wide // TILE, body, 0)

    x_copies, cot_copies = fetch(0, xv_h, xc_h), fetch(1, cv_h, cc_h)
    pool_copies = [
        pltpu.make_async_copy(cpv_h, cpv, in_sem.at[2, 0]),
        pltpu.make_async_copy(cpc_h, cpc, in_sem.at[2, 1]),
    ]
    weight_copies = [
        pltpu.make_async_copy(src, dst, in_sem.at[2, 2 + i])
        for i, (src, dst) in enumerate(((wr_h, wr_in), (ws_h, ws_in), (we_h, we_in)))
    ]
    for cp in weight_copies + x_copies + pool_copies:
        cp.start()

    here = (me.z, me.y, me.x, me.c)
    own = par.at[here]
    own[...] = jnp.zeros(own.shape, F32)
    for i, ref in enumerate((g1_in, s1_in, g2_in, s2_in, g3_in, s3_in)):
        own[i : i + 1, 0 : ref.shape[1]] = ref[...].astype(BF).astype(F32)

    def mask_column(row_of, per, maps):
        lane = lax.broadcasted_iota(jnp.int32, (maps, 16), 1)
        place = lax.broadcasted_iota(jnp.int32, (maps, 16), 0)
        total = jnp.zeros((maps, 16), F32)
        for k in range(per):
            hit = jnp.logical_and(place % per == k, lane == place // per)
            total = total + jnp.where(hit, row_of(k).astype(F32), 0.0)
        return jnp.broadcast_to(jnp.sum(total, axis=1, keepdims=True), (maps, 128))

    for r in (0, 1):
        column = mask_column(lambda k: mv_in[k, r : r + 1, :], mv_in.shape[0], maps_v)
        for col in range(cols_v):
            at = r * row_v + col * maps_v
            mask[at : at + maps_v] = column
    column = mask_column(lambda k: mc_in[k], mc_in.shape[0], maps_c)
    for col in range(cols_c):
        at = pix_v + col * maps_c
        mask[at : at + maps_c] = column

    cnt_own = cnt.at[me.r]
    cnt_own[0:1] = jnp.sum(mask[0:pix_v], axis=0, keepdims=True)
    cnt_own[1:2] = jnp.sum(mask[pix_v:pix], axis=0, keepdims=True)
    cnt_own[2:8] = jnp.zeros((6, 128), F32)

    for cp in weight_copies:
        cp.wait()
    wr[here] = wr_in[...].astype(BF)
    ws[(ALL,) + here] = ws_in[...].astype(BF)
    we[here] = we_in[...].astype(BF)

    pl.semaphore_wait(barrier, len(peers))

    def piece(k, view, halves=(0, 1), form=Gather):
        return form(me, view, ag_s.at[k], ag_r.at[k], *(() if form is GatherPlane else (halves,)))

    part = wide // 2
    small_piece = piece(0, lambda z, y, x, c, h: par.at[z, y, x, c], (0,))
    pieces = [piece(1, lambda z, y, x, c, h: wr.at[z, y, x, c, :, half(h, mid)])]
    for i in range(3):
        pieces.append(
            piece(2 + i, lambda z, y, x, c, h, i=i: ws.at[3 * i : 3 * i + 3, z, y, x, c, :, uneven(h, mid)])
        )
    pieces.append(piece(5, lambda z, y, x, c, h: we.at[z, y, x, c, :, half(h, part, 0, part)]))
    plane = piece(6, lambda z, y, x, c, h: we.at[z, y, x, c, :, half(h, part, part, part)], form=GatherPlane)

    def exchange(k, buf):
        def cp(d, recv):
            peer = (me.r + n_rows - d) % n_rows if recv else (me.r + d) % n_rows
            ref = buf.at[peer if recv else me.r]
            return remote(ref, ref, ex_s.at[k, d - 1], ex_r.at[k, d - 1], {"dp": me.dp, "rows": peer})

        def send():
            for d in range(1, n_rows):
                cp(d, False).start()

        def wait():
            for d in range(1, n_rows):
                cp(d, True).wait_recv()

        def drain():
            for d in range(1, n_rows):
                cp(d, False).wait_send()

        return send, wait, drain

    exchanges = [
        exchange(k, b)
        for k, b in enumerate(
            (cnt, ex1, ex2, ex3.at[0], ex3.at[1], bx1, bx2, bx3.at[0], bx3.at[1])
        )
    ]
    CNT, EX1, EX2, EX3, BX1, BX2, BX3 = 0, 1, 2, 3, 5, 6, 7

    def rim(k, v, c):
        def cps(up):
            peer = {"dp": me.dp, "rows": (me.r + n_rows - 1) % n_rows if up else (me.r + 1) % n_rows}
            base = 0 if up else 2
            vs, vd = (1, 3) if up else (2, 0)
            csrc, cd = (1, 2) if up else (1, 0)
            return [
                remote(
                    v.at[vs, maps_v : maps_v + row_v],
                    v.at[vd, maps_v : maps_v + row_v],
                    halo_s.at[k, base],
                    halo_r.at[k, base],
                    peer,
                ),
                remote(
                    c.at[csrc, maps_c : maps_c + row_c],
                    c.at[cd, maps_c : maps_c + row_c],
                    halo_s.at[k, base + 1],
                    halo_r.at[k, base + 1],
                    peer,
                ),
            ]

        def each(up, fn):
            def body():
                for cp in cps(up):
                    fn(cp)

            return body

        first, last = me.r == 0, me.r == n_rows - 1

        def send():
            pl.when(jnp.logical_not(first))(each(True, lambda cp: cp.start()))
            pl.when(jnp.logical_not(last))(each(False, lambda cp: cp.start()))

        def wait():
            pl.when(jnp.logical_not(last))(each(True, lambda cp: cp.wait_recv()))
            pl.when(jnp.logical_not(first))(each(False, lambda cp: cp.wait_recv()))

        def drain():
            pl.when(jnp.logical_not(first))(each(True, lambda cp: cp.wait_send()))
            pl.when(jnp.logical_not(last))(each(False, lambda cp: cp.wait_send()))

        return send, wait, drain

    rim_h, rim_d = rim(0, hv, hc), rim(1, dv, dc)

    def clear_rims(v, c):
        zv, zc = jnp.zeros((maps_v, mid), BF), jnp.zeros((maps_c, mid), BF)
        for r in range(4):
            v[r, 0:maps_v] = zv
            v[r, maps_v + row_v : 2 * maps_v + row_v] = zv
        for r in range(3):
            c[r, 0:maps_c] = zc
            c[r, maps_c + row_c : 2 * maps_c + row_c] = zc

        @pl.when(me.r == 0)
        def _():
            v[0, maps_v : maps_v + row_v] = jnp.zeros((row_v, mid), BF)
            c[0, maps_c : maps_c + row_c] = jnp.zeros((row_c, mid), BF)

        @pl.when(me.r == n_rows - 1)
        def _():
            v[3, maps_v : maps_v + row_v] = jnp.zeros((row_v, mid), BF)
            c[2, maps_c : maps_c + row_c] = jnp.zeros((row_c, mid), BF)

    def tile_rows(ref, j):
        per = me.nz * TILE // mid
        return ref[j * per : (j + 1) * per]

    def fold(v):
        return jnp.sum(v.reshape(v.shape[0] // 8, 8, v.shape[1]), axis=0)

    def put(buf, j, k, value):
        tiles = buf.shape[2] // TILE
        if isinstance(j, int):
            buf[me.r, 4 * (j // tiles) + k : 4 * (j // tiles) + k + 1, lanes(j % tiles)] = value
        else:
            buf[me.r, pl.ds(4 * (j // tiles) + k, 1), lanes(j % tiles)] = value

    def masked(s):
        return jnp.concatenate([mask[s : s + CH]] * (TILE // 128), axis=1)

    def local_stats(a, buf, n_tiles, first=0):
        def body(j, carry):
            cols = lanes(j + first)
            for grp in (0, 1):
                acc = jnp.zeros((8, TILE), F32)
                for s, g in chunks:
                    if g == grp:
                        acc = acc + fold(a[s : s + CH, cols] * masked(s))
                total = jnp.sum(acc, axis=0, keepdims=True)
                n_own = jnp.maximum(cnt[me.r, grp : grp + 1, 0:1], 1.0)
                mean = total / n_own
                acc = jnp.zeros((8, TILE), F32)
                for s, g in chunks:
                    if g == grp:
                        d = (a[s : s + CH, cols] - mean) * masked(s)
                        acc = acc + fold(d * d)
                put(buf, j, 2 * grp, total)
                put(buf, j, 2 * grp + 1, jnp.sum(acc, axis=0, keepdims=True))
            return carry

        for j in range(n_tiles):
            body(j, 0) if n_tiles <= 2 else None
        if n_tiles > 2:
            lax.fori_loop(0, n_tiles, body, 0)

    def merge_stats(buf, mi, at=0):
        width = buf.shape[2]
        for hf in (0, 1):
            for grp in (0, 1):
                k = 4 * hf + 2 * grp
                total = sum(buf[i, k : k + 1] for i in range(n_rows))
                mean = total / count[grp]
                spread = jnp.zeros_like(mean)
                for i in range(n_rows):
                    n_i = cnt[i, grp : grp + 1, 0:1]
                    off = buf[i, k : k + 1] / jnp.maximum(n_i, 1.0) - mean
                    spread = spread + buf[i, k + 1 : k + 2] + n_i * (off * off)
                mi[2 * grp : 2 * grp + 1, at + hf * width : at + (hf + 1) * width] = mean
                mi[2 * grp + 1 : 2 * grp + 2, at + hf * width : at + (hf + 1) * width] = lax.rsqrt(
                    spread / count[grp] + eps
                )

    def merge_grads(buf, tot, at=0):
        width = buf.shape[2]
        for hf in (0, 1):
            block = buf[0, 4 * hf : 4 * hf + 4]
            for i in range(1, n_rows):
                block = block + buf[i, 4 * hf : 4 * hf + 4]
            tot[0:4, at + hf * width : at + (hf + 1) * width] = block

    def expand_params():
        blocks = par[...].reshape(n_dp * n_rows * 8, 128).astype(BF)
        n_dev = n_dp * n_rows
        for out, width in ((p1, mid), (p3, wide)):
            share = width // n_dev
            step = 512
            for t in range(width // step):
                lane = lax.broadcasted_iota(jnp.int32, (128, step), 1) + t * step
                place = lax.broadcasted_iota(jnp.int32, (128, step), 0)
                pick = jnp.where(lane % share == place, 1.0, 0.0).astype(BF)
                spread = dot(blocks, pick).reshape(n_dev, 8, step)
                owner = (lax.broadcasted_iota(jnp.int32, (8, step), 1) + t * step) // share
                total = jnp.zeros((8, step), F32)
                for d in range(n_dev):
                    total = total + jnp.where(owner == d, spread[d], 0.0)
                out[:, t * step : (t + 1) * step] = total

    def gain(out, i, cols):
        return out[i : i + 1, cols]

    small_piece.start_z()
    small_piece.start_xy()
    pieces[0].start_z()
    pieces[0].start_xy()
    exchanges[CNT][0]()
    plane.start()
    for p in pieces[1:]:
        p.start_xy()
    clear_rims(hv, hc)
    clear_rims(dv, dc)
    for cp in x_copies:
        cp.wait()
    arrange(x)
    for cp in cot_copies:
        cp.start()

    def step0(t):
        pieces[t].got_z(1)
        if t + 1 < len(pieces):
            pieces[t + 1].start_z()
        for k in range(2, me.nz):
            pieces[t].got_z(k)

    for k in range(1, me.nz):
        small_piece.got_z(k)
    step0(0)
    plane.diagonal()
    small_piece.diagonal()
    for t in range(wide // TILE):
        xt[t * TILE : (t + 1) * TILE, :] = x[:, t * TILE : (t + 1) * TILE].T
    step0(1)
    pieces[0].diagonal()
    small_piece.last()
    for cp in cot_copies:
        cp.wait()
    arrange(cot)
    step0(2)
    pieces[1].diagonal()
    pieces[0].last()
    small_piece.finish()
    expand_params()
    pieces[0].finish()
    exchanges[CNT][1]()

    def conv1(j, carry):
        w = wr[:, :, :, :, :, lanes(j)].reshape(wide, TILE)
        a1[:, lanes(j)] = dot(x[...], w)
        return carry

    for j in range(mid // TILE):
        conv1(j, 0)
    local_stats(a1, ex1, mid // TILE)
    exchanges[EX1][0]()
    step0(3)
    pieces[2].diagonal()
    pieces[1].last()
    exchanges[EX1][1]()
    merge_stats(ex1, mi1)

    def store_rows(v, c, s, cols, value):
        if s < pix_v:
            r, o = s // row_v, s % row_v
            v[1 + r, maps_v + o : maps_v + o + CH, cols] = value
        else:
            o = s - pix_v
            c[1, maps_c + o : maps_c + o + CH, cols] = value

    def act(a, mi, i, store):
        def body(j, carry):
            cols = lanes(j)
            scale = [mi[2 * g + 1 : 2 * g + 2, cols] * gain(p1, i, cols) for g in (0, 1)]
            mean = [mi[2 * g : 2 * g + 1, cols] for g in (0, 1)]
            shift = gain(p1, i + 1, cols)
            for s, g in chunks:
                zed = (a[s : s + CH, cols] - mean[g]) * scale[g] + shift
                store(s, cols, (zed * sigmoid(zed) * masked(s)).astype(BF))
            return carry

        for j in range(mid // TILE):
            body(j, 0)

    act(a1, mi1, 0, lambda s, cols, value: store_rows(hv, hc, s, cols, value))
    rim_h[0]()
    step0(4)
    plane.plane()
    pieces[3].diagonal()
    pieces[2].last()
    pieces[1].finish()
    def windows(v, c, dy, dx):
        left = [v[r + dy, dx * maps_v : dx * maps_v + row_v, :] for r in (0, 1)]
        return jnp.concatenate(left + [c[dy, dx * maps_c : dx * maps_c + row_c, :]], axis=0)

    def conv2(dy):
        left = jnp.concatenate([windows(hv, hc, dy, dx) for dx in range(3)], axis=1)
        for j in range(mid // TILE):
            w = ws[3 * dy : 3 * dy + 3, :, :, :, :, :, lanes(j)].reshape(3 * mid, TILE)
            part_sum = dot(left, w)
            a2[:, lanes(j)] = part_sum if dy == 1 else a2[:, lanes(j)] + part_sum

    pieces[2].finish()
    conv2(1)
    pieces[4].diagonal()
    rim_h[1]()
    conv2(0)
    pieces[3].last()
    pieces[3].finish()
    conv2(2)
    local_stats(a2, ex2, mid // TILE)
    exchanges[EX2][0]()
    pieces[4].last()
    exchanges[EX2][1]()
    merge_stats(ex2, mi2)

    def store_h2(s, cols, value):
        h2[s : s + CH, cols] = value

    act(a2, mi2, 2, store_h2)
    for cp in pool_copies:
        cp.wait()

    def conv3(j, carry):
        w = we[:, :, :, :, :, lanes(j)].reshape(mid, TILE)
        a3[:, lanes(j)] = dot(h2[...], w)
        return carry

    tiles = wide // TILE // 2
    pieces[4].finish()
    for j in range(tiles):
        conv3(j, 0)
    local_stats(a3, ex3.at[0], tiles)
    exchanges[EX3][0]()
    plane.last()
    plane.finish()
    for j in range(tiles, 2 * tiles):
        conv3(j, 0)
    local_stats(a3, ex3.at[1], tiles, tiles)
    exchanges[EX3 + 1][0]()
    h2t[...] = h2[...].T
    exchanges[EX3][1]()
    merge_stats(ex3.at[0], mi3)

    def out_copies(j, slot, views, crops):
        return [
            pltpu.make_async_copy(ysv.at[slot], views.at[:, :, :, lanes(j)], out_sem.at[slot, 0]),
            pltpu.make_async_copy(ysc.at[slot], crops.at[:, :, j], out_sem.at[slot, 1]),
        ]

    def store_out(slot, s, value):
        if s < pix_v:
            ysv[slot, :, s % row_v // maps_v, s // row_v, :] = value
        else:
            col, at = (s - pix_v) // maps_c, (s - pix_v) % maps_c
            for k in (0, 1):
                ysc[slot, at : at + CH, col, k, :] = value[:, k * 128 : (k + 1) * 128]

    def last(q, jj, carry):
        for slot in (0, 1):
            j = 2 * jj + slot
            cols = lanes(j)

            def free_slot():
                for cp in out_copies(j, slot, yv_h, yc_h):
                    cp.wait()

            if q > 0:
                free_slot()
            else:
                pl.when(jj > 0)(free_slot)

            mean = [mi3[2 * g : 2 * g + 1, cols] for g in (0, 1)]
            inv = [mi3[2 * g + 1 : 2 * g + 2, cols] for g in (0, 1)]
            scale = [inv[g] * gain(p3, 4, cols) for g in (0, 1)]
            sh = gain(p3, 5, cols)
            sums = [jnp.zeros((8, TILE), F32) for _ in range(4)]
            pooled = [jnp.zeros((CH, TILE), F32) for _ in range((maps_v + maps_c) // CH)]
            per_v, per_c = CH // cpv.shape[1], CH // cpc.shape[1]
            cps = [
                cpv[s : s + per_v, :, cols].reshape(CH, TILE) * (1.0 / valid_v)
                for s in range(0, cpv.shape[0], per_v)
            ] + [
                cpc[s : s + per_c, :, cols].reshape(CH, TILE) * (1.0 / valid_c)
                for s in range(0, cpc.shape[0], per_c)
            ]
            for s, g in chunks:
                which = (s % maps_v) // CH if g == 0 else (maps_v + (s - pix_v) % maps_c) // CH
                rows = slice(s, s + CH)
                m = masked(s)
                off = a3[rows, cols] - mean[g]
                pre = x[rows, cols].astype(F32) + (off * scale[g] + sh)
                sig = sigmoid(pre)
                act_out = pre * sig
                out = act_out * m
                store_out(slot, s, out)
                pooled[which] = pooled[which] + out
                slope = act_out + sig * (1.0 - act_out)
                gp = (cot[rows, cols].astype(F32) + cps[which]) * m * slope
                gpre[rows, cols] = gp
                sums[2 * g] = sums[2 * g] + fold(gp * off)
                sums[2 * g + 1] = sums[2 * g + 1] + fold(gp)
            for k in range(4):
                total = jnp.sum(sums[k], axis=0, keepdims=True)
                put(bx3.at[q], j - q * tiles, k, total * inv[k // 2] if k % 2 == 0 else total)
            for i, value in enumerate(pooled):
                pf[i * CH : (i + 1) * CH, cols] = value
                pb[i * CH : (i + 1) * CH, cols] = value.astype(BF)
            for cp in out_copies(j, slot, yv_h, yc_h):
                cp.start()
        return carry

    core_peer = {"dp": me.dp, "rows": me.x * 2 + 1 - me.c}
    chip_peer = {"dp": me.dp, "rows": (1 - me.x) * 2 + me.c}
    share = pb.shape[0] // 2
    mine, others = pl.ds(me.c * share, share), pl.ds((1 - me.c) * share, share)
    pool_core = remote(pb.at[others], pr.at[0], pool_s.at[0], pool_r.at[0], core_peer)
    pool_chip = remote(pb.at[mine], pr.at[1], pool_s.at[1], pool_r.at[1], chip_peer)
    pool_back = remote(pb.at[mine], pr.at[2], pool_s.at[2], pool_r.at[2], core_peer)
    lax.fori_loop(0, tiles // 2, functools.partial(last, 0), 0)
    exchanges[BX3][0]()
    exchanges[EX3 + 1][1]()
    merge_stats(ex3.at[1], mi3, wide // 2)
    lax.fori_loop(tiles // 2, tiles, functools.partial(last, 1), 0)
    exchanges[BX3 + 1][0]()
    pool_core.start()

    def coefs(mi, tot, gn, cols):
        out = []
        for g in (0, 1):
            mean, inv = mi[2 * g : 2 * g + 1, cols], mi[2 * g + 1 : 2 * g + 2, cols]
            dg, ds = tot[2 * g : 2 * g + 1, cols], tot[2 * g + 1 : 2 * g + 2, cols]
            out.append((mean, gn * inv, ds / count[g], dg / count[g] * inv))
        return out

    def norm_back(gz, a, co, s, cols):
        mean, k0, k1, k2 = co
        return (k0 * (gz - k1 - (a[s : s + CH, cols] - mean) * k2) * masked(s)).astype(BF)

    def grad_three(j, carry):
        cols = lanes(j)
        co = coefs(mi3, tot3, gain(p3, 4, cols), cols)
        for s, g in chunks:
            cot[s : s + CH, cols] = norm_back(gpre[s : s + CH, cols], a3, co[g], s, cols)
        gwe[:, :, :, :, :, cols] = (
            dot(h2t[...], cot[:, cols]).astype(BF).reshape(gwe.shape[:5] + (TILE,))
        )
        return carry

    def reducer(k, view, fc, f3, f2, fz):
        return Reduce(me, view, fc, f3, f2, fz, rs_s.at[k], rs_r.at[k])

    q_we = [
        reducer(
            i,
            lambda z, y, x, c, h, at=i * part: gwe.at[z, y, x, c, :, half(h, part, at, part)],
            lambda z, y, x, h, at=i * part: fc_we.at[z, y, x, :, half(h, part, at, part)],
            lambda h, i=i: f3_we.at[i, h],
            lambda h, i=i: f2_we.at[i, h],
            lambda k, i=i: fz_we.at[i, k],
        )
        for i in range(2)
    ]
    q_ws = [
        reducer(
            2 + i,
            lambda z, y, x, c, h, i=i: gws.at[3 * i : 3 * i + 3, z, y, x, c, :, uneven(h, mid)],
            lambda z, y, x, h, i=i: fc_ws.at[3 * i : 3 * i + 3, z, y, x, :, uneven(h, mid)],
            lambda h, i=i: f3_ws.at[3 * i : 3 * i + 3, :, :, :, uneven(h, mid)],
            lambda h, i=i: f2_ws.at[3 * i : 3 * i + 3, :, :, uneven(h, mid)],
            lambda k, i=i: fz_ws.at[k, 3 * i : 3 * i + 3],
        )
        for i in range(3)
    ]
    few = wr.shape[4] // 2
    q_wr = [
        reducer(
            5 + i,
            lambda z, y, x, c, h, i=i: gwr.at[z, y, x, c, i * few : (i + 1) * few, half(h, mid)],
            lambda z, y, x, h, i=i: fc_wr.at[z, y, x, i * few : (i + 1) * few, half(h, mid)],
            lambda h, i=i: f3_wr.at[h, :, :, i * few : (i + 1) * few],
            lambda h, i=i: f2_wr.at[h, :, i * few : (i + 1) * few],
            lambda k, i=i: fz_wr.at[k, i * few : (i + 1) * few],
        )
        for i in range(2)
    ]

    exchanges[BX3][1]()
    merge_grads(bx3.at[0], tot3)
    for j in range(tiles):
        grad_three(j, 0)
    q_we[0].start()
    exchanges[BX3 + 1][1]()
    merge_grads(bx3.at[1], tot3, wide // 2)
    q_we[0].stage2()
    for j in range(tiles, 2 * tiles):
        grad_three(j, 0)
    q_we[1].start()

    def grad_act(gh, a, mi, i, buf, j):
        cols = lanes(j)
        gn, sh = gain(p1, i, cols), gain(p1, i + 1, cols)
        sums = [jnp.zeros((8, TILE), F32) for _ in range(4)]
        for s, g in chunks:
            rows = slice(s, s + CH)
            mean, inv = mi[2 * g : 2 * g + 1, cols], mi[2 * g + 1 : 2 * g + 2, cols]
            off = a[rows, cols] - mean
            zed = off * (inv * gn) + sh
            sig = sigmoid(zed)
            gz = gh[rows, cols] * masked(s) * (sig * (1.0 + zed * (1.0 - sig)))
            gh[rows, cols] = gz
            sums[2 * g] = sums[2 * g] + fold(gz * off)
            sums[2 * g + 1] = sums[2 * g + 1] + fold(gz)
        for k in range(4):
            total = jnp.sum(sums[k], axis=0, keepdims=True)
            inv = mi[2 * (k // 2) + 1 : 2 * (k // 2) + 2, cols]
            put(buf, j, k, total * inv if k % 2 == 0 else total)

    for j in range(mid // TILE):
        w = tile_rows(we, j).reshape(TILE, wide)
        gact[j, :, :] = dot_t(cot[...], w)

    class Cols:
        def __getitem__(self, key):
            rows, cols = key
            return gact[self.j, rows, :]

        def __setitem__(self, key, value):
            rows, cols = key
            gact[self.j, rows, :] = value

    ghs = Cols()
    for j in range(mid // TILE):
        ghs.j = j
        grad_act(ghs, a2, mi2, 2, bx2, j)
    exchanges[BX2][0]()
    q_we[1].stage2()
    pool_core.wait_recv()
    pb[mine] = (pf[mine] + pr[0].astype(F32)).astype(BF)
    exchanges[BX2][1]()
    merge_grads(bx2, tot2)

    def grad_norm_all(a, mi, tot, i, store):
        for j in range(mid // TILE):
            ghs.j = j
            cols = lanes(j)
            co = coefs(mi, tot, gain(p1, i, cols), cols)
            for s, g in chunks:
                store(s, cols, norm_back(ghs[s : s + CH, cols], a, co[g], s, cols))

    grad_norm_all(a2, mi2, tot2, 2, lambda s, cols, value: store_rows(dv, dc, s, cols, value))
    rim_d[0]()
    q_we[0].stage3()

    def grad_taps(dy):
        right = windows(dv, dc, 1, 1)
        for dx in range(3):
            total = dot_r(windows(hv, hc, dy, dx), right)
            gws[3 * dy + dx] = total.astype(BF).reshape(gws.shape[1:])

    def conv2_back(dy):
        left = jnp.concatenate([windows(dv, dc, 2 - dy, 2 - dx) for dx in range(3)], axis=1)
        for j in range(mid // TILE):
            w = jnp.concatenate(
                [tile_rows(ws.at[3 * dy + dx], j).reshape(TILE, mid) for dx in range(3)], axis=1
            )
            part_sum = dot_t(left, w)
            gact[j] = part_sum if dy == 1 else gact[j] + part_sum

    grad_taps(0)
    q_ws[0].start()
    conv2_back(1)
    grad_taps(1)
    q_ws[1].start()
    q_ws[0].stage2()
    q_we[1].stage3()
    q_we[0].stage4()
    rim_d[1]()
    conv2_back(0)
    q_ws[1].stage2()
    conv2_back(2)
    for j in range(mid // TILE):
        ghs.j = j
        grad_act(ghs, a1, mi1, 0, bx1, j)
    exchanges[BX1][0]()
    grad_taps(2)
    q_ws[2].start()
    q_we[1].stage4()
    q_ws[0].stage3()
    exchanges[BX1][1]()
    merge_grads(bx1, tot1)

    def store_ga1(s, cols, value):
        ga1[s : s + CH, cols] = value

    grad_norm_all(a1, mi1, tot1, 0, store_ga1)
    for t in range(wide // TILE):
        block = dot(xt[t * TILE : (t + 1) * TILE, :], ga1[...]).astype(BF)
        gwr[t // 2, t % 2] = block.reshape(gwr.shape[2:])
    for q in q_wr:
        q.start()
    q_ws[2].stage2()
    q_ws[1].stage3()
    q_wr[0].stage2()
    q_wr[1].stage2()
    q_ws[0].stage4()

    n_dev = n_dp * n_rows

    def three(v):
        hi = v.astype(BF)
        rest = v - hi.astype(F32)
        mid_part = rest.astype(BF)
        return hi, mid_part, (rest - mid_part.astype(F32)).astype(BF)

    def owner_blocks(rows, width):
        share = width // n_dev
        step = 512
        total = jnp.zeros((n_dp * 8, 128), F32)
        for t in range(width // step):
            place = lax.broadcasted_iota(jnp.int32, (step, 128), 1)
            lane = lax.broadcasted_iota(jnp.int32, (step, 128), 0) + t * step
            pick = jnp.where(lane % share == place, 1.0, 0.0).astype(BF)
            owner = (lax.broadcasted_iota(jnp.int32, (8, step), 1) + t * step) // share
            vec = rows[:, t * step : (t + 1) * step]
            stack = jnp.concatenate(
                [jnp.where(owner == d * n_rows + me.r, vec, 0.0) for d in range(n_dp)], axis=0
            )
            for part in three(stack):
                total = total + dot(part, pick)
        return total

    small_rows = [t_[0:1] + t_[2:3] if k == 0 else t_[1:2] + t_[3:4] for t_ in (tot1, tot2) for k in (0, 1)]
    wide_rows = [tot3[0:1] + tot3[2:3], tot3[1:2] + tot3[3:4]]
    narrow = jnp.concatenate(small_rows + [jnp.zeros((4, mid), F32)], axis=0)
    broad = jnp.concatenate([jnp.zeros((4, wide), F32)] + wide_rows + [jnp.zeros((2, wide), F32)], axis=0)
    sb[...] = (owner_blocks(narrow, mid) + owner_blocks(broad, wide)).reshape(sb.shape)

    def small_cp(d, recv):
        peer = (me.dp + n_dp - d) % n_dp if recv else (me.dp + d) % n_dp
        return remote(sb.at[peer], rb.at[d - 1], sm_s.at[d - 1], sm_r.at[d - 1], {"dp": peer, "rows": me.r})

    for d in range(1, n_dp):
        small_cp(d, False).start()
    q_ws[2].stage3()
    q_ws[1].stage4()

    def grad_in(j):
        cols, slot = lanes(j), j % 2
        previous = (j - 2, gv_h, gc_h) if j >= 2 else (wide // TILE - 2 + j, yv_h, yc_h)
        for cp in out_copies(previous[0], slot, previous[1], previous[2]):
            cp.wait()
        w = wr[j // 2, j % 2].reshape(TILE, mid)
        gpre[:, cols] = gpre[:, cols] + dot_t(ga1[...], w)
        for s, g in chunks:
            store_out(slot, s, gpre[s : s + CH, cols])
        for cp in out_copies(j, slot, gv_h, gc_h):
            cp.start()

    grad_in(0)
    grad_in(1)
    q_wr[0].stage3()
    grad_in(2)
    q_wr[1].stage3()
    pool_chip.start()
    q_ws[2].stage4()
    grad_in(3)
    grad_in(4)
    q_wr[0].stage4()
    q_wr[1].stage4()
    pool_chip.wait_send()
    pool_chip.wait_recv()
    pb[mine] = (pb[mine].astype(F32) + pr[1].astype(F32)).astype(BF)
    pool_back.start()
    for j in range(5, wide // TILE):
        grad_in(j)
    gwe_o[:, part:wide] = q_we[1].finish()
    gwe_o[:, 0:part] = q_we[0].finish()
    gws_o[0:3] = q_ws[0].finish()
    pool_core.wait_send()
    pool_back.wait_recv()
    pb[others] = pr[2]
    for out, at, maps, valid in ((poolv_o, 0, maps_v, valid_v), (poolc_o, maps_v, maps_c, valid_c)):
        out[...] = (pb[at : at + maps].astype(F32) * (1.0 / valid)).reshape(out.shape)
    total = sb[me.dp]
    for d in range(1, n_dp):
        small_cp(d, True).wait_recv()
        total = total + rb[d - 1]
    small_o[...] = total
    gws_o[3:6] = q_ws[1].finish()
    gws_o[6:9] = q_ws[2].finish()
    for i, q in enumerate(q_wr):
        gwr_o[i * few : (i + 1) * few] = q.finish()

    pool_back.wait_send()
    for j in (wide // TILE - 2, wide // TILE - 1):
        for cp in out_copies(j, j % 2, gv_h, gc_h):
            cp.wait()
    small_piece.drain()
    for p in pieces + [plane]:
        p.drain()
    for e in exchanges:
        e[2]()
    rim_h[2]()
    rim_d[2]()
    for q in q_we + q_ws + q_wr:
        q.drain()
    for d in range(1, n_dp):
        small_cp(d, False).wait_send()


def hand_over(*refs):
    n = (len(refs) - 8) // 3
    srcs, small, dsts = refs[:n], refs[n], refs[n + 1 : 2 * n + 1]
    cuts, bufs, sem = refs[2 * n + 1 : 2 * n + 7], refs[2 * n + 7 : -1], refs[-1]
    parts = 4
    ways = []
    for i, (src, buf, dst) in enumerate(zip(srcs, bufs, dsts)):
        count = parts if src.shape[0] % parts == 0 else 1
        per = src.shape[0] // count
        for k in range(count):
            rows = slice(k * per, (k + 1) * per)
            ways.append(
                (
                    pltpu.make_async_copy(src.at[rows], buf.at[rows], sem.at[0, i, k]),
                    pltpu.make_async_copy(buf.at[rows], dst.at[rows], sem.at[1, i, k]),
                )
            )
    for inward, _ in ways:
        inward.start()
    for i, ref in enumerate(cuts):
        ref[...] = small[i : i + 1, 0 : ref.shape[1]]
    for inward, outward in ways:
        inward.wait()
        outward.start()
    for _, outward in ways:
        outward.wait()


def block_step(n_dp, n_rows, xv, xc, mv, mc, wr, ws, we, g1, s1, g2, s2, g3, s3, cv, cc, cpv, cpc):
    img, views, rows_v, cols_v, wide = xv.shape
    crops, cols_c = xc.shape[1], xc.shape[3]
    mid = wr.shape[1]
    maps_v, maps_c = img * views, img * crops
    pix_v, pix_c = rows_v * cols_v * maps_v, cols_c * maps_c
    pix = pix_v + pix_c
    valid_v, valid_c = (rows_v * n_rows - 1) * cols_v, (n_rows - 1) * cols_c
    nz, nx = n_dp // 2, n_rows // 2

    def views_in(t):
        return t.transpose(0, 1, 3, 2, 4).reshape(maps_v, cols_v, rows_v, wide)

    def crops_in(t):
        return t.transpose(0, 2, 3, 1, 4).reshape(img, cols_c, crops, wide)

    grid4 = (nz, 2, nx, 2)
    vm = pl.BlockSpec(memory_space=pltpu.VMEM)
    hbm = pl.BlockSpec(memory_space=pl.ANY)
    s_wr, s_we = wr.shape[0], we.shape[0]
    V = pltpu.VMEM
    D = pltpu.SemaphoreType.DMA

    scratch = [
        V((s_wr, mid), F32), V((9, s_we, mid), F32), V((s_we, wide), F32),
        V(grid4 + (s_wr, mid), BF), V((9,) + grid4 + (s_we, mid), BF), V(grid4 + (s_we, wide), BF),
        V(grid4 + (8, 128), F32),
        V((pix, 128), F32), V((cols_v, maps_v, 2, wide), BF), V((img, cols_c, crops, wide), BF),
        V((img, views, wide), F32), V((img, crops, wide), F32),
        V((pix, wide), BF), V((wide, pix), BF), V((pix, wide), BF),
        V((pix, mid), F32), V((pix, mid), F32), V((pix, wide), F32), V((pix, wide), F32),
        V((2, maps_v, cols_v, 2, TILE), F32), V((2, maps_c, cols_c, TILE // 128, 128), F32), V((2, pix, TILE), F32),
        V((4, (cols_v + 2) * maps_v, mid), BF), V((3, (cols_c + 2) * maps_c, mid), BF),
        V((4, (cols_v + 2) * maps_v, mid), BF), V((3, (cols_c + 2) * maps_c, mid), BF),
        V((pix, mid), BF), V((mid, pix), BF), V((pix, mid), BF),
        V(grid4 + (s_wr, mid), BF), V((9,) + grid4 + (s_we, mid), BF), V(grid4 + (s_we, wide), BF),
        V((nz, 2, nx, s_we, wide), BF), V((9, nz, 2, nx, s_we, mid), BF), V((nz, 2, nx, s_wr, mid), BF),
        V((2, 2, nz, 2, s_we, wide // 4), BF), V((9, nz, 2, s_we, mid), BF), V((2, nz, 2, s_wr, mid // 2), BF),
        V((2, 2, nz, s_we, wide // 4), BF), V((9, nz, s_we, mid), BF), V((2, nz, s_wr, mid // 2), BF),
        V((2, nz - 1, s_we, wide // 2), BF), V((nz - 1, 9, s_we, mid), BF), V((nz - 1, s_wr, mid), BF),
        V((8, mid), F32), V((8, wide), F32),
        V((4, mid), F32), V((4, mid), F32), V((4, wide), F32),
        V((n_rows, 8, 128), F32),
        V((n_rows, 8, mid // 2), F32), V((n_rows, 8, mid // 2), F32), V((2, n_rows, 8, wide // 4), F32),
        V((n_rows, 8, mid // 2), F32), V((n_rows, 8, mid // 2), F32), V((2, n_rows, 8, wide // 4), F32),
        V((4, mid), F32), V((4, mid), F32), V((4, wide), F32),
        V((maps_v + maps_c, wide), F32), V((maps_v + maps_c, wide), BF), V((3, (maps_v + maps_c) // 2, wide), BF),
        V((n_dp, 8, 128), F32), V((n_dp - 1, 8, 128), F32),
        D((3, max(cols_v + 1, 5))), D((2, 2)), D((7, 5 * nz + 4)), D((7, 5 * nz + 4)), D((7, 6 + nz)), D((7, 6 + nz)),
        D((9, n_rows - 1)), D((9, n_rows - 1)), D((2, 4)), D((2, 4)), D((3,)), D((3,)), D((n_dp - 1,)), D((n_dp - 1,)),
    ]
    out_v = jax.ShapeDtypeStruct((maps_v, cols_v, 2, wide), F32)
    out_c = jax.ShapeDtypeStruct((maps_c, cols_c, wide // TILE, TILE // 128, 128), F32)
    outs = pl.pallas_call(
        functools.partial(kernel, n_dp, n_rows, (maps_v, cols_v, maps_c, cols_c, valid_v, valid_c)),
        out_shape=[
            out_v, out_c, out_v, out_c,
            jax.ShapeDtypeStruct(cpv.shape, F32), jax.ShapeDtypeStruct(cpc.shape, F32),
            jax.ShapeDtypeStruct((s_wr, mid), F32), jax.ShapeDtypeStruct((9, s_we, mid), F32),
            jax.ShapeDtypeStruct((s_we, wide), F32), jax.ShapeDtypeStruct((8, 128), F32),
        ],
        in_specs=[hbm] * 9 + [vm] * 8,
        out_specs=[hbm] * 4 + [vm] * 6,
        scratch_shapes=scratch,
        compiler_params=pltpu.CompilerParams(
            collective_id=0, has_side_effects=True, vmem_limit_bytes=63 << 20
        ),
    )(
        views_in(xv), crops_in(xc), views_in(cv), crops_in(cc), cpv, cpc,
        wr, ws.reshape(9, s_we, mid), we, mv.transpose(1, 2, 0), mc.transpose(1, 2, 0),
        g1.reshape(1, -1), s1.reshape(1, -1), g2.reshape(1, -1), s2.reshape(1, -1),
        g3.reshape(1, -1), s3.reshape(1, -1),
    )
    e = mid // (n_dp * n_rows)
    f = wide // (n_dp * n_rows)
    big, shapes = outs[:-1], [jax.ShapeDtypeStruct(o.shape, F32) for o in outs[:-1]]
    res = pl.pallas_call(
        hand_over,
        out_shape=shapes + [jax.ShapeDtypeStruct((1, w), F32) for w in (e, e, e, e, f, f)],
        in_specs=[hbm] * len(big) + [vm],
        out_specs=[hbm] * len(big) + [vm] * 6,
        scratch_shapes=[V(o.shape, F32) for o in big] + [D((2, len(big), 4))],
        compiler_params=pltpu.CompilerParams(vmem_limit_bytes=62 << 20),
    )(*outs)
    yv, yc, gv, gc, pool_v, pool_c, gwr, gws, gwe = res[:9]
    small = [r.reshape(-1) for r in res[9:]]

    def views_out(t):
        return t.reshape(img, views, cols_v, rows_v, wide).transpose(0, 1, 3, 2, 4)

    def crops_out(t):
        return t.reshape(img, crops, 1, cols_c, wide)

    return (
        views_out(yv), crops_out(yc),
        pool_v, pool_c,
        views_out(gv), crops_out(gc),
        gwr, gws.reshape(3, 3, s_we, mid), gwe,
        *small,
    )


def fits(xv, xc, we):
    return we.shape[0] % 16 == 0 and xv.shape[2] == 2 and xc.shape[2] == 1


def with_halo(block, sides, width):
    for axis, dim in sides:
        count = lax.axis_size(axis)
        forward = [(i, i + 1) for i in range(count - 1)]
        backward = [(target, source) for source, target in forward]
        low = lax.ppermute(
            lax.slice_in_dim(block, block.shape[dim] - width, None, axis=dim), axis, forward
        )
        high = lax.ppermute(lax.slice_in_dim(block, 0, width, axis=dim), axis, backward)
        block = jnp.concatenate([low, block, high], axis=dim)
    return block


def from_behind(array, axis, by):
    peers = lax.axis_size(axis)
    pairs = [(i, i + by) for i in range(peers) if 0 <= i + by < peers]
    return lax.ppermute(array, axis, pairs)


def silu_slope(value):
    sig = jax.nn.sigmoid(value)
    return sig * (1.0 + value * (1.0 - sig))


def pixel_mask(mask_rows, col_count):
    expanded = jnp.broadcast_to(
        mask_rows.astype(jnp.float32)[..., None], mask_rows.shape + (col_count,)
    )
    return expanded.reshape(-1, 1)


def by_group(in_views, view_value, crop_value):
    return jnp.where(in_views, view_value, crop_value)


def norm_forward(acts, mask_col, view_pixels, in_views, counts, gain_vec, shift_vec):
    masked = acts * mask_col
    totals = lax.psum(
        (jnp.sum(masked[:view_pixels], axis=0), jnp.sum(masked[view_pixels:], axis=0)), "rows"
    )
    centered = acts - by_group(in_views, totals[0] / counts[0], totals[1] / counts[1])
    squares = jnp.square(centered * mask_col)
    spread = lax.psum(
        (jnp.sum(squares[:view_pixels], axis=0), jnp.sum(squares[view_pixels:], axis=0)), "rows"
    )
    inv_rows = by_group(
        in_views, lax.rsqrt(spread[0] / counts[0] + eps), lax.rsqrt(spread[1] / counts[1] + eps)
    )
    normal = centered * inv_rows
    return (normal * gain_vec + shift_vec, normal, inv_rows)


def norm_backward(grad_z, normal, inv_rows, mask_col, view_pixels, in_views, counts, gain_vec):
    product = grad_z * normal
    partials = (
        jnp.sum(product[:view_pixels], axis=0),
        jnp.sum(grad_z[:view_pixels], axis=0),
        jnp.sum(product[view_pixels:], axis=0),
        jnp.sum(grad_z[view_pixels:], axis=0),
    )
    totals = (
        lax.psum(partials[0].astype(jnp.bfloat16), "rows").astype(jnp.float32),
        lax.psum(partials[1].astype(jnp.bfloat16), "rows").astype(jnp.float32),
        lax.psum(partials[2].astype(jnp.bfloat16), "rows").astype(jnp.float32),
        lax.psum(partials[3].astype(jnp.bfloat16), "rows").astype(jnp.float32),
    )
    scale_mean = by_group(in_views, totals[0] / counts[0], totals[2] / counts[1])
    shift_mean = by_group(in_views, totals[1] / counts[0], totals[3] / counts[1])
    grad_acts = gain_vec * inv_rows * (grad_z - shift_mean - normal * scale_mean) * mask_col
    return (grad_acts.astype(jnp.bfloat16), partials[0] + partials[2], partials[1] + partials[3])


def with_rims(feature_map):
    extended = with_halo(feature_map, (("rows", 1),), 1)
    return jnp.pad(extended, ((0, 0), (0, 0), (1, 1), (0, 0)))


def gather_taps(extended, row_count, col_count):
    windows = []
    for row_step in range(3):
        for col_step in range(3):
            windows.append(
                extended[:, row_step : row_step + row_count, col_step : col_step + col_count, :]
            )
    return jnp.concatenate(windows, axis=-1).reshape(-1, 9 * extended.shape[-1])


def spread_taps(grad_patches, map_count, row_count, col_count, mid_width):
    pieces = grad_patches.reshape(map_count, row_count, col_count, 9, mid_width)
    padded = jnp.zeros((map_count, row_count + 2, col_count + 2, mid_width), jnp.float32)
    tap_index = 0
    for row_step in range(3):
        for col_step in range(3):
            padded = padded.at[
                :, row_step : row_step + row_count, col_step : col_step + col_count, :
            ].add(pieces[:, :, :, tap_index, :])
            tap_index += 1
    inside = padded[:, 1 : row_count + 1, 1 : col_count + 1, :]
    from_below = from_behind(
        padded[:, 0, 1 : col_count + 1, :].astype(jnp.bfloat16), "rows", -1
    ).astype(jnp.float32)
    from_above = from_behind(
        padded[:, row_count + 1, 1 : col_count + 1, :].astype(jnp.bfloat16), "rows", 1
    ).astype(jnp.float32)
    inside = inside.at[:, row_count - 1].add(from_below)
    inside = inside.at[:, 0].add(from_above)
    return inside.reshape(-1, mid_width)


def contract_rows(left, right):
    return lax.dot_general(
        left, right, (((0,), (0,)), ((), ())), preferred_element_type=jnp.float32
    )


def contract_cols(left, right):
    return lax.dot_general(
        left, right, (((1,), (1,)), ((), ())), preferred_element_type=jnp.float32
    )


def shards(
    x_views,
    x_crops,
    mask_views,
    mask_crops,
    w_reduce,
    w_spatial,
    w_expand,
    gain_reduce,
    shift_reduce,
    gain_spatial,
    shift_spatial,
    gain_expand,
    shift_expand,
    cot_views,
    cot_crops,
    cot_pool_views,
    cot_pool_crops,
):
    low_type = jnp.bfloat16
    gathered = (
        lax.all_gather(w_reduce.astype(low_type), ("dp", "rows"), axis=0, tiled=True),
        lax.all_gather(w_spatial.astype(low_type), ("dp", "rows"), axis=2, tiled=True),
        lax.all_gather(w_expand.astype(low_type), ("dp", "rows"), axis=0, tiled=True),
        lax.all_gather(gain_reduce.astype(low_type), ("dp", "rows"), axis=0, tiled=True),
        lax.all_gather(shift_reduce.astype(low_type), ("dp", "rows"), axis=0, tiled=True),
        lax.all_gather(gain_spatial.astype(low_type), ("dp", "rows"), axis=0, tiled=True),
        lax.all_gather(shift_spatial.astype(low_type), ("dp", "rows"), axis=0, tiled=True),
        lax.all_gather(gain_expand.astype(low_type), ("dp", "rows"), axis=0, tiled=True),
        lax.all_gather(shift_expand.astype(low_type), ("dp", "rows"), axis=0, tiled=True),
    )
    weight_one, weight_two, weight_three = (gathered[0], gathered[1], gathered[2])
    gain_one, shift_one, gain_two, shift_two, gain_three, shift_three = [
        entry.astype(jnp.float32) for entry in gathered[3:]
    ]
    in_width = weight_one.shape[0]
    mid_width = weight_one.shape[1]
    view_maps = x_views.shape[0] * x_views.shape[1]
    view_rows, view_cols = (x_views.shape[2], x_views.shape[3])
    crop_maps = x_crops.shape[0] * x_crops.shape[1]
    crop_rows, crop_cols = (x_crops.shape[2], x_crops.shape[3])
    view_pixels = view_maps * view_rows * view_cols
    total_pixels = view_pixels + crop_maps * crop_rows * crop_cols
    row_parts = lax.axis_size("rows")
    view_valid = (view_rows * row_parts - 1) * view_cols
    crop_valid = (crop_rows * row_parts - 1) * crop_cols
    counts = (float(view_maps * view_valid), float(crop_maps * crop_valid))
    mask_col = jnp.concatenate(
        [pixel_mask(mask_views, view_cols), pixel_mask(mask_crops, crop_cols)], axis=0
    )
    in_views = lax.broadcasted_iota(jnp.int32, (total_pixels, 1), 0) < view_pixels
    inputs = jnp.concatenate([x_views.reshape(-1, in_width), x_crops.reshape(-1, in_width)], axis=0)
    acts_one = jnp.dot(inputs, weight_one, preferred_element_type=jnp.float32)
    z_one, normal_one, inv_one = norm_forward(
        acts_one, mask_col, view_pixels, in_views, counts, gain_one, shift_one
    )
    hidden_one = (jax.nn.silu(z_one) * mask_col).astype(low_type)
    view_hidden = hidden_one[:view_pixels].reshape(view_maps, view_rows, view_cols, mid_width)
    crop_hidden = hidden_one[view_pixels:].reshape(crop_maps, crop_rows, crop_cols, mid_width)
    patches = jnp.concatenate(
        [
            gather_taps(with_rims(view_hidden), view_rows, view_cols),
            gather_taps(with_rims(crop_hidden), crop_rows, crop_cols),
        ],
        axis=0,
    )
    spatial_flat = weight_two.reshape(9 * mid_width, mid_width)
    acts_two = jnp.dot(patches, spatial_flat, preferred_element_type=jnp.float32)
    z_two, normal_two, inv_two = norm_forward(
        acts_two, mask_col, view_pixels, in_views, counts, gain_two, shift_two
    )
    hidden_two = (jax.nn.silu(z_two) * mask_col).astype(low_type)
    acts_three = jnp.dot(hidden_two, weight_three, preferred_element_type=jnp.float32)
    z_three, normal_three, inv_three = norm_forward(
        acts_three, mask_col, view_pixels, in_views, counts, gain_three, shift_three
    )
    pre_act = inputs.astype(jnp.float32) + z_three
    result = jax.nn.silu(pre_act) * mask_col
    pooled = (
        lax.psum(
            jnp.sum(
                result[:view_pixels].reshape(view_maps, view_rows * view_cols, in_width), axis=1
            ).astype(jnp.bfloat16),
            "rows",
        ).astype(jnp.float32),
        lax.psum(
            jnp.sum(
                result[view_pixels:].reshape(crop_maps, crop_rows * crop_cols, in_width), axis=1
            ).astype(jnp.bfloat16),
            "rows",
        ).astype(jnp.float32),
    )
    pool_views = (pooled[0] / view_valid).reshape(cot_pool_views.shape)
    pool_crops = (pooled[1] / crop_valid).reshape(cot_pool_crops.shape)
    view_grad = (
        cot_views.astype(jnp.float32).reshape(view_maps, view_rows * view_cols, in_width)
        + cot_pool_views.reshape(view_maps, 1, in_width) / view_valid
    )
    crop_grad = (
        cot_crops.astype(jnp.float32).reshape(crop_maps, crop_rows * crop_cols, in_width)
        + cot_pool_crops.reshape(crop_maps, 1, in_width) / crop_valid
    )
    grad_out = jnp.concatenate(
        [view_grad.reshape(-1, in_width), crop_grad.reshape(-1, in_width)], axis=0
    )
    grad_pre = grad_out * mask_col * silu_slope(pre_act)
    grad_three, dgain_three, dshift_three = norm_backward(
        grad_pre, normal_three, inv_three, mask_col, view_pixels, in_views, counts, gain_three
    )
    grad_expand = contract_rows(hidden_two, grad_three)
    grad_hidden_two = contract_cols(grad_three, weight_three)
    grad_z_two = grad_hidden_two * mask_col * silu_slope(z_two)
    grad_two, dgain_two, dshift_two = norm_backward(
        grad_z_two, normal_two, inv_two, mask_col, view_pixels, in_views, counts, gain_two
    )
    grad_spatial = contract_rows(patches, grad_two).reshape(3, 3, mid_width, mid_width)
    grad_patches = contract_cols(grad_two, spatial_flat)
    grad_hidden_one = jnp.concatenate(
        [
            spread_taps(grad_patches[:view_pixels], view_maps, view_rows, view_cols, mid_width),
            spread_taps(grad_patches[view_pixels:], crop_maps, crop_rows, crop_cols, mid_width),
        ],
        axis=0,
    )
    grad_z_one = grad_hidden_one * mask_col * silu_slope(z_one)
    grad_one, dgain_one, dshift_one = norm_backward(
        grad_z_one, normal_one, inv_one, mask_col, view_pixels, in_views, counts, gain_one
    )
    grad_reduce = contract_rows(inputs, grad_one)
    grad_inputs = contract_cols(grad_one, weight_one) + grad_pre
    summed = (
        lax.psum_scatter(grad_reduce, ("dp", "rows"), scatter_dimension=0, tiled=True),
        lax.psum_scatter(grad_spatial, ("dp", "rows"), scatter_dimension=2, tiled=True),
        lax.psum_scatter(grad_expand, ("dp", "rows"), scatter_dimension=0, tiled=True),
        lax.psum_scatter(dgain_one, ("dp", "rows"), scatter_dimension=0, tiled=True),
        lax.psum_scatter(dshift_one, ("dp", "rows"), scatter_dimension=0, tiled=True),
        lax.psum_scatter(dgain_two, ("dp", "rows"), scatter_dimension=0, tiled=True),
        lax.psum_scatter(dshift_two, ("dp", "rows"), scatter_dimension=0, tiled=True),
        lax.psum_scatter(dgain_three, ("dp", "rows"), scatter_dimension=0, tiled=True),
        lax.psum_scatter(dshift_three, ("dp", "rows"), scatter_dimension=0, tiled=True),
    )
    out_views = result[:view_pixels].reshape(x_views.shape)
    out_crops = result[view_pixels:].reshape(x_crops.shape)
    grad_views = grad_inputs[:view_pixels].reshape(x_views.shape)
    grad_crops = grad_inputs[view_pixels:].reshape(x_crops.shape)
    return (
        out_views,
        out_crops,
        pool_views,
        pool_crops,
        grad_views,
        grad_crops,
        summed[0],
        summed[1],
        summed[2],
        summed[3],
        summed[4],
        summed[5],
        summed[6],
        summed[7],
        summed[8],
    )


def solution(mesh):
    in_specs = (
        P("dp", None, "rows", None, None),
        P("dp", None, "rows", None, None),
        P("dp", None, "rows"),
        P("dp", None, "rows"),
        P(("dp", "rows"), None),
        P(None, None, ("dp", "rows"), None),
        P(("dp", "rows"), None),
        P(("dp", "rows")),
        P(("dp", "rows")),
        P(("dp", "rows")),
        P(("dp", "rows")),
        P(("dp", "rows")),
        P(("dp", "rows")),
        P("dp", None, "rows", None, None),
        P("dp", None, "rows", None, None),
        P("dp", None, None),
        P("dp", None, None),
    )
    out_specs = (
        P("dp", None, "rows", None, None),
        P("dp", None, "rows", None, None),
        P("dp", None, None),
        P("dp", None, None),
        P("dp", None, "rows", None, None),
        P("dp", None, "rows", None, None),
        P(("dp", "rows"), None),
        P(None, None, ("dp", "rows"), None),
        P(("dp", "rows"), None),
        P(("dp", "rows")),
        P(("dp", "rows")),
        P(("dp", "rows")),
        P(("dp", "rows")),
        P(("dp", "rows")),
        P(("dp", "rows")),
    )
    def step(*args):
        if fits(args[0], args[1], args[6]):
            return block_step(mesh.shape["dp"], mesh.shape["rows"], *args)
        return shards(*args)

    return jax.shard_map(step, mesh=mesh, in_specs=in_specs, out_specs=out_specs, check_vma=False)
```

```python
import functools

import jax
import jax.numpy as jnp
from jax import lax
from jax.experimental import pallas as pl
from jax.experimental.pallas import tpu as pltpu
from jax.sharding import PartitionSpec as P

MESH = pl.DeviceIdType.MESH
ALL = slice(None)
BF = jnp.bfloat16
F32 = jnp.float32
eps = 1e-05
TILE = 256


def lanes(j, width=TILE):
    if isinstance(j, int):
        return slice(j * width, (j + 1) * width)
    return pl.ds(pl.multiple_of(j * width, width), width)


def half(h, width, at=0, whole=None):
    if h is None:
        return ALL if whole is None else slice(at, at + whole)
    return slice(at + h * (width // 2), at + (h + 1) * (width // 2))


def dot(a, b):
    return lax.dot_general(a, b, (((1,), (0,)), ((), ())), preferred_element_type=F32)


def dot_t(a, b):
    return lax.dot_general(a, b, (((1,), (1,)), ((), ())), preferred_element_type=F32)


def dot_r(a, b):
    return lax.dot_general(a, b, (((0,), (0,)), ((), ())), preferred_element_type=F32)


def sigmoid(v):
    return 0.5 * jnp.tanh(0.5 * v) + 0.5


def uneven(h, width):
    return ALL if h is None else slice(h * (width // 4), width if h else width // 4)


class Place:
    def __init__(self, n_dp, n_rows):
        self.ny, self.nc = 2, 2
        self.nz, self.nx = n_dp // 2, n_rows // 2
        self.n_dp, self.n_rows = n_dp, n_rows
        self.dp, self.r = lax.axis_index("dp"), lax.axis_index("rows")
        self.z, self.y = self.dp // 2, self.dp % 2
        self.x, self.c = self.r // 2, self.r % 2

    def dev(self, z, y, x, c):
        return {"dp": z * self.ny + y, "rows": x * self.nc + c}


def remote(src, dst, ssem, rsem, to):
    return pltpu.make_async_remote_copy(
        src_ref=src, dst_ref=dst, send_sem=ssem, recv_sem=rsem, device_id=to, device_id_type=MESH
    )


class Piece:
    def __init__(self, me, view, ssem, rsem):
        self.me, self.view, self.s, self.r, self.sent = me, view, ssem, rsem, []
        self.px = me.dev(me.z, me.y, 1 - me.x, me.c)
        self.py = me.dev(me.z, 1 - me.y, me.x, me.c)
        self.pc = me.dev(me.z, me.y, me.x, 1 - me.c)

    def pz(self, k):
        return self.me.dev((self.me.z + k) % self.me.nz, self.me.y, self.me.x, self.me.c)

    def send(self, k, src, dst, to):
        cp = remote(src, dst, self.s.at[k], self.r.at[k], to)
        cp.start()
        self.sent.append(cp)

    def got(self, k, dst):
        remote(dst, dst, self.s.at[k], self.r.at[k], self.pc).wait_recv()

    def drain(self):
        for cp in self.sent:
            cp.wait_send()


class Gather(Piece):
    def __init__(self, me, view, ssem, rsem, halves=(0, 1)):
        super().__init__(me, view, ssem, rsem)
        self.halves, n = halves, me.nz
        self.X, self.Y, self.D, self.C = n - 1, 2 * n - 1, (3 * n - 1, 4 * n - 1), 5 * n - 1

    def share(self, k, z, y, x, h, to):
        ref = self.view(z, y, x, self.me.c, h)
        self.send(k, ref, ref, to)

    def wait(self, k, z, y, x, h, c=None):
        self.got(k, self.view(z, y, x, self.me.c if c is None else c, h))

    def source(self, k):
        return (self.me.z + self.me.nz - k) % self.me.nz

    def start_z(self):
        me = self.me
        for k in range(1, me.nz):
            self.share(k - 1, me.z, me.y, me.x, None, self.pz(k))

    def start_xy(self):
        me = self.me
        self.share(self.X, me.z, me.y, me.x, None, self.px)
        self.share(self.Y, me.z, me.y, me.x, None, self.py)

    def got_z(self, k):
        me, z = self.me, self.source(k)
        self.wait(k - 1, z, me.y, me.x, None)
        self.share(self.X + k, z, me.y, me.x, None, self.px)
        self.share(self.Y + k, z, me.y, me.x, None, self.py)
        if k == me.nz - 1:
            self.share(self.C, ALL, me.y, me.x, None, self.pc)

    def diagonal(self):
        me = self.me
        for k in range(me.nz):
            z = self.source(k)
            self.wait(self.Y + k, z, 1 - me.y, me.x, None)
            self.share(self.D[0] + k, z, 1 - me.y, me.x, 0, self.px)
            self.wait(self.X + k, z, me.y, 1 - me.x, None)
            if 1 in self.halves:
                self.share(self.D[1] + k, z, me.y, 1 - me.x, 1, self.py)
        self.share(self.C + 1, ALL, 1 - me.y, me.x, None, self.pc)
        self.share(self.C + 2, ALL, me.y, 1 - me.x, None, self.pc)

    def last(self):
        me = self.me
        for h in self.halves:
            for k in range(me.nz):
                self.wait(self.D[h] + k, self.source(k), 1 - me.y, 1 - me.x, h)
            self.share(self.C + 3 + h, ALL, 1 - me.y, 1 - me.x, h, self.pc)

    def finish(self):
        me, o = self.me, 1 - self.me.c
        self.wait(self.C, ALL, me.y, me.x, None, o)
        self.wait(self.C + 1, ALL, 1 - me.y, me.x, None, o)
        self.wait(self.C + 2, ALL, me.y, 1 - me.x, None, o)
        for h in self.halves:
            self.wait(self.C + 3 + h, ALL, 1 - me.y, 1 - me.x, h, o)


class GatherPlane(Gather):
    def start(self):
        me = self.me
        self.share(0, me.z, me.y, me.x, None, self.px)
        self.share(1, me.z, me.y, me.x, None, self.py)

    def diagonal(self):
        me = self.me
        self.wait(1, me.z, 1 - me.y, me.x, None)
        self.share(2, me.z, 1 - me.y, me.x, 0, self.px)
        self.wait(0, me.z, me.y, 1 - me.x, None)
        self.share(3, me.z, me.y, 1 - me.x, 1, self.py)

    def plane(self):
        me = self.me
        for h in (0, 1):
            self.wait(2 + h, me.z, 1 - me.y, 1 - me.x, h)
        for k in range(1, me.nz):
            self.share(3 + k, me.z, ALL, ALL, None, self.pz(k))
        self.share(4 + me.nz, me.z, ALL, ALL, None, self.pc)

    def last(self):
        for k in range(1, self.me.nz):
            self.wait(3 + k, self.source(k), ALL, ALL, None)
            self.share(4 + self.me.nz + k, self.source(k), ALL, ALL, None, self.pc)

    def finish(self):
        for k in range(self.me.nz):
            self.wait(4 + self.me.nz + k, self.source(k), ALL, ALL, None, 1 - self.me.c)


class Reduce:
    def __init__(self, me, view, from_core, from_third, from_second, from_z, ssem, rsem):
        self.me, self.view, self.s, self.r = me, view, ssem, rsem
        self.fc, self.f3, self.f2, self.fz = from_core, from_third, from_second, from_z

    def core(self):
        me = self.me
        return remote(
            self.view(ALL, ALL, ALL, 1 - me.c, None),
            self.fc(ALL, ALL, ALL, None),
            self.s.at[0],
            self.r.at[0],
            me.dev(me.z, me.y, me.x, 1 - me.c),
        )

    def third(self, h):
        me = self.me
        place = (ALL, ALL, 1 - me.x) if h == 0 else (ALL, 1 - me.y, ALL)
        to = (me.z, me.y, 1 - me.x, me.c) if h == 0 else (me.z, 1 - me.y, me.x, me.c)
        return remote(
            self.view(*place, me.c, h), self.f3(h), self.s.at[1 + h], self.r.at[1 + h], me.dev(*to)
        )

    def second(self, h):
        me = self.me
        place = (ALL, 1 - me.y, me.x) if h == 0 else (ALL, me.y, 1 - me.x)
        to = (me.z, 1 - me.y, me.x, me.c) if h == 0 else (me.z, me.y, 1 - me.x, me.c)
        return remote(
            self.view(*place, me.c, h), self.f2(h), self.s.at[3 + h], self.r.at[3 + h], me.dev(*to)
        )

    def along_z(self, dz):
        me = self.me
        z = (me.z + dz) % me.nz
        return remote(
            self.view(z, me.y, me.x, me.c, None),
            self.fz(dz - 1),
            self.s.at[4 + dz],
            self.r.at[4 + dz],
            me.dev(z, me.y, me.x, me.c),
        )

    def start(self):
        self.core().start()

    def stage2(self):
        me = self.me
        self.core().wait_recv()
        for h in (0, 1):
            first = (ALL, ALL, 1 - me.x) if h == 0 else (ALL, 1 - me.y, ALL)
            ref = self.view(*first, me.c, h)
            ref[...] = ref[...] + self.fc(*first, h)[...]
            self.third(h).start()
        for h in (0, 1):
            rest = (ALL, ALL, me.x) if h == 0 else (ALL, me.y, ALL)
            ref = self.view(*rest, me.c, h)
            ref[...] = ref[...] + self.fc(*rest, h)[...]

    def stage3(self):
        me = self.me
        for h in (0, 1):
            self.third(h).wait_recv()
            kept = (ALL, ALL, me.x) if h == 0 else (ALL, me.y, ALL)
            ref = self.view(*kept, me.c, h)
            ref[...] = ref[...] + self.f3(h)[...]
            self.second(h).start()

    def stage4(self):
        me = self.me
        for h in (0, 1):
            self.second(h).wait_recv()
            ref = self.view(ALL, me.y, me.x, me.c, h)
            ref[...] = ref[...] + self.f2(h)[...]
        for dz in range(1, me.nz):
            self.along_z(dz).start()

    def finish(self):
        me = self.me
        total = self.view(me.z, me.y, me.x, me.c, None)[...].astype(F32)
        for dz in range(1, me.nz):
            self.along_z(dz).wait_recv()
            total = total + self.fz(dz - 1)[...].astype(F32)
        return total

    def drain(self):
        self.core().wait_send()
        for h in (0, 1):
            self.third(h).wait_send()
            self.second(h).wait_send()
        for dz in range(1, self.me.nz):
            self.along_z(dz).wait_send()


def kernel(n_dp, n_rows, sizes, *refs):
    (
        xv_h, xc_h, cv_h, cc_h, cpv_h, cpc_h, wr_h, ws_h, we_h, mv_in, mc_in,
        g1_in, s1_in, g2_in, s2_in, g3_in, s3_in,
        yv_h, yc_h, gv_h, gc_h, poolv_h, poolc_h, gwe_h, gwr_o, gws_o, small_o,
        poolv_o, poolc_o, gwe_o, res_sem, wr_in, ws_in, we_in, wr, ws, we, par, mask, raw_v, raw_c, cpv, cpc, x, xt, cot, a1, a2, a3, gpre, ysv, ysc, gact,
        hv, hc, dv, dc, h2, h2t, ga1, gwr, gws, gwe,
        fc_we, fc_ws, fc_wr, f3_we, f3_ws, f3_wr, f2_we, f2_ws, f2_wr, fz_we, fz_ws, fz_wr,
        p1, p3, mi1, mi2, mi3, cnt, ex1, ex2, ex3, bx1, bx2, bx3, tot1, tot2, tot3,
        pf, pb, pr, sb, rb,
        in_sem, out_sem, ag_s, ag_r, rs_s, rs_r, ex_s, ex_r, halo_s, halo_r, pool_s, pool_r, sm_s, sm_r,
    ) = refs
    (maps_v, cols_v, maps_c, cols_c, valid_v, valid_c) = sizes
    me = Place(n_dp, n_rows)
    mid, wide = a1.shape[1], a3.shape[1]
    pix_v = 2 * cols_v * maps_v
    pix = a1.shape[0]
    row_v, row_c = cols_v * maps_v, cols_c * maps_c
    count = (float(maps_v * valid_v), float(maps_c * valid_c))
    CH = 32
    chunks = [(s, 0 if s < pix_v else 1) for s in range(0, pix, CH)]

    barrier = pltpu.get_barrier_semaphore()
    peers = [{"dp": me.dp, "rows": (me.r + d) % n_rows} for d in range(1, n_rows)]
    peers += [{"dp": (me.dp + d) % n_dp, "rows": me.r} for d in range(1, n_dp)]
    for peer in peers:
        pl.semaphore_signal(barrier, inc=1, device_id=peer, device_id_type=MESH)

    def fetch(k, views, crops):
        return [
            pltpu.make_async_copy(views.at[:, col], raw_v.at[col], in_sem.at[k, col]) for col in range(cols_v)
        ] + [pltpu.make_async_copy(crops, raw_c, in_sem.at[k, cols_v])]

    def arrange(out):
        def body(j, carry):
            cols = lanes(j)
            for col in range(cols_v):
                for r in (0, 1):
                    at = r * row_v + col * maps_v
                    out[at : at + maps_v, cols] = raw_v[col, :, r, cols]
            for col in range(cols_c):
                at = pix_v + col * maps_c
                out[at : at + maps_c, cols] = raw_c[:, col, :, cols].reshape(maps_c, TILE)
            return carry

        lax.fori_loop(0, wide // TILE, body, 0)

    x_copies, cot_copies = fetch(0, xv_h, xc_h), fetch(1, cv_h, cc_h)
    pool_copies = [
        pltpu.make_async_copy(cpv_h, cpv, in_sem.at[2, 0]),
        pltpu.make_async_copy(cpc_h, cpc, in_sem.at[2, 1]),
    ]
    weight_copies = [
        pltpu.make_async_copy(src, dst, in_sem.at[2, 2 + i])
        for i, (src, dst) in enumerate(((wr_h, wr_in), (ws_h, ws_in), (we_h, we_in)))
    ]
    for cp in weight_copies + x_copies + pool_copies:
        cp.start()

    here = (me.z, me.y, me.x, me.c)
    own = par.at[here]
    own[...] = jnp.zeros(own.shape, F32)
    for i, ref in enumerate((g1_in, s1_in, g2_in, s2_in, g3_in, s3_in)):
        own[i : i + 1, 0 : ref.shape[1]] = ref[...].astype(BF).astype(F32)

    def mask_column(row_of, per, maps):
        lane = lax.broadcasted_iota(jnp.int32, (maps, 16), 1)
        place = lax.broadcasted_iota(jnp.int32, (maps, 16), 0)
        total = jnp.zeros((maps, 16), F32)
        for k in range(per):
            hit = jnp.logical_and(place % per == k, lane == place // per)
            total = total + jnp.where(hit, row_of(k).astype(F32), 0.0)
        return jnp.broadcast_to(jnp.sum(total, axis=1, keepdims=True), (maps, 128))

    for r in (0, 1):
        column = mask_column(lambda k: mv_in[k, r : r + 1, :], mv_in.shape[0], maps_v)
        for col in range(cols_v):
            at = r * row_v + col * maps_v
            mask[at : at + maps_v] = column
    column = mask_column(lambda k: mc_in[k], mc_in.shape[0], maps_c)
    for col in range(cols_c):
        at = pix_v + col * maps_c
        mask[at : at + maps_c] = column

    cnt_own = cnt.at[me.r]
    cnt_own[0:1] = jnp.sum(mask[0:pix_v], axis=0, keepdims=True)
    cnt_own[1:2] = jnp.sum(mask[pix_v:pix], axis=0, keepdims=True)
    cnt_own[2:8] = jnp.zeros((6, 128), F32)

    for cp in weight_copies:
        cp.wait()
    wr[here] = wr_in[...].astype(BF)
    ws[(ALL,) + here] = ws_in[...].astype(BF)
    we[here] = we_in[...].astype(BF)

    pl.semaphore_wait(barrier, len(peers))

    def piece(k, view, halves=(0, 1), form=Gather):
        return form(me, view, ag_s.at[k], ag_r.at[k], *(() if form is GatherPlane else (halves,)))

    part = wide // 2
    small_piece = piece(0, lambda z, y, x, c, h: par.at[z, y, x, c], (0,))
    pieces = [piece(1, lambda z, y, x, c, h: wr.at[z, y, x, c, :, half(h, mid)])]
    for i in range(3):
        pieces.append(
            piece(2 + i, lambda z, y, x, c, h, i=i: ws.at[3 * i : 3 * i + 3, z, y, x, c, :, uneven(h, mid)])
        )
    pieces.append(piece(5, lambda z, y, x, c, h: we.at[z, y, x, c, :, half(h, part, 0, part)]))
    plane = piece(6, lambda z, y, x, c, h: we.at[z, y, x, c, :, half(h, part, part, part)], form=GatherPlane)

    def exchange(k, buf):
        def cp(d, recv):
            peer = (me.r + n_rows - d) % n_rows if recv else (me.r + d) % n_rows
            ref = buf.at[peer if recv else me.r]
            return remote(ref, ref, ex_s.at[k, d - 1], ex_r.at[k, d - 1], {"dp": me.dp, "rows": peer})

        def send():
            for d in range(1, n_rows):
                cp(d, False).start()

        def wait():
            for d in range(1, n_rows):
                cp(d, True).wait_recv()

        def drain():
            for d in range(1, n_rows):
                cp(d, False).wait_send()

        return send, wait, drain

    exchanges = [
        exchange(k, b)
        for k, b in enumerate(
            (cnt, ex1, ex2, ex3.at[0], ex3.at[1], bx1, bx2, bx3.at[0], bx3.at[1])
        )
    ]
    CNT, EX1, EX2, EX3, BX1, BX2, BX3 = 0, 1, 2, 3, 5, 6, 7

    def rim(k, v, c):
        def cps(up):
            peer = {"dp": me.dp, "rows": (me.r + n_rows - 1) % n_rows if up else (me.r + 1) % n_rows}
            base = 0 if up else 2
            vs, vd = (1, 3) if up else (2, 0)
            csrc, cd = (1, 2) if up else (1, 0)
            return [
                remote(
                    v.at[vs, maps_v : maps_v + row_v],
                    v.at[vd, maps_v : maps_v + row_v],
                    halo_s.at[k, base],
                    halo_r.at[k, base],
                    peer,
                ),
                remote(
                    c.at[csrc, maps_c : maps_c + row_c],
                    c.at[cd, maps_c : maps_c + row_c],
                    halo_s.at[k, base + 1],
                    halo_r.at[k, base + 1],
                    peer,
                ),
            ]

        def each(up, fn):
            def body():
                for cp in cps(up):
                    fn(cp)

            return body

        first, last = me.r == 0, me.r == n_rows - 1

        def send():
            pl.when(jnp.logical_not(first))(each(True, lambda cp: cp.start()))
            pl.when(jnp.logical_not(last))(each(False, lambda cp: cp.start()))

        def wait():
            pl.when(jnp.logical_not(last))(each(True, lambda cp: cp.wait_recv()))
            pl.when(jnp.logical_not(first))(each(False, lambda cp: cp.wait_recv()))

        def drain():
            pl.when(jnp.logical_not(first))(each(True, lambda cp: cp.wait_send()))
            pl.when(jnp.logical_not(last))(each(False, lambda cp: cp.wait_send()))

        return send, wait, drain

    rim_h, rim_d = rim(0, hv, hc), rim(1, dv, dc)

    def clear_rims(v, c):
        zv, zc = jnp.zeros((maps_v, mid), BF), jnp.zeros((maps_c, mid), BF)
        for r in range(4):
            v[r, 0:maps_v] = zv
            v[r, maps_v + row_v : 2 * maps_v + row_v] = zv
        for r in range(3):
            c[r, 0:maps_c] = zc
            c[r, maps_c + row_c : 2 * maps_c + row_c] = zc

        @pl.when(me.r == 0)
        def _():
            v[0, maps_v : maps_v + row_v] = jnp.zeros((row_v, mid), BF)
            c[0, maps_c : maps_c + row_c] = jnp.zeros((row_c, mid), BF)

        @pl.when(me.r == n_rows - 1)
        def _():
            v[3, maps_v : maps_v + row_v] = jnp.zeros((row_v, mid), BF)
            c[2, maps_c : maps_c + row_c] = jnp.zeros((row_c, mid), BF)

    def tile_rows(ref, j):
        per = me.nz * TILE // mid
        return ref[j * per : (j + 1) * per]

    def fold(v):
        return jnp.sum(v.reshape(v.shape[0] // 8, 8, v.shape[1]), axis=0)

    def put(buf, j, k, value):
        tiles = buf.shape[2] // TILE
        if isinstance(j, int):
            buf[me.r, 4 * (j // tiles) + k : 4 * (j // tiles) + k + 1, lanes(j % tiles)] = value
        else:
            buf[me.r, pl.ds(4 * (j // tiles) + k, 1), lanes(j % tiles)] = value

    def masked(s):
        return jnp.concatenate([mask[s : s + CH]] * (TILE // 128), axis=1)

    def local_stats(a, buf, n_tiles, first=0):
        def body(j, carry):
            cols = lanes(j + first)
            for grp in (0, 1):
                acc = jnp.zeros((8, TILE), F32)
                for s, g in chunks:
                    if g == grp:
                        acc = acc + fold(a[s : s + CH, cols] * masked(s))
                total = jnp.sum(acc, axis=0, keepdims=True)
                n_own = jnp.maximum(cnt[me.r, grp : grp + 1, 0:1], 1.0)
                mean = total / n_own
                acc = jnp.zeros((8, TILE), F32)
                for s, g in chunks:
                    if g == grp:
                        d = (a[s : s + CH, cols] - mean) * masked(s)
                        acc = acc + fold(d * d)
                put(buf, j, 2 * grp, total)
                put(buf, j, 2 * grp + 1, jnp.sum(acc, axis=0, keepdims=True))
            return carry

        for j in range(n_tiles):
            body(j, 0) if n_tiles <= 2 else None
        if n_tiles > 2:
            lax.fori_loop(0, n_tiles, body, 0)

    def merge_stats(buf, mi, at=0):
        width = buf.shape[2]
        for hf in (0, 1):
            for grp in (0, 1):
                k = 4 * hf + 2 * grp
                total = sum(buf[i, k : k + 1] for i in range(n_rows))
                mean = total / count[grp]
                spread = jnp.zeros_like(mean)
                for i in range(n_rows):
                    n_i = cnt[i, grp : grp + 1, 0:1]
                    off = buf[i, k : k + 1] / jnp.maximum(n_i, 1.0) - mean
                    spread = spread + buf[i, k + 1 : k + 2] + n_i * (off * off)
                mi[2 * grp : 2 * grp + 1, at + hf * width : at + (hf + 1) * width] = mean
                mi[2 * grp + 1 : 2 * grp + 2, at + hf * width : at + (hf + 1) * width] = lax.rsqrt(
                    spread / count[grp] + eps
                )

    def merge_grads(buf, tot, at=0):
        width = buf.shape[2]
        for hf in (0, 1):
            block = buf[0, 4 * hf : 4 * hf + 4]
            for i in range(1, n_rows):
                block = block + buf[i, 4 * hf : 4 * hf + 4]
            tot[0:4, at + hf * width : at + (hf + 1) * width] = block

    def expand_params():
        blocks = par[...].reshape(n_dp * n_rows * 8, 128).astype(BF)
        n_dev = n_dp * n_rows
        for out, width in ((p1, mid), (p3, wide)):
            share = width // n_dev
            step = 512
            for t in range(width // step):
                lane = lax.broadcasted_iota(jnp.int32, (128, step), 1) + t * step
                place = lax.broadcasted_iota(jnp.int32, (128, step), 0)
                pick = jnp.where(lane % share == place, 1.0, 0.0).astype(BF)
                spread = dot(blocks, pick).reshape(n_dev, 8, step)
                owner = (lax.broadcasted_iota(jnp.int32, (8, step), 1) + t * step) // share
                total = jnp.zeros((8, step), F32)
                for d in range(n_dev):
                    total = total + jnp.where(owner == d, spread[d], 0.0)
                out[:, t * step : (t + 1) * step] = total

    def gain(out, i, cols):
        return out[i : i + 1, cols]

    small_piece.start_z()
    small_piece.start_xy()
    pieces[0].start_z()
    pieces[0].start_xy()
    exchanges[CNT][0]()
    plane.start()
    for p in pieces[1:]:
        p.start_xy()
    clear_rims(hv, hc)
    clear_rims(dv, dc)
    for cp in x_copies:
        cp.wait()
    arrange(x)
    for cp in cot_copies:
        cp.start()

    def step0(t):
        pieces[t].got_z(1)
        if t + 1 < len(pieces):
            pieces[t + 1].start_z()
        for k in range(2, me.nz):
            pieces[t].got_z(k)

    for k in range(1, me.nz):
        small_piece.got_z(k)
    step0(0)
    plane.diagonal()
    small_piece.diagonal()
    for t in range(wide // TILE):
        xt[t * TILE : (t + 1) * TILE, :] = x[:, t * TILE : (t + 1) * TILE].T
    step0(1)
    pieces[0].diagonal()
    small_piece.last()
    for cp in cot_copies:
        cp.wait()
    arrange(cot)
    step0(2)
    pieces[1].diagonal()
    pieces[0].last()
    small_piece.finish()
    expand_params()
    pieces[0].finish()
    exchanges[CNT][1]()

    def conv1(j, carry):
        w = wr[:, :, :, :, :, lanes(j)].reshape(wide, TILE)
        a1[:, lanes(j)] = dot(x[...], w)
        return carry

    for j in range(mid // TILE):
        conv1(j, 0)
    local_stats(a1, ex1, mid // TILE)
    exchanges[EX1][0]()
    step0(3)
    pieces[2].diagonal()
    pieces[1].last()
    exchanges[EX1][1]()
    merge_stats(ex1, mi1)

    def store_rows(v, c, s, cols, value):
        if s < pix_v:
            r, o = s // row_v, s % row_v
            v[1 + r, maps_v + o : maps_v + o + CH, cols] = value
        else:
            o = s - pix_v
            c[1, maps_c + o : maps_c + o + CH, cols] = value

    def act(a, mi, i, store):
        def body(j, carry):
            cols = lanes(j)
            scale = [mi[2 * g + 1 : 2 * g + 2, cols] * gain(p1, i, cols) for g in (0, 1)]
            mean = [mi[2 * g : 2 * g + 1, cols] for g in (0, 1)]
            shift = gain(p1, i + 1, cols)
            for s, g in chunks:
                zed = (a[s : s + CH, cols] - mean[g]) * scale[g] + shift
                store(s, cols, (zed * sigmoid(zed) * masked(s)).astype(BF))
            return carry

        for j in range(mid // TILE):
            body(j, 0)

    act(a1, mi1, 0, lambda s, cols, value: store_rows(hv, hc, s, cols, value))
    rim_h[0]()
    step0(4)
    plane.plane()
    pieces[3].diagonal()
    pieces[2].last()
    pieces[1].finish()
    def windows(v, c, dy, dx):
        left = [v[r + dy, dx * maps_v : dx * maps_v + row_v, :] for r in (0, 1)]
        return jnp.concatenate(left + [c[dy, dx * maps_c : dx * maps_c + row_c, :]], axis=0)

    def conv2(dy):
        left = jnp.concatenate([windows(hv, hc, dy, dx) for dx in range(3)], axis=1)
        for j in range(mid // TILE):
            w = ws[3 * dy : 3 * dy + 3, :, :, :, :, :, lanes(j)].reshape(3 * mid, TILE)
            part_sum = dot(left, w)
            a2[:, lanes(j)] = part_sum if dy == 1 else a2[:, lanes(j)] + part_sum

    pieces[2].finish()
    conv2(1)
    pieces[4].diagonal()
    rim_h[1]()
    conv2(0)
    pieces[3].last()
    pieces[3].finish()
    conv2(2)
    local_stats(a2, ex2, mid // TILE)
    exchanges[EX2][0]()
    pieces[4].last()
    exchanges[EX2][1]()
    merge_stats(ex2, mi2)

    def store_h2(s, cols, value):
        h2[s : s + CH, cols] = value

    act(a2, mi2, 2, store_h2)
    for cp in pool_copies:
        cp.wait()

    def conv3(j, carry):
        w = we[:, :, :, :, :, lanes(j)].reshape(mid, TILE)
        a3[:, lanes(j)] = dot(h2[...], w)
        return carry

    tiles = wide // TILE // 2
    pieces[4].finish()
    for j in range(tiles):
        conv3(j, 0)
    local_stats(a3, ex3.at[0], tiles)
    exchanges[EX3][0]()
    plane.last()
    plane.finish()
    for j in range(tiles, 2 * tiles):
        conv3(j, 0)
    local_stats(a3, ex3.at[1], tiles, tiles)
    exchanges[EX3 + 1][0]()
    h2t[...] = h2[...].T
    exchanges[EX3][1]()
    merge_stats(ex3.at[0], mi3)

    def out_copies(j, slot, views, crops):
        return [
            pltpu.make_async_copy(ysv.at[slot], views.at[:, :, :, lanes(j)], out_sem.at[slot, 0]),
            pltpu.make_async_copy(ysc.at[slot], crops.at[:, :, j], out_sem.at[slot, 1]),
        ]

    def store_out(slot, s, value):
        if s < pix_v:
            ysv[slot, :, s % row_v // maps_v, s // row_v, :] = value
        else:
            col, at = (s - pix_v) // maps_c, (s - pix_v) % maps_c
            for k in (0, 1):
                ysc[slot, at : at + CH, col, k, :] = value[:, k * 128 : (k + 1) * 128]

    def last(q, jj, carry):
        for slot in (0, 1):
            j = 2 * jj + slot
            cols = lanes(j)

            def free_slot():
                for cp in out_copies(j, slot, yv_h, yc_h):
                    cp.wait()

            if q > 0:
                free_slot()
            else:
                pl.when(jj > 0)(free_slot)

            mean = [mi3[2 * g : 2 * g + 1, cols] for g in (0, 1)]
            inv = [mi3[2 * g + 1 : 2 * g + 2, cols] for g in (0, 1)]
            scale = [inv[g] * gain(p3, 4, cols) for g in (0, 1)]
            sh = gain(p3, 5, cols)
            sums = [jnp.zeros((8, TILE), F32) for _ in range(4)]
            pooled = [jnp.zeros((CH, TILE), F32) for _ in range((maps_v + maps_c) // CH)]
            per_v, per_c = CH // cpv.shape[1], CH // cpc.shape[1]
            cps = [
                cpv[s : s + per_v, :, cols].reshape(CH, TILE) * (1.0 / valid_v)
                for s in range(0, cpv.shape[0], per_v)
            ] + [
                cpc[s : s + per_c, :, cols].reshape(CH, TILE) * (1.0 / valid_c)
                for s in range(0, cpc.shape[0], per_c)
            ]
            for s, g in chunks:
                which = (s % maps_v) // CH if g == 0 else (maps_v + (s - pix_v) % maps_c) // CH
                rows = slice(s, s + CH)
                m = masked(s)
                off = a3[rows, cols] - mean[g]
                pre = x[rows, cols].astype(F32) + (off * scale[g] + sh)
                sig = sigmoid(pre)
                act_out = pre * sig
                out = act_out * m
                store_out(slot, s, out)
                pooled[which] = pooled[which] + out
                slope = act_out + sig * (1.0 - act_out)
                gp = (cot[rows, cols].astype(F32) + cps[which]) * m * slope
                gpre[rows, cols] = gp
                sums[2 * g] = sums[2 * g] + fold(gp * off)
                sums[2 * g + 1] = sums[2 * g + 1] + fold(gp)
            for k in range(4):
                total = jnp.sum(sums[k], axis=0, keepdims=True)
                put(bx3.at[q], j - q * tiles, k, total * inv[k // 2] if k % 2 == 0 else total)
            for i, value in enumerate(pooled):
                pf[i * CH : (i + 1) * CH, cols] = value
                pb[i * CH : (i + 1) * CH, cols] = value.astype(BF)
            for cp in out_copies(j, slot, yv_h, yc_h):
                cp.start()
        return carry

    core_peer = {"dp": me.dp, "rows": me.x * 2 + 1 - me.c}
    chip_peer = {"dp": me.dp, "rows": (1 - me.x) * 2 + me.c}
    share = pb.shape[0] // 2
    mine, others = pl.ds(me.c * share, share), pl.ds((1 - me.c) * share, share)
    pool_core = remote(pb.at[others], pr.at[0], pool_s.at[0], pool_r.at[0], core_peer)
    pool_chip = remote(pb.at[mine], pr.at[1], pool_s.at[1], pool_r.at[1], chip_peer)
    pool_back = remote(pb.at[mine], pr.at[2], pool_s.at[2], pool_r.at[2], core_peer)
    lax.fori_loop(0, tiles // 2, functools.partial(last, 0), 0)
    exchanges[BX3][0]()
    exchanges[EX3 + 1][1]()
    merge_stats(ex3.at[1], mi3, wide // 2)
    lax.fori_loop(tiles // 2, tiles, functools.partial(last, 1), 0)
    exchanges[BX3 + 1][0]()
    pool_core.start()

    def coefs(mi, tot, gn, cols):
        out = []
        for g in (0, 1):
            mean, inv = mi[2 * g : 2 * g + 1, cols], mi[2 * g + 1 : 2 * g + 2, cols]
            dg, ds = tot[2 * g : 2 * g + 1, cols], tot[2 * g + 1 : 2 * g + 2, cols]
            out.append((mean, gn * inv, ds / count[g], dg / count[g] * inv))
        return out

    def norm_back(gz, a, co, s, cols):
        mean, k0, k1, k2 = co
        return (k0 * (gz - k1 - (a[s : s + CH, cols] - mean) * k2) * masked(s)).astype(BF)

    def grad_three(j, carry):
        cols = lanes(j)
        co = coefs(mi3, tot3, gain(p3, 4, cols), cols)
        for s, g in chunks:
            cot[s : s + CH, cols] = norm_back(gpre[s : s + CH, cols], a3, co[g], s, cols)
        gwe[:, :, :, :, :, cols] = (
            dot(h2t[...], cot[:, cols]).astype(BF).reshape(gwe.shape[:5] + (TILE,))
        )
        return carry

    def reducer(k, view, fc, f3, f2, fz):
        return Reduce(me, view, fc, f3, f2, fz, rs_s.at[k], rs_r.at[k])

    q_we = [
        reducer(
            i,
            lambda z, y, x, c, h, at=i * part: gwe.at[z, y, x, c, :, half(h, part, at, part)],
            lambda z, y, x, h, at=i * part: fc_we.at[z, y, x, :, half(h, part, at, part)],
            lambda h, i=i: f3_we.at[i, h],
            lambda h, i=i: f2_we.at[i, h],
            lambda k, i=i: fz_we.at[i, k],
        )
        for i in range(2)
    ]
    q_ws = [
        reducer(
            2 + i,
            lambda z, y, x, c, h, i=i: gws.at[3 * i : 3 * i + 3, z, y, x, c, :, uneven(h, mid)],
            lambda z, y, x, h, i=i: fc_ws.at[3 * i : 3 * i + 3, z, y, x, :, uneven(h, mid)],
            lambda h, i=i: f3_ws.at[3 * i : 3 * i + 3, :, :, :, uneven(h, mid)],
            lambda h, i=i: f2_ws.at[3 * i : 3 * i + 3, :, :, uneven(h, mid)],
            lambda k, i=i: fz_ws.at[k, 3 * i : 3 * i + 3],
        )
        for i in range(3)
    ]
    few = wr.shape[4] // 2
    q_wr = [
        reducer(
            5 + i,
            lambda z, y, x, c, h, i=i: gwr.at[z, y, x, c, i * few : (i + 1) * few, half(h, mid)],
            lambda z, y, x, h, i=i: fc_wr.at[z, y, x, i * few : (i + 1) * few, half(h, mid)],
            lambda h, i=i: f3_wr.at[h, :, :, i * few : (i + 1) * few],
            lambda h, i=i: f2_wr.at[h, :, i * few : (i + 1) * few],
            lambda k, i=i: fz_wr.at[k, i * few : (i + 1) * few],
        )
        for i in range(2)
    ]

    exchanges[BX3][1]()
    merge_grads(bx3.at[0], tot3)
    for j in range(tiles):
        grad_three(j, 0)
    q_we[0].start()
    exchanges[BX3 + 1][1]()
    merge_grads(bx3.at[1], tot3, wide // 2)
    q_we[0].stage2()
    for j in range(tiles, 2 * tiles):
        grad_three(j, 0)
    q_we[1].start()

    def grad_act(gh, a, mi, i, buf, j):
        cols = lanes(j)
        gn, sh = gain(p1, i, cols), gain(p1, i + 1, cols)
        sums = [jnp.zeros((8, TILE), F32) for _ in range(4)]
        for s, g in chunks:
            rows = slice(s, s + CH)
            mean, inv = mi[2 * g : 2 * g + 1, cols], mi[2 * g + 1 : 2 * g + 2, cols]
            off = a[rows, cols] - mean
            zed = off * (inv * gn) + sh
            sig = sigmoid(zed)
            gz = gh[rows, cols] * masked(s) * (sig * (1.0 + zed * (1.0 - sig)))
            gh[rows, cols] = gz
            sums[2 * g] = sums[2 * g] + fold(gz * off)
            sums[2 * g + 1] = sums[2 * g + 1] + fold(gz)
        for k in range(4):
            total = jnp.sum(sums[k], axis=0, keepdims=True)
            inv = mi[2 * (k // 2) + 1 : 2 * (k // 2) + 2, cols]
            put(buf, j, k, total * inv if k % 2 == 0 else total)

    for j in range(mid // TILE):
        w = tile_rows(we, j).reshape(TILE, wide)
        gact[j, :, :] = dot_t(cot[...], w)

    class Cols:
        def __getitem__(self, key):
            rows, cols = key
            return gact[self.j, rows, :]

        def __setitem__(self, key, value):
            rows, cols = key
            gact[self.j, rows, :] = value

    ghs = Cols()
    for j in range(mid // TILE):
        ghs.j = j
        grad_act(ghs, a2, mi2, 2, bx2, j)
    exchanges[BX2][0]()
    q_we[1].stage2()
    pool_core.wait_recv()
    pb[mine] = (pf[mine] + pr[0].astype(F32)).astype(BF)
    exchanges[BX2][1]()
    merge_grads(bx2, tot2)

    def grad_norm_all(a, mi, tot, i, store):
        for j in range(mid // TILE):
            ghs.j = j
            cols = lanes(j)
            co = coefs(mi, tot, gain(p1, i, cols), cols)
            for s, g in chunks:
                store(s, cols, norm_back(ghs[s : s + CH, cols], a, co[g], s, cols))

    grad_norm_all(a2, mi2, tot2, 2, lambda s, cols, value: store_rows(dv, dc, s, cols, value))
    rim_d[0]()
    q_we[0].stage3()

    def grad_taps(dy):
        right = windows(dv, dc, 1, 1)
        for dx in range(3):
            total = dot_r(windows(hv, hc, dy, dx), right)
            gws[3 * dy + dx] = total.astype(BF).reshape(gws.shape[1:])

    def conv2_back(dy):
        left = jnp.concatenate([windows(dv, dc, 2 - dy, 2 - dx) for dx in range(3)], axis=1)
        for j in range(mid // TILE):
            w = jnp.concatenate(
                [tile_rows(ws.at[3 * dy + dx], j).reshape(TILE, mid) for dx in range(3)], axis=1
            )
            part_sum = dot_t(left, w)
            gact[j] = part_sum if dy == 1 else gact[j] + part_sum

    grad_taps(0)
    q_ws[0].start()
    grad_taps(1)
    q_ws[1].start()
    q_ws[0].stage2()
    conv2_back(1)
    q_we[1].stage3()
    q_ws[1].stage2()
    q_we[0].stage4()
    rim_d[1]()
    conv2_back(0)
    conv2_back(2)
    for j in range(mid // TILE):
        ghs.j = j
        grad_act(ghs, a1, mi1, 0, bx1, j)
    exchanges[BX1][0]()
    grad_taps(2)
    q_ws[2].start()
    q_we[1].stage4()
    q_ws[0].stage3()
    exchanges[BX1][1]()
    merge_grads(bx1, tot1)

    def store_ga1(s, cols, value):
        ga1[s : s + CH, cols] = value

    grad_norm_all(a1, mi1, tot1, 0, store_ga1)
    for t in range(wide // TILE):
        block = dot(xt[t * TILE : (t + 1) * TILE, :], ga1[...]).astype(BF)
        gwr[t // 2, t % 2] = block.reshape(gwr.shape[2:])
    for q in q_wr:
        q.start()
    q_ws[2].stage2()
    q_ws[1].stage3()
    q_wr[0].stage2()
    q_wr[1].stage2()
    q_ws[0].stage4()

    n_dev = n_dp * n_rows

    def three(v):
        hi = v.astype(BF)
        rest = v - hi.astype(F32)
        mid_part = rest.astype(BF)
        return hi, mid_part, (rest - mid_part.astype(F32)).astype(BF)

    def owner_blocks(rows, width):
        share = width // n_dev
        step = 512
        total = jnp.zeros((n_dp * 8, 128), F32)
        for t in range(width // step):
            place = lax.broadcasted_iota(jnp.int32, (step, 128), 1)
            lane = lax.broadcasted_iota(jnp.int32, (step, 128), 0) + t * step
            pick = jnp.where(lane % share == place, 1.0, 0.0).astype(BF)
            owner = (lax.broadcasted_iota(jnp.int32, (8, step), 1) + t * step) // share
            vec = rows[:, t * step : (t + 1) * step]
            stack = jnp.concatenate(
                [jnp.where(owner == d * n_rows + me.r, vec, 0.0) for d in range(n_dp)], axis=0
            )
            for part in three(stack):
                total = total + dot(part, pick)
        return total

    small_rows = [t_[0:1] + t_[2:3] if k == 0 else t_[1:2] + t_[3:4] for t_ in (tot1, tot2) for k in (0, 1)]
    wide_rows = [tot3[0:1] + tot3[2:3], tot3[1:2] + tot3[3:4]]
    narrow = jnp.concatenate(small_rows + [jnp.zeros((4, mid), F32)], axis=0)
    broad = jnp.concatenate([jnp.zeros((4, wide), F32)] + wide_rows + [jnp.zeros((2, wide), F32)], axis=0)
    sb[...] = (owner_blocks(narrow, mid) + owner_blocks(broad, wide)).reshape(sb.shape)

    def small_cp(d, recv):
        peer = (me.dp + n_dp - d) % n_dp if recv else (me.dp + d) % n_dp
        return remote(sb.at[peer], rb.at[d - 1], sm_s.at[d - 1], sm_r.at[d - 1], {"dp": peer, "rows": me.r})

    for d in range(1, n_dp):
        small_cp(d, False).start()
    q_ws[2].stage3()
    q_ws[1].stage4()

    def grad_in(j):
        cols, slot = lanes(j), j % 2
        previous = (j - 2, gv_h, gc_h) if j >= 2 else (wide // TILE - 2 + j, yv_h, yc_h)
        for cp in out_copies(previous[0], slot, previous[1], previous[2]):
            cp.wait()
        w = wr[j // 2, j % 2].reshape(TILE, mid)
        gpre[:, cols] = gpre[:, cols] + dot_t(ga1[...], w)
        for s, g in chunks:
            store_out(slot, s, gpre[s : s + CH, cols])
        for cp in out_copies(j, slot, gv_h, gc_h):
            cp.start()

    grad_in(0)
    grad_in(1)
    q_wr[0].stage3()
    grad_in(2)
    q_wr[1].stage3()
    pool_chip.start()
    q_ws[2].stage4()
    grad_in(3)
    grad_in(4)
    q_wr[0].stage4()
    q_wr[1].stage4()
    pool_chip.wait_send()
    pool_chip.wait_recv()
    pb[mine] = (pb[mine].astype(F32) + pr[1].astype(F32)).astype(BF)
    pool_back.start()
    for j in range(5, wide // TILE):
        grad_in(j)
    gwe_o[:, part:wide] = q_we[1].finish()
    gwe_o[:, 0:part] = q_we[0].finish()
    gws_o[0:3] = q_ws[0].finish()
    pool_core.wait_send()
    pool_back.wait_recv()
    pb[others] = pr[2]
    for out, at, maps, valid in ((poolv_o, 0, maps_v, valid_v), (poolc_o, maps_v, maps_c, valid_c)):
        out[...] = (pb[at : at + maps].astype(F32) * (1.0 / valid)).reshape(out.shape)
    results = [
        pltpu.make_async_copy(src, dst, res_sem.at[i])
        for i, (src, dst) in enumerate(((poolv_o, poolv_h), (poolc_o, poolc_h), (gwe_o, gwe_h)))
    ]
    for cp in results:
        cp.start()
    total = sb[me.dp]
    for d in range(1, n_dp):
        small_cp(d, True).wait_recv()
        total = total + rb[d - 1]
    small_o[...] = total
    gws_o[3:6] = q_ws[1].finish()
    gws_o[6:9] = q_ws[2].finish()
    for i, q in enumerate(q_wr):
        gwr_o[i * few : (i + 1) * few] = q.finish()

    for cp in results:
        cp.wait()
    pool_back.wait_send()
    for j in (wide // TILE - 2, wide // TILE - 1):
        for cp in out_copies(j, j % 2, gv_h, gc_h):
            cp.wait()
    small_piece.drain()
    for p in pieces + [plane]:
        p.drain()
    for e in exchanges:
        e[2]()
    rim_h[2]()
    rim_d[2]()
    for q in q_we + q_ws + q_wr:
        q.drain()
    for d in range(1, n_dp):
        small_cp(d, False).wait_send()


def hand_over(*refs):
    n = (len(refs) - 8) // 3
    srcs, small, dsts = refs[:n], refs[n], refs[n + 1 : 2 * n + 1]
    cuts, bufs, sem = refs[2 * n + 1 : 2 * n + 7], refs[2 * n + 7 : -1], refs[-1]
    parts = 2
    ways = []
    for i, (src, buf, dst) in enumerate(zip(srcs, bufs, dsts)):
        count = parts if src.shape[0] % parts == 0 else 1
        per = src.shape[0] // count
        for k in range(count):
            rows = slice(k * per, (k + 1) * per)
            ways.append(
                (
                    k,
                    pltpu.make_async_copy(src.at[rows], buf.at[rows], sem.at[0, i, k]),
                    pltpu.make_async_copy(buf.at[rows], dst.at[rows], sem.at[1, i, k]),
                )
            )
    ways.sort(key=lambda way: way[0])
    for _, inward, _ in ways:
        inward.start()
    for i, ref in enumerate(cuts):
        ref[...] = small[i : i + 1, 0 : ref.shape[1]]
    for _, inward, outward in ways:
        inward.wait()
        outward.start()
    for _, _, outward in ways:
        outward.wait()


def block_step(n_dp, n_rows, xv, xc, mv, mc, wr, ws, we, g1, s1, g2, s2, g3, s3, cv, cc, cpv, cpc):
    img, views, rows_v, cols_v, wide = xv.shape
    crops, cols_c = xc.shape[1], xc.shape[3]
    mid = wr.shape[1]
    maps_v, maps_c = img * views, img * crops
    pix_v, pix_c = rows_v * cols_v * maps_v, cols_c * maps_c
    pix = pix_v + pix_c
    valid_v, valid_c = (rows_v * n_rows - 1) * cols_v, (n_rows - 1) * cols_c
    nz, nx = n_dp // 2, n_rows // 2

    def views_in(t):
        return t.transpose(0, 1, 3, 2, 4).reshape(maps_v, cols_v, rows_v, wide)

    def crops_in(t):
        return t.transpose(0, 2, 3, 1, 4).reshape(img, cols_c, crops, wide)

    grid4 = (nz, 2, nx, 2)
    vm = pl.BlockSpec(memory_space=pltpu.VMEM)
    hbm = pl.BlockSpec(memory_space=pl.ANY)
    s_wr, s_we = wr.shape[0], we.shape[0]
    V = pltpu.VMEM
    D = pltpu.SemaphoreType.DMA

    scratch = [
        V(cpv.shape, F32), V(cpc.shape, F32), V((s_we, wide), F32), D((3,)),
        V((s_wr, mid), F32), V((9, s_we, mid), F32), V((s_we, wide), F32),
        V(grid4 + (s_wr, mid), BF), V((9,) + grid4 + (s_we, mid), BF), V(grid4 + (s_we, wide), BF),
        V(grid4 + (8, 128), F32),
        V((pix, 128), F32), V((cols_v, maps_v, 2, wide), BF), V((img, cols_c, crops, wide), BF),
        V((img, views, wide), F32), V((img, crops, wide), F32),
        V((pix, wide), BF), V((wide, pix), BF), V((pix, wide), BF),
        V((pix, mid), F32), V((pix, mid), F32), V((pix, wide), F32), V((pix, wide), F32),
        V((2, maps_v, cols_v, 2, TILE), F32), V((2, maps_c, cols_c, TILE // 128, 128), F32), V((2, pix, TILE), F32),
        V((4, (cols_v + 2) * maps_v, mid), BF), V((3, (cols_c + 2) * maps_c, mid), BF),
        V((4, (cols_v + 2) * maps_v, mid), BF), V((3, (cols_c + 2) * maps_c, mid), BF),
        V((pix, mid), BF), V((mid, pix), BF), V((pix, mid), BF),
        V(grid4 + (s_wr, mid), BF), V((9,) + grid4 + (s_we, mid), BF), V(grid4 + (s_we, wide), BF),
        V((nz, 2, nx, s_we, wide), BF), V((9, nz, 2, nx, s_we, mid), BF), V((nz, 2, nx, s_wr, mid), BF),
        V((2, 2, nz, 2, s_we, wide // 4), BF), V((9, nz, 2, s_we, mid), BF), V((2, nz, 2, s_wr, mid // 2), BF),
        V((2, 2, nz, s_we, wide // 4), BF), V((9, nz, s_we, mid), BF), V((2, nz, s_wr, mid // 2), BF),
        V((2, nz - 1, s_we, wide // 2), BF), V((nz - 1, 9, s_we, mid), BF), V((nz - 1, s_wr, mid), BF),
        V((8, mid), F32), V((8, wide), F32),
        V((4, mid), F32), V((4, mid), F32), V((4, wide), F32),
        V((n_rows, 8, 128), F32),
        V((n_rows, 8, mid // 2), F32), V((n_rows, 8, mid // 2), F32), V((2, n_rows, 8, wide // 4), F32),
        V((n_rows, 8, mid // 2), F32), V((n_rows, 8, mid // 2), F32), V((2, n_rows, 8, wide // 4), F32),
        V((4, mid), F32), V((4, mid), F32), V((4, wide), F32),
        V((maps_v + maps_c, wide), F32), V((maps_v + maps_c, wide), BF), V((3, (maps_v + maps_c) // 2, wide), BF),
        V((n_dp, 8, 128), F32), V((n_dp - 1, 8, 128), F32),
        D((3, max(cols_v + 1, 5))), D((2, 2)), D((7, 5 * nz + 4)), D((7, 5 * nz + 4)), D((7, 6 + nz)), D((7, 6 + nz)),
        D((9, n_rows - 1)), D((9, n_rows - 1)), D((2, 4)), D((2, 4)), D((3,)), D((3,)), D((n_dp - 1,)), D((n_dp - 1,)),
    ]
    out_v = jax.ShapeDtypeStruct((maps_v, cols_v, 2, wide), F32)
    out_c = jax.ShapeDtypeStruct((maps_c, cols_c, wide // TILE, TILE // 128, 128), F32)
    outs = pl.pallas_call(
        functools.partial(kernel, n_dp, n_rows, (maps_v, cols_v, maps_c, cols_c, valid_v, valid_c)),
        out_shape=[
            out_v, out_c, out_v, out_c,
            jax.ShapeDtypeStruct(cpv.shape, F32), jax.ShapeDtypeStruct(cpc.shape, F32),
            jax.ShapeDtypeStruct((s_we, wide), F32), jax.ShapeDtypeStruct((s_wr, mid), F32),
            jax.ShapeDtypeStruct((9, s_we, mid), F32), jax.ShapeDtypeStruct((8, 128), F32),
        ],
        in_specs=[hbm] * 9 + [vm] * 8,
        out_specs=[hbm] * 7 + [vm] * 3,
        scratch_shapes=scratch,
        compiler_params=pltpu.CompilerParams(
            collective_id=0, has_side_effects=True, vmem_limit_bytes=63 << 20
        ),
    )(
        views_in(xv), crops_in(xc), views_in(cv), crops_in(cc), cpv, cpc,
        wr, ws.reshape(9, s_we, mid), we, mv.transpose(1, 2, 0), mc.transpose(1, 2, 0),
        g1.reshape(1, -1), s1.reshape(1, -1), g2.reshape(1, -1), s2.reshape(1, -1),
        g3.reshape(1, -1), s3.reshape(1, -1),
    )
    e = mid // (n_dp * n_rows)
    f = wide // (n_dp * n_rows)
    big, shapes = outs[:-1], [jax.ShapeDtypeStruct(o.shape, F32) for o in outs[:-1]]
    res = pl.pallas_call(
        hand_over,
        out_shape=shapes + [jax.ShapeDtypeStruct((1, w), F32) for w in (e, e, e, e, f, f)],
        in_specs=[hbm] * len(big) + [vm],
        out_specs=[hbm] * len(big) + [vm] * 6,
        scratch_shapes=[V(o.shape, F32) for o in big] + [D((2, len(big), 4))],
        compiler_params=pltpu.CompilerParams(vmem_limit_bytes=62 << 20),
    )(*outs)
    yv, yc, gv, gc, pool_v, pool_c, gwe, gwr, gws = res[:9]
    small = [r.reshape(-1) for r in res[9:]]

    def views_out(t):
        return t.reshape(img, views, cols_v, rows_v, wide).transpose(0, 1, 3, 2, 4)

    def crops_out(t):
        return t.reshape(img, crops, 1, cols_c, wide)

    return (
        views_out(yv), crops_out(yc),
        pool_v, pool_c,
        views_out(gv), crops_out(gc),
        gwr, gws.reshape(3, 3, s_we, mid), gwe,
        *small,
    )


def fits(xv, xc, we):
    return we.shape[0] % 16 == 0 and xv.shape[2] == 2 and xc.shape[2] == 1


def with_halo(block, sides, width):
    for axis, dim in sides:
        count = lax.axis_size(axis)
        forward = [(i, i + 1) for i in range(count - 1)]
        backward = [(target, source) for source, target in forward]
        low = lax.ppermute(
            lax.slice_in_dim(block, block.shape[dim] - width, None, axis=dim), axis, forward
        )
        high = lax.ppermute(lax.slice_in_dim(block, 0, width, axis=dim), axis, backward)
        block = jnp.concatenate([low, block, high], axis=dim)
    return block


def from_behind(array, axis, by):
    peers = lax.axis_size(axis)
    pairs = [(i, i + by) for i in range(peers) if 0 <= i + by < peers]
    return lax.ppermute(array, axis, pairs)


def silu_slope(value):
    sig = jax.nn.sigmoid(value)
    return sig * (1.0 + value * (1.0 - sig))


def pixel_mask(mask_rows, col_count):
    expanded = jnp.broadcast_to(
        mask_rows.astype(jnp.float32)[..., None], mask_rows.shape + (col_count,)
    )
    return expanded.reshape(-1, 1)


def by_group(in_views, view_value, crop_value):
    return jnp.where(in_views, view_value, crop_value)


def norm_forward(acts, mask_col, view_pixels, in_views, counts, gain_vec, shift_vec):
    masked = acts * mask_col
    totals = lax.psum(
        (jnp.sum(masked[:view_pixels], axis=0), jnp.sum(masked[view_pixels:], axis=0)), "rows"
    )
    centered = acts - by_group(in_views, totals[0] / counts[0], totals[1] / counts[1])
    squares = jnp.square(centered * mask_col)
    spread = lax.psum(
        (jnp.sum(squares[:view_pixels], axis=0), jnp.sum(squares[view_pixels:], axis=0)), "rows"
    )
    inv_rows = by_group(
        in_views, lax.rsqrt(spread[0] / counts[0] + eps), lax.rsqrt(spread[1] / counts[1] + eps)
    )
    normal = centered * inv_rows
    return (normal * gain_vec + shift_vec, normal, inv_rows)


def norm_backward(grad_z, normal, inv_rows, mask_col, view_pixels, in_views, counts, gain_vec):
    product = grad_z * normal
    partials = (
        jnp.sum(product[:view_pixels], axis=0),
        jnp.sum(grad_z[:view_pixels], axis=0),
        jnp.sum(product[view_pixels:], axis=0),
        jnp.sum(grad_z[view_pixels:], axis=0),
    )
    totals = (
        lax.psum(partials[0].astype(jnp.bfloat16), "rows").astype(jnp.float32),
        lax.psum(partials[1].astype(jnp.bfloat16), "rows").astype(jnp.float32),
        lax.psum(partials[2].astype(jnp.bfloat16), "rows").astype(jnp.float32),
        lax.psum(partials[3].astype(jnp.bfloat16), "rows").astype(jnp.float32),
    )
    scale_mean = by_group(in_views, totals[0] / counts[0], totals[2] / counts[1])
    shift_mean = by_group(in_views, totals[1] / counts[0], totals[3] / counts[1])
    grad_acts = gain_vec * inv_rows * (grad_z - shift_mean - normal * scale_mean) * mask_col
    return (grad_acts.astype(jnp.bfloat16), partials[0] + partials[2], partials[1] + partials[3])


def with_rims(feature_map):
    extended = with_halo(feature_map, (("rows", 1),), 1)
    return jnp.pad(extended, ((0, 0), (0, 0), (1, 1), (0, 0)))


def gather_taps(extended, row_count, col_count):
    windows = []
    for row_step in range(3):
        for col_step in range(3):
            windows.append(
                extended[:, row_step : row_step + row_count, col_step : col_step + col_count, :]
            )
    return jnp.concatenate(windows, axis=-1).reshape(-1, 9 * extended.shape[-1])


def spread_taps(grad_patches, map_count, row_count, col_count, mid_width):
    pieces = grad_patches.reshape(map_count, row_count, col_count, 9, mid_width)
    padded = jnp.zeros((map_count, row_count + 2, col_count + 2, mid_width), jnp.float32)
    tap_index = 0
    for row_step in range(3):
        for col_step in range(3):
            padded = padded.at[
                :, row_step : row_step + row_count, col_step : col_step + col_count, :
            ].add(pieces[:, :, :, tap_index, :])
            tap_index += 1
    inside = padded[:, 1 : row_count + 1, 1 : col_count + 1, :]
    from_below = from_behind(
        padded[:, 0, 1 : col_count + 1, :].astype(jnp.bfloat16), "rows", -1
    ).astype(jnp.float32)
    from_above = from_behind(
        padded[:, row_count + 1, 1 : col_count + 1, :].astype(jnp.bfloat16), "rows", 1
    ).astype(jnp.float32)
    inside = inside.at[:, row_count - 1].add(from_below)
    inside = inside.at[:, 0].add(from_above)
    return inside.reshape(-1, mid_width)


def contract_rows(left, right):
    return lax.dot_general(
        left, right, (((0,), (0,)), ((), ())), preferred_element_type=jnp.float32
    )


def contract_cols(left, right):
    return lax.dot_general(
        left, right, (((1,), (1,)), ((), ())), preferred_element_type=jnp.float32
    )


def shards(
    x_views,
    x_crops,
    mask_views,
    mask_crops,
    w_reduce,
    w_spatial,
    w_expand,
    gain_reduce,
    shift_reduce,
    gain_spatial,
    shift_spatial,
    gain_expand,
    shift_expand,
    cot_views,
    cot_crops,
    cot_pool_views,
    cot_pool_crops,
):
    low_type = jnp.bfloat16
    gathered = (
        lax.all_gather(w_reduce.astype(low_type), ("dp", "rows"), axis=0, tiled=True),
        lax.all_gather(w_spatial.astype(low_type), ("dp", "rows"), axis=2, tiled=True),
        lax.all_gather(w_expand.astype(low_type), ("dp", "rows"), axis=0, tiled=True),
        lax.all_gather(gain_reduce.astype(low_type), ("dp", "rows"), axis=0, tiled=True),
        lax.all_gather(shift_reduce.astype(low_type), ("dp", "rows"), axis=0, tiled=True),
        lax.all_gather(gain_spatial.astype(low_type), ("dp", "rows"), axis=0, tiled=True),
        lax.all_gather(shift_spatial.astype(low_type), ("dp", "rows"), axis=0, tiled=True),
        lax.all_gather(gain_expand.astype(low_type), ("dp", "rows"), axis=0, tiled=True),
        lax.all_gather(shift_expand.astype(low_type), ("dp", "rows"), axis=0, tiled=True),
    )
    weight_one, weight_two, weight_three = (gathered[0], gathered[1], gathered[2])
    gain_one, shift_one, gain_two, shift_two, gain_three, shift_three = [
        entry.astype(jnp.float32) for entry in gathered[3:]
    ]
    in_width = weight_one.shape[0]
    mid_width = weight_one.shape[1]
    view_maps = x_views.shape[0] * x_views.shape[1]
    view_rows, view_cols = (x_views.shape[2], x_views.shape[3])
    crop_maps = x_crops.shape[0] * x_crops.shape[1]
    crop_rows, crop_cols = (x_crops.shape[2], x_crops.shape[3])
    view_pixels = view_maps * view_rows * view_cols
    total_pixels = view_pixels + crop_maps * crop_rows * crop_cols
    row_parts = lax.axis_size("rows")
    view_valid = (view_rows * row_parts - 1) * view_cols
    crop_valid = (crop_rows * row_parts - 1) * crop_cols
    counts = (float(view_maps * view_valid), float(crop_maps * crop_valid))
    mask_col = jnp.concatenate(
        [pixel_mask(mask_views, view_cols), pixel_mask(mask_crops, crop_cols)], axis=0
    )
    in_views = lax.broadcasted_iota(jnp.int32, (total_pixels, 1), 0) < view_pixels
    inputs = jnp.concatenate([x_views.reshape(-1, in_width), x_crops.reshape(-1, in_width)], axis=0)
    acts_one = jnp.dot(inputs, weight_one, preferred_element_type=jnp.float32)
    z_one, normal_one, inv_one = norm_forward(
        acts_one, mask_col, view_pixels, in_views, counts, gain_one, shift_one
    )
    hidden_one = (jax.nn.silu(z_one) * mask_col).astype(low_type)
    view_hidden = hidden_one[:view_pixels].reshape(view_maps, view_rows, view_cols, mid_width)
    crop_hidden = hidden_one[view_pixels:].reshape(crop_maps, crop_rows, crop_cols, mid_width)
    patches = jnp.concatenate(
        [
            gather_taps(with_rims(view_hidden), view_rows, view_cols),
            gather_taps(with_rims(crop_hidden), crop_rows, crop_cols),
        ],
        axis=0,
    )
    spatial_flat = weight_two.reshape(9 * mid_width, mid_width)
    acts_two = jnp.dot(patches, spatial_flat, preferred_element_type=jnp.float32)
    z_two, normal_two, inv_two = norm_forward(
        acts_two, mask_col, view_pixels, in_views, counts, gain_two, shift_two
    )
    hidden_two = (jax.nn.silu(z_two) * mask_col).astype(low_type)
    acts_three = jnp.dot(hidden_two, weight_three, preferred_element_type=jnp.float32)
    z_three, normal_three, inv_three = norm_forward(
        acts_three, mask_col, view_pixels, in_views, counts, gain_three, shift_three
    )
    pre_act = inputs.astype(jnp.float32) + z_three
    result = jax.nn.silu(pre_act) * mask_col
    pooled = (
        lax.psum(
            jnp.sum(
                result[:view_pixels].reshape(view_maps, view_rows * view_cols, in_width), axis=1
            ).astype(jnp.bfloat16),
            "rows",
        ).astype(jnp.float32),
        lax.psum(
            jnp.sum(
                result[view_pixels:].reshape(crop_maps, crop_rows * crop_cols, in_width), axis=1
            ).astype(jnp.bfloat16),
            "rows",
        ).astype(jnp.float32),
    )
    pool_views = (pooled[0] / view_valid).reshape(cot_pool_views.shape)
    pool_crops = (pooled[1] / crop_valid).reshape(cot_pool_crops.shape)
    view_grad = (
        cot_views.astype(jnp.float32).reshape(view_maps, view_rows * view_cols, in_width)
        + cot_pool_views.reshape(view_maps, 1, in_width) / view_valid
    )
    crop_grad = (
        cot_crops.astype(jnp.float32).reshape(crop_maps, crop_rows * crop_cols, in_width)
        + cot_pool_crops.reshape(crop_maps, 1, in_width) / crop_valid
    )
    grad_out = jnp.concatenate(
        [view_grad.reshape(-1, in_width), crop_grad.reshape(-1, in_width)], axis=0
    )
    grad_pre = grad_out * mask_col * silu_slope(pre_act)
    grad_three, dgain_three, dshift_three = norm_backward(
        grad_pre, normal_three, inv_three, mask_col, view_pixels, in_views, counts, gain_three
    )
    grad_expand = contract_rows(hidden_two, grad_three)
    grad_hidden_two = contract_cols(grad_three, weight_three)
    grad_z_two = grad_hidden_two * mask_col * silu_slope(z_two)
    grad_two, dgain_two, dshift_two = norm_backward(
        grad_z_two, normal_two, inv_two, mask_col, view_pixels, in_views, counts, gain_two
    )
    grad_spatial = contract_rows(patches, grad_two).reshape(3, 3, mid_width, mid_width)
    grad_patches = contract_cols(grad_two, spatial_flat)
    grad_hidden_one = jnp.concatenate(
        [
            spread_taps(grad_patches[:view_pixels], view_maps, view_rows, view_cols, mid_width),
            spread_taps(grad_patches[view_pixels:], crop_maps, crop_rows, crop_cols, mid_width),
        ],
        axis=0,
    )
    grad_z_one = grad_hidden_one * mask_col * silu_slope(z_one)
    grad_one, dgain_one, dshift_one = norm_backward(
        grad_z_one, normal_one, inv_one, mask_col, view_pixels, in_views, counts, gain_one
    )
    grad_reduce = contract_rows(inputs, grad_one)
    grad_inputs = contract_cols(grad_one, weight_one) + grad_pre
    summed = (
        lax.psum_scatter(grad_reduce, ("dp", "rows"), scatter_dimension=0, tiled=True),
        lax.psum_scatter(grad_spatial, ("dp", "rows"), scatter_dimension=2, tiled=True),
        lax.psum_scatter(grad_expand, ("dp", "rows"), scatter_dimension=0, tiled=True),
        lax.psum_scatter(dgain_one, ("dp", "rows"), scatter_dimension=0, tiled=True),
        lax.psum_scatter(dshift_one, ("dp", "rows"), scatter_dimension=0, tiled=True),
        lax.psum_scatter(dgain_two, ("dp", "rows"), scatter_dimension=0, tiled=True),
        lax.psum_scatter(dshift_two, ("dp", "rows"), scatter_dimension=0, tiled=True),
        lax.psum_scatter(dgain_three, ("dp", "rows"), scatter_dimension=0, tiled=True),
        lax.psum_scatter(dshift_three, ("dp", "rows"), scatter_dimension=0, tiled=True),
    )
    out_views = result[:view_pixels].reshape(x_views.shape)
    out_crops = result[view_pixels:].reshape(x_crops.shape)
    grad_views = grad_inputs[:view_pixels].reshape(x_views.shape)
    grad_crops = grad_inputs[view_pixels:].reshape(x_crops.shape)
    return (
        out_views,
        out_crops,
        pool_views,
        pool_crops,
        grad_views,
        grad_crops,
        summed[0],
        summed[1],
        summed[2],
        summed[3],
        summed[4],
        summed[5],
        summed[6],
        summed[7],
        summed[8],
    )


def solution(mesh):
    in_specs = (
        P("dp", None, "rows", None, None),
        P("dp", None, "rows", None, None),
        P("dp", None, "rows"),
        P("dp", None, "rows"),
        P(("dp", "rows"), None),
        P(None, None, ("dp", "rows"), None),
        P(("dp", "rows"), None),
        P(("dp", "rows")),
        P(("dp", "rows")),
        P(("dp", "rows")),
        P(("dp", "rows")),
        P(("dp", "rows")),
        P(("dp", "rows")),
        P("dp", None, "rows", None, None),
        P("dp", None, "rows", None, None),
        P("dp", None, None),
        P("dp", None, None),
    )
    out_specs = (
        P("dp", None, "rows", None, None),
        P("dp", None, "rows", None, None),
        P("dp", None, None),
        P("dp", None, None),
        P("dp", None, "rows", None, None),
        P("dp", None, "rows", None, None),
        P(("dp", "rows"), None),
        P(None, None, ("dp", "rows"), None),
        P(("dp", "rows"), None),
        P(("dp", "rows")),
        P(("dp", "rows")),
        P(("dp", "rows")),
        P(("dp", "rows")),
        P(("dp", "rows")),
        P(("dp", "rows")),
    )
    def step(*args):
        if fits(args[0], args[1], args[6]):
            return block_step(mesh.shape["dp"], mesh.shape["rows"], *args)
        return shards(*args)

    return jax.shard_map(step, mesh=mesh, in_specs=in_specs, out_specs=out_specs, check_vma=False)
```
